32 devices in a mesh: section: 2 (over core), dp: 16 (over z, y, x).
Axes of the slice: x: 2, y: 2, z: 4, core: 2. Of those that a mesh axis runs over, the one named last changes fastest.
Arguments:
- tokens: bfloat16 [32768, 768], P('dp'), may hold values from -6 to 6
- out_grad: bfloat16 [32768, 768], P('dp'), may hold values from -6 to 6
- seq_lengths: int32 [32, 8], P('dp'), may hold values from 0 to 1024, as said below
- half_weights: bfloat16 [2, 768, 3072], P('section', 'dp'), may hold values from -0.21875 to 0.21875
- down_weight: bfloat16 [3072, 768], P(('section', 'dp')), may hold values from -0.109375 to 0.109375
- pre_gain: float32 [768], replicated, may hold values from 0.25 to 1.75
- pre_shift: float32 [768], replicated, may hold values from -2 to 2
- query_bias: float32 [768], replicated, may hold values from -2 to 2
- value_bias: float32 [768], replicated, may hold values from -2 to 2
- sub_gain: float32 [768], replicated, may hold values from 0.25 to 1.75
- sub_shift: float32 [768], replicated, may hold values from -2 to 2
- out_bias: float32 [768], replicated, may hold values from -2 to 2
- ffn_gain: float32 [768], replicated, may hold values from 0.25 to 1.75
- ffn_shift: float32 [768], replicated, may hold values from -2 to 2
- up_bias: float32 [3072], replicated, may hold values from -2 to 2
- mid_gain: float32 [3072], replicated, may hold values from 0.25 to 1.75
- mid_shift: float32 [3072], replicated, may hold values from -2 to 2
- down_bias: float32 [768], replicated, may hold values from -2 to 2
Outputs:
- layer_out: float32 [32768, 768], P('dp')
- tokens_grad: float32 [32768, 768], P('dp', 'section')
- half_weights_grad: float32 [2, 768, 3072], P('section', 'dp')
- down_weight_grad: float32 [3072, 768], P(('section', 'dp'))
- pre_gain_grad: float32 [768], P(('section', 'dp'))
- pre_shift_grad: float32 [768], P(('section', 'dp'))
- query_bias_grad: float32 [768], P(('section', 'dp'))
- value_bias_grad: float32 [768], P(('section', 'dp'))
- sub_gain_grad: float32 [768], P(('section', 'dp'))
- sub_shift_grad: float32 [768], P(('section', 'dp'))
- out_bias_grad: float32 [768], P(('section', 'dp'))
- ffn_gain_grad: float32 [768], P(('section', 'dp'))
- ffn_shift_grad: float32 [768], P(('section', 'dp'))
- up_bias_grad: float32 [3072], P(('section', 'dp'))
- mid_gain_grad: float32 [3072], P(('section', 'dp'))
- mid_shift_grad: float32 [3072], P(('section', 'dp'))
- down_bias_grad: float32 [768], P(('section', 'dp'))
The draws below stay inside these ranges and needn't reach their ends.
Inputs may be any that keep to these rules, and one draw needn't show every extreme that they name: `seq_lengths`: row b lists the lengths of the sequences packed one after another from the first row of micro-batch b; they sum to at most 1024, and the rows after them are padding. Zero marks an unused slot. Some micro-batch holds a single sequence of 1024 rows.
All inputs are finite; a program needn't handle non-finite values.
Results may differ from the reference program's by a relative error of at most 0.013.
Values may be sent and summed in bfloat16 or wider, within the bound.
A program may use at most 136 MiB of HBM per device.

```python
import jax
import jax.numpy as jnp
from jax import lax

D = 768
HEADS = 12
HEAD_DIM = 64
FF = 3072
MB_ROWS = 1024
SEQS = 8
BATCHES = 32
ROWS = 32768


def draw_seq_lengths(key, part):
    keys = jax.random.split(key, 4)
    count = BATCHES
    index = jnp.arange(count, dtype=jnp.int32)
    padding = jax.random.randint(keys[0], (count,), 0, MB_ROWS // 4 + 1)
    single = jax.random.randint(keys[1], (count,), 0, 4) == 0
    chosen = jax.random.randint(keys[2], (), 0, count)
    single = single | (index == chosen)
    padding = jnp.where(index == chosen, 0, padding)
    filled = MB_ROWS - padding
    cuts = jax.random.randint(keys[3], (count, SEQS - 1), 0, MB_ROWS + 1)
    cuts = jnp.sort(cuts * filled[:, None] // MB_ROWS, axis=1)
    bounds = jnp.concatenate([jnp.zeros((count, 1), jnp.int32), cuts, filled[:, None]], axis=1)
    pieces = bounds[:, 1:] - bounds[:, :-1]
    whole = jnp.concatenate([filled[:, None], jnp.zeros((count, SEQS - 1), jnp.int32)], axis=1)
    return jnp.where(single[:, None], whole, pieces).astype(jnp.int32)


def strengthened(values, rng, source, target, shards_of, factor):
    owner, partner = [(jnp.arange(values.shape[axis_at]) // (values.shape[axis_at] // shards_of)).reshape([-1 if axis == axis_at else 1 for axis in range(values.ndim)]) for axis_at in (source, target)]
    chosen = jax.random.permutation(rng, shards_of)[partner]
    strong = (owner == chosen) | (owner == (partner + shards_of // 2) % shards_of)
    return jnp.where(strong, factor * values, values)


def steps_of(key, dims, shards, low, largest):
    level = 1.0
    for position, blocks in shards:
        draws = jax.random.uniform(jax.random.fold_in(jax.random.fold_in(key, 6), position), (blocks,), jnp.float32, low / len(shards), largest / len(shards))
        level = level * jnp.repeat(jnp.exp(draws), dims[position] // blocks).reshape((-1,) + (1,) * (len(dims) - 1 - position))
    return level


def normal_values(own_key, shape, width, bound, shards=(), held_as=jnp.bfloat16):
    array = width * jax.random.normal(own_key, shape, jnp.float32)
    if shards:
        array = array * steps_of(own_key, shape, shards, -0.22, 0.18)
    return jnp.clip(array, -bound, bound).astype(held_as)


def gaussian_with(own_key, dims, scale, limit, cuts, heavy, kind=jnp.bfloat16):
    array = scale * jax.random.normal(own_key, dims, jnp.float32)
    if cuts:
        array = array * steps_of(own_key, dims, cuts, -0.22, 0.18)
    return jnp.clip(strengthened(array, jax.random.fold_in(own_key, 3), *heavy), -limit, limit).astype(kind)


def setup_inputs(seed: int = 0) -> dict:
    arg_keys = jax.random.split(jax.random.key(seed), 19)
    tokens = gaussian_with(arg_keys[0], (ROWS, D), 1.0, 6.0, ((0, 16),), (0, 1, 16, 2.0))
    out_grad = normal_values(arg_keys[1], (ROWS, D), 1.0, 6.0, ((0, 16),))
    seq_lengths = draw_seq_lengths(jax.random.fold_in(arg_keys[18], 71), 0)
    half_weights = normal_values(arg_keys[3], (2, D, FF), D ** -0.5, 0.21875, ((0, 2), (1, 16)))
    down_weight = normal_values(arg_keys[4], (FF, D), FF ** -0.5, 0.109375, ((0, 32),))
    pre_gain = jnp.clip(1.0 + 0.15 * jax.random.normal(arg_keys[5], (D,), jnp.float32), 0.25, 1.75)
    pre_shift = normal_values(arg_keys[6], (D,), 0.4, 2.0, (), jnp.float32)
    query_bias = normal_values(arg_keys[7], (D,), 0.4, 2.0, (), jnp.float32)
    value_bias = normal_values(arg_keys[8], (D,), 0.4, 2.0, (), jnp.float32)
    sub_gain = jnp.clip(1.0 + 0.15 * jax.random.normal(arg_keys[9], (D,), jnp.float32), 0.25, 1.75)
    sub_shift = normal_values(arg_keys[10], (D,), 0.4, 2.0, (), jnp.float32)
    out_bias = normal_values(arg_keys[11], (D,), 0.4, 2.0, (), jnp.float32)
    ffn_gain = jnp.clip(1.0 + 0.15 * jax.random.normal(arg_keys[12], (D,), jnp.float32), 0.25, 1.75)
    ffn_shift = normal_values(arg_keys[13], (D,), 0.4, 2.0, (), jnp.float32)
    up_bias = normal_values(arg_keys[14], (FF,), 0.4, 2.0, (), jnp.float32)
    mid_gain = jnp.clip(1.0 + 0.15 * jax.random.normal(arg_keys[15], (FF,), jnp.float32), 0.25, 1.75)
    mid_shift = normal_values(arg_keys[16], (FF,), 0.4, 2.0, (), jnp.float32)
    down_bias = normal_values(arg_keys[17], (D,), 0.4, 2.0, (), jnp.float32)
    return {"tokens": tokens, "out_grad": out_grad, "seq_lengths": seq_lengths, "half_weights": half_weights, "down_weight": down_weight, "pre_gain": pre_gain, "pre_shift": pre_shift, "query_bias": query_bias, "value_bias": value_bias, "sub_gain": sub_gain, "sub_shift": sub_shift, "out_bias": out_bias, "ffn_gain": ffn_gain, "ffn_shift": ffn_shift, "up_bias": up_bias, "mid_gain": mid_gain, "mid_shift": mid_shift, "down_bias": down_bias}


@jax.custom_vjp
def low(v):
    return lax.optimization_barrier(v.astype(jnp.bfloat16)).astype(jnp.float32)

@jax.custom_vjp
def low_back(v):
    return v

def low_keep(v):
    return (low(v), None)

def low_pass(kept, grad):
    return (grad,)

def back_keep(v):
    return (v, None)

def back_low(kept, grad):
    return (low(grad),)
low.defvjp(low_keep, low_pass)
low_back.defvjp(back_keep, back_low)

def layer_norm(value, gain, shift):
    center = lax.optimization_barrier(jnp.mean(value, axis=-1, keepdims=True))
    centered = value - center
    spread = lax.optimization_barrier(jnp.mean(centered * centered, axis=-1, keepdims=True))
    return centered * lax.rsqrt(spread + 1e-05) * gain + shift

def row_masks(lengths_row, count):
    ends = jnp.cumsum(lengths_row)
    index = jnp.arange(count, dtype=jnp.int32)
    segment = lax.optimization_barrier(jnp.sum((index[:, None] >= ends[None, :]).astype(jnp.int32), axis=1))
    alive = segment < lengths_row.shape[0]
    same = segment[:, None] == segment[None, :]
    causal = index[None, :] <= index[:, None]
    allowed = same & causal & (alive[:, None] | (index[:, None] == index[None, :]))
    return (alive.astype(jnp.float32), allowed)

def matmul(left, right):
    return jnp.dot(left, right, precision=lax.Precision.HIGHEST, preferred_element_type=jnp.float32)

def both_ways(value):
    return low(low_back(value))

def reference(tokens, out_grad, seq_lengths, half_weights, down_weight, pre_gain, pre_shift, query_bias, value_bias, sub_gain, sub_shift, out_bias, ffn_gain, ffn_shift, up_bias, mid_gain, mid_shift, down_bias):
    stacked = half_weights.astype(jnp.float32)
    inputs = tokens.astype(jnp.float32).reshape(BATCHES, MB_ROWS, D)
    cotangent = out_grad.astype(jnp.float32).reshape(BATCHES, MB_ROWS, D)
    vectors = (pre_gain, pre_shift, query_bias, value_bias, sub_gain, sub_shift, out_bias, ffn_gain, ffn_shift, up_bias, mid_gain, mid_shift, down_bias)

    def forward(inputs, qkv_weight, out_weight, up_weight, down_w, vectors):
        pg, ps, qb, vb, sg, ss, ob, fg, fs, ub, mg, ms, db = vectors

        def block(x_block, lengths_row):
            alive, allowed = row_masks(lengths_row, MB_ROWS)
            normed = low(layer_norm(x_block, pg, ps))
            biases = jnp.concatenate([qb, jnp.zeros((D,), jnp.float32), vb])
            projected = matmul(normed, qkv_weight) + biases
            query = both_ways(projected[:, :D]).reshape(MB_ROWS, HEADS, HEAD_DIM)
            key = both_ways(projected[:, D:2 * D]).reshape(MB_ROWS, HEADS, HEAD_DIM)
            value = both_ways(projected[:, 2 * D:]).reshape(MB_ROWS, HEADS, HEAD_DIM)
            raw = jnp.einsum('qhd,khd->hqk', query, key, precision=lax.Precision.HIGHEST, preferred_element_type=jnp.float32) * HEAD_DIM ** (-0.5)
            scores = jnp.where(allowed[None], low_back(raw), -1e+30)
            peak = lax.optimization_barrier(jnp.max(scores, axis=-1, keepdims=True))
            raised = jnp.exp(scores - peak)
            soft = raised / lax.optimization_barrier(jnp.sum(raised, axis=-1, keepdims=True))
            probs = low(soft)
            context = jnp.einsum('hqk,khd->qhd', probs, value, precision=lax.Precision.HIGHEST, preferred_element_type=jnp.float32)
            context = low_back(context.reshape(MB_ROWS, D))
            mixed = low(layer_norm(context, sg, ss))
            branch = low_back(matmul(mixed, out_weight) + ob)
            hidden = both_ways(x_block + alive[:, None] * branch)
            normed_ffn = low(layer_norm(hidden, fg, fs))
            upper = low_back(matmul(normed_ffn, up_weight) + ub)
            middle = low(layer_norm(jax.nn.gelu(upper, approximate=False), mg, ms))
            ffn_out = both_ways(matmul(middle, down_w) + db)
            return hidden + alive[:, None] * ffn_out
        block = jax.checkpoint(block)

        def step(carry, pieces):
            return (carry, block(pieces[0], pieces[1]))
        carry, outputs = lax.scan(step, None, (inputs, seq_lengths))
        return outputs
    primals = (inputs, stacked[0][:, :3 * D], stacked[0][:, 3 * D:], stacked[1], down_weight.astype(jnp.float32), vectors)
    outputs, backward = jax.vjp(forward, *primals)
    grad_in, grad_qkv, grad_out, grad_up, grad_down, grad_vec = backward(cotangent)
    grad_half = jnp.stack([jnp.concatenate([grad_qkv, grad_out], axis=1), grad_up])
    return (outputs.reshape(ROWS, D), grad_in.reshape(ROWS, D), grad_half, grad_down, grad_vec[0], grad_vec[1], grad_vec[2], grad_vec[3], grad_vec[4], grad_vec[5], grad_vec[6], grad_vec[7], grad_vec[8], grad_vec[9], grad_vec[10], grad_vec[11], grad_vec[12])
```

```python
import jax
import jax.numpy as jnp
from jax import lax
from jax.sharding import PartitionSpec as P

HEAD_DIM = 64


EPS = 1e-05


def layer_norm(value, gain, shift):
    center = jnp.mean(value, axis=-1, keepdims=True)
    centered = value - center
    spread = jnp.mean(centered * centered, axis=-1, keepdims=True)
    return centered * lax.rsqrt(spread + EPS) * gain + shift


def exact_gelu(value):
    return jax.nn.gelu(value, approximate=False)


def row_masks(lengths_row, count):
    slots = jnp.arange(lengths_row.shape[0], dtype=jnp.int32)
    ends = jnp.sum(jnp.where(slots[:, None] <= slots[None, :], lengths_row[:, None], 0), axis=0)
    index = jnp.arange(count, dtype=jnp.int32)
    segment = jnp.sum((index[:, None] >= ends[None, :]).astype(jnp.int32), axis=1)
    alive = segment < lengths_row.shape[0]
    same = segment[:, None] == segment[None, :]
    causal = index[None, :] <= index[:, None]
    allowed = same & causal & (alive[:, None] | (index[:, None] == index[None, :]))
    return (alive.astype(jnp.float32), allowed)


def split_groups(block, groups):
    return block.reshape(block.shape[0], groups, -1).transpose(1, 0, 2)


def join_groups(block):
    return block.transpose(1, 0, 2).reshape(block.shape[1], -1)


def per_head(block):
    return block.reshape(block.shape[0], -1, HEAD_DIM)


def masked_scores(query, key, allowed):
    scores = jnp.einsum(
        "qhd,khd->hqk", per_head(query), per_head(key), preferred_element_type=jnp.float32
    )
    return jnp.where(allowed[None], scores * HEAD_DIM ** (-0.5), -1e30)


def contract_rows(left, right):
    return lax.dot_general(
        left, right, (((0,), (0,)), ((), ())), preferred_element_type=jnp.float32
    )


def contract_cols(left, right):
    return lax.dot_general(
        left, right, (((1,), (1,)), ((), ())), preferred_element_type=jnp.float32
    )


def attention_forward(x_block, alive, allowed, weights, vectors):
    pre_gain, pre_shift, query_bias, value_bias, sub_gain, sub_shift, out_bias = vectors
    count, width = x_block.shape
    groups = width // (4 * HEAD_DIM)
    inputs = x_block.astype(jnp.float32)
    normed = layer_norm(inputs, pre_gain, pre_shift).astype(jnp.bfloat16)
    biases = jnp.concatenate([query_bias, jnp.zeros_like(query_bias), value_bias])
    projected = (
        jnp.dot(normed, weights[:, : 3 * width], preferred_element_type=jnp.float32) + biases
    ).astype(jnp.bfloat16)
    query = split_groups(projected[:, :width], groups)
    key = split_groups(projected[:, width : 2 * width], groups)
    value = split_groups(projected[:, 2 * width :], groups)

    def one_group(parts):
        query_g, key_g, value_g = parts
        scores = masked_scores(query_g, key_g, allowed)
        peak = jnp.max(scores, axis=-1, keepdims=True)
        raised = jnp.exp(scores - peak)
        denominator = jnp.sum(raised, axis=-1, keepdims=True)
        attention = (raised / denominator).astype(jnp.bfloat16)
        context = jnp.einsum(
            "hqk,khd->qhd", attention, per_head(value_g), preferred_element_type=jnp.float32
        )
        return (context.reshape(count, -1), (peak + jnp.log(denominator))[..., 0])

    context, logsum = lax.map(one_group, (query, key, value))
    context = join_groups(context)
    mixed = layer_norm(context, sub_gain, sub_shift).astype(jnp.bfloat16)
    branch = jnp.dot(mixed, weights[:, 3 * width :], preferred_element_type=jnp.float32) + out_bias
    hidden = (inputs + alive[:, None] * branch).astype(jnp.bfloat16)
    return (hidden, projected, logsum, context)


def attention_backward(
    x_block, alive, allowed, weights, vectors, projected, logsum, context, grad_hidden
):
    pre_gain, pre_shift, query_bias, value_bias, sub_gain, sub_shift, out_bias = vectors
    count, width = x_block.shape
    groups = width // (4 * HEAD_DIM)
    upstream = grad_hidden.astype(jnp.float32)
    grad_branch = (alive[:, None] * upstream).astype(jnp.bfloat16)
    mixed, mixed_back = jax.vjp(layer_norm, context, sub_gain, sub_shift)
    mixed = mixed.astype(jnp.bfloat16)
    out_weight = weights[:, 3 * width :]
    grad_out_weight = contract_rows(mixed, grad_branch)
    grad_out_bias = jnp.sum(grad_branch.astype(jnp.float32), axis=0)
    grad_mixed = contract_cols(grad_branch, out_weight)
    grad_context, grad_sub_gain, grad_sub_shift = mixed_back(grad_mixed)
    grad_context = split_groups(grad_context.astype(jnp.bfloat16), groups)
    query = split_groups(projected[:, :width], groups)
    key = split_groups(projected[:, width : 2 * width], groups)
    value = split_groups(projected[:, 2 * width :], groups)

    def one_group(parts):
        query_g, key_g, value_g, grad_g, logsum_g = parts
        scores = masked_scores(query_g, key_g, allowed)
        soft = jnp.exp(scores - logsum_g[..., None])
        grad_heads = per_head(grad_g)
        grad_soft = jnp.einsum(
            "qhd,khd->hqk", grad_heads, per_head(value_g), preferred_element_type=jnp.float32
        )
        grad_value = jnp.einsum(
            "hqk,qhd->khd",
            soft.astype(jnp.bfloat16),
            grad_heads,
            preferred_element_type=jnp.float32,
        )
        inner = jnp.sum(soft * grad_soft, axis=-1, keepdims=True)
        grad_scores = (soft * (grad_soft - inner)).astype(jnp.bfloat16)
        scale = HEAD_DIM ** (-0.5)
        grad_query = (
            jnp.einsum(
                "hqk,khd->qhd", grad_scores, per_head(key_g), preferred_element_type=jnp.float32
            )
            * scale
        )
        grad_key = (
            jnp.einsum(
                "hqk,qhd->khd", grad_scores, per_head(query_g), preferred_element_type=jnp.float32
            )
            * scale
        )
        return (
            grad_query.reshape(count, -1),
            grad_key.reshape(count, -1),
            grad_value.reshape(count, -1),
        )

    grad_query, grad_key, grad_value = lax.map(one_group, (query, key, value, grad_context, logsum))
    grad_projected = jnp.concatenate(
        [join_groups(grad_query), join_groups(grad_key), join_groups(grad_value)], axis=1
    ).astype(jnp.bfloat16)
    inputs = x_block.astype(jnp.float32)
    normed, normed_back = jax.vjp(layer_norm, inputs, pre_gain, pre_shift)
    normed = normed.astype(jnp.bfloat16)
    grad_qkv_weight = contract_rows(normed, grad_projected)
    column_sums = jnp.sum(grad_projected.astype(jnp.float32), axis=0)
    grad_normed = contract_cols(grad_projected, weights[:, : 3 * width])
    grad_inputs, grad_pre_gain, grad_pre_shift = normed_back(grad_normed)
    grad_block = jnp.concatenate([grad_qkv_weight, grad_out_weight], axis=1)
    small = (
        grad_pre_gain,
        grad_pre_shift,
        column_sums[:width],
        column_sums[2 * width :],
        grad_sub_gain,
        grad_sub_shift,
        grad_out_bias,
    )
    return (upstream + grad_inputs, grad_block, small)


def feed_forward(arrived, dy_block, alive, up_weight, down_full, vectors):
    ffn_gain, ffn_shift, up_bias, mid_gain, mid_shift, down_bias = vectors
    hidden = arrived.astype(jnp.float32)
    normed, normed_back = jax.vjp(layer_norm, hidden, ffn_gain, ffn_shift)
    normed = normed.astype(jnp.bfloat16)
    upper = jnp.dot(normed, up_weight, preferred_element_type=jnp.float32) + up_bias
    active, active_back = jax.vjp(exact_gelu, upper)
    middle, middle_back = jax.vjp(layer_norm, active, mid_gain, mid_shift)
    middle = middle.astype(jnp.bfloat16)
    result = (jnp.dot(middle, down_full, preferred_element_type=jnp.float32) + down_bias).astype(
        jnp.bfloat16
    )
    upstream = dy_block.astype(jnp.float32)
    grad_result = (alive[:, None] * upstream).astype(jnp.bfloat16)
    grad_down = contract_rows(middle, grad_result)
    grad_down_bias = jnp.sum(grad_result.astype(jnp.float32), axis=0)
    grad_middle = contract_cols(grad_result, down_full)
    grad_active, grad_mid_gain, grad_mid_shift = middle_back(grad_middle)
    grad_upper = active_back(grad_active)[0].astype(jnp.bfloat16)
    grad_up = contract_rows(normed, grad_upper)
    grad_up_bias = jnp.sum(grad_upper.astype(jnp.float32), axis=0)
    grad_normed = contract_cols(grad_upper, up_weight)
    grad_inputs, grad_ffn_gain, grad_ffn_shift = normed_back(grad_normed)
    grad_back = (upstream + grad_inputs).astype(jnp.bfloat16)
    small = (
        grad_ffn_gain,
        grad_ffn_shift,
        grad_up_bias,
        grad_mid_gain,
        grad_mid_shift,
        grad_down_bias,
    )
    return (jnp.stack([result, grad_back]), grad_up, grad_down, small)


def shards(
    tokens,
    out_grad,
    seq_lengths,
    half_weights,
    down_weight,
    *all_vectors,
):
    section = lax.axis_index("section")
    sections = lax.axis_size("section")
    both = ("section", "dp")
    width = tokens.shape[1]
    batches = seq_lengths.shape[0]
    count = tokens.shape[0] // batches
    own_batches = batches // sections
    own_rows = own_batches * count
    hidden_units = half_weights.shape[2]
    shares = sections * lax.axis_size("dp")
    attention_vectors = all_vectors[:7]
    ffn_vectors = all_vectors[7:]

    blocks = lax.all_gather(half_weights[0], both, axis=0, tiled=True)
    blocks = blocks.reshape(sections, width, hidden_units)
    down_full = lax.all_gather(down_weight, both, axis=0, tiled=True)
    attention_block, up_block = blocks[0], blocks[1]

    def own(array, rows):
        return lax.dynamic_slice_in_dim(array, section * rows, rows, axis=0)

    x_rows = own(tokens, own_rows)
    dy_rows = own(out_grad, own_rows)
    lengths = own(seq_lengths, own_batches)

    def step(index):
        x_block = x_rows[index * count : (index + 1) * count]
        dy_block = dy_rows[index * count : (index + 1) * count]
        alive, allowed = row_masks(lengths[index], count)
        hidden, projected, logsum, context = attention_forward(
            x_block, alive, allowed, attention_block, attention_vectors
        )
        stacked, grad_up, grad_down, ffn_small = feed_forward(
            hidden, dy_block, alive, up_block, down_full, ffn_vectors
        )
        out_block = hidden.astype(jnp.float32) + alive[:, None] * stacked[0].astype(jnp.float32)
        grad_x, grad_attention, attention_small = attention_backward(
            x_block,
            alive,
            allowed,
            attention_block,
            attention_vectors,
            projected,
            logsum,
            context,
            stacked[1],
        )
        return (out_block, grad_x), (grad_attention, grad_up, grad_down, attention_small + ffn_small)

    rows, sums = step(0)
    outputs, grads = [rows[0]], [rows[1]]
    for index in range(1, own_batches):
        rows, more = step(index)
        outputs.append(rows[0])
        grads.append(rows[1])
        sums = jax.tree.map(lambda total, extra: total + extra, sums, more)
    out_block = jnp.concatenate(outputs, axis=0)
    grad_rows = jnp.concatenate(grads, axis=0)
    grad_attention, grad_up, grad_down, vectors = sums

    block_part = lax.psum_scatter(
        jnp.concatenate([grad_attention, grad_up], axis=0), both, scatter_dimension=0, tiled=True
    )
    down_part = lax.psum_scatter(grad_down, both, scatter_dimension=0, tiled=True)
    packed = jnp.concatenate([vector.reshape(shares, -1) for vector in vectors], axis=1)
    packed = lax.psum_scatter(packed, both, scatter_dimension=0, tiled=True).reshape(-1)
    parts, start = [], 0
    for vector in vectors:
        size = vector.shape[0] // shares
        parts.append(packed[start : start + size])
        start += size

    layer_out = lax.all_gather(out_block, "section", axis=0, tiled=True)
    tokens_grad = lax.all_to_all(grad_rows, "section", split_axis=1, concat_axis=0, tiled=True)
    return (layer_out, tokens_grad, block_part[None], down_part, *parts)


def solution(mesh):
    placed = (
        P("dp", None),
        P("dp", None),
        P("dp", None),
        P("section", "dp", None),
        P(("section", "dp"), None),
        P(),
        P(),
        P(),
        P(),
        P(),
        P(),
        P(),
        P(),
        P(),
        P(),
        P(),
        P(),
        P(),
    )
    return jax.shard_map(
        shards,
        mesh=mesh,
        in_specs=placed,
        out_specs=(
            P("dp", None),
            P("dp", "section"),
            P("section", "dp", None),
            P(("section", "dp"), None),
            P(("section", "dp")),
            P(("section", "dp")),
            P(("section", "dp")),
            P(("section", "dp")),
            P(("section", "dp")),
            P(("section", "dp")),
            P(("section", "dp")),
            P(("section", "dp")),
            P(("section", "dp")),
            P(("section", "dp")),
            P(("section", "dp")),
            P(("section", "dp")),
            P(("section", "dp")),
        ),
        check_vma=False,
    )
```

```python
import functools
import math

import jax
import jax.numpy as jnp
from jax import lax
from jax.experimental import pallas as pl
from jax.experimental.pallas import tpu as pltpu
from jax.sharding import PartitionSpec as P

HEAD_DIM = 64
PAIR = 2 * HEAD_DIM
EPS = 1e-05
BLOCK = 256
F32 = jnp.float32
BF16 = jnp.bfloat16
VMEM_LIMIT = 60 * 1024 * 1024


def nn(left, right):
    return lax.dot_general(left, right, (((1,), (0,)), ((), ())), preferred_element_type=F32)


def nt(left, right):
    return lax.dot_general(left, right, (((1,), (1,)), ((), ())), preferred_element_type=F32)


def tn(left, right):
    return lax.dot_general(left, right, (((0,), (0,)), ((), ())), preferred_element_type=F32)


def col_sum(value):
    return jnp.sum(value, axis=0, keepdims=True)


def normalized(value):
    center = jnp.mean(value, axis=-1, keepdims=True)
    centered = value - center
    spread = jnp.mean(centered * centered, axis=-1, keepdims=True)
    scale = lax.rsqrt(spread + EPS)
    return centered * scale, scale


def norm_back(hat, scale, gain, upstream):
    scaled = upstream * gain
    first = jnp.mean(scaled, axis=-1, keepdims=True)
    second = jnp.mean(scaled * hat, axis=-1, keepdims=True)
    return (scaled - first - hat * second) * scale


def params(**more):
    return pltpu.CompilerParams(vmem_limit_bytes=VMEM_LIMIT, **more)


def whole(shape):
    return pl.BlockSpec(shape, lambda *_: (0,) * len(shape))


def project_kernel(x_ref, w_ref, gain_ref, shift_ref, bias_ref, out_ref, normed_ref):
    hat, _ = normalized(x_ref[...].astype(F32))
    normed = (hat * gain_ref[...] + shift_ref[...]).astype(BF16)
    normed_ref[...] = normed
    out_ref[...] = (nn(normed, w_ref[...]) + bias_ref[...]).astype(BF16)


def project(x, weight, gain, shift, bias):
    rows, width = x.shape
    return pl.pallas_call(
        project_kernel,
        grid=(rows // BLOCK,),
        in_specs=[
            pl.BlockSpec((BLOCK, width), lambda i: (i, 0)),
            whole((width, 3 * width)),
            whole((1, width)),
            whole((1, width)),
            whole((1, 3 * width)),
        ],
        out_specs=[
            pl.BlockSpec((BLOCK, 3 * width), lambda i: (i, 0)),
            pl.BlockSpec((BLOCK, width), lambda i: (i, 0)),
        ],
        out_shape=[
            jax.ShapeDtypeStruct((rows, 3 * width), BF16),
            jax.ShapeDtypeStruct((rows, width), BF16),
        ],
        compiler_params=params(),
        name="project",
    )(x, weight, gain, shift, bias)


def allowed_mask(start, key_at, keys, queries):
    key = key_at + lax.broadcasted_iota(jnp.int32, (keys, queries), 0)
    return key >= start


def head_rows(pair_t, head):
    row = lax.broadcasted_iota(jnp.int32, pair_t.shape, 0)
    mine = (row < HEAD_DIM) if head == 0 else (row >= HEAD_DIM)
    return jnp.where(mine, pair_t, jnp.zeros_like(pair_t))


def head_cols(pair, head):
    col = lax.broadcasted_iota(jnp.int32, pair.shape, 1)
    mine = (col < HEAD_DIM) if head == 0 else (col >= HEAD_DIM)
    return jnp.where(mine, pair, jnp.zeros_like(pair))


def masked_scores(key, query_t, start, block):
    keys = (block + 1) * BLOCK
    scores = nn(key[:keys], query_t)
    index = lax.broadcasted_iota(jnp.int32, (keys, BLOCK), 0)
    ok = index >= start
    last = block * BLOCK + lax.broadcasted_iota(jnp.int32, (keys, BLOCK), 1)
    ok = ok & (index <= last)
    return jnp.where(ok, scores, -1e30)


def attend_kernel(q_ref, k_ref, v_ref, start_ref, out_ref, lse_ref):
    rows = q_ref.shape[0]
    query_t = (q_ref[...].astype(F32) * HEAD_DIM**-0.5).T.astype(BF16)
    key = k_ref[...]
    value_t = v_ref[...].astype(F32).T.astype(BF16)
    for block in range(rows // BLOCK):
        at = slice(block * BLOCK, (block + 1) * BLOCK)
        keys = (block + 1) * BLOCK
        start = start_ref[:, at]
        outs = []
        for head in range(2):
            scores = masked_scores(key, head_rows(query_t[:, at], head), start, block)
            peak = jnp.max(scores, axis=0, keepdims=True)
            raised = jnp.exp(scores - peak)
            total = jnp.sum(raised, axis=0, keepdims=True)
            lanes = slice(head * HEAD_DIM, (head + 1) * HEAD_DIM)
            probs = (raised * (1.0 / total)).astype(BF16)
            outs.append(nn(value_t[lanes, :keys], probs))
            lse_ref[0, head : head + 1, at] = peak + jnp.log(total)
        out_ref[at, :] = jnp.concatenate(outs, axis=0).T


def attend(projected, start):
    rows, columns = projected.shape
    width = columns // 3
    pairs = width // PAIR
    return pl.pallas_call(
        attend_kernel,
        grid=(pairs,),
        in_specs=[
            pl.BlockSpec((rows, PAIR), lambda p: (0, p)),
            pl.BlockSpec((rows, PAIR), lambda p: (0, pairs + p)),
            pl.BlockSpec((rows, PAIR), lambda p: (0, 2 * pairs + p)),
            whole((1, rows)),
        ],
        out_specs=[
            pl.BlockSpec((rows, PAIR), lambda p: (0, p)),
            pl.BlockSpec((1, 2, rows), lambda p: (p, 0, 0)),
        ],
        out_shape=[
            jax.ShapeDtypeStruct((rows, width), F32),
            jax.ShapeDtypeStruct((pairs, 2, rows), F32),
        ],
        compiler_params=params(),
        name="attend",
    )(projected, projected, projected, start)


def attend_back_kernel(q_ref, k_ref, v_ref, g_ref, o_ref, lse_ref, start_ref, dq_ref, dk_ref, dv_ref, dk_acc, dv_acc):
    rows = q_ref.shape[0]
    scale = HEAD_DIM**-0.5
    scaled = q_ref[...].astype(F32) * scale
    query = scaled.astype(BF16)
    query_t = scaled.T.astype(BF16)
    key = k_ref[...]
    key_t = key.astype(F32).T.astype(BF16)
    value = v_ref[...]
    grad = g_ref[...]
    grad_f = grad.astype(F32)
    grad_t = grad_f.T.astype(BF16)
    weighted_t = (grad_f * o_ref[...]).T
    dk_acc[...] = jnp.zeros_like(dk_acc)
    dv_acc[...] = jnp.zeros_like(dv_acc)
    for block in range(rows // BLOCK):
        at = slice(block * BLOCK, (block + 1) * BLOCK)
        keys = (block + 1) * BLOCK
        start = start_ref[:, at]
        outs = []
        for head in range(2):
            lanes = slice(head * HEAD_DIM, (head + 1) * HEAD_DIM)
            inner = col_sum(weighted_t[lanes, at])
            scores = masked_scores(key, head_rows(query_t[:, at], head), start, block)
            soft = jnp.exp(scores - lse_ref[0, head : head + 1, at])
            grad_soft = nn(value[:keys], head_rows(grad_t[:, at], head))
            grad_scores = (soft * (grad_soft - inner)).astype(BF16)
            dv_acc[:keys, :] += nn(soft.astype(BF16), head_cols(grad[at], head))
            dk_acc[:keys, :] += nn(grad_scores, head_cols(query[at], head))
            outs.append(nn(key_t[lanes, :keys], grad_scores))
        dq_ref[at, :] = (jnp.concatenate(outs, axis=0) * scale).T.astype(BF16)
    dk_ref[...] = dk_acc[...].astype(BF16)
    dv_ref[...] = dv_acc[...].astype(BF16)


def attend_back(projected, grad_context, context, lse, start):
    rows, columns = projected.shape
    width = columns // 3
    pairs = width // PAIR
    pair = pl.BlockSpec((rows, PAIR), lambda p: (0, p))
    return pl.pallas_call(
        attend_back_kernel,
        grid=(pairs,),
        in_specs=[
            pair,
            pl.BlockSpec((rows, PAIR), lambda p: (0, pairs + p)),
            pl.BlockSpec((rows, PAIR), lambda p: (0, 2 * pairs + p)),
            pair,
            pair,
            pl.BlockSpec((1, 2, rows), lambda p: (p, 0, 0)),
            whole((1, rows)),
        ],
        out_specs=[pair] * 3,
        out_shape=[jax.ShapeDtypeStruct((rows, width), BF16)] * 3,
        scratch_shapes=[pltpu.VMEM((rows, PAIR), F32), pltpu.VMEM((rows, PAIR), F32)],
        compiler_params=params(),
        name="attend_back",
    )(projected, projected, projected, grad_context, context, lse, start)


def gelu_parts(value):
    phi = 0.5 * (1.0 + lax.erf(value * (1.0 / math.sqrt(2.0))))
    bell = jnp.exp(-0.5 * value * value) * (1.0 / math.sqrt(2.0 * math.pi))
    return value * phi, phi + value * bell


def middle_kernel(
    x_ref, dy_ref, ctx_ref, alive_ref, wo_ref, wu_ref, wd_ref,
    sg_ref, ss_ref, ob_ref, fg_ref, fs_ref, ub_ref, mg_ref, ms_ref, db_ref,
    out_ref, ghid_ref, gctx_ref, mixed_ref, gbranch_ref, nffn_ref, gup_ref, mid_ref, gffn_ref,
    narrow_ref, wide_ref,
):
    step = pl.program_id(0)

    @pl.when(step == 0)
    def _():
        narrow_ref[...] = jnp.zeros_like(narrow_ref)
        wide_ref[...] = jnp.zeros_like(wide_ref)

    alive = alive_ref[...]
    ctx_hat, ctx_scale = normalized(ctx_ref[...])
    mixed = (ctx_hat * sg_ref[...] + ss_ref[...]).astype(BF16)
    mixed_ref[...] = mixed
    branch = nn(mixed, wo_ref[...]) + ob_ref[...]
    hidden = (x_ref[...].astype(F32) + alive * branch).astype(BF16).astype(F32)
    hid_hat, hid_scale = normalized(hidden)
    nffn = (hid_hat * fg_ref[...] + fs_ref[...]).astype(BF16)
    nffn_ref[...] = nffn
    upper = nn(nffn, wu_ref[...]) + ub_ref[...]
    active, slope = gelu_parts(upper)
    act_hat, act_scale = normalized(active)
    mid = (act_hat * mg_ref[...] + ms_ref[...]).astype(BF16)
    mid_ref[...] = mid
    result = (nn(mid, wd_ref[...]) + db_ref[...]).astype(BF16).astype(F32)
    out_ref[...] = hidden + alive * result

    upstream = dy_ref[...].astype(F32)
    gffn = (alive * upstream).astype(BF16)
    gffn_ref[...] = gffn
    gmid = nt(gffn, wd_ref[...])
    gact = norm_back(act_hat, act_scale, mg_ref[...], gmid)
    gup = (gact * slope).astype(BF16)
    gup_ref[...] = gup
    wide_ref[0:1, :] += col_sum(gup.astype(F32))
    wide_ref[1:2, :] += col_sum(gmid * act_hat)
    wide_ref[2:3, :] += col_sum(gmid)
    gnffn = nt(gup, wu_ref[...])
    ghid = (upstream + norm_back(hid_hat, hid_scale, fg_ref[...], gnffn)).astype(BF16)
    ghid_ref[...] = ghid
    gbranch = (alive * ghid.astype(F32)).astype(BF16)
    gbranch_ref[...] = gbranch
    gmixed = nt(gbranch, wo_ref[...])
    gctx_ref[...] = norm_back(ctx_hat, ctx_scale, sg_ref[...], gmixed).astype(BF16)
    narrow_ref[0:1, :] += col_sum(gmixed * ctx_hat)
    narrow_ref[1:2, :] += col_sum(gmixed)
    narrow_ref[2:3, :] += col_sum(gbranch.astype(F32))
    narrow_ref[3:4, :] += col_sum(gnffn * hid_hat)
    narrow_ref[4:5, :] += col_sum(gnffn)
    narrow_ref[5:6, :] += col_sum(gffn.astype(F32))


def middle(x, dy, context, alive, attention_block, up_weight, down_weight, vectors):
    rows, width = x.shape
    hidden = up_weight.shape[1]
    row = pl.BlockSpec((BLOCK, width), lambda i: (i, 0))
    row_wide = pl.BlockSpec((BLOCK, hidden), lambda i: (i, 0))
    once = dict(pipeline_mode=pl.Buffered(1))
    narrow = whole((1, width))
    wide = whole((1, hidden))
    def shape(columns, dtype):
        return jax.ShapeDtypeStruct((rows, columns), dtype)
    return pl.pallas_call(
        middle_kernel,
        grid=(rows // BLOCK,),
        in_specs=[
            row, row, row,
            pl.BlockSpec((BLOCK, 1), lambda i: (i, 0)),
            pl.BlockSpec((width, width), lambda i: (0, 3), **once),
            pl.BlockSpec((width, hidden), lambda i: (0, 0), **once),
            pl.BlockSpec((hidden, width), lambda i: (0, 0), **once),
            narrow, narrow, narrow, narrow, narrow, wide, wide, wide, narrow,
        ],
        out_specs=[row, row, row, row, row, row, row_wide, row_wide, row, whole((8, width)), whole((8, hidden))],
        out_shape=[
            shape(width, F32), shape(width, BF16), shape(width, BF16), shape(width, BF16), shape(width, BF16),
            shape(width, BF16), shape(hidden, BF16), shape(hidden, BF16), shape(width, BF16),
            jax.ShapeDtypeStruct((8, width), F32), jax.ShapeDtypeStruct((8, hidden), F32),
        ],
        compiler_params=params(),
        name="middle",
    )(x, dy, context, alive, attention_block, up_weight, down_weight, *vectors)


def outer_kernel(left_ref, right_ref, out_ref):
    out_ref[...] = tn(left_ref[...], right_ref[...]).astype(out_ref.dtype)


def outer(left, right, tile, dtype, name):
    rows, across = left.shape
    columns = right.shape[1]
    return pl.pallas_call(
        outer_kernel,
        grid=(across // tile,),
        in_specs=[pl.BlockSpec((rows, tile), lambda i: (0, i)), whole((rows, columns))],
        out_specs=pl.BlockSpec((tile, columns), lambda i: (i, 0)),
        out_shape=jax.ShapeDtypeStruct((across, columns), dtype),
        compiler_params=params(),
        name=name,
    )(left, right)


def project_back_kernel(dq_ref, dk_ref, dv_ref, w_ref, x_ref, ghid_ref, gain_ref, out_ref, narrow_ref):
    step = pl.program_id(0)
    width = x_ref.shape[1]

    @pl.when(step == 0)
    def _():
        narrow_ref[...] = jnp.zeros_like(narrow_ref)

    dq, dk, dv = dq_ref[...], dk_ref[...], dv_ref[...]
    gnormed = nt(dq, w_ref[:, :width]) + nt(dk, w_ref[:, width : 2 * width]) + nt(dv, w_ref[:, 2 * width :])
    hat, scale = normalized(x_ref[...].astype(F32))
    out_ref[...] = ghid_ref[...].astype(F32) + norm_back(hat, scale, gain_ref[...], gnormed)
    narrow_ref[0:1, :] += col_sum(gnormed * hat)
    narrow_ref[1:2, :] += col_sum(gnormed)
    narrow_ref[2:3, :] += col_sum(dq.astype(F32))
    narrow_ref[3:4, :] += col_sum(dv.astype(F32))


def project_back(dq, dk, dv, weight, x, ghid, gain):
    rows, width = x.shape
    row = pl.BlockSpec((BLOCK, width), lambda i: (i, 0))
    return pl.pallas_call(
        project_back_kernel,
        grid=(rows // BLOCK,),
        in_specs=[row, row, row, whole((width, 3 * width)), row, row, whole((1, width))],
        out_specs=[row, whole((8, width))],
        out_shape=[jax.ShapeDtypeStruct((rows, width), F32), jax.ShapeDtypeStruct((8, width), F32)],
        compiler_params=params(),
        name="project_back",
    )(dq, dk, dv, weight, x, ghid, gain)


def row_marks(lengths_row, count):
    slots = jnp.arange(lengths_row.shape[0], dtype=jnp.int32)
    ends = jnp.sum(jnp.where(slots[:, None] <= slots[None, :], lengths_row[:, None], 0), axis=0)
    index = jnp.arange(count, dtype=jnp.int32)
    before = jnp.where(ends[None, :] <= index[:, None], ends[None, :], 0)
    alive = index < jnp.max(ends)
    start = jnp.where(alive, jnp.max(before, axis=1), index)
    return alive.astype(F32)[:, None], start[None, :]


def one_batch(x, dy, lengths_row, attention_block, up_weight, down_weight, vectors):
    (pre_gain, pre_shift, query_bias, value_bias, sub_gain, sub_shift, out_bias,
     ffn_gain, ffn_shift, up_bias, mid_gain, mid_shift, down_bias) = [v[None, :] for v in vectors]
    count, width = x.shape
    alive, start = row_marks(lengths_row, count)
    bias = jnp.concatenate([query_bias, jnp.zeros_like(query_bias), value_bias], axis=1)
    projected, normed = project(x, attention_block, pre_gain, pre_shift, bias)
    context, lse = attend(projected, start)
    out, ghid, gctx, mixed, gbranch, nffn, gup, mid, gffn, narrow, wide = middle(
        x, dy, context, alive, attention_block, up_weight, down_weight,
        (sub_gain, sub_shift, out_bias, ffn_gain, ffn_shift, up_bias, mid_gain, mid_shift, down_bias),
    )
    grad_up = outer(nffn, gup, 256, F32, "outer_up")
    grad_down = outer(mid, gffn, 512, F32, "outer_down")
    dq, dk, dv = attend_back(projected, gctx, context, lse, start)
    grad_out = outer(mixed, gbranch, 256, F32, "outer_out")
    grad_x, pre = project_back(dq, dk, dv, attention_block, x, ghid, pre_gain)
    grads = [outer(normed, d, 256, F32, "outer_qkv") for d in (dq, dk, dv)]
    grad_attention = jnp.concatenate(grads + [grad_out], axis=1)
    small = (pre[0], pre[1], pre[2], pre[3], narrow[0], narrow[1], narrow[2], narrow[3], narrow[4],
             wide[0], wide[1], wide[2], narrow[5])
    return (out, grad_x), (grad_attention, grad_up, grad_down, small)


def shards(tokens, out_grad, seq_lengths, half_weights, down_weight, *all_vectors):
    section = lax.axis_index("section")
    sections = lax.axis_size("section")
    both = ("section", "dp")
    width = tokens.shape[1]
    batches = seq_lengths.shape[0]
    count = tokens.shape[0] // batches
    own_batches = batches // sections
    own_rows = own_batches * count
    hidden_units = half_weights.shape[2]
    shares = sections * lax.axis_size("dp")

    blocks = lax.all_gather(half_weights[0], both, axis=0, tiled=True)
    blocks = blocks.reshape(sections, width, hidden_units)
    down_full = lax.all_gather(down_weight, both, axis=0, tiled=True)

    def own(array, rows):
        return lax.dynamic_slice_in_dim(array, section * rows, rows, axis=0)

    x_rows = own(tokens, own_rows)
    dy_rows = own(out_grad, own_rows)
    lengths = own(seq_lengths, own_batches)
    rows, sums = [], None
    for index in range(own_batches):
        at = slice(index * count, (index + 1) * count)
        row, more = one_batch(x_rows[at], dy_rows[at], lengths[index], blocks[0], blocks[1], down_full, all_vectors)
        rows.append(row)
        sums = more if sums is None else jax.tree.map(jnp.add, sums, more)
    out_block = jnp.concatenate([row[0] for row in rows], axis=0)
    grad_rows = jnp.concatenate([row[1] for row in rows], axis=0)
    grad_attention, grad_up, grad_down, vectors = sums

    block_part = lax.psum_scatter(
        jnp.concatenate([grad_attention, grad_up], axis=0), both, scatter_dimension=0, tiled=True
    )
    down_part = lax.psum_scatter(grad_down, both, scatter_dimension=0, tiled=True)
    packed = jnp.concatenate([vector.reshape(shares, -1) for vector in vectors], axis=1)
    packed = lax.psum_scatter(packed, both, scatter_dimension=0, tiled=True).reshape(-1)
    parts, start = [], 0
    for vector in vectors:
        size = vector.shape[0] // shares
        parts.append(packed[start : start + size])
        start += size

    layer_out = lax.all_gather(out_block, "section", axis=0, tiled=True)
    tokens_grad = lax.all_to_all(grad_rows, "section", split_axis=1, concat_axis=0, tiled=True)
    return (layer_out, tokens_grad, block_part[None], down_part, *parts)


def solution(mesh):
    replicated = P()
    return jax.shard_map(
        shards,
        mesh=mesh,
        in_specs=(P("dp", None), P("dp", None), P("dp", None), P("section", "dp", None), P(("section", "dp"), None))
        + (replicated,) * 13,
        out_specs=(P("dp", None), P("dp", "section"), P("section", "dp", None), P(("section", "dp"), None))
        + (P(("section", "dp")),) * 13,
        check_vma=False,
    )
```

```python
import functools
import math

import jax
import jax.numpy as jnp
from jax import lax
from jax.experimental import pallas as pl
from jax.experimental.pallas import tpu as pltpu
from jax.sharding import PartitionSpec as P

HEAD_DIM = 64
PAIR = 2 * HEAD_DIM
EPS = 1e-05
BLOCK = 256
F32 = jnp.float32
BF16 = jnp.bfloat16
VMEM_LIMIT = 60 * 1024 * 1024


def nn(left, right):
    return lax.dot_general(left, right, (((1,), (0,)), ((), ())), preferred_element_type=F32)


def nt(left, right):
    return lax.dot_general(left, right, (((1,), (1,)), ((), ())), preferred_element_type=F32)


def tn(left, right):
    return lax.dot_general(left, right, (((0,), (0,)), ((), ())), preferred_element_type=F32)


def col_sum(value):
    return jnp.sum(value, axis=0, keepdims=True)


def normalized(value):
    center = jnp.mean(value, axis=-1, keepdims=True)
    centered = value - center
    spread = jnp.mean(centered * centered, axis=-1, keepdims=True)
    scale = lax.rsqrt(spread + EPS)
    return centered * scale, scale


def norm_back(hat, scale, gain, upstream):
    scaled = upstream * gain
    first = jnp.mean(scaled, axis=-1, keepdims=True)
    second = jnp.mean(scaled * hat, axis=-1, keepdims=True)
    return (scaled - first - hat * second) * scale


def params(**more):
    return pltpu.CompilerParams(vmem_limit_bytes=VMEM_LIMIT, **more)


def side_by_side(ref):
    return jnp.concatenate([ref[b] for b in range(6)], axis=1)


def stacked(ref):
    return jnp.concatenate([jnp.concatenate([ref[3 * h + k] for k in range(3)], axis=1) for h in range(2)], axis=0)


def whole(shape):
    return pl.BlockSpec(shape, lambda *_: (0,) * len(shape))


def project_kernel(x_ref, w_ref, gain_ref, shift_ref, bias_ref, out_ref, normed_ref):
    hat, _ = normalized(x_ref[...].astype(F32))
    normed = (hat * gain_ref[...] + shift_ref[...]).astype(BF16)
    normed_ref[...] = normed
    out_ref[...] = (nn(normed, w_ref[...]) + bias_ref[...]).astype(BF16)


def project(x, weight, gain, shift, bias):
    rows, width = x.shape
    return pl.pallas_call(
        project_kernel,
        grid=(rows // BLOCK,),
        in_specs=[
            pl.BlockSpec((BLOCK, width), lambda i: (i, 0)),
            whole((width, 3 * width)),
            whole((1, width)),
            whole((1, width)),
            whole((1, 3 * width)),
        ],
        out_specs=[
            pl.BlockSpec((BLOCK, 3 * width), lambda i: (i, 0)),
            pl.BlockSpec((BLOCK, width), lambda i: (i, 0)),
        ],
        out_shape=[
            jax.ShapeDtypeStruct((rows, 3 * width), BF16),
            jax.ShapeDtypeStruct((rows, width), BF16),
        ],
        compiler_params=params(),
        name="project",
    )(x, weight, gain, shift, bias)


def allowed_mask(start, key_at, keys, queries):
    key = key_at + lax.broadcasted_iota(jnp.int32, (keys, queries), 0)
    return key >= start


def head_rows(pair_t, head):
    row = lax.broadcasted_iota(jnp.int32, pair_t.shape, 0)
    mine = (row < HEAD_DIM) if head == 0 else (row >= HEAD_DIM)
    return jnp.where(mine, pair_t, jnp.zeros_like(pair_t))


def head_cols(pair, head):
    col = lax.broadcasted_iota(jnp.int32, pair.shape, 1)
    mine = (col < HEAD_DIM) if head == 0 else (col >= HEAD_DIM)
    return jnp.where(mine, pair, jnp.zeros_like(pair))


def masked_scores(key, query_t, start, block):
    keys = (block + 1) * BLOCK
    scores = nn(key[:keys], query_t)
    index = lax.broadcasted_iota(jnp.int32, (keys, BLOCK), 0)
    ok = index >= start
    last = block * BLOCK + lax.broadcasted_iota(jnp.int32, (keys, BLOCK), 1)
    ok = ok & (index <= last)
    return jnp.where(ok, scores, -1e30)


def attend_kernel(q_ref, k_ref, v_ref, start_ref, out_ref, lse_ref):
    rows = q_ref.shape[0]
    query_t = (q_ref[...].astype(F32) * HEAD_DIM**-0.5).T.astype(BF16)
    key = k_ref[...]
    value_t = v_ref[...].astype(F32).T.astype(BF16)
    for block in range(rows // BLOCK):
        at = slice(block * BLOCK, (block + 1) * BLOCK)
        keys = (block + 1) * BLOCK
        start = start_ref[:, at]
        outs = []
        for head in range(2):
            scores = masked_scores(key, head_rows(query_t[:, at], head), start, block)
            peak = jnp.max(scores, axis=0, keepdims=True)
            raised = jnp.exp(scores - peak)
            total = jnp.sum(raised, axis=0, keepdims=True)
            lanes = slice(head * HEAD_DIM, (head + 1) * HEAD_DIM)
            probs = (raised * (1.0 / total)).astype(BF16)
            outs.append(nn(value_t[lanes, :keys], probs))
            lse_ref[0, head : head + 1, at] = peak + jnp.log(total)
        out_ref[at, :] = jnp.concatenate(outs, axis=0).T


def attend(projected, start):
    rows, columns = projected.shape
    width = columns // 3
    pairs = width // PAIR
    return pl.pallas_call(
        attend_kernel,
        grid=(pairs,),
        in_specs=[
            pl.BlockSpec((rows, PAIR), lambda p: (0, p)),
            pl.BlockSpec((rows, PAIR), lambda p: (0, pairs + p)),
            pl.BlockSpec((rows, PAIR), lambda p: (0, 2 * pairs + p)),
            whole((1, rows)),
        ],
        out_specs=[
            pl.BlockSpec((rows, PAIR), lambda p: (0, p)),
            pl.BlockSpec((1, 2, rows), lambda p: (p, 0, 0)),
        ],
        out_shape=[
            jax.ShapeDtypeStruct((rows, width), F32),
            jax.ShapeDtypeStruct((pairs, 2, rows), F32),
        ],
        compiler_params=params(),
        name="attend",
    )(projected, projected, projected, start)


def attend_back_kernel(q_ref, k_ref, v_ref, g_ref, o_ref, lse_ref, start_ref, dq_ref, dk_ref, dv_ref, dk_acc, dv_acc):
    rows = q_ref.shape[0]
    scale = HEAD_DIM**-0.5
    scaled = q_ref[...].astype(F32) * scale
    query = scaled.astype(BF16)
    query_t = scaled.T.astype(BF16)
    key = k_ref[...]
    key_t = key.astype(F32).T.astype(BF16)
    value = v_ref[...]
    grad = g_ref[...]
    grad_f = grad.astype(F32)
    grad_t = grad_f.T.astype(BF16)
    weighted_t = (grad_f * o_ref[...]).T
    dk_acc[...] = jnp.zeros_like(dk_acc)
    dv_acc[...] = jnp.zeros_like(dv_acc)
    for block in range(rows // BLOCK):
        at = slice(block * BLOCK, (block + 1) * BLOCK)
        keys = (block + 1) * BLOCK
        start = start_ref[:, at]
        outs = []
        for head in range(2):
            lanes = slice(head * HEAD_DIM, (head + 1) * HEAD_DIM)
            inner = col_sum(weighted_t[lanes, at])
            scores = masked_scores(key, head_rows(query_t[:, at], head), start, block)
            soft = jnp.exp(scores - lse_ref[0, head : head + 1, at])
            grad_soft = nn(value[:keys], head_rows(grad_t[:, at], head))
            grad_scores = (soft * (grad_soft - inner)).astype(BF16)
            dv_acc[:keys, :] += nn(soft.astype(BF16), head_cols(grad[at], head))
            dk_acc[:keys, :] += nn(grad_scores, head_cols(query[at], head))
            outs.append(nn(key_t[lanes, :keys], grad_scores))
        dq_ref[at, :] = (jnp.concatenate(outs, axis=0) * scale).T.astype(BF16)
    dk_ref[...] = dk_acc[...].astype(BF16)
    dv_ref[...] = dv_acc[...].astype(BF16)


def attend_back(projected, grad_context, context, lse, start):
    rows, columns = projected.shape
    width = columns // 3
    pairs = width // PAIR
    pair = pl.BlockSpec((rows, PAIR), lambda p: (0, p))
    return pl.pallas_call(
        attend_back_kernel,
        grid=(pairs,),
        in_specs=[
            pair,
            pl.BlockSpec((rows, PAIR), lambda p: (0, pairs + p)),
            pl.BlockSpec((rows, PAIR), lambda p: (0, 2 * pairs + p)),
            pair,
            pair,
            pl.BlockSpec((1, 2, rows), lambda p: (p, 0, 0)),
            whole((1, rows)),
        ],
        out_specs=[pair] * 3,
        out_shape=[jax.ShapeDtypeStruct((rows, width), BF16)] * 3,
        scratch_shapes=[pltpu.VMEM((rows, PAIR), F32), pltpu.VMEM((rows, PAIR), F32)],
        compiler_params=params(),
        name="attend_back",
    )(projected, projected, projected, grad_context, context, lse, start)


def gelu_parts(value):
    phi = 0.5 * (1.0 + lax.erf(value * (1.0 / math.sqrt(2.0))))
    bell = jnp.exp(-0.5 * value * value) * (1.0 / math.sqrt(2.0 * math.pi))
    return value * phi, phi + value * bell


def middle_kernel(
    x_ref, dy_ref, ctx_ref, alive_ref, wo_ref, wu_ref, wd_ref,
    sg_ref, ss_ref, ob_ref, fg_ref, fs_ref, ub_ref, mg_ref, ms_ref, db_ref,
    out_ref, ghid_ref, gctx_ref, mixed_ref, gbranch_ref, nffn_ref, gup_ref, mid_ref, gffn_ref,
    narrow_ref, wide_ref,
):
    step = pl.program_id(0)

    @pl.when(step == 0)
    def _():
        narrow_ref[...] = jnp.zeros_like(narrow_ref)
        wide_ref[...] = jnp.zeros_like(wide_ref)

    out_weight = side_by_side(wo_ref)
    up_weight = side_by_side(wu_ref)
    down_weight = stacked(wd_ref)
    alive = alive_ref[...]
    ctx_hat, ctx_scale = normalized(ctx_ref[...])
    mixed = (ctx_hat * sg_ref[...] + ss_ref[...]).astype(BF16)
    mixed_ref[...] = mixed
    branch = nn(mixed, out_weight) + ob_ref[...]
    hidden = (x_ref[...].astype(F32) + alive * branch).astype(BF16).astype(F32)
    hid_hat, hid_scale = normalized(hidden)
    nffn = (hid_hat * fg_ref[...] + fs_ref[...]).astype(BF16)
    nffn_ref[...] = nffn
    upper = nn(nffn, up_weight) + ub_ref[...]
    active, slope = gelu_parts(upper)
    act_hat, act_scale = normalized(active)
    mid = (act_hat * mg_ref[...] + ms_ref[...]).astype(BF16)
    mid_ref[...] = mid
    result = (nn(mid, down_weight) + db_ref[...]).astype(BF16).astype(F32)
    out_ref[...] = hidden + alive * result

    upstream = dy_ref[...].astype(F32)
    gffn = (alive * upstream).astype(BF16)
    gffn_ref[...] = gffn
    gmid = nt(gffn, down_weight)
    gact = norm_back(act_hat, act_scale, mg_ref[...], gmid)
    gup = (gact * slope).astype(BF16)
    gup_ref[...] = gup
    wide_ref[0:1, :] += col_sum(gup.astype(F32))
    wide_ref[1:2, :] += col_sum(gmid * act_hat)
    wide_ref[2:3, :] += col_sum(gmid)
    gnffn = nt(gup, up_weight)
    ghid = (upstream + norm_back(hid_hat, hid_scale, fg_ref[...], gnffn)).astype(BF16)
    ghid_ref[...] = ghid
    gbranch = (alive * ghid.astype(F32)).astype(BF16)
    gbranch_ref[...] = gbranch
    gmixed = nt(gbranch, out_weight)
    gctx_ref[...] = norm_back(ctx_hat, ctx_scale, sg_ref[...], gmixed).astype(BF16)
    narrow_ref[0:1, :] += col_sum(gmixed * ctx_hat)
    narrow_ref[1:2, :] += col_sum(gmixed)
    narrow_ref[2:3, :] += col_sum(gbranch.astype(F32))
    narrow_ref[3:4, :] += col_sum(gnffn * hid_hat)
    narrow_ref[4:5, :] += col_sum(gnffn)
    narrow_ref[5:6, :] += col_sum(gffn.astype(F32))


def middle(x, dy, context, alive, out_weight, up_weight, down_weight, vectors):
    rows, width = x.shape
    hidden = 6 * up_weight.shape[2]
    row = pl.BlockSpec((BLOCK, width), lambda i: (i, 0))
    row_wide = pl.BlockSpec((BLOCK, hidden), lambda i: (i, 0))
    once = dict(pipeline_mode=pl.Buffered(1))
    narrow = whole((1, width))
    wide = whole((1, hidden))
    def shape(columns, dtype):
        return jax.ShapeDtypeStruct((rows, columns), dtype)
    return pl.pallas_call(
        middle_kernel,
        grid=(rows // BLOCK,),
        in_specs=[
            row, row, row,
            pl.BlockSpec((BLOCK, 1), lambda i: (i, 0)),
            pl.BlockSpec(out_weight.shape, lambda i: (0, 0, 0), **once),
            pl.BlockSpec(up_weight.shape, lambda i: (0, 0, 0), **once),
            pl.BlockSpec(down_weight.shape, lambda i: (0, 0, 0), **once),
            narrow, narrow, narrow, narrow, narrow, wide, wide, wide, narrow,
        ],
        out_specs=[row, row, row, row, row, row, row_wide, row_wide, row, whole((8, width)), whole((8, hidden))],
        out_shape=[
            shape(width, F32), shape(width, BF16), shape(width, BF16), shape(width, BF16), shape(width, BF16),
            shape(width, BF16), shape(hidden, BF16), shape(hidden, BF16), shape(width, BF16),
            jax.ShapeDtypeStruct((8, width), F32), jax.ShapeDtypeStruct((8, hidden), F32),
        ],
        compiler_params=params(),
        name="middle",
    )(x, dy, context, alive, out_weight, up_weight, down_weight, *vectors)


def outer_kernel(left_ref, right_ref, out_ref):
    out_ref[...] = tn(left_ref[...], right_ref[...]).astype(out_ref.dtype)


def outer(left, right, tile, dtype, name):
    rows, across = left.shape
    columns = right.shape[1]
    return pl.pallas_call(
        outer_kernel,
        grid=(across // tile,),
        in_specs=[pl.BlockSpec((rows, tile), lambda i: (0, i)), whole((rows, columns))],
        out_specs=pl.BlockSpec((tile, columns), lambda i: (i, 0)),
        out_shape=jax.ShapeDtypeStruct((across, columns), dtype),
        compiler_params=params(),
        name=name,
    )(left, right)


def project_back_kernel(dq_ref, dk_ref, dv_ref, w_ref, x_ref, ghid_ref, gain_ref, out_ref, narrow_ref):
    step = pl.program_id(0)
    width = x_ref.shape[1]

    @pl.when(step == 0)
    def _():
        narrow_ref[...] = jnp.zeros_like(narrow_ref)

    dq, dk, dv = dq_ref[...], dk_ref[...], dv_ref[...]
    gnormed = sum(
        nt(d, jnp.concatenate([w_ref[2 * n], w_ref[2 * n + 1]], axis=1)) for n, d in enumerate((dq, dk, dv))
    )
    hat, scale = normalized(x_ref[...].astype(F32))
    out_ref[...] = ghid_ref[...].astype(F32) + norm_back(hat, scale, gain_ref[...], gnormed)
    narrow_ref[0:1, :] += col_sum(gnormed * hat)
    narrow_ref[1:2, :] += col_sum(gnormed)
    narrow_ref[2:3, :] += col_sum(dq.astype(F32))
    narrow_ref[3:4, :] += col_sum(dv.astype(F32))


def project_back(dq, dk, dv, weight, x, ghid, gain):
    rows, width = x.shape
    row = pl.BlockSpec((BLOCK, width), lambda i: (i, 0))
    return pl.pallas_call(
        project_back_kernel,
        grid=(rows // BLOCK,),
        in_specs=[row, row, row, whole(weight.shape), row, row, whole((1, width))],
        out_specs=[row, whole((8, width))],
        out_shape=[jax.ShapeDtypeStruct((rows, width), F32), jax.ShapeDtypeStruct((8, width), F32)],
        compiler_params=params(),
        name="project_back",
    )(dq, dk, dv, weight, x, ghid, gain)


def row_marks(lengths_row, count):
    slots = jnp.arange(lengths_row.shape[0], dtype=jnp.int32)
    ends = jnp.sum(jnp.where(slots[:, None] <= slots[None, :], lengths_row[:, None], 0), axis=0)
    index = jnp.arange(count, dtype=jnp.int32)
    before = jnp.where(ends[None, :] <= index[:, None], ends[None, :], 0)
    alive = index < jnp.max(ends)
    start = jnp.where(alive, jnp.max(before, axis=1), index)
    return alive.astype(F32)[:, None], start[None, :]


MESH = pl.DeviceIdType.MESH
BITS = 4
CHAINS = ((3, 2, 1, 0), (0, 3, 2, 1), (1, 0, 3, 2))


def place():
    core = lax.axis_index("section")
    chip = lax.axis_index("dp")
    return core, chip, [(chip // (1 << bit)) % 2 for bit in range(BITS)]


def partner_of(chip, bits, bit):
    return chip + (1 - 2 * bits[bit]) * (1 << bit)


def at_bits(ref, values):
    return ref.at[tuple(values[bit] for bit in reversed(range(BITS)))]


def remote(source, target, sems, device):
    return pltpu.make_async_remote_copy(
        src_ref=source, dst_ref=target, send_sem=sems[0], recv_sem=sems[1], device_id=device, device_id_type=MESH
    )


class Gather:
    def __init__(self, own, other, order, sems, pass_sems):
        self.own, self.other, self.order = own, other, order
        self.sems, self.pass_sems = sems, pass_sems
        self.core, self.chip, self.bits = place()

    def step(self, stage):
        done = self.order[:stage]
        values = [slice(None) if bit in done else self.bits[bit] for bit in range(BITS)]
        part = at_bits(self.own, values)
        device = (self.core, partner_of(self.chip, self.bits, self.order[stage]))
        return remote(part, part, (self.sems.at[0, stage], self.sems.at[1, stage]), device)

    def onward(self, stage, ref):
        done = self.order[:stage]
        values = [slice(None) if bit in done else self.bits[bit] for bit in range(BITS)]
        values[self.order[stage]] = 1 - self.bits[self.order[stage]]
        part = at_bits(ref, values)
        return remote(part, part, (self.pass_sems.at[0, stage], self.pass_sems.at[1, stage]), (1 - self.core, self.chip))

    def arrive(self, stage):
        self.step(stage).wait_recv()
        if stage + 1 < BITS:
            self.step(stage + 1).start()
        self.onward(stage, self.own).start()

    def passed(self, stage):
        self.onward(stage, self.other).wait_recv()

    def drain(self):
        for stage in range(BITS):
            self.step(stage).wait_send()
            self.onward(stage, self.own).wait_send()


def greet():
    core, chip, bits = place()
    barrier = pltpu.get_barrier_semaphore()
    others = [(1 - core, chip)] + [(core, partner_of(chip, bits, bit)) for bit in range(BITS)]
    for other in others:
        pl.semaphore_signal(barrier, inc=1, device_id=other, device_id_type=MESH)
    pl.semaphore_wait(barrier, len(others))


def seed(parts, full, me, sems, sender):
    core, chip, bits = place()
    moves = []
    for index, (source, block) in enumerate(parts):
        here = at_bits(full.at[block], bits)
        moves.append((pltpu.make_async_copy(source, here, sems.at[0, index]),
                      remote(source, here, (sems.at[1, index], sems.at[2, index]), (1 - core, chip))))

    def begin():
        for local, far in moves:
            local.start()
            far.start()

    def finish_sender():
        for local, far in moves:
            local.wait()
            far.wait_send()

    def finish_other():
        for local, far in moves:
            far.wait_recv()

    return begin, finish_sender, finish_other


def front_kernel(
    x_ref, half_ref, down_ref, gain_ref, shift_ref, bias_ref, start_ref,
    projected_ref, normed_ref, context_ref, lse_ref, wqkv_ref, wo_ref, wup_ref, wdown_ref,
    seed_q, seed_o, seed_u, seed_d, chain_q, chain_o, chain_u, chain_d, pass_q, pass_o, pass_u, pass_d,
):
    core, chip, bits = place()
    rows, width = x_ref.shape
    cq, co, cu = width // 2, width // 6, 2 * width // 3
    cq = 3 * width // 6
    cd = width // 3
    is_first = core == 0
    q_begin, q_sent, q_got = seed(
        [(half_ref.at[:, b * cq : (b + 1) * cq], b) for b in range(6)], wqkv_ref, None, seed_q, None)
    o_begin, o_sent, o_got = seed(
        [(half_ref.at[:, 3 * width + b * co : 3 * width + (b + 1) * co], b) for b in range(6)], wo_ref, None, seed_o, None)
    u_begin, u_sent, u_got = seed(
        [(half_ref.at[:, b * cu : (b + 1) * cu], b) for b in range(6)], wup_ref, None, seed_u, None)

    def chains(full, sems, passes):
        return [
            Gather(full.at[3 * core + k], full.at[3 * (1 - core) + k], CHAINS[k], sems.at[k], passes.at[k])
            for k in range(3)
        ]

    q_chains = chains(wqkv_ref, chain_q, pass_q)
    o_chains = chains(wo_ref, chain_o, pass_o)
    u_chains = chains(wup_ref, chain_u, pass_u)
    d_chains = chains(wdown_ref, chain_d, pass_d)

    greet()

    @pl.when(is_first)
    def _():
        q_begin()

    d_moves = []
    for k in range(3):
        source = down_ref.at[:, k * cd : (k + 1) * cd]
        here = at_bits(wdown_ref.at[3 * core + k], bits)
        d_moves.append((pltpu.make_async_copy(source, here, seed_d.at[0, k]),
                        remote(source, here, (seed_d.at[1, k], seed_d.at[2, k]), (1 - core, chip))))
    for local, far in d_moves:
        local.start()
        far.start()

    @pl.when(is_first)
    def _():
        o_begin()

    @pl.when(core == 1)
    def _():
        u_begin()

    @pl.when(is_first)
    def _():
        q_sent()

    @pl.when(core == 1)
    def _():
        q_got()

    for chain in q_chains:
        chain.step(0).start()

    hat, _ = normalized(x_ref[...].astype(F32))
    normed_ref[...] = (hat * gain_ref[...] + shift_ref[...]).astype(BF16)

    for stage in range(BITS - 1):
        for chain in q_chains:
            chain.arrive(stage)

    @pl.when(is_first)
    def _():
        o_sent()
        u_got()

    @pl.when(core == 1)
    def _():
        u_sent()
        o_got()

    for local, far in d_moves:
        local.wait()
        far.wait()
    late = [chain for group in zip(u_chains, o_chains, d_chains) for chain in group]
    for chain in late:
        chain.step(0).start()

    for chain in q_chains:
        chain.arrive(BITS - 1)
    for chain in late:
        chain.arrive(0)
    for stage in range(BITS):
        for chain in q_chains:
            chain.passed(stage)

    normed = normed_ref[...]
    for b in range(6):
        cols = slice(b * cq, (b + 1) * cq)
        weight = wqkv_ref[b].reshape(width, cq)
        projected_ref[:, cols] = (nn(normed, weight) + bias_ref[:, cols]).astype(BF16)

    pairs = width // PAIR
    for chain in late:
        chain.arrive(1)

    def one_pair(pair, carry):
        at_q = pl.ds(pl.multiple_of(pair * PAIR, PAIR), PAIR)
        at_k = pl.ds(pl.multiple_of(width + pair * PAIR, PAIR), PAIR)
        at_v = pl.ds(pl.multiple_of(2 * width + pair * PAIR, PAIR), PAIR)
        query_t = (projected_ref[:, at_q].astype(F32) * HEAD_DIM**-0.5).T.astype(BF16)
        key = projected_ref[:, at_k]
        value_t = projected_ref[:, at_v].astype(F32).T.astype(BF16)
        for block in range(rows // BLOCK):
            at = slice(block * BLOCK, (block + 1) * BLOCK)
            keys = (block + 1) * BLOCK
            start = start_ref[:, at]
            outs = []
            for head in range(2):
                scores = masked_scores(key, head_rows(query_t[:, at], head), start, block)
                peak = jnp.max(scores, axis=0, keepdims=True)
                raised = jnp.exp(scores - peak)
                total = jnp.sum(raised, axis=0, keepdims=True)
                lanes = slice(head * HEAD_DIM, (head + 1) * HEAD_DIM)
                probs = (raised * (1.0 / total)).astype(BF16)
                outs.append(nn(value_t[lanes, :keys], probs))
                lse_ref[pair, head : head + 1, at] = peak + jnp.log(total)
            context_ref[at, at_q] = jnp.concatenate(outs, axis=0).T

        @pl.when(pair == 2)
        def _():
            for chain in late:
                chain.arrive(2)

        return carry

    lax.fori_loop(0, pairs, one_pair, 0)

    for chain in late:
        chain.arrive(3)
    for stage in range(BITS):
        for chain in late:
            chain.passed(stage)
    for chain in q_chains + late:
        chain.drain()


def front(x, half, down, gain, shift, bias, start):
    rows, width = x.shape
    mine = half.shape[0]
    mine_down = down.shape[0]
    box = (2,) * BITS
    pairs = width // PAIR
    anywhere = pl.BlockSpec(memory_space=pl.ANY)
    vmem = pl.BlockSpec(memory_space=pltpu.VMEM)
    dma = pltpu.SemaphoreType.DMA
    return pl.pallas_call(
        front_kernel,
        in_specs=[vmem, anywhere, anywhere, vmem, vmem, vmem, vmem],
        out_specs=[vmem, vmem, vmem, vmem, vmem, anywhere, anywhere, anywhere],
        out_shape=[
            jax.ShapeDtypeStruct((rows, 3 * width), BF16),
            jax.ShapeDtypeStruct((rows, width), BF16),
            jax.ShapeDtypeStruct((rows, width), F32),
            jax.ShapeDtypeStruct((pairs, 2, rows), F32),
            jax.ShapeDtypeStruct((6,) + box + (mine, width // 2), BF16),
            jax.ShapeDtypeStruct((6,) + box + (mine, width // 6), BF16),
            jax.ShapeDtypeStruct((6,) + box + (mine, 2 * width // 3), BF16),
            jax.ShapeDtypeStruct((6,) + box + (mine_down, width // 3), BF16),
        ],
        scratch_shapes=[dma((3, 6))] * 3 + [dma((3, 3))] + [dma((3, 2, BITS))] * 8,
        compiler_params=params(collective_id=1, has_side_effects=True),
        name="front",
    )(x, half, down, gain, shift, bias, start)


def one_batch(x, dy, lengths_row, attend_all, vectors):
    (pre_gain, pre_shift, query_bias, value_bias, sub_gain, sub_shift, out_bias,
     ffn_gain, ffn_shift, up_bias, mid_gain, mid_shift, down_bias) = [v[None, :] for v in vectors]
    count, width = x.shape
    alive, start = row_marks(lengths_row, count)
    bias = jnp.concatenate([query_bias, jnp.zeros_like(query_bias), value_bias], axis=1)
    projected, normed, context, lse, qkv, out_weight, up_weight, down_weight = attend_all(
        x, pre_gain, pre_shift, bias, start
    )
    out, ghid, gctx, mixed, gbranch, nffn, gup, mid, gffn, narrow, wide = middle(
        x, dy, context, alive, out_weight, up_weight, down_weight,
        (sub_gain, sub_shift, out_bias, ffn_gain, ffn_shift, up_bias, mid_gain, mid_shift, down_bias),
    )
    grad_up = outer(nffn, gup, 256, F32, "outer_up")
    grad_down = outer(mid, gffn, 512, F32, "outer_down")
    dq, dk, dv = attend_back(projected, gctx, context, lse, start)
    grad_out = outer(mixed, gbranch, 256, F32, "outer_out")
    grad_x, pre = project_back(dq, dk, dv, qkv, x, ghid, pre_gain)
    grads = [outer(normed, d, 256, F32, "outer_qkv") for d in (dq, dk, dv)]
    grad_attention = jnp.concatenate(grads + [grad_out], axis=1)
    small = (pre[0], pre[1], pre[2], pre[3], narrow[0], narrow[1], narrow[2], narrow[3], narrow[4],
             wide[0], wide[1], wide[2], narrow[5])
    return (out, grad_x), (grad_attention, grad_up, grad_down, small)


def shards(tokens, out_grad, seq_lengths, half_weights, down_weight, *all_vectors):
    section = lax.axis_index("section")
    sections = lax.axis_size("section")
    both = ("section", "dp")
    width = tokens.shape[1]
    batches = seq_lengths.shape[0]
    count = tokens.shape[0] // batches
    own_batches = batches // sections
    own_rows = own_batches * count
    hidden_units = half_weights.shape[2]
    shares = sections * lax.axis_size("dp")

    fused = (
        sections == 2
        and shares == sections << BITS
        and own_batches == 1
        and half_weights.shape[1] % 16 == 0
        and down_weight.shape[0] % 16 == 0
    )
    if fused:

        def attend_all(x, gain, shift, bias, start):
            *rest, qkv, out_weight, up_weight, down_full = front(
                x, half_weights[0], down_weight, gain, shift, bias, start
            )
            blocks = [w.reshape(6, -1, w.shape[-1]) for w in (qkv, out_weight, up_weight, down_full)]
            return (*rest, *blocks)

    else:
        blocks = lax.all_gather(half_weights[0], both, axis=0, tiled=True)
        blocks = blocks.reshape(sections, width, hidden_units)
        down_full = lax.all_gather(down_weight, both, axis=0, tiled=True)

        def in_blocks(array):
            return array.reshape(array.shape[0], 6, -1).transpose(1, 0, 2)

        out_weight = in_blocks(blocks[0][:, 3 * width :])
        up_weight = in_blocks(blocks[1])
        down_blocks = down_full.reshape(2, -1, 3, width // 3).transpose(0, 2, 1, 3)
        down_blocks = down_blocks.reshape(6, -1, width // 3)
        qkv = blocks[0][:, : 3 * width]

        def attend_all(x, gain, shift, bias, start):
            projected, normed = project(x, qkv, gain, shift, bias)
            context, lse = attend(projected, start)
            return projected, normed, context, lse, in_blocks(qkv), out_weight, up_weight, down_blocks

    def own(array, rows):
        return lax.dynamic_slice_in_dim(array, section * rows, rows, axis=0)

    x_rows = own(tokens, own_rows)
    dy_rows = own(out_grad, own_rows)
    lengths = own(seq_lengths, own_batches)
    rows, sums = [], None
    for index in range(own_batches):
        at = slice(index * count, (index + 1) * count)
        row, more = one_batch(x_rows[at], dy_rows[at], lengths[index], attend_all, all_vectors)
        rows.append(row)
        sums = more if sums is None else jax.tree.map(jnp.add, sums, more)
    out_block = jnp.concatenate([row[0] for row in rows], axis=0)
    grad_rows = jnp.concatenate([row[1] for row in rows], axis=0)
    grad_attention, grad_up, grad_down, vectors = sums

    block_part = lax.psum_scatter(
        jnp.concatenate([grad_attention, grad_up], axis=0), both, scatter_dimension=0, tiled=True
    )
    down_part = lax.psum_scatter(grad_down, both, scatter_dimension=0, tiled=True)
    packed = jnp.concatenate([vector.reshape(shares, -1) for vector in vectors], axis=1)
    packed = lax.psum_scatter(packed, both, scatter_dimension=0, tiled=True).reshape(-1)
    parts, start = [], 0
    for vector in vectors:
        size = vector.shape[0] // shares
        parts.append(packed[start : start + size])
        start += size

    layer_out = lax.all_gather(out_block, "section", axis=0, tiled=True)
    tokens_grad = lax.all_to_all(grad_rows, "section", split_axis=1, concat_axis=0, tiled=True)
    return (layer_out, tokens_grad, block_part[None], down_part, *parts)


def solution(mesh):
    replicated = P()
    return jax.shard_map(
        shards,
        mesh=mesh,
        in_specs=(P("dp", None), P("dp", None), P("dp", None), P("section", "dp", None), P(("section", "dp"), None))
        + (replicated,) * 13,
        out_specs=(P("dp", None), P("dp", "section"), P("section", "dp", None), P(("section", "dp"), None))
        + (P(("section", "dp")),) * 13,
        check_vma=False,
    )
```

```python
import functools
import math

import jax
import jax.numpy as jnp
from jax import lax
from jax.experimental import pallas as pl
from jax.experimental.pallas import tpu as pltpu
from jax.sharding import PartitionSpec as P

HEAD_DIM = 64
PAIR = 2 * HEAD_DIM
EPS = 1e-05
BLOCK = 256
F32 = jnp.float32
BF16 = jnp.bfloat16
VMEM_LIMIT = 60 * 1024 * 1024


def nn(left, right):
    return lax.dot_general(left, right, (((1,), (0,)), ((), ())), preferred_element_type=F32)


def nt(left, right):
    return lax.dot_general(left, right, (((1,), (1,)), ((), ())), preferred_element_type=F32)


def tn(left, right):
    return lax.dot_general(left, right, (((0,), (0,)), ((), ())), preferred_element_type=F32)


def col_sum(value):
    return jnp.sum(value, axis=0, keepdims=True)


def normalized(value):
    center = jnp.mean(value, axis=-1, keepdims=True)
    centered = value - center
    spread = jnp.mean(centered * centered, axis=-1, keepdims=True)
    scale = lax.rsqrt(spread + EPS)
    return centered * scale, scale


def norm_back(hat, scale, gain, upstream):
    scaled = upstream * gain
    first = jnp.mean(scaled, axis=-1, keepdims=True)
    second = jnp.mean(scaled * hat, axis=-1, keepdims=True)
    return (scaled - first - hat * second) * scale


def params(**more):
    return pltpu.CompilerParams(vmem_limit_bytes=VMEM_LIMIT, **more)


def split_rest(ref):
    _, width, columns = ref.shape
    cu, co, cd = 4 * columns // 9, columns // 9, 2 * columns // 9
    up = jnp.concatenate([ref[b, :, :cu] for b in range(6)], axis=1)
    out = jnp.concatenate([ref[b, :, cu : cu + co] for b in range(6)], axis=1)
    halves = []
    for h in range(2):
        parts = []
        for n in range(2):
            at = cu + co + n * cd
            part = jnp.concatenate([ref[3 * h + k, :, at : at + cd] for k in range(3)], axis=1)
            parts.append(part.reshape(1 << BITS, 1, width >> BITS, width))
        halves.append(jnp.concatenate(parts, axis=1).reshape(2 * width, width))
    return out, up, jnp.concatenate(halves, axis=0)


def whole(shape):
    return pl.BlockSpec(shape, lambda *_: (0,) * len(shape))


def project_kernel(x_ref, w_ref, gain_ref, shift_ref, bias_ref, out_ref, normed_ref):
    hat, _ = normalized(x_ref[...].astype(F32))
    normed = (hat * gain_ref[...] + shift_ref[...]).astype(BF16)
    normed_ref[...] = normed
    out_ref[...] = (nn(normed, w_ref[...]) + bias_ref[...]).astype(BF16)


def project(x, weight, gain, shift, bias):
    rows, width = x.shape
    return pl.pallas_call(
        project_kernel,
        grid=(rows // BLOCK,),
        in_specs=[
            pl.BlockSpec((BLOCK, width), lambda i: (i, 0)),
            whole((width, 3 * width)),
            whole((1, width)),
            whole((1, width)),
            whole((1, 3 * width)),
        ],
        out_specs=[
            pl.BlockSpec((BLOCK, 3 * width), lambda i: (i, 0)),
            pl.BlockSpec((BLOCK, width), lambda i: (i, 0)),
        ],
        out_shape=[
            jax.ShapeDtypeStruct((rows, 3 * width), BF16),
            jax.ShapeDtypeStruct((rows, width), BF16),
        ],
        compiler_params=params(),
        name="project",
    )(x, weight, gain, shift, bias)


def allowed_mask(start, key_at, keys, queries):
    key = key_at + lax.broadcasted_iota(jnp.int32, (keys, queries), 0)
    return key >= start


def head_rows(pair_t, head):
    row = lax.broadcasted_iota(jnp.int32, pair_t.shape, 0)
    mine = (row < HEAD_DIM) if head == 0 else (row >= HEAD_DIM)
    return jnp.where(mine, pair_t, jnp.zeros_like(pair_t))


def head_cols(pair, head):
    col = lax.broadcasted_iota(jnp.int32, pair.shape, 1)
    mine = (col < HEAD_DIM) if head == 0 else (col >= HEAD_DIM)
    return jnp.where(mine, pair, jnp.zeros_like(pair))


def masked_scores(key, query_t, start, block):
    keys = (block + 1) * BLOCK
    scores = nn(key[:keys], query_t)
    index = lax.broadcasted_iota(jnp.int32, (keys, BLOCK), 0)
    ok = index >= start
    last = block * BLOCK + lax.broadcasted_iota(jnp.int32, (keys, BLOCK), 1)
    ok = ok & (index <= last)
    return jnp.where(ok, scores, -1e30)


def attend_pair(query, key, value, start_ref, out_ref, lse_ref):
    query_t = (query.astype(F32) * HEAD_DIM**-0.5).T.astype(BF16)
    value_t = value.astype(F32).T.astype(BF16)
    for block in range(query.shape[0] // BLOCK):
        at = slice(block * BLOCK, (block + 1) * BLOCK)
        keys = (block + 1) * BLOCK
        start = start_ref[:, at]
        outs = []
        for head in range(2):
            scores = masked_scores(key, head_rows(query_t[:, at], head), start, block)
            peak = jnp.max(scores, axis=0, keepdims=True)
            raised = jnp.exp(scores - peak)
            total = jnp.sum(raised, axis=0, keepdims=True)
            lanes = slice(head * HEAD_DIM, (head + 1) * HEAD_DIM)
            probs = (raised * (1.0 / total)).astype(BF16)
            outs.append(nn(value_t[lanes, :keys], probs))
            lse_ref[head : head + 1, at] = peak + jnp.log(total)
        out_ref[at, :] = jnp.concatenate(outs, axis=0).T


def attend_kernel(q_ref, k_ref, v_ref, start_ref, out_ref, lse_ref):
    attend_pair(q_ref[...], k_ref[...], v_ref[...], start_ref, out_ref, lse_ref.at[0])


def attend(projected, start):
    rows, columns = projected.shape
    width = columns // 3
    pairs = width // PAIR
    return pl.pallas_call(
        attend_kernel,
        grid=(pairs,),
        in_specs=[
            pl.BlockSpec((rows, PAIR), lambda p: (0, p)),
            pl.BlockSpec((rows, PAIR), lambda p: (0, pairs + p)),
            pl.BlockSpec((rows, PAIR), lambda p: (0, 2 * pairs + p)),
            whole((1, rows)),
        ],
        out_specs=[
            pl.BlockSpec((rows, PAIR), lambda p: (0, p)),
            pl.BlockSpec((1, 2, rows), lambda p: (p, 0, 0)),
        ],
        out_shape=[
            jax.ShapeDtypeStruct((rows, width), F32),
            jax.ShapeDtypeStruct((pairs, 2, rows), F32),
        ],
        compiler_params=params(),
        name="attend",
    )(projected, projected, projected, start)


def attend_back_pair(query, key, value, grad, context, lse_ref, start_ref, dq_ref, dk_ref, dv_ref, dk_acc, dv_acc):
    scale = HEAD_DIM**-0.5
    scaled = query.astype(F32) * scale
    query = scaled.astype(BF16)
    query_t = scaled.T.astype(BF16)
    key_t = key.astype(F32).T.astype(BF16)
    grad_f = grad.astype(F32)
    grad_t = grad_f.T.astype(BF16)
    weighted_t = (grad_f * context).T
    dk_acc[...] = jnp.zeros_like(dk_acc)
    dv_acc[...] = jnp.zeros_like(dv_acc)
    for block in range(query.shape[0] // BLOCK):
        at = slice(block * BLOCK, (block + 1) * BLOCK)
        keys = (block + 1) * BLOCK
        start = start_ref[:, at]
        outs = []
        for head in range(2):
            lanes = slice(head * HEAD_DIM, (head + 1) * HEAD_DIM)
            inner = col_sum(weighted_t[lanes, at])
            scores = masked_scores(key, head_rows(query_t[:, at], head), start, block)
            soft = jnp.exp(scores - lse_ref[head : head + 1, at])
            grad_soft = nn(value[:keys], head_rows(grad_t[:, at], head))
            grad_scores = (soft * (grad_soft - inner)).astype(BF16)
            dv_acc[:keys, :] += nn(soft.astype(BF16), head_cols(grad[at], head))
            dk_acc[:keys, :] += nn(grad_scores, head_cols(query[at], head))
            outs.append(nn(key_t[lanes, :keys], grad_scores))
        dq_ref[at, :] = (jnp.concatenate(outs, axis=0) * scale).T.astype(BF16)
    dk_ref[...] = dk_acc[...].astype(BF16)
    dv_ref[...] = dv_acc[...].astype(BF16)


def attend_back_kernel(q_ref, k_ref, v_ref, g_ref, o_ref, lse_ref, start_ref, dq_ref, dk_ref, dv_ref, dk_acc, dv_acc):
    attend_back_pair(
        q_ref[...], k_ref[...], v_ref[...], g_ref[...], o_ref[...], lse_ref.at[0], start_ref,
        dq_ref, dk_ref, dv_ref, dk_acc, dv_acc,
    )


def attend_back(projected, grad_context, context, lse, start):
    rows, columns = projected.shape
    width = columns // 3
    pairs = width // PAIR
    pair = pl.BlockSpec((rows, PAIR), lambda p: (0, p))
    return pl.pallas_call(
        attend_back_kernel,
        grid=(pairs,),
        in_specs=[
            pair,
            pl.BlockSpec((rows, PAIR), lambda p: (0, pairs + p)),
            pl.BlockSpec((rows, PAIR), lambda p: (0, 2 * pairs + p)),
            pair,
            pair,
            pl.BlockSpec((1, 2, rows), lambda p: (p, 0, 0)),
            whole((1, rows)),
        ],
        out_specs=[pair] * 3,
        out_shape=[jax.ShapeDtypeStruct((rows, width), BF16)] * 3,
        scratch_shapes=[pltpu.VMEM((rows, PAIR), F32), pltpu.VMEM((rows, PAIR), F32)],
        compiler_params=params(),
        name="attend_back",
    )(projected, projected, projected, grad_context, context, lse, start)


def gelu_parts(value):
    phi = 0.5 * (1.0 + lax.erf(value * (1.0 / math.sqrt(2.0))))
    bell = jnp.exp(-0.5 * value * value) * (1.0 / math.sqrt(2.0 * math.pi))
    return value * phi, phi + value * bell


def middle_kernel(
    x_ref, dy_ref, ctx_ref, alive_ref, rest_ref,
    sg_ref, ss_ref, ob_ref, fg_ref, fs_ref, ub_ref, mg_ref, ms_ref, db_ref,
    out_ref, ghid_ref, gctx_ref, mixed_ref, gbranch_ref, nffn_ref, gup_ref, mid_ref, gffn_ref,
    narrow_ref, wide_ref,
):
    step = pl.program_id(0)

    @pl.when(step == 0)
    def _():
        narrow_ref[...] = jnp.zeros_like(narrow_ref)
        wide_ref[...] = jnp.zeros_like(wide_ref)

    out_weight, up_weight, down_weight = split_rest(rest_ref)
    alive = alive_ref[...]
    ctx_hat, ctx_scale = normalized(ctx_ref[...])
    mixed = (ctx_hat * sg_ref[...] + ss_ref[...]).astype(BF16)
    mixed_ref[...] = mixed
    branch = nn(mixed, out_weight) + ob_ref[...]
    hidden = (x_ref[...].astype(F32) + alive * branch).astype(BF16).astype(F32)
    hid_hat, hid_scale = normalized(hidden)
    nffn = (hid_hat * fg_ref[...] + fs_ref[...]).astype(BF16)
    nffn_ref[...] = nffn
    upper = nn(nffn, up_weight) + ub_ref[...]
    active, slope = gelu_parts(upper)
    act_hat, act_scale = normalized(active)
    mid = (act_hat * mg_ref[...] + ms_ref[...]).astype(BF16)
    mid_ref[...] = mid
    result = (nn(mid, down_weight) + db_ref[...]).astype(BF16).astype(F32)
    out_ref[...] = hidden + alive * result

    upstream = dy_ref[...].astype(F32)
    gffn = (alive * upstream).astype(BF16)
    gffn_ref[...] = gffn
    gmid = nt(gffn, down_weight)
    gact = norm_back(act_hat, act_scale, mg_ref[...], gmid)
    gup = (gact * slope).astype(BF16)
    gup_ref[...] = gup
    wide_ref[0:1, :] += col_sum(gup.astype(F32))
    wide_ref[1:2, :] += col_sum(gmid * act_hat)
    wide_ref[2:3, :] += col_sum(gmid)
    gnffn = nt(gup, up_weight)
    ghid = (upstream + norm_back(hid_hat, hid_scale, fg_ref[...], gnffn)).astype(BF16)
    ghid_ref[...] = ghid
    gbranch = (alive * ghid.astype(F32)).astype(BF16)
    gbranch_ref[...] = gbranch
    gmixed = nt(gbranch, out_weight)
    gctx_ref[...] = norm_back(ctx_hat, ctx_scale, sg_ref[...], gmixed).astype(BF16)
    narrow_ref[0:1, :] += col_sum(gmixed * ctx_hat)
    narrow_ref[1:2, :] += col_sum(gmixed)
    narrow_ref[2:3, :] += col_sum(gbranch.astype(F32))
    narrow_ref[3:4, :] += col_sum(gnffn * hid_hat)
    narrow_ref[4:5, :] += col_sum(gnffn)
    narrow_ref[5:6, :] += col_sum(gffn.astype(F32))


def middle(x, dy, context, alive, rest, vectors):
    rows, width = x.shape
    hidden = 4 * width
    row = pl.BlockSpec((BLOCK, width), lambda i: (i, 0))
    row_wide = pl.BlockSpec((BLOCK, hidden), lambda i: (i, 0))
    once = dict(pipeline_mode=pl.Buffered(1))
    narrow = whole((1, width))
    wide = whole((1, hidden))
    def shape(columns, dtype):
        return jax.ShapeDtypeStruct((rows, columns), dtype)
    return pl.pallas_call(
        middle_kernel,
        grid=(rows // BLOCK,),
        in_specs=[
            row, row, row,
            pl.BlockSpec((BLOCK, 1), lambda i: (i, 0)),
            pl.BlockSpec(rest.shape, lambda i: (0, 0, 0), **once),
            narrow, narrow, narrow, narrow, narrow, wide, wide, wide, narrow,
        ],
        out_specs=[row, row, row, row, row, row, row_wide, row_wide, row, whole((8, width)), whole((8, hidden))],
        out_shape=[
            shape(width, F32), shape(width, BF16), shape(width, BF16), shape(width, BF16), shape(width, BF16),
            shape(width, BF16), shape(hidden, BF16), shape(hidden, BF16), shape(width, BF16),
            jax.ShapeDtypeStruct((8, width), F32), jax.ShapeDtypeStruct((8, hidden), F32),
        ],
        compiler_params=params(),
        name="middle",
    )(x, dy, context, alive, rest, *vectors)


def outer_kernel(left_ref, right_ref, out_ref):
    out_ref[...] = tn(left_ref[...], right_ref[...]).astype(out_ref.dtype)


def outer(left, right, tile, dtype, name):
    rows, across = left.shape
    columns = right.shape[1]
    return pl.pallas_call(
        outer_kernel,
        grid=(across // tile,),
        in_specs=[pl.BlockSpec((rows, tile), lambda i: (0, i)), whole((rows, columns))],
        out_specs=pl.BlockSpec((tile, columns), lambda i: (i, 0)),
        out_shape=jax.ShapeDtypeStruct((across, columns), dtype),
        compiler_params=params(),
        name=name,
    )(left, right)


def project_back_kernel(dq_ref, dk_ref, dv_ref, w_ref, x_ref, ghid_ref, gain_ref, out_ref, narrow_ref):
    step = pl.program_id(0)
    width = x_ref.shape[1]

    @pl.when(step == 0)
    def _():
        narrow_ref[...] = jnp.zeros_like(narrow_ref)

    dq, dk, dv = dq_ref[...], dk_ref[...], dv_ref[...]
    gnormed = nt(dq, w_ref[:, :width]) + nt(dk, w_ref[:, width : 2 * width]) + nt(dv, w_ref[:, 2 * width :])
    hat, scale = normalized(x_ref[...].astype(F32))
    out_ref[...] = ghid_ref[...].astype(F32) + norm_back(hat, scale, gain_ref[...], gnormed)
    narrow_ref[0:1, :] += col_sum(gnormed * hat)
    narrow_ref[1:2, :] += col_sum(gnormed)
    narrow_ref[2:3, :] += col_sum(dq.astype(F32))
    narrow_ref[3:4, :] += col_sum(dv.astype(F32))


def project_back(dq, dk, dv, weight, x, ghid, gain):
    rows, width = x.shape
    row = pl.BlockSpec((BLOCK, width), lambda i: (i, 0))
    return pl.pallas_call(
        project_back_kernel,
        grid=(rows // BLOCK,),
        in_specs=[row, row, row, whole(weight.shape), row, row, whole((1, width))],
        out_specs=[row, whole((8, width))],
        out_shape=[jax.ShapeDtypeStruct((rows, width), F32), jax.ShapeDtypeStruct((8, width), F32)],
        compiler_params=params(),
        name="project_back",
    )(dq, dk, dv, weight, x, ghid, gain)


def row_marks(lengths_row, count):
    slots = jnp.arange(lengths_row.shape[0], dtype=jnp.int32)
    ends = jnp.sum(jnp.where(slots[:, None] <= slots[None, :], lengths_row[:, None], 0), axis=0)
    index = jnp.arange(count, dtype=jnp.int32)
    before = jnp.where(ends[None, :] <= index[:, None], ends[None, :], 0)
    alive = index < jnp.max(ends)
    start = jnp.where(alive, jnp.max(before, axis=1), index)
    return alive.astype(F32)[:, None], start[None, :]


MESH = pl.DeviceIdType.MESH
BITS = 4
CHAINS = ((3, 2, 1, 0), (0, 3, 2, 1), (1, 0, 3, 2))


def place():
    core = lax.axis_index("section")
    chip = lax.axis_index("dp")
    return core, chip, [(chip // (1 << bit)) % 2 for bit in range(BITS)]


def partner_of(chip, bits, bit):
    return chip + (1 - 2 * bits[bit]) * (1 << bit)


def at_bits(ref, values):
    return ref.at[tuple(values[bit] for bit in reversed(range(BITS)))]


def remote(source, target, sems, device):
    return pltpu.make_async_remote_copy(
        src_ref=source, dst_ref=target, send_sem=sems[0], recv_sem=sems[1], device_id=device, device_id_type=MESH
    )


class Gather:
    def __init__(self, own, other, order, sems, pass_sems):
        self.own, self.other, self.order = own, other, order
        self.sems, self.pass_sems = sems, pass_sems
        self.core, self.chip, self.bits = place()

    def step(self, stage):
        done = self.order[:stage]
        values = [slice(None) if bit in done else self.bits[bit] for bit in range(BITS)]
        part = at_bits(self.own, values)
        device = (self.core, partner_of(self.chip, self.bits, self.order[stage]))
        return remote(part, part, (self.sems.at[0, stage], self.sems.at[1, stage]), device)

    def onward(self, stage, ref):
        done = self.order[:stage]
        values = [slice(None) if bit in done else self.bits[bit] for bit in range(BITS)]
        values[self.order[stage]] = 1 - self.bits[self.order[stage]]
        part = at_bits(ref, values)
        return remote(part, part, (self.pass_sems.at[0, stage], self.pass_sems.at[1, stage]), (1 - self.core, self.chip))

    def arrive(self, stage):
        self.step(stage).wait_recv()
        if stage + 1 < BITS:
            self.step(stage + 1).start()
        self.onward(stage, self.own).start()

    def passed(self, stage):
        self.onward(stage, self.other).wait_recv()

    def drain(self):
        for stage in range(BITS):
            self.step(stage).wait_send()
            self.onward(stage, self.own).wait_send()


def greet():
    core, chip, bits = place()
    barrier = pltpu.get_barrier_semaphore()
    others = [(1 - core, chip)] + [(core, partner_of(chip, bits, bit)) for bit in range(BITS)]
    for other in others:
        pl.semaphore_signal(barrier, inc=1, device_id=other, device_id_type=MESH)
    pl.semaphore_wait(barrier, len(others))


def seed(parts, sems):
    core, chip, bits = place()
    moves = []
    for index, (source, block) in enumerate(parts):
        here = at_bits(block, bits)
        local = pltpu.make_async_copy(source, here, sems.at[0, index])
        far = remote(source, here, (sems.at[1, index], sems.at[2, index]), (1 - core, chip))
        moves.append((local, far))

    def begin():
        for local, far in moves:
            local.start()
            far.start()

    def sent():
        for local, far in moves:
            local.wait()
            far.wait_send()

    def got():
        for _, far in moves:
            far.wait_recv()

    return begin, sent, got


def front_kernel(
    x_ref, half_ref, down_ref, gain_ref, shift_ref, bias_ref, start_ref,
    projected_ref, normed_ref, context_ref, lse_ref, wqkv_ref, rest_ref,
    seed_q, seed_o, seed_u, seed_d, chain_q, chain_r, pass_q, pass_r,
):
    core, chip, bits = place()
    rows, width = x_ref.shape
    mine = half_ref.shape[0]
    cq, co, cu, cd = width // 2, width // 6, 2 * width // 3, width // 3
    first = core == 0
    second = core == 1
    box = (slice(None),) * BITS
    q_begin, q_sent, q_got = seed(
        [(half_ref.at[:, b * cq : (b + 1) * cq], wqkv_ref.at[b]) for b in range(6)], seed_q)
    o_begin, o_sent, o_got = seed(
        [(half_ref.at[:, 3 * width + b * co : 3 * width + (b + 1) * co],
          rest_ref.at[(b, *box, slice(None), slice(cu, cu + co))]) for b in range(6)], seed_o)
    u_begin, u_sent, u_got = seed(
        [(half_ref.at[:, b * cu : (b + 1) * cu],
          rest_ref.at[(b, *box, slice(None), slice(0, cu))]) for b in range(6)], seed_u)
    d_begin, d_sent, d_got = seed(
        [(down_ref.at[n * mine : (n + 1) * mine, k * cd : (k + 1) * cd],
          rest_ref.at[(3 * core + k, *box, slice(None), slice(cu + co + n * cd, cu + co + (n + 1) * cd))])
         for k in range(3) for n in range(2)], seed_d)
    _, _, d_other = seed(
        [(down_ref.at[n * mine : (n + 1) * mine, k * cd : (k + 1) * cd],
          rest_ref.at[(3 * (1 - core) + k, *box, slice(None), slice(cu + co + n * cd, cu + co + (n + 1) * cd))])
         for k in range(3) for n in range(2)], seed_d)

    def chains(full, sems, passes):
        return [
            Gather(full.at[3 * core + k], full.at[3 * (1 - core) + k], CHAINS[k], sems.at[k], passes.at[k])
            for k in range(3)
        ]

    q_chains = chains(wqkv_ref, chain_q, pass_q)
    late = chains(rest_ref, chain_r, pass_r)

    greet()
    pl.when(first)(q_begin)
    d_begin()
    pl.when(first)(o_begin)
    pl.when(second)(u_begin)
    pl.when(first)(q_sent)
    pl.when(second)(q_got)
    for chain in q_chains:
        chain.step(0).start()

    hat, _ = normalized(x_ref[...].astype(F32))
    normed_ref[...] = (hat * gain_ref[...] + shift_ref[...]).astype(BF16)

    for stage in range(BITS - 1):
        for chain in q_chains:
            chain.arrive(stage)

    @pl.when(first)
    def _():
        o_sent()
        u_got()

    @pl.when(second)
    def _():
        u_sent()
        o_got()

    d_sent()
    d_other()
    for chain in late:
        chain.step(0).start()
    for chain in q_chains:
        chain.arrive(BITS - 1)
    for chain in late:
        chain.arrive(0)
    for stage in range(BITS):
        for chain in q_chains:
            chain.passed(stage)

    normed = normed_ref[...]
    for b in range(6):
        cols = slice(b * cq, (b + 1) * cq)
        weight = wqkv_ref[b].reshape(width, cq)
        projected_ref[:, cols] = (nn(normed, weight) + bias_ref[:, cols]).astype(BF16)

    pairs = width // PAIR
    for chain in late:
        chain.arrive(1)

    def one_pair(pair, carry):
        at_q = pl.ds(pl.multiple_of(pair * PAIR, PAIR), PAIR)
        at_k = pl.ds(pl.multiple_of(width + pair * PAIR, PAIR), PAIR)
        at_v = pl.ds(pl.multiple_of(2 * width + pair * PAIR, PAIR), PAIR)
        attend_pair(
            projected_ref[:, at_q], projected_ref[:, at_k], projected_ref[:, at_v], start_ref,
            context_ref.at[:, at_q], lse_ref.at[pair],
        )

        @pl.when(pair == 2)
        def _():
            for chain in late:
                chain.arrive(2)

        return carry

    lax.fori_loop(0, pairs, one_pair, 0)

    for chain in late:
        chain.arrive(3)
    for stage in range(BITS):
        for chain in late:
            chain.passed(stage)
    for chain in q_chains + late:
        chain.drain()


def front(x, half, down, gain, shift, bias, start):
    rows, width = x.shape
    mine = half.shape[0]
    box = (2,) * BITS
    pairs = width // PAIR
    anywhere = pl.BlockSpec(memory_space=pl.ANY)
    vmem = pl.BlockSpec(memory_space=pltpu.VMEM)
    dma = pltpu.SemaphoreType.DMA
    return pl.pallas_call(
        front_kernel,
        in_specs=[vmem, anywhere, anywhere, vmem, vmem, vmem, vmem],
        out_specs=[vmem, vmem, vmem, vmem, vmem, anywhere],
        out_shape=[
            jax.ShapeDtypeStruct((rows, 3 * width), BF16),
            jax.ShapeDtypeStruct((rows, width), BF16),
            jax.ShapeDtypeStruct((rows, width), F32),
            jax.ShapeDtypeStruct((pairs, 2, rows), F32),
            jax.ShapeDtypeStruct((6,) + box + (mine, width // 2), BF16),
            jax.ShapeDtypeStruct((6,) + box + (mine, 3 * width // 2), BF16),
        ],
        scratch_shapes=[dma((3, 6))] * 4 + [dma((3, 2, BITS))] * 4,
        compiler_params=params(collective_id=1, has_side_effects=True),
        name="front",
    )(x, half, down, gain, shift, bias, start)


ORDERS = tuple(tuple(reversed(chain)) for chain in CHAINS)


def outer_rest_kernel(nffn_ref, gup_ref, mixed_ref, gbranch_ref, mid_ref, gffn_ref, out_ref, nffn_t, mixed_t, mid_t):
    block = pl.program_id(0)
    rows, width = nffn_ref.shape
    cu, co, cd = 2 * width // 3, width // 6, width // 3

    @pl.when(block == 0)
    def _():
        nffn_t[...] = nffn_ref[...].T
        mixed_t[...] = mixed_ref[...].T

    @pl.when(block % 3 == 0)
    def _():
        mid_t[...] = mid_ref[...].T

    out_ref[0, :, :cu] = nn(nffn_t[...], gup_ref[...]).astype(BF16)
    out_ref[0, :, cu : cu + co] = nn(mixed_t[...], gbranch_ref[...]).astype(BF16)
    down = nn(mid_t[...], gffn_ref[...]).astype(BF16)
    chips = 1 << BITS
    down = down.reshape(chips, 2, width // chips, cd)
    for n in range(2):
        at = cu + co + n * cd
        out_ref[0, :, at : at + cd] = down[:, n].reshape(width, cd)


def outer_rest(nffn, gup, mixed, gbranch, mid, gffn):
    rows, width = nffn.shape
    cu, co, cd = 2 * width // 3, width // 6, width // 3
    return pl.pallas_call(
        outer_rest_kernel,
        grid=(6,),
        in_specs=[
            whole((rows, width)),
            pl.BlockSpec((rows, cu), lambda b: (0, b)),
            whole((rows, width)),
            pl.BlockSpec((rows, co), lambda b: (0, b)),
            pl.BlockSpec((rows, 2 * width), lambda b: (0, b // 3)),
            pl.BlockSpec((rows, cd), lambda b: (0, b % 3)),
        ],
        out_specs=pl.BlockSpec((1, width, 3 * width // 2), lambda b: (b, 0, 0)),
        out_shape=jax.ShapeDtypeStruct((6, width, 3 * width // 2), BF16),
        scratch_shapes=[
            pltpu.VMEM((width, rows), BF16), pltpu.VMEM((width, rows), BF16), pltpu.VMEM((2 * width, rows), BF16)
        ],
        compiler_params=params(),
        name="outer_rest",
    )(nffn, gup, mixed, gbranch, mid, gffn)


class Scatter:
    def __init__(self, total, landings, order, sems, final):
        self.total, self.landings, self.order, self.sems, self.final = total, landings, order, sems, final
        self.core, self.chip, self.bits = place()

    def send(self, stage):
        values = [slice(None)] * BITS
        for bit in self.order[:stage]:
            values[bit] = self.bits[bit]
        values[self.order[stage]] = 1 - self.bits[self.order[stage]]
        device = (self.core, partner_of(self.chip, self.bits, self.order[stage]))
        sems = (self.sems.at[0, stage], self.sems.at[1, stage])
        return remote(at_bits(self.total, values), self.landings[stage], sems, device)

    def arrive(self, stage):
        self.send(stage).wait_recv()
        landing = self.landings[stage]
        values = [None] * BITS
        for bit in self.order[: stage + 1]:
            values[bit] = self.bits[bit]
        free = [bit for bit in reversed(range(BITS)) if values[bit] is None]
        if not free:
            at = tuple(self.bits[bit] for bit in reversed(range(BITS)))
            self.final[...] = self.total[at].astype(F32) + landing[...].astype(F32)
            return
        for index in range(1 << len(free)):
            picks = [(index >> (len(free) - 1 - n)) & 1 for n in range(len(free))]
            for bit, pick in zip(free, picks):
                values[bit] = pick
            at = tuple(values[bit] for bit in reversed(range(BITS)))
            self.total[at] = self.total[at] + landing[tuple(picks)]
        self.send(stage + 1).start()

    def drain(self):
        for stage in range(BITS):
            self.send(stage).wait_send()


def back_kernel(
    projected_ref, gctx_ref, context_ref, lse_ref, start_ref, normed_ref, x_ref, ghid_ref, gain_ref, wqkv_ref,
    narrow_ref, wide_ref, rest_ref, rows_ref,
    layer_ref, grad_ref, half_ref, down_ref, slim_ref, broad_ref,
    dproj, dk_acc, dv_acc, normed_t, far_rows,
    total_r, first_r, r0, r1, r2, r3, final_r, other_r,
    total_q, far_q, first_q, q0, q1, q2, q3, final_q, other_q,
    small, small_in,
    local_sems, swap_sems, chain_r, chain_q, small_sems,
):
    core, chip, bits = place()
    rows, width = x_ref.shape
    mine = half_ref.shape[0]
    pairs = width // PAIR
    cq, co, cu, cd = width // 2, width // 6, 2 * width // 3, width // 3
    sibling = (1 - core, chip)
    first = core == 0
    second = core == 1

    def swap(index, source, target):
        return remote(source, target, (swap_sems.at[0, index], swap_sems.at[1, index]), sibling)

    r_chains = [
        Scatter(total_r.at[k], [r0.at[k], r1.at[k], r2.at[k], r3.at[k]], ORDERS[k], chain_r.at[k], final_r.at[k])
        for k in range(3)
    ]
    q_chains = [
        Scatter(total_q.at[k], [q0.at[k], q1.at[k], q2.at[k], q3.at[k]], ORDERS[k], chain_q.at[k], final_q.at[k])
        for k in range(3)
    ]

    greet()
    own_rest = pltpu.make_async_copy(rest_ref.at[pl.ds(3 * core, 3)], total_r, local_sems.at[0])
    far_rest = swap(0, rest_ref.at[pl.ds(3 * (1 - core), 3)], first_r)
    own_rows = pltpu.make_async_copy(rows_ref, layer_ref.at[core], local_sems.at[1])
    out_rows = swap(1, rows_ref, layer_ref.at[core])
    far_rest.start()
    own_rest.start()
    normed_t[...] = normed_ref[...].T

    def begin(chains, total, landed):
        for k, chain in enumerate(chains):
            for index in range(1 << BITS):
                at = (k,) + tuple((index >> bit) & 1 for bit in reversed(range(BITS)))
                total[at] = total[at] + landed[at]
            chain.send(0).start()

    def one_pair(pair, carry):
        @pl.when(pair == 1)
        def _():
            own_rest.wait()
            far_rest.wait_recv()
            begin(r_chains, total_r, first_r)
            out_rows.start()
            own_rows.start()

        @pl.when(pair == 5)
        def _():
            for chain in r_chains:
                chain.arrive(0)

        at_q = pl.ds(pl.multiple_of(pair * PAIR, PAIR), PAIR)
        at_k = pl.ds(pl.multiple_of(width + pair * PAIR, PAIR), PAIR)
        at_v = pl.ds(pl.multiple_of(2 * width + pair * PAIR, PAIR), PAIR)
        attend_back_pair(
            projected_ref[:, at_q], projected_ref[:, at_k], projected_ref[:, at_v], gctx_ref[:, at_q],
            context_ref[:, at_q], lse_ref.at[pair], start_ref,
            dproj.at[:, at_q], dproj.at[:, at_k], dproj.at[:, at_v], dk_acc, dv_acc,
        )
        return carry

    lax.fori_loop(0, pairs, one_pair, 0)

    def qkv_block(block):
        grad = dproj[:, pl.ds(pl.multiple_of(block * cq, PAIR), cq)]
        return nn(normed_t[...], grad).astype(BF16).reshape((2,) * BITS + (mine, cq))

    for k in range(3):
        far_q[k] = qkv_block(3 * (1 - core) + k)
    swap_q = swap(2, far_q, first_q)
    swap_q.start()
    for k in range(3):
        total_q[k] = qkv_block(3 * core + k)
    swap_q.wait_recv()
    begin(q_chains, total_q, first_q)
    for chain in r_chains:
        chain.arrive(1)

    small[0] = jnp.zeros_like(small[0])

    def one_block(step, carry):
        at = pl.ds(pl.multiple_of(step * BLOCK, BLOCK), BLOCK)
        gnormed = jnp.zeros((BLOCK, width), F32)
        for n in range(3):
            weight = jnp.concatenate([wqkv_ref[2 * n + b].reshape(width, cq) for b in range(2)], axis=1)
            gnormed = gnormed + nt(dproj[at, n * width : (n + 1) * width], weight)
        hat, scale = normalized(x_ref[at, :].astype(F32))
        grad_x = ghid_ref[at, :].astype(F32) + norm_back(hat, scale, gain_ref[...], gnormed)

        @pl.when(first)
        def _():
            grad_ref[0, at, :] = grad_x[:, :cq]
            far_rows[at, :] = grad_x[:, cq:]

        @pl.when(second)
        def _():
            grad_ref[1, at, :] = grad_x[:, cq:]
            far_rows[at, :] = grad_x[:, :cq]

        small[0, 0:1, :] += col_sum(gnormed * hat)
        small[0, 1:2, :] += col_sum(gnormed)
        small[0, 2:3, :] += col_sum(dproj[at, :width].astype(F32))
        small[0, 3:4, :] += col_sum(dproj[at, 2 * width :].astype(F32))
        return carry

    lax.fori_loop(0, rows // BLOCK, one_block, 0)
    swap_x = swap(3, far_rows, grad_ref.at[core])
    swap_x.start()
    small[0, 4:10, :] = narrow_ref[0:6, :]
    for n in range(3):
        for part in range(4):
            row = 10 + 4 * n + part
            small[0, row : row + 1, :] = wide_ref[n : n + 1, part * width : (part + 1) * width]

    def small_step(stage):
        device = sibling if stage == 0 else (core, partner_of(chip, bits, stage - 1))
        return remote(small.at[stage], small_in.at[stage], (small_sems.at[0, stage], small_sems.at[1, stage]), device)

    def small_arrive(stage):
        small_step(stage).wait_recv()
        small[stage + 1] = small[stage] + small_in[stage]
        if stage < BITS:
            small_step(stage + 1).start()

    small_step(0).start()
    for chain in q_chains:
        chain.arrive(0)
    small_arrive(0)
    for chain in r_chains:
        chain.arrive(2)
    for chain in q_chains:
        chain.arrive(1)
    small_arrive(1)
    for chain in r_chains:
        chain.arrive(3)
    swap_r = swap(4, final_r, other_r)
    swap_r.start()
    for chain in q_chains:
        chain.arrive(2)
    small_arrive(2)
    for k in range(3):
        for n in range(2):
            at = cu + co + n * cd
            down_ref[n * mine : (n + 1) * mine, k * cd : (k + 1) * cd] = final_r[k, :, at : at + cd]
    for chain in q_chains:
        chain.arrive(3)
    swap_f = swap(5, final_q, other_q)
    swap_f.start()
    small_arrive(3)
    swap_r.wait_recv()
    small_arrive(4)

    sums = small[BITS + 1]
    share = core * (1 << BITS) + chip

    def pick(values, each):
        lane = lax.broadcasted_iota(jnp.int32, (values.shape[1], 128), 0)
        column = lax.broadcasted_iota(jnp.int32, (values.shape[1], 128), 1)
        wanted = ((lane == share * each + column) & (column < each)).astype(F32)
        return lax.dot_general(
            values, wanted, (((1,), (0,)), ((), ())), precision=lax.Precision.HIGHEST, preferred_element_type=F32
        )

    shares = 2 << BITS
    slim_ref[...] = pick(sums[0:16], width // shares)
    broad_ref[...] = jnp.zeros_like(broad_ref)
    for n in range(3):
        row = jnp.concatenate([sums[10 + 4 * n + part : 11 + 4 * n + part] for part in range(4)], axis=1)
        broad_ref[n : n + 1, :] = pick(jnp.broadcast_to(row, (8, 4 * width)), 4 * width // shares)[0:1]

    swap_f.wait_recv()

    @pl.when(first)
    def _():
        for k in range(3):
            half_ref[:, k * cq : (k + 1) * cq] = final_q[k]
            half_ref[:, (3 + k) * cq : (4 + k) * cq] = other_q[k]
            half_ref[:, 3 * width + k * co : 3 * width + (k + 1) * co] = final_r[k, :, cu : cu + co]
            half_ref[:, 3 * width + (3 + k) * co : 3 * width + (4 + k) * co] = other_r[k, :, cu : cu + co]

    @pl.when(second)
    def _():
        for k in range(3):
            half_ref[:, k * cu : (k + 1) * cu] = other_r[k, :, :cu]
            half_ref[:, (3 + k) * cu : (4 + k) * cu] = final_r[k, :, :cu]

    swap(3, far_rows, grad_ref.at[1 - core]).wait_recv()
    swap(1, rows_ref, layer_ref.at[1 - core]).wait_recv()
    own_rows.wait()
    for done in (far_rest, out_rows, swap_q, swap_x, swap_r, swap_f):
        done.wait_send()
    for stage in range(BITS + 1):
        small_step(stage).wait_send()
    for chain in r_chains + q_chains:
        chain.drain()


def back(projected, gctx, context, lse, start, normed, x, ghid, gain, wqkv, narrow, wide, rest, out_rows):
    rows, width = x.shape
    box = (2,) * BITS
    mine = width >> BITS
    cq, cr = width // 2, 3 * width // 2
    anywhere = pl.BlockSpec(memory_space=pl.ANY)
    vmem = pl.BlockSpec(memory_space=pltpu.VMEM)
    dma = pltpu.SemaphoreType.DMA

    def held(*shape, dtype=BF16):
        return pltpu.VMEM(shape, dtype)

    def landings(columns):
        return [held(3, *box[stage + 1 :], mine, columns) for stage in range(BITS)]

    return pl.pallas_call(
        back_kernel,
        in_specs=[vmem] * 12 + [anywhere] * 2,
        out_specs=[anywhere] + [vmem] * 5,
        out_shape=[
            jax.ShapeDtypeStruct((2, rows, width), F32),
            jax.ShapeDtypeStruct((2, rows, cq), F32),
            jax.ShapeDtypeStruct((mine, 4 * width), F32),
            jax.ShapeDtypeStruct((2 * mine, width), F32),
            jax.ShapeDtypeStruct((16, 128), F32),
            jax.ShapeDtypeStruct((8, 128), F32),
        ],
        scratch_shapes=[
            held(rows, 3 * width), held(rows, PAIR, dtype=F32), held(rows, PAIR, dtype=F32), held(width, rows),
            held(rows, cq, dtype=F32),
            held(3, *box, mine, cr), held(3, *box, mine, cr), *landings(cr),
            held(3, mine, cr, dtype=F32), held(3, mine, cr, dtype=F32),
            held(3, *box, mine, cq), held(3, *box, mine, cq), held(3, *box, mine, cq), *landings(cq),
            held(3, mine, cq, dtype=F32), held(3, mine, cq, dtype=F32),
            held(BITS + 2, 24, width, dtype=F32), held(BITS + 1, 24, width, dtype=F32),
            dma((2,)), dma((2, 6)), dma((3, 2, BITS)), dma((3, 2, BITS)), dma((2, BITS + 1)),
        ],
        compiler_params=params(collective_id=2, has_side_effects=True),
        name="back",
    )(projected, gctx, context, lse, start, normed, x, ghid, gain, wqkv, narrow, wide,
      rest.reshape((6,) + box + (mine, cr)), out_rows)


def unpacked(vectors):
    return [vector[None, :] for vector in vectors]


def marks_and_bias(x, lengths_row, query_bias, value_bias):
    alive, start = row_marks(lengths_row, x.shape[0])
    bias = jnp.concatenate([query_bias, jnp.zeros_like(query_bias), value_bias], axis=1)
    return alive, start, bias


def fused_batch(x, dy, lengths_row, half, down, vectors):
    (pre_gain, pre_shift, query_bias, value_bias, sub_gain, sub_shift, out_bias,
     ffn_gain, ffn_shift, up_bias, mid_gain, mid_shift, down_bias) = unpacked(vectors)
    count, width = x.shape
    alive, start, bias = marks_and_bias(x, lengths_row, query_bias, value_bias)
    projected, normed, context, lse, wqkv, rest = front(x, half, down, pre_gain, pre_shift, bias, start)
    out, ghid, gctx, mixed, gbranch, nffn, gup, mid, gffn, narrow, wide = middle(
        x, dy, context, alive, rest.reshape(6, width, -1),
        (sub_gain, sub_shift, out_bias, ffn_gain, ffn_shift, up_bias, mid_gain, mid_shift, down_bias),
    )
    grads = outer_rest(nffn, gup, mixed, gbranch, mid, gffn)
    layer, grad_x, half_grad, down_grad, slim, broad = back(
        projected, gctx, context, lse, start, normed, x, ghid, pre_gain, wqkv, narrow, wide, grads, out
    )
    shares = 2 << BITS
    slim = slim[:10, : width // shares]
    broad = broad[:3, : 4 * width // shares]
    small = (slim[0], slim[1], slim[2], slim[3], slim[4], slim[5], slim[6], slim[7], slim[8],
             broad[0], broad[1], broad[2], slim[9])
    return layer.reshape(-1, width), grad_x.reshape(-1, width // 2), half_grad[None], down_grad, *small


def one_batch(x, dy, lengths_row, qkv, rest, vectors):
    (pre_gain, pre_shift, query_bias, value_bias, sub_gain, sub_shift, out_bias,
     ffn_gain, ffn_shift, up_bias, mid_gain, mid_shift, down_bias) = unpacked(vectors)
    alive, start, bias = marks_and_bias(x, lengths_row, query_bias, value_bias)
    projected, normed = project(x, qkv, pre_gain, pre_shift, bias)
    context, lse = attend(projected, start)
    out, ghid, gctx, mixed, gbranch, nffn, gup, mid, gffn, narrow, wide = middle(
        x, dy, context, alive, rest,
        (sub_gain, sub_shift, out_bias, ffn_gain, ffn_shift, up_bias, mid_gain, mid_shift, down_bias),
    )
    grad_up = outer(nffn, gup, 256, F32, "outer_up")
    grad_down = outer(mid, gffn, 512, F32, "outer_down")
    dq, dk, dv = attend_back(projected, gctx, context, lse, start)
    grad_out = outer(mixed, gbranch, 256, F32, "outer_out")
    grad_x, pre = project_back(dq, dk, dv, qkv, x, ghid, pre_gain)
    grads = [outer(normed, d, 256, F32, "outer_qkv") for d in (dq, dk, dv)]
    grad_attention = jnp.concatenate(grads + [grad_out], axis=1)
    small = (pre[0], pre[1], pre[2], pre[3], narrow[0], narrow[1], narrow[2], narrow[3], narrow[4],
             wide[0], wide[1], wide[2], narrow[5])
    return (out, grad_x), (grad_attention, grad_up, grad_down, small)


def shards(tokens, out_grad, seq_lengths, half_weights, down_weight, *all_vectors):
    section = lax.axis_index("section")
    sections = lax.axis_size("section")
    both = ("section", "dp")
    width = tokens.shape[1]
    batches = seq_lengths.shape[0]
    count = tokens.shape[0] // batches
    own_batches = batches // sections
    own_rows = own_batches * count
    hidden_units = half_weights.shape[2]
    shares = sections * lax.axis_size("dp")

    def own(array, rows):
        return lax.dynamic_slice_in_dim(array, section * rows, rows, axis=0)

    x_rows = own(tokens, own_rows)
    dy_rows = own(out_grad, own_rows)
    lengths = own(seq_lengths, own_batches)
    if (
        sections == 2
        and shares == sections << BITS
        and own_batches == 1
        and half_weights.shape[1] % 16 == 0
        and down_weight.shape[0] == 2 * half_weights.shape[1]
        and hidden_units == 4 * width
    ):
        return fused_batch(x_rows, dy_rows, lengths[0], half_weights[0], down_weight, all_vectors)

    blocks = lax.all_gather(half_weights[0], both, axis=0, tiled=True)
    blocks = blocks.reshape(sections, width, hidden_units)
    down_full = lax.all_gather(down_weight, both, axis=0, tiled=True)
    qkv = blocks[0][:, : 3 * width]

    def in_blocks(array):
        return array.reshape(array.shape[0], 6, -1).transpose(1, 0, 2)

    down_blocks = down_full.reshape(2, 1 << BITS, 2, width >> BITS, 3, width // 3).transpose(0, 4, 1, 3, 2, 5)
    down_blocks = down_blocks.reshape(6, width, 2 * width // 3)
    rest = jnp.concatenate([in_blocks(blocks[1]), in_blocks(blocks[0][:, 3 * width :]), down_blocks], axis=2)
    rows, sums = [], None
    for index in range(own_batches):
        at = slice(index * count, (index + 1) * count)
        row, more = one_batch(x_rows[at], dy_rows[at], lengths[index], qkv, rest, all_vectors)
        rows.append(row)
        sums = more if sums is None else jax.tree.map(jnp.add, sums, more)
    out_block = jnp.concatenate([row[0] for row in rows], axis=0)
    grad_rows = jnp.concatenate([row[1] for row in rows], axis=0)
    grad_attention, grad_up, grad_down, vectors = sums

    block_part = lax.psum_scatter(
        jnp.concatenate([grad_attention, grad_up], axis=0), both, scatter_dimension=0, tiled=True
    )
    down_part = lax.psum_scatter(grad_down, both, scatter_dimension=0, tiled=True)
    packed = jnp.concatenate([vector.reshape(shares, -1) for vector in vectors], axis=1)
    packed = lax.psum_scatter(packed, both, scatter_dimension=0, tiled=True).reshape(-1)
    parts, start = [], 0
    for vector in vectors:
        size = vector.shape[0] // shares
        parts.append(packed[start : start + size])
        start += size

    layer_out = lax.all_gather(out_block, "section", axis=0, tiled=True)
    tokens_grad = lax.all_to_all(grad_rows, "section", split_axis=1, concat_axis=0, tiled=True)
    return (layer_out, tokens_grad, block_part[None], down_part, *parts)


def solution(mesh):
    replicated = P()
    return jax.shard_map(
        shards,
        mesh=mesh,
        in_specs=(P("dp", None), P("dp", None), P("dp", None), P("section", "dp", None), P(("section", "dp"), None))
        + (replicated,) * 13,
        out_specs=(P("dp", None), P("dp", "section"), P("section", "dp", None), P(("section", "dp"), None))
        + (P(("section", "dp")),) * 13,
        check_vma=False,
    )
```

```python
import functools
import math

import jax
import jax.numpy as jnp
from jax import lax
from jax.experimental import pallas as pl
from jax.experimental.pallas import tpu as pltpu
from jax.sharding import PartitionSpec as P

HEAD_DIM = 64
PAIR = 2 * HEAD_DIM
EPS = 1e-05
BLOCK = 256
F32 = jnp.float32
BF16 = jnp.bfloat16
VMEM_LIMIT = 60 * 1024 * 1024


def nn(left, right):
    return lax.dot_general(left, right, (((1,), (0,)), ((), ())), preferred_element_type=F32)


def nt(left, right):
    return lax.dot_general(left, right, (((1,), (1,)), ((), ())), preferred_element_type=F32)


def tn(left, right):
    return lax.dot_general(left, right, (((0,), (0,)), ((), ())), preferred_element_type=F32)


def col_sum(value):
    return jnp.sum(value, axis=0, keepdims=True)


def normalized(value):
    center = jnp.mean(value, axis=-1, keepdims=True)
    centered = value - center
    spread = jnp.mean(centered * centered, axis=-1, keepdims=True)
    scale = lax.rsqrt(spread + EPS)
    return centered * scale, scale


def norm_back(hat, scale, gain, upstream):
    scaled = upstream * gain
    first = jnp.mean(scaled, axis=-1, keepdims=True)
    second = jnp.mean(scaled * hat, axis=-1, keepdims=True)
    return (scaled - first - hat * second) * scale


def params(**more):
    return pltpu.CompilerParams(vmem_limit_bytes=VMEM_LIMIT, **more)


def split_rest(ref):
    _, width, columns = ref.shape
    cu, co, cd = 4 * columns // 9, columns // 9, 2 * columns // 9
    up = jnp.concatenate([ref[b, :, :cu] for b in range(6)], axis=1)
    out = jnp.concatenate([ref[b, :, cu : cu + co] for b in range(6)], axis=1)
    halves = []
    for h in range(2):
        parts = []
        for n in range(2):
            at = cu + co + n * cd
            part = jnp.concatenate([ref[3 * h + k, :, at : at + cd] for k in range(3)], axis=1)
            parts.append(part.reshape(1 << BITS, 1, width >> BITS, width))
        halves.append(jnp.concatenate(parts, axis=1).reshape(2 * width, width))
    return out, up, jnp.concatenate(halves, axis=0)


def whole(shape):
    return pl.BlockSpec(shape, lambda *_: (0,) * len(shape))


def project_kernel(x_ref, w_ref, gain_ref, shift_ref, bias_ref, out_ref, normed_ref):
    hat, _ = normalized(x_ref[...].astype(F32))
    normed = (hat * gain_ref[...] + shift_ref[...]).astype(BF16)
    normed_ref[...] = normed
    out_ref[...] = (nn(normed, w_ref[...]) + bias_ref[...]).astype(BF16)


def project(x, weight, gain, shift, bias):
    rows, width = x.shape
    return pl.pallas_call(
        project_kernel,
        grid=(rows // BLOCK,),
        in_specs=[
            pl.BlockSpec((BLOCK, width), lambda i: (i, 0)),
            whole((width, 3 * width)),
            whole((1, width)),
            whole((1, width)),
            whole((1, 3 * width)),
        ],
        out_specs=[
            pl.BlockSpec((BLOCK, 3 * width), lambda i: (i, 0)),
            pl.BlockSpec((BLOCK, width), lambda i: (i, 0)),
        ],
        out_shape=[
            jax.ShapeDtypeStruct((rows, 3 * width), BF16),
            jax.ShapeDtypeStruct((rows, width), BF16),
        ],
        compiler_params=params(),
        name="project",
    )(x, weight, gain, shift, bias)


def allowed_mask(start, key_at, keys, queries):
    key = key_at + lax.broadcasted_iota(jnp.int32, (keys, queries), 0)
    return key >= start


def head_rows(pair_t, head):
    row = lax.broadcasted_iota(jnp.int32, pair_t.shape, 0)
    mine = (row < HEAD_DIM) if head == 0 else (row >= HEAD_DIM)
    return jnp.where(mine, pair_t, jnp.zeros_like(pair_t))


def head_cols(pair, head):
    col = lax.broadcasted_iota(jnp.int32, pair.shape, 1)
    mine = (col < HEAD_DIM) if head == 0 else (col >= HEAD_DIM)
    return jnp.where(mine, pair, jnp.zeros_like(pair))


def score_parts(key, query_t, start, block):
    before = block * BLOCK
    parts = []
    if block:
        index = lax.broadcasted_iota(jnp.int32, (before, BLOCK), 0)
        parts.append((slice(0, before), jnp.where(index >= start, nn(key[:before], query_t), -1e30)))
    index = lax.broadcasted_iota(jnp.int32, (BLOCK, BLOCK), 0)
    last = lax.broadcasted_iota(jnp.int32, (BLOCK, BLOCK), 1)
    ok = (index >= start - before) & (index <= last)
    own = slice(before, before + BLOCK)
    parts.append((own, jnp.where(ok, nn(key[own], query_t), -1e30)))
    return parts


def attend_pair(query, key, value, start_ref, out_ref, lse_ref):
    query_t = (query.astype(F32) * HEAD_DIM**-0.5).T.astype(BF16)
    value_t = value.astype(F32).T.astype(BF16)
    for block in range(query.shape[0] // BLOCK):
        at = slice(block * BLOCK, (block + 1) * BLOCK)
        start = start_ref[:, at]
        outs = []
        for head in range(2):
            lanes = slice(head * HEAD_DIM, (head + 1) * HEAD_DIM)
            parts = score_parts(key, head_rows(query_t[:, at], head), start, block)
            peak = functools.reduce(jnp.maximum, [jnp.max(scores, axis=0, keepdims=True) for _, scores in parts])
            total = jnp.zeros((1, BLOCK), F32)
            out = jnp.zeros((HEAD_DIM, BLOCK), F32)
            for keys, scores in parts:
                raised = jnp.exp(scores - peak)
                total = total + col_sum(raised)
                out = out + nn(value_t[lanes, keys], raised.astype(BF16))
            outs.append(out * (1.0 / total))
            lse_ref[head : head + 1, at] = peak + jnp.log(total)
        out_ref[at, :] = jnp.concatenate(outs, axis=0).T


def attend_kernel(q_ref, k_ref, v_ref, start_ref, out_ref, lse_ref):
    attend_pair(q_ref[...], k_ref[...], v_ref[...], start_ref, out_ref, lse_ref.at[0])


def attend(projected, start):
    rows, columns = projected.shape
    width = columns // 3
    pairs = width // PAIR
    return pl.pallas_call(
        attend_kernel,
        grid=(pairs,),
        in_specs=[
            pl.BlockSpec((rows, PAIR), lambda p: (0, p)),
            pl.BlockSpec((rows, PAIR), lambda p: (0, pairs + p)),
            pl.BlockSpec((rows, PAIR), lambda p: (0, 2 * pairs + p)),
            whole((1, rows)),
        ],
        out_specs=[
            pl.BlockSpec((rows, PAIR), lambda p: (0, p)),
            pl.BlockSpec((1, 2, rows), lambda p: (p, 0, 0)),
        ],
        out_shape=[
            jax.ShapeDtypeStruct((rows, width), F32),
            jax.ShapeDtypeStruct((pairs, 2, rows), F32),
        ],
        compiler_params=params(),
        name="attend",
    )(projected, projected, projected, start)


def attend_back_pair(query, key, value, grad, context, lse_ref, start_ref, dq_ref, dk_ref, dv_ref, dk_acc, dv_acc):
    scale = HEAD_DIM**-0.5
    scaled = query.astype(F32) * scale
    query = scaled.astype(BF16)
    query_t = scaled.T.astype(BF16)
    key_t = key.astype(F32).T.astype(BF16)
    grad_f = grad.astype(F32)
    grad_t = grad_f.T.astype(BF16)
    weighted_t = (grad_f * context).T
    dk_acc[...] = jnp.zeros_like(dk_acc)
    dv_acc[...] = jnp.zeros_like(dv_acc)
    for block in range(query.shape[0] // BLOCK):
        at = slice(block * BLOCK, (block + 1) * BLOCK)
        start = start_ref[:, at]
        outs = []
        for head in range(2):
            lanes = slice(head * HEAD_DIM, (head + 1) * HEAD_DIM)
            inner = col_sum(weighted_t[lanes, at])
            log_total = lse_ref[head : head + 1, at]
            grad_head = head_rows(grad_t[:, at], head)
            out = jnp.zeros((HEAD_DIM, BLOCK), F32)
            for keys, scores in score_parts(key, head_rows(query_t[:, at], head), start, block):
                soft = jnp.exp(scores - log_total)
                grad_scores = (soft * (nn(value[keys], grad_head) - inner)).astype(BF16)
                dv_acc[keys, :] += nn(soft.astype(BF16), head_cols(grad[at], head))
                dk_acc[keys, :] += nn(grad_scores, head_cols(query[at], head))
                out = out + nn(key_t[lanes, keys], grad_scores)
            outs.append(out)
        dq_ref[at, :] = (jnp.concatenate(outs, axis=0) * scale).T.astype(BF16)
    dk_ref[...] = dk_acc[...].astype(BF16)
    dv_ref[...] = dv_acc[...].astype(BF16)


def attend_back_kernel(q_ref, k_ref, v_ref, g_ref, o_ref, lse_ref, start_ref, dq_ref, dk_ref, dv_ref, dk_acc, dv_acc):
    attend_back_pair(
        q_ref[...], k_ref[...], v_ref[...], g_ref[...], o_ref[...], lse_ref.at[0], start_ref,
        dq_ref, dk_ref, dv_ref, dk_acc, dv_acc,
    )


def attend_back(projected, grad_context, context, lse, start):
    rows, columns = projected.shape
    width = columns // 3
    pairs = width // PAIR
    pair = pl.BlockSpec((rows, PAIR), lambda p: (0, p))
    return pl.pallas_call(
        attend_back_kernel,
        grid=(pairs,),
        in_specs=[
            pair,
            pl.BlockSpec((rows, PAIR), lambda p: (0, pairs + p)),
            pl.BlockSpec((rows, PAIR), lambda p: (0, 2 * pairs + p)),
            pair,
            pair,
            pl.BlockSpec((1, 2, rows), lambda p: (p, 0, 0)),
            whole((1, rows)),
        ],
        out_specs=[pair] * 3,
        out_shape=[jax.ShapeDtypeStruct((rows, width), BF16)] * 3,
        scratch_shapes=[pltpu.VMEM((rows, PAIR), F32), pltpu.VMEM((rows, PAIR), F32)],
        compiler_params=params(),
        name="attend_back",
    )(projected, projected, projected, grad_context, context, lse, start)


def gelu_parts(value):
    phi = 0.5 * (1.0 + lax.erf(value * (1.0 / math.sqrt(2.0))))
    bell = jnp.exp(-0.5 * value * value) * (1.0 / math.sqrt(2.0 * math.pi))
    return value * phi, phi + value * bell


def middle_kernel(
    x_ref, dy_ref, ctx_ref, alive_ref, rest_ref,
    sg_ref, ss_ref, ob_ref, fg_ref, fs_ref, ub_ref, mg_ref, ms_ref, db_ref,
    out_ref, ghid_ref, gctx_ref, mixed_ref, gbranch_ref, nffn_ref, gup_ref, mid_ref, gffn_ref,
    narrow_ref, wide_ref,
):
    step = pl.program_id(0)

    @pl.when(step == 0)
    def _():
        narrow_ref[...] = jnp.zeros_like(narrow_ref)
        wide_ref[...] = jnp.zeros_like(wide_ref)

    out_weight, up_weight, down_weight = split_rest(rest_ref)
    alive = alive_ref[...]
    ctx_hat, ctx_scale = normalized(ctx_ref[...])
    mixed = (ctx_hat * sg_ref[...] + ss_ref[...]).astype(BF16)
    mixed_ref[...] = mixed
    branch = nn(mixed, out_weight) + ob_ref[...]
    hidden = (x_ref[...].astype(F32) + alive * branch).astype(BF16).astype(F32)
    hid_hat, hid_scale = normalized(hidden)
    nffn = (hid_hat * fg_ref[...] + fs_ref[...]).astype(BF16)
    nffn_ref[...] = nffn
    upper = nn(nffn, up_weight) + ub_ref[...]
    active, slope = gelu_parts(upper)
    act_hat, act_scale = normalized(active)
    mid = (act_hat * mg_ref[...] + ms_ref[...]).astype(BF16)
    mid_ref[...] = mid
    result = (nn(mid, down_weight) + db_ref[...]).astype(BF16).astype(F32)
    out_ref[...] = hidden + alive * result

    upstream = dy_ref[...].astype(F32)
    gffn = (alive * upstream).astype(BF16)
    gffn_ref[...] = gffn
    gmid = nt(gffn, down_weight)
    gact = norm_back(act_hat, act_scale, mg_ref[...], gmid)
    gup = (gact * slope).astype(BF16)
    gup_ref[...] = gup
    wide_ref[0:1, :] += col_sum(gup.astype(F32))
    wide_ref[1:2, :] += col_sum(gmid * act_hat)
    wide_ref[2:3, :] += col_sum(gmid)
    gnffn = nt(gup, up_weight)
    ghid = (upstream + norm_back(hid_hat, hid_scale, fg_ref[...], gnffn)).astype(BF16)
    ghid_ref[...] = ghid
    gbranch = (alive * ghid.astype(F32)).astype(BF16)
    gbranch_ref[...] = gbranch
    gmixed = nt(gbranch, out_weight)
    gctx_ref[...] = norm_back(ctx_hat, ctx_scale, sg_ref[...], gmixed).astype(BF16)
    narrow_ref[0:1, :] += col_sum(gmixed * ctx_hat)
    narrow_ref[1:2, :] += col_sum(gmixed)
    narrow_ref[2:3, :] += col_sum(gbranch.astype(F32))
    narrow_ref[3:4, :] += col_sum(gnffn * hid_hat)
    narrow_ref[4:5, :] += col_sum(gnffn)
    narrow_ref[5:6, :] += col_sum(gffn.astype(F32))


def middle(x, dy, context, alive, rest, vectors):
    rows, width = x.shape
    hidden = 4 * width
    row = pl.BlockSpec((BLOCK, width), lambda i: (i, 0))
    row_wide = pl.BlockSpec((BLOCK, hidden), lambda i: (i, 0))
    once = dict(pipeline_mode=pl.Buffered(1))
    narrow = whole((1, width))
    wide = whole((1, hidden))
    def shape(columns, dtype):
        return jax.ShapeDtypeStruct((rows, columns), dtype)
    return pl.pallas_call(
        middle_kernel,
        grid=(rows // BLOCK,),
        in_specs=[
            row, row, row,
            pl.BlockSpec((BLOCK, 1), lambda i: (i, 0)),
            pl.BlockSpec(rest.shape, lambda i: (0, 0, 0), **once),
            narrow, narrow, narrow, narrow, narrow, wide, wide, wide, narrow,
        ],
        out_specs=[row, row, row, row, row, row, row_wide, row_wide, row, whole((8, width)), whole((8, hidden))],
        out_shape=[
            shape(width, F32), shape(width, BF16), shape(width, BF16), shape(width, BF16), shape(width, BF16),
            shape(width, BF16), shape(hidden, BF16), shape(hidden, BF16), shape(width, BF16),
            jax.ShapeDtypeStruct((8, width), F32), jax.ShapeDtypeStruct((8, hidden), F32),
        ],
        compiler_params=params(),
        name="middle",
    )(x, dy, context, alive, rest, *vectors)


def outer_kernel(left_ref, right_ref, out_ref):
    out_ref[...] = tn(left_ref[...], right_ref[...]).astype(out_ref.dtype)


def outer(left, right, tile, dtype, name):
    rows, across = left.shape
    columns = right.shape[1]
    return pl.pallas_call(
        outer_kernel,
        grid=(across // tile,),
        in_specs=[pl.BlockSpec((rows, tile), lambda i: (0, i)), whole((rows, columns))],
        out_specs=pl.BlockSpec((tile, columns), lambda i: (i, 0)),
        out_shape=jax.ShapeDtypeStruct((across, columns), dtype),
        compiler_params=params(),
        name=name,
    )(left, right)


def project_back_kernel(dq_ref, dk_ref, dv_ref, w_ref, x_ref, ghid_ref, gain_ref, out_ref, narrow_ref):
    step = pl.program_id(0)
    width = x_ref.shape[1]

    @pl.when(step == 0)
    def _():
        narrow_ref[...] = jnp.zeros_like(narrow_ref)

    dq, dk, dv = dq_ref[...], dk_ref[...], dv_ref[...]
    gnormed = nt(dq, w_ref[:, :width]) + nt(dk, w_ref[:, width : 2 * width]) + nt(dv, w_ref[:, 2 * width :])
    hat, scale = normalized(x_ref[...].astype(F32))
    out_ref[...] = ghid_ref[...].astype(F32) + norm_back(hat, scale, gain_ref[...], gnormed)
    narrow_ref[0:1, :] += col_sum(gnormed * hat)
    narrow_ref[1:2, :] += col_sum(gnormed)
    narrow_ref[2:3, :] += col_sum(dq.astype(F32))
    narrow_ref[3:4, :] += col_sum(dv.astype(F32))


def project_back(dq, dk, dv, weight, x, ghid, gain):
    rows, width = x.shape
    row = pl.BlockSpec((BLOCK, width), lambda i: (i, 0))
    return pl.pallas_call(
        project_back_kernel,
        grid=(rows // BLOCK,),
        in_specs=[row, row, row, whole(weight.shape), row, row, whole((1, width))],
        out_specs=[row, whole((8, width))],
        out_shape=[jax.ShapeDtypeStruct((rows, width), F32), jax.ShapeDtypeStruct((8, width), F32)],
        compiler_params=params(),
        name="project_back",
    )(dq, dk, dv, weight, x, ghid, gain)


def row_marks(lengths_row, count):
    slots = jnp.arange(lengths_row.shape[0], dtype=jnp.int32)
    ends = jnp.sum(jnp.where(slots[:, None] <= slots[None, :], lengths_row[:, None], 0), axis=0)
    index = jnp.arange(count, dtype=jnp.int32)
    before = jnp.where(ends[None, :] <= index[:, None], ends[None, :], 0)
    alive = index < jnp.max(ends)
    start = jnp.where(alive, jnp.max(before, axis=1), index)
    return alive.astype(F32)[:, None], start[None, :]


MESH = pl.DeviceIdType.MESH
BITS = 4
CHAINS = ((3, 2, 1, 0), (0, 3, 2, 1), (1, 0, 3, 2))


def place():
    core = lax.axis_index("section")
    chip = lax.axis_index("dp")
    return core, chip, [(chip // (1 << bit)) % 2 for bit in range(BITS)]


def partner_of(chip, bits, bit):
    return chip + (1 - 2 * bits[bit]) * (1 << bit)


def at_bits(ref, values):
    return ref.at[tuple(values[bit] for bit in reversed(range(BITS)))]


def remote(source, target, sems, device):
    return pltpu.make_async_remote_copy(
        src_ref=source, dst_ref=target, send_sem=sems[0], recv_sem=sems[1], device_id=device, device_id_type=MESH
    )


class Gather:
    def __init__(self, own, other, order, sems, pass_sems):
        self.own, self.other, self.order = own, other, order
        self.sems, self.pass_sems = sems, pass_sems
        self.core, self.chip, self.bits = place()

    def step(self, stage):
        done = self.order[:stage]
        values = [slice(None) if bit in done else self.bits[bit] for bit in range(BITS)]
        part = at_bits(self.own, values)
        device = (self.core, partner_of(self.chip, self.bits, self.order[stage]))
        return remote(part, part, (self.sems.at[0, stage], self.sems.at[1, stage]), device)

    def onward(self, stage, ref):
        done = self.order[:stage]
        values = [slice(None) if bit in done else self.bits[bit] for bit in range(BITS)]
        values[self.order[stage]] = 1 - self.bits[self.order[stage]]
        part = at_bits(ref, values)
        return remote(part, part, (self.pass_sems.at[0, stage], self.pass_sems.at[1, stage]), (1 - self.core, self.chip))

    def arrive(self, stage):
        self.step(stage).wait_recv()
        if stage + 1 < BITS:
            self.step(stage + 1).start()
        self.onward(stage, self.own).start()

    def passed(self, stage):
        self.onward(stage, self.other).wait_recv()

    def drain(self):
        for stage in range(BITS):
            self.step(stage).wait_send()
            self.onward(stage, self.own).wait_send()


def greet():
    core, chip, bits = place()
    barrier = pltpu.get_barrier_semaphore()
    others = [(1 - core, chip)] + [(core, partner_of(chip, bits, bit)) for bit in range(BITS)]
    for other in others:
        pl.semaphore_signal(barrier, inc=1, device_id=other, device_id_type=MESH)
    pl.semaphore_wait(barrier, len(others))


def seed(parts, sems):
    core, chip, bits = place()
    moves = []
    for index, (source, block) in enumerate(parts):
        here = at_bits(block, bits)
        local = pltpu.make_async_copy(source, here, sems.at[0, index])
        far = remote(source, here, (sems.at[1, index], sems.at[2, index]), (1 - core, chip))
        moves.append((local, far))

    def begin():
        for local, far in moves:
            local.start()
            far.start()

    def sent():
        for local, far in moves:
            local.wait()
            far.wait_send()

    def got():
        for _, far in moves:
            far.wait_recv()

    return begin, sent, got


def as_row(ref):
    return ref[...].reshape(1, -1)


def lengths_of(lengths_ref, core):
    return [lengths_ref[core, slot] for slot in range(lengths_ref.shape[1])]


def alive_rows(lengths_ref, core, at, rows):
    index = at + lax.broadcasted_iota(jnp.int32, (rows, 1), 0)
    return (index < sum(lengths_of(lengths_ref, core))).astype(F32)


def start_row(lengths_ref, core, count):
    index = lax.broadcasted_iota(jnp.int32, (1, count), 1)
    start = jnp.zeros((1, count), jnp.int32)
    end = jnp.int32(0)
    for length in lengths_of(lengths_ref, core):
        end = end + length
        start = jnp.where(index >= end, end, start)
    return jnp.where(index < end, start, index)


def front_kernel(
    tokens_ref, upstream_ref, lengths_ref, half_ref, down_ref,
    pg_ref, ps_ref, qb_ref, vb_ref, sg_ref, ss_ref, ob_ref, fg_ref, fs_ref, ub_ref, mg_ref, ms_ref,
    projected_out, normed_out, context_out, lse_out, start_out, wq0_out, wq1_out, wuo_out, wd_ref,
    mixed_out, nffn_out, hidden_out, mid_out, hat_out, slope_out, scale_out, gdown_out,
    hidden, gffn, broad, hat, mid, normed, mixed, context, lse, start, wq0, wq1, wuo, mid_t, gdown, scales,
    seed_q0, seed_q1, seed_o, seed_u, seed_d, chain_q0, chain_q1, chain_u, chain_d, pass_q0, pass_q1, pass_u, pass_d,
    load_sems, save_sems, row_sems, grad_sems,
):
    core, chip, bits = place()
    rows, width = hidden.shape
    mine = half_ref.shape[0]
    pairs = width // PAIR
    co, cu, cd = width // 6, 2 * width // 3, width // 3
    cg = 3 * PAIR
    first = core == 0
    second = core == 1
    box = (slice(None),) * BITS

    def group_parts(full, groups):
        return [
            (half_ref.at[:, n * width + (2 * g + c) * PAIR : n * width + (2 * g + c + 1) * PAIR],
             full.at[(3 * c + n, *box, slice(None), slice(at * PAIR, (at + 1) * PAIR))])
            for at, g in enumerate(groups) for c in range(2) for n in range(3)
        ]

    q0_begin, q0_sent, q0_got = seed(group_parts(wq0, [0]), seed_q0)
    q1_begin, q1_sent, q1_got = seed(group_parts(wq1, [1, 2]), seed_q1)
    o_begin, o_sent, o_got = seed(
        [(half_ref.at[:, 3 * width + b * co : 3 * width + (b + 1) * co],
          wuo.at[(b, *box, slice(None), slice(cu, cu + co))]) for b in range(6)], seed_o)
    u_begin, u_sent, u_got = seed(
        [(half_ref.at[:, b * cu : (b + 1) * cu],
          wuo.at[(b, *box, slice(None), slice(0, cu))]) for b in range(6)], seed_u)

    def down_parts(which):
        return [
            (down_ref.at[n * mine : (n + 1) * mine, k * cd : (k + 1) * cd],
             wd_ref.at[(3 * which + k, *box, slice(None), slice(n * cd, (n + 1) * cd))])
            for k in range(3) for n in range(2)
        ]

    d_begin, d_sent, _ = seed(down_parts(core), seed_d)
    _, _, d_got = seed(down_parts(1 - core), seed_d)

    def chains(full, sems, passes):
        return [
            Gather(full.at[3 * core + k], full.at[3 * (1 - core) + k], CHAINS[k], sems.at[k], passes.at[k])
            for k in range(3)
        ]

    q0_chains = chains(wq0, chain_q0, pass_q0)
    q1_chains = chains(wq1, chain_q1, pass_q1)
    u_chains = chains(wuo, chain_u, pass_u)
    d_chains = chains(wd_ref, chain_d, pass_d)

    def launch(group):
        for chain in group:
            chain.step(0).start()

    def arrive(group, stage):
        for chain in group:
            chain.arrive(stage)

    def passed(group):
        for stage in range(BITS):
            for chain in group:
                chain.passed(stage)

    own_rows = pl.ds(pl.multiple_of(core * rows, rows), rows)
    loads = [
        pltpu.make_async_copy(tokens_ref.at[own_rows], hidden, load_sems.at[0]),
        pltpu.make_async_copy(upstream_ref.at[own_rows], gffn, load_sems.at[1]),
    ]
    loads[0].start()
    greet()
    pl.when(first)(q0_begin)
    pl.when(first)(q1_begin)
    pl.when(first)(o_begin)
    pl.when(second)(u_begin)
    d_begin()
    loads[1].start()
    pl.when(first)(q0_sent)
    pl.when(second)(q0_got)
    launch(q0_chains)

    loads[0].wait()
    value, _ = normalized(hidden[...].astype(F32))
    normed[...] = (value * as_row(pg_ref) + as_row(ps_ref)).astype(BF16)
    start[...] = start_row(lengths_ref, core, rows)
    saves = []

    def save(source, target):
        saves.append(pltpu.make_async_copy(source, target, save_sems.at[len(saves)]))
        saves[-1].start()

    save(normed, normed_out)
    save(start, start_out)
    arrive(q0_chains, 0)

    @pl.when(first)
    def _():
        q1_sent()
        o_sent()
        u_got()

    @pl.when(second)
    def _():
        u_sent()
        q1_got()
        o_got()

    d_sent()
    d_got()
    arrive(q0_chains, 1)
    launch(q1_chains)
    arrive(q0_chains, 2)
    arrive(q1_chains, 0)
    arrive(q0_chains, 3)
    launch(u_chains)
    passed(q0_chains)

    query_bias, value_bias = as_row(qb_ref), as_row(vb_ref)

    def project_group(group, weights):
        biases = []
        for c in range(2):
            at = slice((2 * group + c) * PAIR, (2 * group + c + 1) * PAIR)
            biases += [query_bias[:, at], jnp.zeros((1, PAIR), F32), value_bias[:, at]]
        cols = slice(group * 2 * cg, (group + 1) * 2 * cg)
        weight = jnp.concatenate(weights, axis=1)
        broad[:, cols] = (nn(normed[...], weight) + jnp.concatenate(biases, axis=1)).astype(BF16)

    project_group(0, [wq0[b].reshape(width, PAIR) for b in range(6)])
    arrive(q1_chains, 1)

    def one_pair(pair, carry):
        @pl.when(pair == 1)
        def _():
            arrive(q1_chains, 2)
            arrive(u_chains, 0)

        @pl.when(pair == 2)
        def _():
            arrive(q1_chains, 3)
            launch(d_chains)
            passed(q1_chains)
            for group in range(1, 3):
                at = slice((group - 1) * PAIR, group * PAIR)
                project_group(group, [wq1[(b, *box, slice(None), at)].reshape(width, PAIR) for b in range(6)])
            pltpu.make_async_copy(broad.at[:, : 3 * width], projected_out, load_sems.at[0]).start()

        @pl.when(pair == 3)
        def _():
            arrive(u_chains, 1)

        @pl.when(pair == 4)
        def _():
            arrive(d_chains, 0)

        @pl.when(pair == 5)
        def _():
            arrive(u_chains, 2)

        at_q = pl.ds(pl.multiple_of(pair * cg, PAIR), PAIR)
        at_k = pl.ds(pl.multiple_of(pair * cg + PAIR, PAIR), PAIR)
        at_v = pl.ds(pl.multiple_of(pair * cg + 2 * PAIR, PAIR), PAIR)
        at_out = pl.ds(pl.multiple_of(pair * PAIR, PAIR), PAIR)
        attend_pair(broad[:, at_q], broad[:, at_k], broad[:, at_v], start, context.at[:, at_out], lse.at[pair])
        return carry

    lax.fori_loop(0, pairs, one_pair, 0)
    save(context, context_out)
    save(lse, lse_out)
    save(wq0, wq0_out)
    save(wq1, wq1_out)
    arrive(d_chains, 1)
    arrive(u_chains, 3)
    passed(u_chains)
    save(wuo, wuo_out)
    loads[1].wait()
    pltpu.make_async_copy(broad.at[:, : 3 * width], projected_out, load_sems.at[0]).wait()
    saves[0].wait()

    def row_saves(step):
        at = pl.ds(pl.multiple_of(step * BLOCK, BLOCK), BLOCK)
        pieces = [(mixed, mixed_out), (normed, nffn_out), (hidden, hidden_out), (mid, mid_out), (hat, hat_out),
                  (broad, slope_out)]
        return [
            pltpu.make_async_copy(source.at[at], target.at[at], row_sems.at[index, step])
            for index, (source, target) in enumerate(pieces)
        ]

    def one_block(step, carry):
        at = pl.ds(pl.multiple_of(step * BLOCK, BLOCK), BLOCK)
        alive = alive_rows(lengths_ref, core, step * BLOCK, BLOCK)
        ctx_hat, _ = normalized(context[at, :])
        mix = (ctx_hat * as_row(sg_ref) + as_row(ss_ref)).astype(BF16)
        mixed[at, :] = mix
        out_weight = jnp.concatenate([wuo[(b, *box, slice(None), slice(cu, cu + co))].reshape(width, co) for b in range(6)], axis=1)
        branch = nn(mix, out_weight) + as_row(ob_ref)
        hid = (hidden[at, :].astype(F32) + alive * branch).astype(BF16)
        hidden[at, :] = hid
        hid_hat, _ = normalized(hid.astype(F32))
        nffn = (hid_hat * as_row(fg_ref) + as_row(fs_ref)).astype(BF16)
        normed[at, :] = nffn
        up_weight = jnp.concatenate([wuo[(b, *box, slice(None), slice(0, cu))].reshape(width, cu) for b in range(6)], axis=1)
        active, slope = gelu_parts(nn(nffn, up_weight) + as_row(ub_ref))
        broad[at, :] = slope.astype(BF16)
        act_hat, act_scale = normalized(active)
        hat[at, :] = act_hat.astype(BF16)
        mid[at, :] = (act_hat * as_row(mg_ref) + as_row(ms_ref)).astype(BF16)
        scales[at, :] = act_scale
        gffn[at, :] = (alive * gffn[at, :].astype(F32)).astype(BF16)
        for copy in row_saves(step):
            copy.start()

        @pl.when(step == 1)
        def _():
            arrive(d_chains, 2)

        return carry

    steps = rows // BLOCK
    lax.fori_loop(0, steps, one_block, 0)
    arrive(d_chains, 3)
    save(scales, scale_out)

    def grad_save(h, k):
        return pltpu.make_async_copy(gdown.at[k], gdown_out.at[3 * h + k], grad_sems.at[h, k])

    for h in range(2):
        mid_t[...] = mid[:, 2 * h * width : 2 * (h + 1) * width].T
        for k in range(3):
            grad = nn(mid_t[...], gffn[:, k * cd : (k + 1) * cd]).astype(BF16)
            grad = grad.reshape(1 << BITS, 2, mine, cd)
            if h:
                grad_save(0, k).wait()
            for n in range(2):
                gdown[k, :, :, n * cd : (n + 1) * cd] = grad[:, n]
            grad_save(h, k).start()
    for k in range(3):
        grad_save(1, k).wait()

    passed(d_chains)

    def finish(step, carry):
        for copy in row_saves(step):
            copy.wait()
        return carry

    lax.fori_loop(0, steps, finish, 0)
    for copy in saves[1:]:
        copy.wait()
    for chain in q0_chains + q1_chains + u_chains + d_chains:
        chain.drain()


def front(tokens, upstream, lengths, half, down, vectors):
    width = tokens.shape[1]
    rows = tokens.shape[0] // 2
    mine = half.shape[0]
    box = (2,) * BITS
    pairs = width // PAIR
    wide = 4 * width
    anywhere = pl.BlockSpec(memory_space=pl.ANY)
    vmem = pl.BlockSpec(memory_space=pltpu.VMEM)
    smem = pl.BlockSpec(memory_space=pltpu.SMEM)
    dma = pltpu.SemaphoreType.DMA
    sizes = dict(q0=PAIR, q1=2 * PAIR, u=5 * width // 6, d=2 * width // 3)
    shape = jax.ShapeDtypeStruct
    steps = rows // BLOCK
    return pl.pallas_call(
        front_kernel,
        in_specs=[anywhere, anywhere, smem, anywhere, anywhere] + [vmem] * len(vectors),
        out_specs=[anywhere] * 17,
        out_shape=[
            shape((rows, 3 * width), BF16), shape((rows, width), BF16), shape((rows, width), F32),
            shape((pairs, 2, rows), F32), shape((1, rows), jnp.int32),
            *[shape((6, *box, mine, columns), BF16) for columns in sizes.values()],
            shape((rows, width), BF16), shape((rows, width), BF16), shape((rows, width), BF16),
            shape((rows, wide), BF16), shape((rows, wide), BF16), shape((rows, wide), BF16), shape((rows, 1), F32),
            shape((6, 1 << BITS, mine, 2 * width // 3), BF16),
        ],
        scratch_shapes=[
            pltpu.VMEM((rows, width), BF16), pltpu.VMEM((rows, width), BF16), pltpu.VMEM((rows, wide), BF16),
            pltpu.VMEM((rows, wide), BF16), pltpu.VMEM((rows, wide), BF16), pltpu.VMEM((rows, width), BF16),
            pltpu.VMEM((rows, width), BF16), pltpu.VMEM((rows, width), F32), pltpu.VMEM((pairs, 2, rows), F32),
            pltpu.VMEM((1, rows), jnp.int32),
            *[pltpu.VMEM((6, *box, mine, sizes[name]), BF16) for name in ("q0", "q1", "u")],
            pltpu.VMEM((2 * width, rows), BF16), pltpu.VMEM((3, 1 << BITS, mine, 2 * width // 3), BF16),
            pltpu.VMEM((rows, 1), F32),
            dma((3, 6)), dma((3, 12)), dma((3, 6)), dma((3, 6)), dma((3, 6)),
            *[dma((3, 2, BITS))] * 8,
            dma((2,)), dma((8,)), dma((6, steps)), dma((2, 3)),
        ],
        compiler_params=params(collective_id=1, has_side_effects=True),
        name="front",
    )(tokens, upstream, lengths, half, down, *vectors)


ORDERS = tuple(tuple(reversed(chain)) for chain in CHAINS)


class Scatter:
    def __init__(self, total, landings, order, sems, final):
        self.total, self.landings, self.order, self.sems, self.final = total, landings, order, sems, final
        self.core, self.chip, self.bits = place()

    def send(self, stage):
        values = [slice(None)] * BITS
        for bit in self.order[:stage]:
            values[bit] = self.bits[bit]
        values[self.order[stage]] = 1 - self.bits[self.order[stage]]
        device = (self.core, partner_of(self.chip, self.bits, self.order[stage]))
        sems = (self.sems.at[0, stage], self.sems.at[1, stage])
        return remote(at_bits(self.total, values), self.landings[stage], sems, device)

    def begin(self, landed):
        for index in range(1 << BITS):
            at = tuple((index >> bit) & 1 for bit in reversed(range(BITS)))
            self.total[at] = self.total[at] + landed[at]
        self.send(0).start()

    def arrive(self, stage):
        self.send(stage).wait_recv()
        landing = self.landings[stage]
        values = [None] * BITS
        for bit in self.order[: stage + 1]:
            values[bit] = self.bits[bit]
        free = [bit for bit in reversed(range(BITS)) if values[bit] is None]
        if not free:
            at = tuple(self.bits[bit] for bit in reversed(range(BITS)))
            self.final[...] = self.total[at].astype(F32) + landing[...].astype(F32)
            return
        for index in range(1 << len(free)):
            picks = [(index >> (len(free) - 1 - n)) & 1 for n in range(len(free))]
            for bit, pick in zip(free, picks):
                values[bit] = pick
            at = tuple(values[bit] for bit in reversed(range(BITS)))
            self.total[at] = self.total[at] + landing[tuple(picks)]
        self.send(stage + 1).start()

    def drain(self):
        for stage in range(BITS):
            self.send(stage).wait_send()


def scatters(total, landings, sems, final):
    return [
        Scatter(total.at[k], [landing.at[k] for landing in landings], ORDERS[k], sems.at[k], final.at[k])
        for k in range(3)
    ]


def feed_body(
    hidden_steps, upstream_ref, context_ref, hidden_ref, mid_ref, hat_ref, slope_ref, scale_ref, lengths_ref, wuo_ref, wd_ref,
    sg_ref, fg_ref, mg_ref, db_ref, gdown_ref,
    ghid_ref, gctx_ref, gbranch_ref, gup_ref, narrow_ref, wide_ref, layer_ref, down_ref,
    out_rows, total, landed, l0, l1, l2, l3, final, swap_sems, chain_sems, local_sems, out_sems,
):
    core, chip, bits = place()
    step = pl.program_id(0)
    steps = pl.num_programs(0)
    width = hidden_ref.shape[1]
    mine = width >> BITS
    co, cu, cd = width // 6, 2 * width // 3, width // 3
    sibling = (1 - core, chip)
    chains = scatters(total, [l0, l1, l2, l3], chain_sems, final)
    own = pltpu.make_async_copy(gdown_ref.at[pl.ds(3 * core, 3)], total, local_sems.at[0])
    far = remote(gdown_ref.at[pl.ds(3 * (1 - core), 3)], landed, (swap_sems.at[0], swap_sems.at[1]), sibling)

    def out_copies(at_step, which):
        at = pl.ds(pl.multiple_of(at_step * BLOCK, BLOCK), BLOCK)
        target = layer_ref.at[which, at]
        return (pltpu.make_async_copy(out_rows.at[at], target, out_sems.at[0, at_step]),
                remote(out_rows.at[at], target, (out_sems.at[1, at_step], out_sems.at[2, at_step]), sibling))

    @pl.when(step == 0)
    def _():
        greet()
        far.start()
        own.start()
        narrow_ref[...] = jnp.zeros_like(narrow_ref)
        wide_ref[...] = jnp.zeros_like(wide_ref)

    @pl.when(step == 1)
    def _():
        own.wait()
        far.wait_recv()
        for k, chain in enumerate(chains):
            chain.begin(landed.at[k])

    for stage in range(2):
        @pl.when(step == stage + 2)
        def _():
            for chain in chains:
                chain.arrive(stage)

    up_weight = jnp.concatenate([wuo_ref[b, :, :cu] for b in range(6)], axis=1)
    out_weight = jnp.concatenate([wuo_ref[b, :, cu:] for b in range(6)], axis=1)
    halves = []
    for h in range(2):
        parts = []
        for n in range(2):
            part = jnp.concatenate([wd_ref[3 * h + k, :, n * cd : (n + 1) * cd] for k in range(3)], axis=1)
            parts.append(part.reshape(1 << BITS, 1, mine, width))
        halves.append(jnp.concatenate(parts, axis=1).reshape(2 * width, width))
    down_weight = jnp.concatenate(halves, axis=0)

    alive = alive_rows(lengths_ref, core, step * BLOCK, BLOCK)
    hidden = hidden_ref[...].astype(F32)
    result = (nn(mid_ref[...], down_weight) + as_row(db_ref)).astype(BF16).astype(F32)
    out_rows[pl.ds(pl.multiple_of(step * BLOCK, BLOCK), BLOCK), :] = hidden + alive * result
    for copy in out_copies(step, core):
        copy.start()

    upstream = upstream_ref[...].astype(F32)
    gffn = (alive * upstream).astype(BF16)
    gmid = nt(gffn, down_weight)
    act_hat = hat_ref[...].astype(F32)
    gact = norm_back(act_hat, scale_ref[...], as_row(mg_ref), gmid)
    gup = (gact * slope_ref[...].astype(F32)).astype(BF16)
    gup_ref[...] = gup
    wide_ref[0:1, :] += col_sum(gup.astype(F32))
    wide_ref[1:2, :] += col_sum(gmid * act_hat)
    wide_ref[2:3, :] += col_sum(gmid)
    gnffn = nt(gup, up_weight)
    hid_hat, hid_scale = normalized(hidden)
    ghid = (upstream + norm_back(hid_hat, hid_scale, as_row(fg_ref), gnffn)).astype(BF16)
    ghid_ref[...] = ghid
    gbranch = (alive * ghid.astype(F32)).astype(BF16)
    gbranch_ref[...] = gbranch
    gmixed = nt(gbranch, out_weight)
    ctx_hat, ctx_scale = normalized(context_ref[...])
    gctx_ref[...] = norm_back(ctx_hat, ctx_scale, as_row(sg_ref), gmixed).astype(BF16)
    narrow_ref[0:1, :] += col_sum(gmixed * ctx_hat)
    narrow_ref[1:2, :] += col_sum(gmixed)
    narrow_ref[2:3, :] += col_sum(gbranch.astype(F32))
    narrow_ref[3:4, :] += col_sum(gnffn * hid_hat)
    narrow_ref[4:5, :] += col_sum(gnffn)
    narrow_ref[5:6, :] += col_sum(gffn.astype(F32))

    @pl.when(step == steps - 1)
    def _():
        for stage in range(2, BITS):
            for chain in chains:
                chain.arrive(stage)
        for k in range(3):
            for n in range(2):
                down_ref[n * mine : (n + 1) * mine, k * cd : (k + 1) * cd] = final[k, :, n * cd : (n + 1) * cd]
        for index in range(hidden_steps):
            local, away = out_copies(index, core)
            local.wait()
            away.wait_send()
            out_copies(index, 1 - core)[1].wait_recv()
        far.wait_send()
        for chain in chains:
            chain.drain()


def feed(upstream, context, hidden, mid, hat, slope, scale, lengths, wuo, wd, vectors, gdown):
    rows, width = hidden.shape
    wide = 4 * width
    steps = rows // BLOCK
    box = (2,) * BITS
    mine = width >> BITS
    columns = 2 * width // 3
    row = pl.BlockSpec((BLOCK, width), lambda i: (i, 0))
    row_wide = pl.BlockSpec((BLOCK, wide), lambda i: (i, 0))
    once = dict(pipeline_mode=pl.Buffered(1))
    anywhere = pl.BlockSpec(memory_space=pl.ANY)
    vmem = pl.BlockSpec(memory_space=pltpu.VMEM)
    smem = pl.BlockSpec(memory_space=pltpu.SMEM)
    dma = pltpu.SemaphoreType.DMA
    shape = jax.ShapeDtypeStruct

    def held(*size, dtype=BF16):
        return pltpu.VMEM(size, dtype)

    return pl.pallas_call(
        functools.partial(feed_body, steps),
        grid=(steps,),
        in_specs=[
            pl.BlockSpec((BLOCK, width), lambda i: (lax.axis_index("section") * steps + i, 0)),
            row, row, row_wide, row_wide, row_wide, pl.BlockSpec((BLOCK, 1), lambda i: (i, 0)), smem,
            pl.BlockSpec(wuo.shape, lambda i: (0, 0, 0), **once),
            pl.BlockSpec(wd.shape, lambda i: (0, 0, 0), **once),
            *[vmem] * 4, anywhere,
        ],
        out_specs=[row, row, row, row_wide, whole((8, width)), whole((8, wide)), anywhere, vmem],
        out_shape=[
            shape((rows, width), BF16), shape((rows, width), BF16), shape((rows, width), BF16), shape((rows, wide), BF16),
            shape((8, width), F32), shape((8, wide), F32), shape((2, rows, width), F32), shape((2 * mine, width), F32),
        ],
        scratch_shapes=[
            held(rows, width, dtype=F32), held(3, *box, mine, columns), held(3, *box, mine, columns),
            *[held(3, *box[stage + 1 :], mine, columns) for stage in range(BITS)],
            held(3, mine, columns, dtype=F32),
            dma((2,)), dma((3, 2, BITS)), dma((1,)), dma((3, steps)),
        ],
        compiler_params=params(collective_id=3, has_side_effects=True),
        name="feed",
    )(upstream, context, hidden, mid, hat, slope, scale, lengths, wuo, wd, *vectors,
      gdown.reshape((6,) + box + (mine, columns)))


def outer_two_kernel(nffn_ref, gup_ref, mixed_ref, gbranch_ref, layer_ref, out_ref, copy_ref, nffn_t, mixed_t):
    block = pl.program_id(0)
    width = nffn_ref.shape[1]
    cu = 2 * width // 3
    copy_ref[...] = layer_ref[...]

    @pl.when(block == 0)
    def _():
        nffn_t[...] = nffn_ref[...].T
        mixed_t[...] = mixed_ref[...].T

    out_ref[0, :, :cu] = nn(nffn_t[...], gup_ref[...]).astype(BF16)
    out_ref[0, :, cu:] = nn(mixed_t[...], gbranch_ref[...]).astype(BF16)


def outer_two(nffn, gup, mixed, gbranch, layer):
    rows, width = nffn.shape
    cu, co = 2 * width // 3, width // 6
    columns = pl.BlockSpec((layer.shape[0], co), lambda b: (0, b))
    return pl.pallas_call(
        outer_two_kernel,
        grid=(6,),
        in_specs=[
            whole((rows, width)), pl.BlockSpec((rows, cu), lambda b: (0, b)),
            whole((rows, width)), pl.BlockSpec((rows, co), lambda b: (0, b)), columns,
        ],
        out_specs=[pl.BlockSpec((1, width, cu + co), lambda b: (b, 0, 0)), columns],
        out_shape=[jax.ShapeDtypeStruct((6, width, cu + co), BF16), jax.ShapeDtypeStruct(layer.shape, F32)],
        scratch_shapes=[pltpu.VMEM((width, rows), BF16), pltpu.VMEM((width, rows), BF16)],
        compiler_params=params(),
        name="outer_two",
    )(nffn, gup, mixed, gbranch, layer)


def back_kernel(
    projected_ref, gctx_ref, context_ref, lse_ref, start_ref, normed_ref, tokens_ref, ghid_ref, gain_ref, wq0_ref, wq1_ref,
    narrow_ref, wide_ref, rest_ref,
    grad_ref, half_ref, slim_ref, broad_ref,
    x_rows, dproj, dk_acc, dv_acc, normed_t, far_rows,
    total_r, first_r, r0, r1, r2, r3, final_r, other_r,
    total_q, far_q, first_q, q0, q1, q2, q3, final_q, other_q,
    small, small_in,
    local_sems, swap_sems, chain_r, chain_q, small_sems,
):
    core, chip, bits = place()
    rows, width = x_rows.shape
    mine = half_ref.shape[0]
    pairs = width // PAIR
    co, cu, cq = width // 6, 2 * width // 3, width // 2
    cg = 3 * PAIR
    sibling = (1 - core, chip)
    first = core == 0
    second = core == 1

    def swap(index, source, target):
        return remote(source, target, (swap_sems.at[0, index], swap_sems.at[1, index]), sibling)

    r_chains = scatters(total_r, [r0, r1, r2, r3], chain_r, final_r)
    q_chains = [
        scatters(total_q.at[g], [landing.at[g] for landing in (q0, q1, q2, q3)], chain_q.at[g], final_q.at[g])
        for g in range(3)
    ]

    own_x = pltpu.make_async_copy(
        tokens_ref.at[pl.ds(pl.multiple_of(core * rows, rows), rows)], x_rows, local_sems.at[1])
    own_x.start()
    greet()
    own_rest = pltpu.make_async_copy(rest_ref.at[pl.ds(3 * core, 3)], total_r, local_sems.at[0])
    far_rest = swap(0, rest_ref.at[pl.ds(3 * (1 - core), 3)], first_r)
    far_rest.start()
    own_rest.start()
    normed_t[...] = normed_ref[...].T

    def swap_q(group):
        return swap(3 + group, far_q.at[group], first_q.at[group])

    def make(group):
        for which, target in ((1 - core, far_q), (core, total_q)):
            at = pl.ds(pl.multiple_of(group * 2 * cg + which * cg, PAIR), cg)
            grad = nn(normed_t[...], dproj[:, at]).astype(BF16)
            for n in range(3):
                target[group, n] = grad[:, n * PAIR : (n + 1) * PAIR].reshape((2,) * BITS + (mine, PAIR))
            if target is far_q:
                swap_q(group).start()

    def begin(group):
        swap_q(group).wait_recv()
        for k, chain in enumerate(q_chains[group]):
            chain.begin(first_q.at[group, k])

    def arrive(chains, stage):
        for chain in chains:
            chain.arrive(stage)

    def one_pair(pair, carry):
        @pl.when(pair == 1)
        def _():
            own_rest.wait()
            far_rest.wait_recv()
            for k, chain in enumerate(r_chains):
                chain.begin(first_r.at[k])

        @pl.when(pair == 2)
        def _():
            make(0)

        @pl.when(pair == 3)
        def _():
            begin(0)

        @pl.when(pair == 4)
        def _():
            arrive(r_chains, 0)
            make(1)

        @pl.when(pair == 5)
        def _():
            arrive(q_chains[0], 0)
            begin(1)

        at_q = pl.ds(pl.multiple_of(pair * cg, PAIR), PAIR)
        at_k = pl.ds(pl.multiple_of(pair * cg + PAIR, PAIR), PAIR)
        at_v = pl.ds(pl.multiple_of(pair * cg + 2 * PAIR, PAIR), PAIR)
        at_c = pl.ds(pl.multiple_of(pair * PAIR, PAIR), PAIR)
        attend_back_pair(
            projected_ref[:, at_q], projected_ref[:, at_k], projected_ref[:, at_v], gctx_ref[:, at_c],
            context_ref[:, at_c], lse_ref.at[pair], start_ref,
            dproj.at[:, at_q], dproj.at[:, at_k], dproj.at[:, at_v], dk_acc, dv_acc,
        )
        return carry

    lax.fori_loop(0, pairs, one_pair, 0)
    make(2)
    arrive(q_chains[0], 1)
    arrive(q_chains[1], 0)
    arrive(r_chains, 1)
    begin(2)
    own_x.wait()
    small[0] = jnp.zeros_like(small[0])

    def one_block(step, carry):
        at = pl.ds(pl.multiple_of(step * BLOCK, BLOCK), BLOCK)
        gnormed = jnp.zeros((BLOCK, width), F32)
        for group in range(3):
            if group == 0:
                blocks = [wq0_ref[b].reshape(width, PAIR) for b in range(6)]
            else:
                cols = slice((group - 1) * PAIR, group * PAIR)
                blocks = [wq1_ref[(b,) + (slice(None),) * (BITS + 1) + (cols,)].reshape(width, PAIR) for b in range(6)]
            weight = jnp.concatenate(blocks, axis=1)
            gnormed = gnormed + nt(dproj[at, group * 2 * cg : (group + 1) * 2 * cg], weight)
        hat, scale = normalized(x_rows[at, :].astype(F32))
        grad_x = ghid_ref[at, :].astype(F32) + norm_back(hat, scale, as_row(gain_ref), gnormed)

        @pl.when(first)
        def _():
            grad_ref[0, at, :] = grad_x[:, :cq]
            far_rows[at, :] = grad_x[:, cq:]

        @pl.when(second)
        def _():
            grad_ref[1, at, :] = grad_x[:, cq:]
            far_rows[at, :] = grad_x[:, :cq]

        small[0, 0:1, :] += col_sum(gnormed * hat)
        small[0, 1:2, :] += col_sum(gnormed)
        for row, part in ((2, 0), (3, 2)):
            grads = [dproj[at, p * cg + part * PAIR : p * cg + (part + 1) * PAIR].astype(F32) for p in range(pairs)]
            small[0, row : row + 1, :] += col_sum(jnp.concatenate(grads, axis=1))

        @pl.when(step == 1)
        def _():
            arrive(q_chains[0], 2)
            arrive(q_chains[1], 1)

        @pl.when(step == 2)
        def _():
            arrive(q_chains[2], 0)
            arrive(q_chains[0], 3)

        @pl.when(step == 3)
        def _():
            arrive(r_chains, 2)
            arrive(q_chains[1], 2)

        return carry

    lax.fori_loop(0, rows // BLOCK, one_block, 0)
    swap_x = swap(1, far_rows, grad_ref.at[core])
    small[0, 4:10, :] = narrow_ref[0:6, :]
    for n in range(3):
        for part in range(4):
            row = 10 + 4 * n + part
            small[0, row : row + 1, :] = wide_ref[n : n + 1, part * width : (part + 1) * width]

    def small_step(stage):
        device = sibling if stage == 0 else (core, partner_of(chip, bits, stage - 1))
        return remote(small.at[stage], small_in.at[stage], (small_sems.at[0, stage], small_sems.at[1, stage]), device)

    def small_arrive(stage):
        small_step(stage).wait_recv()
        small[stage + 1] = small[stage] + small_in[stage]
        if stage < BITS:
            small_step(stage + 1).start()

    small_step(0).start()
    swap_x.start()
    arrive(q_chains[2], 1)
    small_arrive(0)
    arrive(q_chains[1], 3)
    arrive(r_chains, 3)
    swap_r = swap(2, final_r, other_r)
    swap_r.start()
    small_arrive(1)
    arrive(q_chains[2], 2)
    small_arrive(2)
    arrive(q_chains[2], 3)
    swap_f = swap(6, final_q, other_q)
    swap_f.start()
    small_arrive(3)
    swap_r.wait_recv()
    small_arrive(4)

    sums = small[BITS + 1]
    share = core * (1 << BITS) + chip

    def pick(values, each):
        lane = lax.broadcasted_iota(jnp.int32, (values.shape[1], 128), 0)
        column = lax.broadcasted_iota(jnp.int32, (values.shape[1], 128), 1)
        wanted = ((lane == share * each + column) & (column < each)).astype(F32)
        return lax.dot_general(
            values, wanted, (((1,), (0,)), ((), ())), precision=lax.Precision.HIGHEST, preferred_element_type=F32
        )

    shares = 2 << BITS
    slim_ref[...] = pick(sums[0:16], width // shares)
    broad_ref[...] = jnp.zeros_like(broad_ref)
    for n in range(3):
        row = jnp.concatenate([sums[10 + 4 * n + part : 11 + 4 * n + part] for part in range(4)], axis=1)
        broad_ref[n : n + 1, :] = pick(jnp.broadcast_to(row, (8, 4 * width)), 4 * width // shares)[0:1]

    swap_f.wait_recv()

    @pl.when(first)
    def _():
        for k in range(3):
            for g in range(3):
                for c, source in ((0, final_q), (1, other_q)):
                    at = k * width + (2 * g + c) * PAIR
                    half_ref[:, at : at + PAIR] = source[g, k]
            half_ref[:, 3 * width + k * co : 3 * width + (k + 1) * co] = final_r[k, :, cu:]
            half_ref[:, 3 * width + (3 + k) * co : 3 * width + (4 + k) * co] = other_r[k, :, cu:]

    @pl.when(second)
    def _():
        for k in range(3):
            half_ref[:, k * cu : (k + 1) * cu] = other_r[k, :, :cu]
            half_ref[:, (3 + k) * cu : (4 + k) * cu] = final_r[k, :, :cu]

    swap(1, far_rows, grad_ref.at[1 - core]).wait_recv()
    for done in (far_rest, swap_x, swap_r, swap_f, swap_q(0), swap_q(1), swap_q(2)):
        done.wait_send()
    for stage in range(BITS + 1):
        small_step(stage).wait_send()
    for chain in r_chains + q_chains[0] + q_chains[1] + q_chains[2]:
        chain.drain()


def back(projected, gctx, context, lse, start, normed, tokens, ghid, gain, wq0, wq1, narrow, wide, rest):
    rows, width = normed.shape
    box = (2,) * BITS
    mine = width >> BITS
    cq, cr = width // 2, 5 * width // 6
    anywhere = pl.BlockSpec(memory_space=pl.ANY)
    vmem = pl.BlockSpec(memory_space=pltpu.VMEM)
    dma = pltpu.SemaphoreType.DMA

    def held(*shape, dtype=BF16):
        return pltpu.VMEM(shape, dtype)

    def landings(*lead):
        return [held(*lead[:-1], *box[stage + 1 :], mine, lead[-1]) for stage in range(BITS)]

    return pl.pallas_call(
        back_kernel,
        in_specs=[vmem] * 6 + [anywhere] + [vmem] * 6 + [anywhere],
        out_specs=[vmem] * 4,
        out_shape=[
            jax.ShapeDtypeStruct((2, rows, cq), F32),
            jax.ShapeDtypeStruct((mine, 4 * width), F32),
            jax.ShapeDtypeStruct((16, 128), F32),
            jax.ShapeDtypeStruct((8, 128), F32),
        ],
        scratch_shapes=[
            held(rows, width), held(rows, 3 * width), held(rows, PAIR, dtype=F32), held(rows, PAIR, dtype=F32),
            held(width, rows), held(rows, cq, dtype=F32),
            held(3, *box, mine, cr), held(3, *box, mine, cr), *landings(3, cr),
            held(3, mine, cr, dtype=F32), held(3, mine, cr, dtype=F32),
            held(3, 3, *box, mine, PAIR), held(3, 3, *box, mine, PAIR), held(3, 3, *box, mine, PAIR),
            *landings(3, 3, PAIR),
            held(3, 3, mine, PAIR, dtype=F32), held(3, 3, mine, PAIR, dtype=F32),
            held(BITS + 2, 24, width, dtype=F32), held(BITS + 1, 24, width, dtype=F32),
            dma((2,)), dma((2, 7)), dma((3, 2, BITS)), dma((3, 3, 2, BITS)), dma((2, BITS + 1)),
        ],
        compiler_params=params(collective_id=2, has_side_effects=True),
        name="back",
    )(projected, gctx, context, lse, start, normed, tokens, ghid, gain, wq0, wq1, narrow, wide,
      rest.reshape((6,) + box + (mine, cr)))


def fused_batch(tokens, out_grad, lengths, half, down, vectors):
    (pre_gain, pre_shift, query_bias, value_bias, sub_gain, sub_shift, out_bias,
     ffn_gain, ffn_shift, up_bias, mid_gain, mid_shift, down_bias) = vectors
    width = tokens.shape[1]
    (projected, normed, context, lse, start, wq0, wq1, wuo, wd, mixed, nffn, hidden, mid, hat, slope, scale, gdown) = front(
        tokens, out_grad, lengths, half, down,
        (pre_gain, pre_shift, query_bias, value_bias, sub_gain, sub_shift, out_bias, ffn_gain, ffn_shift, up_bias,
         mid_gain, mid_shift),
    )
    ghid, gctx, gbranch, gup, narrow, wide, layer, down_grad = feed(
        out_grad, context, hidden, mid, hat, slope, scale, lengths, wuo.reshape(6, width, -1), wd.reshape(6, width, -1),
        (sub_gain, ffn_gain, mid_gain, down_bias), gdown,
    )
    grads, layer = outer_two(nffn, gup, mixed, gbranch, layer.reshape(-1, width))
    grad_x, half_grad, slim, broad = back(
        projected, gctx, context, lse, start, normed, tokens, ghid, pre_gain, wq0, wq1, narrow, wide, grads
    )
    shares = 2 << BITS
    slim = slim[:10, : width // shares]
    broad = broad[:3, : 4 * width // shares]
    small = (slim[0], slim[1], slim[2], slim[3], slim[4], slim[5], slim[6], slim[7], slim[8],
             broad[0], broad[1], broad[2], slim[9])
    return layer, grad_x.reshape(-1, width // 2), half_grad[None], down_grad, *small


def unpacked(vectors):
    return [vector[None, :] for vector in vectors]


def marks_and_bias(x, lengths_row, query_bias, value_bias):
    alive, start = row_marks(lengths_row, x.shape[0])
    bias = jnp.concatenate([query_bias, jnp.zeros_like(query_bias), value_bias], axis=1)
    return alive, start, bias


def one_batch(x, dy, lengths_row, qkv, rest, vectors):
    (pre_gain, pre_shift, query_bias, value_bias, sub_gain, sub_shift, out_bias,
     ffn_gain, ffn_shift, up_bias, mid_gain, mid_shift, down_bias) = unpacked(vectors)
    alive, start, bias = marks_and_bias(x, lengths_row, query_bias, value_bias)
    projected, normed = project(x, qkv, pre_gain, pre_shift, bias)
    context, lse = attend(projected, start)
    out, ghid, gctx, mixed, gbranch, nffn, gup, mid, gffn, narrow, wide = middle(
        x, dy, context, alive, rest,
        (sub_gain, sub_shift, out_bias, ffn_gain, ffn_shift, up_bias, mid_gain, mid_shift, down_bias),
    )
    grad_up = outer(nffn, gup, 256, F32, "outer_up")
    grad_down = outer(mid, gffn, 512, F32, "outer_down")
    dq, dk, dv = attend_back(projected, gctx, context, lse, start)
    grad_out = outer(mixed, gbranch, 256, F32, "outer_out")
    grad_x, pre = project_back(dq, dk, dv, qkv, x, ghid, pre_gain)
    grads = [outer(normed, d, 256, F32, "outer_qkv") for d in (dq, dk, dv)]
    grad_attention = jnp.concatenate(grads + [grad_out], axis=1)
    small = (pre[0], pre[1], pre[2], pre[3], narrow[0], narrow[1], narrow[2], narrow[3], narrow[4],
             wide[0], wide[1], wide[2], narrow[5])
    return (out, grad_x), (grad_attention, grad_up, grad_down, small)


def shards(tokens, out_grad, seq_lengths, half_weights, down_weight, *all_vectors):
    section = lax.axis_index("section")
    sections = lax.axis_size("section")
    both = ("section", "dp")
    width = tokens.shape[1]
    batches = seq_lengths.shape[0]
    count = tokens.shape[0] // batches
    own_batches = batches // sections
    own_rows = own_batches * count
    hidden_units = half_weights.shape[2]
    shares = sections * lax.axis_size("dp")

    if (
        sections == 2
        and shares == sections << BITS
        and own_batches == 1
        and half_weights.shape[1] % 16 == 0
        and down_weight.shape[0] == 2 * half_weights.shape[1]
        and hidden_units == 4 * width
    ):
        return fused_batch(tokens, out_grad, seq_lengths, half_weights[0], down_weight, all_vectors)

    def own(array, rows):
        return lax.dynamic_slice_in_dim(array, section * rows, rows, axis=0)

    x_rows = own(tokens, own_rows)
    dy_rows = own(out_grad, own_rows)
    lengths = own(seq_lengths, own_batches)
    blocks = lax.all_gather(half_weights[0], both, axis=0, tiled=True)
    blocks = blocks.reshape(sections, width, hidden_units)
    down_full = lax.all_gather(down_weight, both, axis=0, tiled=True)
    qkv = blocks[0][:, : 3 * width]

    def in_blocks(array):
        return array.reshape(array.shape[0], 6, -1).transpose(1, 0, 2)

    down_blocks = down_full.reshape(2, 1 << BITS, 2, width >> BITS, 3, width // 3).transpose(0, 4, 1, 3, 2, 5)
    down_blocks = down_blocks.reshape(6, width, 2 * width // 3)
    rest = jnp.concatenate([in_blocks(blocks[1]), in_blocks(blocks[0][:, 3 * width :]), down_blocks], axis=2)
    rows, sums = [], None
    for index in range(own_batches):
        at = slice(index * count, (index + 1) * count)
        row, more = one_batch(x_rows[at], dy_rows[at], lengths[index], qkv, rest, all_vectors)
        rows.append(row)
        sums = more if sums is None else jax.tree.map(jnp.add, sums, more)
    out_block = jnp.concatenate([row[0] for row in rows], axis=0)
    grad_rows = jnp.concatenate([row[1] for row in rows], axis=0)
    grad_attention, grad_up, grad_down, vectors = sums

    block_part = lax.psum_scatter(
        jnp.concatenate([grad_attention, grad_up], axis=0), both, scatter_dimension=0, tiled=True
    )
    down_part = lax.psum_scatter(grad_down, both, scatter_dimension=0, tiled=True)
    packed = jnp.concatenate([vector.reshape(shares, -1) for vector in vectors], axis=1)
    packed = lax.psum_scatter(packed, both, scatter_dimension=0, tiled=True).reshape(-1)
    parts, start = [], 0
    for vector in vectors:
        size = vector.shape[0] // shares
        parts.append(packed[start : start + size])
        start += size

    layer_out = lax.all_gather(out_block, "section", axis=0, tiled=True)
    tokens_grad = lax.all_to_all(grad_rows, "section", split_axis=1, concat_axis=0, tiled=True)
    return (layer_out, tokens_grad, block_part[None], down_part, *parts)


def solution(mesh):
    replicated = P()
    return jax.shard_map(
        shards,
        mesh=mesh,
        in_specs=(P("dp", None), P("dp", None), P("dp", None), P("section", "dp", None), P(("section", "dp"), None))
        + (replicated,) * 13,
        out_specs=(P("dp", None), P("dp", "section"), P("section", "dp", None), P(("section", "dp"), None))
        + (P(("section", "dp")),) * 13,
        check_vma=False,
    )
```

```python
import functools
import math

import jax
import jax.numpy as jnp
from jax import lax
from jax.experimental import pallas as pl
from jax.experimental.pallas import tpu as pltpu
from jax.sharding import PartitionSpec as P

HEAD_DIM = 64
PAIR = 2 * HEAD_DIM
EPS = 1e-05
BLOCK = 256
F32 = jnp.float32
BF16 = jnp.bfloat16
VMEM_LIMIT = 60 * 1024 * 1024


def nn(left, right):
    return lax.dot_general(left, right, (((1,), (0,)), ((), ())), preferred_element_type=F32)


def nt(left, right):
    return lax.dot_general(left, right, (((1,), (1,)), ((), ())), preferred_element_type=F32)


def tn(left, right):
    return lax.dot_general(left, right, (((0,), (0,)), ((), ())), preferred_element_type=F32)


def col_sum(value):
    return jnp.sum(value, axis=0, keepdims=True)


def normalized(value):
    center = jnp.mean(value, axis=-1, keepdims=True)
    centered = value - center
    spread = jnp.mean(centered * centered, axis=-1, keepdims=True)
    scale = lax.rsqrt(spread + EPS)
    return centered * scale, scale


def norm_back(hat, scale, gain, upstream):
    scaled = upstream * gain
    first = jnp.mean(scaled, axis=-1, keepdims=True)
    second = jnp.mean(scaled * hat, axis=-1, keepdims=True)
    return (scaled - first - hat * second) * scale


def params(**more):
    return pltpu.CompilerParams(vmem_limit_bytes=VMEM_LIMIT, **more)


def split_rest(ref):
    _, width, columns = ref.shape
    cu, co, cd = 4 * columns // 9, columns // 9, 2 * columns // 9
    up = jnp.concatenate([ref[b, :, :cu] for b in range(6)], axis=1)
    out = jnp.concatenate([ref[b, :, cu : cu + co] for b in range(6)], axis=1)
    halves = []
    for h in range(2):
        parts = []
        for n in range(2):
            at = cu + co + n * cd
            part = jnp.concatenate([ref[3 * h + k, :, at : at + cd] for k in range(3)], axis=1)
            parts.append(part.reshape(CHIPS, 1, width // CHIPS, width))
        halves.append(jnp.concatenate(parts, axis=1).reshape(2 * width, width))
    return out, up, jnp.concatenate(halves, axis=0)


def whole(shape):
    return pl.BlockSpec(shape, lambda *_: (0,) * len(shape))


def project_kernel(x_ref, w_ref, gain_ref, shift_ref, bias_ref, out_ref, normed_ref):
    hat, _ = normalized(x_ref[...].astype(F32))
    normed = (hat * gain_ref[...] + shift_ref[...]).astype(BF16)
    normed_ref[...] = normed
    out_ref[...] = (nn(normed, w_ref[...]) + bias_ref[...]).astype(BF16)


def project(x, weight, gain, shift, bias):
    rows, width = x.shape
    return pl.pallas_call(
        project_kernel,
        grid=(rows // BLOCK,),
        in_specs=[
            pl.BlockSpec((BLOCK, width), lambda i: (i, 0)),
            whole((width, 3 * width)),
            whole((1, width)),
            whole((1, width)),
            whole((1, 3 * width)),
        ],
        out_specs=[
            pl.BlockSpec((BLOCK, 3 * width), lambda i: (i, 0)),
            pl.BlockSpec((BLOCK, width), lambda i: (i, 0)),
        ],
        out_shape=[
            jax.ShapeDtypeStruct((rows, 3 * width), BF16),
            jax.ShapeDtypeStruct((rows, width), BF16),
        ],
        compiler_params=params(),
        name="project",
    )(x, weight, gain, shift, bias)


def allowed_mask(start, key_at, keys, queries):
    key = key_at + lax.broadcasted_iota(jnp.int32, (keys, queries), 0)
    return key >= start


def head_rows(pair_t, head):
    row = lax.broadcasted_iota(jnp.int32, pair_t.shape, 0)
    mine = (row < HEAD_DIM) if head == 0 else (row >= HEAD_DIM)
    return jnp.where(mine, pair_t, jnp.zeros_like(pair_t))


def head_cols(pair, head):
    col = lax.broadcasted_iota(jnp.int32, pair.shape, 1)
    mine = (col < HEAD_DIM) if head == 0 else (col >= HEAD_DIM)
    return jnp.where(mine, pair, jnp.zeros_like(pair))


def score_parts(key, query_t, start, block):
    before = block * BLOCK
    parts = []
    if block:
        index = lax.broadcasted_iota(jnp.int32, (before, BLOCK), 0)
        parts.append((slice(0, before), jnp.where(index >= start, nn(key[:before], query_t), -1e30)))
    index = lax.broadcasted_iota(jnp.int32, (BLOCK, BLOCK), 0)
    last = lax.broadcasted_iota(jnp.int32, (BLOCK, BLOCK), 1)
    ok = (index >= start - before) & (index <= last)
    own = slice(before, before + BLOCK)
    parts.append((own, jnp.where(ok, nn(key[own], query_t), -1e30)))
    return parts


def attend_pair(query, key, value, start_ref, out_ref, lse_ref):
    query_t = (query.astype(F32) * HEAD_DIM**-0.5).T.astype(BF16)
    value_t = value.astype(F32).T.astype(BF16)
    for block in range(query.shape[0] // BLOCK):
        at = slice(block * BLOCK, (block + 1) * BLOCK)
        start = start_ref[:, at]
        outs = []
        for head in range(2):
            lanes = slice(head * HEAD_DIM, (head + 1) * HEAD_DIM)
            parts = score_parts(key, head_rows(query_t[:, at], head), start, block)
            peak = functools.reduce(jnp.maximum, [jnp.max(scores, axis=0, keepdims=True) for _, scores in parts])
            total = jnp.zeros((1, BLOCK), F32)
            out = jnp.zeros((HEAD_DIM, BLOCK), F32)
            for keys, scores in parts:
                raised = jnp.exp(scores - peak)
                total = total + col_sum(raised)
                out = out + nn(value_t[lanes, keys], raised.astype(BF16))
            outs.append(out * (1.0 / total))
            lse_ref[head : head + 1, at] = peak + jnp.log(total)
        out_ref[at, :] = jnp.concatenate(outs, axis=0).T


def attend_kernel(q_ref, k_ref, v_ref, start_ref, out_ref, lse_ref):
    attend_pair(q_ref[...], k_ref[...], v_ref[...], start_ref, out_ref, lse_ref.at[0])


def attend(projected, start):
    rows, columns = projected.shape
    width = columns // 3
    pairs = width // PAIR
    return pl.pallas_call(
        attend_kernel,
        grid=(pairs,),
        in_specs=[
            pl.BlockSpec((rows, PAIR), lambda p: (0, p)),
            pl.BlockSpec((rows, PAIR), lambda p: (0, pairs + p)),
            pl.BlockSpec((rows, PAIR), lambda p: (0, 2 * pairs + p)),
            whole((1, rows)),
        ],
        out_specs=[
            pl.BlockSpec((rows, PAIR), lambda p: (0, p)),
            pl.BlockSpec((1, 2, rows), lambda p: (p, 0, 0)),
        ],
        out_shape=[
            jax.ShapeDtypeStruct((rows, width), F32),
            jax.ShapeDtypeStruct((pairs, 2, rows), F32),
        ],
        compiler_params=params(),
        name="attend",
    )(projected, projected, projected, start)


def attend_back_pair(query, key, value, grad, context, lse_ref, start_ref, dq_ref, dk_ref, dv_ref, dk_acc, dv_acc):
    scale = HEAD_DIM**-0.5
    scaled = query.astype(F32) * scale
    query = scaled.astype(BF16)
    query_t = scaled.T.astype(BF16)
    key_t = key.astype(F32).T.astype(BF16)
    grad_f = grad.astype(F32)
    grad_t = grad_f.T.astype(BF16)
    weighted_t = (grad_f * context).T
    dk_acc[...] = jnp.zeros_like(dk_acc)
    dv_acc[...] = jnp.zeros_like(dv_acc)
    for block in range(query.shape[0] // BLOCK):
        at = slice(block * BLOCK, (block + 1) * BLOCK)
        start = start_ref[:, at]
        outs = []
        for head in range(2):
            lanes = slice(head * HEAD_DIM, (head + 1) * HEAD_DIM)
            inner = col_sum(weighted_t[lanes, at])
            log_total = lse_ref[head : head + 1, at]
            grad_head = head_rows(grad_t[:, at], head)
            out = jnp.zeros((HEAD_DIM, BLOCK), F32)
            for keys, scores in score_parts(key, head_rows(query_t[:, at], head), start, block):
                soft = jnp.exp(scores - log_total)
                grad_scores = (soft * (nn(value[keys], grad_head) - inner)).astype(BF16)
                dv_acc[keys, :] += nn(soft.astype(BF16), head_cols(grad[at], head))
                dk_acc[keys, :] += nn(grad_scores, head_cols(query[at], head))
                out = out + nn(key_t[lanes, keys], grad_scores)
            outs.append(out)
        dq_ref[at, :] = (jnp.concatenate(outs, axis=0) * scale).T.astype(BF16)
    dk_ref[...] = dk_acc[...].astype(BF16)
    dv_ref[...] = dv_acc[...].astype(BF16)


def attend_back_kernel(q_ref, k_ref, v_ref, g_ref, o_ref, lse_ref, start_ref, dq_ref, dk_ref, dv_ref, dk_acc, dv_acc):
    attend_back_pair(
        q_ref[...], k_ref[...], v_ref[...], g_ref[...], o_ref[...], lse_ref.at[0], start_ref,
        dq_ref, dk_ref, dv_ref, dk_acc, dv_acc,
    )


def attend_back(projected, grad_context, context, lse, start):
    rows, columns = projected.shape
    width = columns // 3
    pairs = width // PAIR
    pair = pl.BlockSpec((rows, PAIR), lambda p: (0, p))
    return pl.pallas_call(
        attend_back_kernel,
        grid=(pairs,),
        in_specs=[
            pair,
            pl.BlockSpec((rows, PAIR), lambda p: (0, pairs + p)),
            pl.BlockSpec((rows, PAIR), lambda p: (0, 2 * pairs + p)),
            pair,
            pair,
            pl.BlockSpec((1, 2, rows), lambda p: (p, 0, 0)),
            whole((1, rows)),
        ],
        out_specs=[pair] * 3,
        out_shape=[jax.ShapeDtypeStruct((rows, width), BF16)] * 3,
        scratch_shapes=[pltpu.VMEM((rows, PAIR), F32), pltpu.VMEM((rows, PAIR), F32)],
        compiler_params=params(),
        name="attend_back",
    )(projected, projected, projected, grad_context, context, lse, start)


def gelu_parts(value):
    phi = 0.5 * (1.0 + lax.erf(value * (1.0 / math.sqrt(2.0))))
    bell = jnp.exp(-0.5 * value * value) * (1.0 / math.sqrt(2.0 * math.pi))
    return value * phi, phi + value * bell


def middle_kernel(
    x_ref, dy_ref, ctx_ref, alive_ref, rest_ref,
    sg_ref, ss_ref, ob_ref, fg_ref, fs_ref, ub_ref, mg_ref, ms_ref, db_ref,
    out_ref, ghid_ref, gctx_ref, mixed_ref, gbranch_ref, nffn_ref, gup_ref, mid_ref, gffn_ref,
    narrow_ref, wide_ref,
):
    step = pl.program_id(0)

    @pl.when(step == 0)
    def _():
        narrow_ref[...] = jnp.zeros_like(narrow_ref)
        wide_ref[...] = jnp.zeros_like(wide_ref)

    out_weight, up_weight, down_weight = split_rest(rest_ref)
    alive = alive_ref[...]
    ctx_hat, ctx_scale = normalized(ctx_ref[...])
    mixed = (ctx_hat * sg_ref[...] + ss_ref[...]).astype(BF16)
    mixed_ref[...] = mixed
    branch = nn(mixed, out_weight) + ob_ref[...]
    hidden = (x_ref[...].astype(F32) + alive * branch).astype(BF16).astype(F32)
    hid_hat, hid_scale = normalized(hidden)
    nffn = (hid_hat * fg_ref[...] + fs_ref[...]).astype(BF16)
    nffn_ref[...] = nffn
    upper = nn(nffn, up_weight) + ub_ref[...]
    active, slope = gelu_parts(upper)
    act_hat, act_scale = normalized(active)
    mid = (act_hat * mg_ref[...] + ms_ref[...]).astype(BF16)
    mid_ref[...] = mid
    result = (nn(mid, down_weight) + db_ref[...]).astype(BF16).astype(F32)
    out_ref[...] = hidden + alive * result

    upstream = dy_ref[...].astype(F32)
    gffn = (alive * upstream).astype(BF16)
    gffn_ref[...] = gffn
    gmid = nt(gffn, down_weight)
    gact = norm_back(act_hat, act_scale, mg_ref[...], gmid)
    gup = (gact * slope).astype(BF16)
    gup_ref[...] = gup
    wide_ref[0:1, :] += col_sum(gup.astype(F32))
    wide_ref[1:2, :] += col_sum(gmid * act_hat)
    wide_ref[2:3, :] += col_sum(gmid)
    gnffn = nt(gup, up_weight)
    ghid = (upstream + norm_back(hid_hat, hid_scale, fg_ref[...], gnffn)).astype(BF16)
    ghid_ref[...] = ghid
    gbranch = (alive * ghid.astype(F32)).astype(BF16)
    gbranch_ref[...] = gbranch
    gmixed = nt(gbranch, out_weight)
    gctx_ref[...] = norm_back(ctx_hat, ctx_scale, sg_ref[...], gmixed).astype(BF16)
    narrow_ref[0:1, :] += col_sum(gmixed * ctx_hat)
    narrow_ref[1:2, :] += col_sum(gmixed)
    narrow_ref[2:3, :] += col_sum(gbranch.astype(F32))
    narrow_ref[3:4, :] += col_sum(gnffn * hid_hat)
    narrow_ref[4:5, :] += col_sum(gnffn)
    narrow_ref[5:6, :] += col_sum(gffn.astype(F32))


def middle(x, dy, context, alive, rest, vectors):
    rows, width = x.shape
    hidden = 4 * width
    row = pl.BlockSpec((BLOCK, width), lambda i: (i, 0))
    row_wide = pl.BlockSpec((BLOCK, hidden), lambda i: (i, 0))
    once = dict(pipeline_mode=pl.Buffered(1))
    narrow = whole((1, width))
    wide = whole((1, hidden))
    def shape(columns, dtype):
        return jax.ShapeDtypeStruct((rows, columns), dtype)
    return pl.pallas_call(
        middle_kernel,
        grid=(rows // BLOCK,),
        in_specs=[
            row, row, row,
            pl.BlockSpec((BLOCK, 1), lambda i: (i, 0)),
            pl.BlockSpec(rest.shape, lambda i: (0, 0, 0), **once),
            narrow, narrow, narrow, narrow, narrow, wide, wide, wide, narrow,
        ],
        out_specs=[row, row, row, row, row, row, row_wide, row_wide, row, whole((8, width)), whole((8, hidden))],
        out_shape=[
            shape(width, F32), shape(width, BF16), shape(width, BF16), shape(width, BF16), shape(width, BF16),
            shape(width, BF16), shape(hidden, BF16), shape(hidden, BF16), shape(width, BF16),
            jax.ShapeDtypeStruct((8, width), F32), jax.ShapeDtypeStruct((8, hidden), F32),
        ],
        compiler_params=params(),
        name="middle",
    )(x, dy, context, alive, rest, *vectors)


def outer_kernel(left_ref, right_ref, out_ref):
    out_ref[...] = tn(left_ref[...], right_ref[...]).astype(out_ref.dtype)


def outer(left, right, tile, dtype, name):
    rows, across = left.shape
    columns = right.shape[1]
    return pl.pallas_call(
        outer_kernel,
        grid=(across // tile,),
        in_specs=[pl.BlockSpec((rows, tile), lambda i: (0, i)), whole((rows, columns))],
        out_specs=pl.BlockSpec((tile, columns), lambda i: (i, 0)),
        out_shape=jax.ShapeDtypeStruct((across, columns), dtype),
        compiler_params=params(),
        name=name,
    )(left, right)


def project_back_kernel(dq_ref, dk_ref, dv_ref, w_ref, x_ref, ghid_ref, gain_ref, out_ref, narrow_ref):
    step = pl.program_id(0)
    width = x_ref.shape[1]

    @pl.when(step == 0)
    def _():
        narrow_ref[...] = jnp.zeros_like(narrow_ref)

    dq, dk, dv = dq_ref[...], dk_ref[...], dv_ref[...]
    gnormed = nt(dq, w_ref[:, :width]) + nt(dk, w_ref[:, width : 2 * width]) + nt(dv, w_ref[:, 2 * width :])
    hat, scale = normalized(x_ref[...].astype(F32))
    out_ref[...] = ghid_ref[...].astype(F32) + norm_back(hat, scale, gain_ref[...], gnormed)
    narrow_ref[0:1, :] += col_sum(gnormed * hat)
    narrow_ref[1:2, :] += col_sum(gnormed)
    narrow_ref[2:3, :] += col_sum(dq.astype(F32))
    narrow_ref[3:4, :] += col_sum(dv.astype(F32))


def project_back(dq, dk, dv, weight, x, ghid, gain):
    rows, width = x.shape
    row = pl.BlockSpec((BLOCK, width), lambda i: (i, 0))
    return pl.pallas_call(
        project_back_kernel,
        grid=(rows // BLOCK,),
        in_specs=[row, row, row, whole(weight.shape), row, row, whole((1, width))],
        out_specs=[row, whole((8, width))],
        out_shape=[jax.ShapeDtypeStruct((rows, width), F32), jax.ShapeDtypeStruct((8, width), F32)],
        compiler_params=params(),
        name="project_back",
    )(dq, dk, dv, weight, x, ghid, gain)


def row_marks(lengths_row, count):
    slots = jnp.arange(lengths_row.shape[0], dtype=jnp.int32)
    ends = jnp.sum(jnp.where(slots[:, None] <= slots[None, :], lengths_row[:, None], 0), axis=0)
    index = jnp.arange(count, dtype=jnp.int32)
    before = jnp.where(ends[None, :] <= index[:, None], ends[None, :], 0)
    alive = index < jnp.max(ends)
    start = jnp.where(alive, jnp.max(before, axis=1), index)
    return alive.astype(F32)[:, None], start[None, :]


MESH = pl.DeviceIdType.MESH
BOX = (4, 2, 2)
CHIPS = 16
X_AT, Y_AT, D_AT, MOVES = 3, 7, 11, 15


class Place:
    def __init__(self):
        self.core = lax.axis_index("section")
        self.chip = lax.axis_index("dp")
        self.z, self.y, self.x = self.chip // 4, (self.chip // 2) % 2, self.chip % 2
        high, low = self.z // 2, self.z % 2
        self.zs = [self.z, self.z + 1 - 2 * low, self.z + 2 - 4 * high, 3 - self.z]

    def at(self, z, y, x):
        return (self.core, z * 4 + y * 2 + x)

    def sibling(self):
        return (1 - self.core, self.chip)

    def over_z(self, k):
        return self.at(self.zs[k], self.y, self.x)

    def over_y(self):
        return self.at(self.z, 1 - self.y, self.x)

    def over_x(self):
        return self.at(self.z, self.y, 1 - self.x)

    def across(self):
        return self.at(self.z, 1 - self.y, 1 - self.x)


def remote(source, target, sems, device):
    return pltpu.make_async_remote_copy(
        src_ref=source, dst_ref=target, send_sem=sems[0], recv_sem=sems[1], device_id=device, device_id_type=MESH
    )


def greet(me):
    barrier = pltpu.get_barrier_semaphore()
    others = [me.sibling(), me.over_x(), me.over_y(), me.across()] + [me.over_z(k) for k in (1, 2, 3)]
    for other in others:
        pl.semaphore_signal(barrier, inc=1, device_id=other, device_id_type=MESH)
    pl.semaphore_wait(barrier, len(others))


class Gather:
    def __init__(self, full, sems, pass_sems):
        self.me = Place()
        self.own = full.at[pl.ds(3 * self.me.core, 3)]
        self.other = full.at[pl.ds(3 * (1 - self.me.core), 3)]
        self.sems, self.pass_sems = sems, pass_sems

    def move(self, index, z, y, x, device):
        part = self.own.at[:, z, y, x]
        return remote(part, part, (self.sems.at[0, index], self.sems.at[1, index]), device)

    def to_z(self, k):
        me = self.me
        return self.move(k - 1, me.z, me.y, me.x, me.over_z(k))

    def to_x(self, k):
        me = self.me
        return self.move(X_AT + k, me.zs[k], me.y, me.x, me.over_x())

    def to_y(self, k):
        me = self.me
        return self.move(Y_AT + k, me.zs[k], me.y, me.x, me.over_y())

    def onward(self, k):
        me = self.me
        if k < 2:
            return self.move(D_AT + k, me.zs[k], me.y, 1 - me.x, me.over_y())
        return self.move(D_AT + k, me.zs[k], 1 - me.y, me.x, me.over_x())

    def across_core(self, index, ref):
        me = self.me
        every = slice(None)
        place = [(every, me.y, 1 - me.x), (every, 1 - me.y, me.x), (every, 1 - me.y, 1 - me.x)]
        z, y, x = (me.zs[index + 1], me.y, me.x) if index < 3 else place[index - 3]
        part = ref.at[:, z, y, x]
        return remote(part, part, (self.pass_sems.at[0, index], self.pass_sems.at[1, index]), me.sibling())

    def launch(self):
        for k in (1, 2, 3):
            self.to_z(k).start()
        self.to_x(0).start()
        self.to_y(0).start()

    def from_z(self, k):
        self.to_z(k).wait_recv()
        self.to_x(k).start()
        self.to_y(k).start()
        self.across_core(k - 1, self.own).start()

    def arrive(self, stage):
        if stage == 0:
            self.from_z(1)
            self.to_x(0).wait_recv()
            self.onward(0).start()
        elif stage == 1:
            self.from_z(2)
            self.from_z(3)
            self.to_x(1).wait_recv()
            self.onward(1).start()
        elif stage == 2:
            for k in (2, 3):
                self.to_y(k).wait_recv()
                self.onward(k).start()
            for k in (2, 3):
                self.to_x(k).wait_recv()
            for k in (0, 1):
                self.to_y(k).wait_recv()
            self.across_core(3, self.own).start()
            self.across_core(4, self.own).start()
        else:
            for k in range(4):
                self.onward(k).wait_recv()
            self.across_core(5, self.own).start()

    def passed(self):
        for index in range(6):
            self.across_core(index, self.other).wait_recv()

    def drain(self):
        for k in (1, 2, 3):
            self.to_z(k).wait_send()
        for k in range(4):
            for move in (self.to_x(k), self.to_y(k), self.onward(k)):
                move.wait_send()
        for index in range(6):
            self.across_core(index, self.own).wait_send()


def seed(parts, sems):
    me = Place()
    moves = []
    for index, (source, full, block, cols) in enumerate(parts):
        here = full.at[block, me.z, me.y, me.x, :, cols]
        local = pltpu.make_async_copy(source, here, sems.at[0, index])
        far = remote(source, here, (sems.at[1, index], sems.at[2, index]), me.sibling())
        moves.append((local, far))

    def begin():
        for local, far in moves:
            local.start()
            far.start()

    def sent():
        for local, far in moves:
            local.wait()
            far.wait_send()

    def got():
        for _, far in moves:
            far.wait_recv()

    return begin, sent, got


def lane_groups(value):
    groups = [value[:, at : at + 128] for at in range(0, value.shape[1], 128)]
    return functools.reduce(jnp.add, groups)


def as_row(ref):
    return ref[...].reshape(1, -1)


def lengths_of(lengths_ref, core):
    return [lengths_ref[core, slot] for slot in range(lengths_ref.shape[1])]


def alive_rows(lengths_ref, core, at, rows):
    index = at + lax.broadcasted_iota(jnp.int32, (rows, 1), 0)
    return (index < sum(lengths_of(lengths_ref, core))).astype(F32)


def start_row(lengths_ref, core, count):
    index = lax.broadcasted_iota(jnp.int32, (1, count), 1)
    start = jnp.zeros((1, count), jnp.int32)
    end = jnp.int32(0)
    for length in lengths_of(lengths_ref, core):
        end = end + length
        start = jnp.where(index >= end, end, start)
    return jnp.where(index < end, start, index)


def front_kernel(
    tokens_ref, upstream_ref, lengths_ref, half_ref, down_ref,
    pg_ref, ps_ref, qb_ref, vb_ref, sg_ref, ss_ref, ob_ref, fg_ref, fs_ref, ub_ref, mg_ref, ms_ref,
    projected_out, normed_out, context_out, lse_out, start_out, wq0_out, wq1_out, wuo_out, wd_ref,
    mixed_out, nffn_out, hidden_out, mid_out, hat_out, slope_out, scale_out, gdown_out,
    hidden, gffn, broad, hat, mid, normed, mixed, context, lse, start, wq0, wq1, wuo, mid_t, gdown, scales, active,
    seed_q0, seed_q1, seed_o, seed_u, seed_d, chain_q0, chain_q1, chain_u, chain_d, pass_q0, pass_q1, pass_u, pass_d,
    load_sems, save_sems, row_sems, grad_sems,
):
    me = Place()
    core = me.core
    rows, width = hidden.shape
    mine = half_ref.shape[0]
    pairs = width // PAIR
    co, cu, cd = width // 6, 2 * width // 3, width // 3
    cg = 3 * PAIR
    first = core == 0
    second = core == 1
    box = (slice(None),) * 3

    def group_parts(full, groups):
        return [
            (half_ref.at[:, n * width + (2 * g + c) * PAIR : n * width + (2 * g + c + 1) * PAIR],
             full, 3 * c + n, slice(at * PAIR, (at + 1) * PAIR))
            for at, g in enumerate(groups) for c in range(2) for n in range(3)
        ]

    q0_begin, q0_sent, q0_got = seed(group_parts(wq0, [0]), seed_q0)
    q1_begin, q1_sent, q1_got = seed(group_parts(wq1, [1, 2]), seed_q1)
    o_begin, o_sent, o_got = seed(
        [(half_ref.at[:, 3 * width + b * co : 3 * width + (b + 1) * co],
          wuo, b, slice(cu, cu + co)) for b in range(6)], seed_o)
    u_begin, u_sent, u_got = seed(
        [(half_ref.at[:, b * cu : (b + 1) * cu],
          wuo, b, slice(0, cu)) for b in range(6)], seed_u)

    def down_parts(which):
        return [
            (down_ref.at[n * mine : (n + 1) * mine, k * cd : (k + 1) * cd],
             wd_ref, 3 * which + k, slice(n * cd, (n + 1) * cd))
            for k in range(3) for n in range(2)
        ]

    d_begin, d_sent, _ = seed(down_parts(core), seed_d)
    _, _, d_got = seed(down_parts(1 - core), seed_d)

    gather_q0 = Gather(wq0, chain_q0, pass_q0)
    gather_q1 = Gather(wq1, chain_q1, pass_q1)
    gather_u = Gather(wuo, chain_u, pass_u)
    gather_d = Gather(wd_ref, chain_d, pass_d)

    own_rows = pl.ds(pl.multiple_of(core * rows, rows), rows)
    loads = [
        pltpu.make_async_copy(tokens_ref.at[own_rows], hidden, load_sems.at[0]),
        pltpu.make_async_copy(upstream_ref.at[own_rows], gffn, load_sems.at[1]),
    ]
    loads[0].start()
    greet(me)
    pl.when(first)(q0_begin)
    pl.when(first)(q1_begin)
    pl.when(first)(o_begin)
    pl.when(second)(u_begin)
    d_begin()
    loads[1].start()
    pl.when(first)(q0_sent)
    pl.when(second)(q0_got)
    gather_q0.launch()

    loads[0].wait()
    value, _ = normalized(hidden[...].astype(F32))
    normed[...] = (value * as_row(pg_ref) + as_row(ps_ref)).astype(BF16)
    start[...] = start_row(lengths_ref, core, rows)
    saves = []

    def save(source, target):
        saves.append(pltpu.make_async_copy(source, target, save_sems.at[len(saves)]))
        saves[-1].start()

    save(normed, normed_out)
    save(start, start_out)
    gather_q0.arrive(0)

    @pl.when(first)
    def _():
        q1_sent()
        o_sent()
        u_got()

    @pl.when(second)
    def _():
        u_sent()
        q1_got()
        o_got()

    d_sent()
    d_got()
    gather_q1.launch()
    gather_q0.arrive(1)
    gather_q0.arrive(2)
    gather_q1.arrive(0)
    gather_u.launch()
    gather_q0.arrive(3)
    gather_q0.passed()

    query_bias, value_bias = as_row(qb_ref), as_row(vb_ref)

    def project_group(group, weights):
        biases = []
        for c in range(2):
            at = slice((2 * group + c) * PAIR, (2 * group + c + 1) * PAIR)
            biases += [query_bias[:, at], jnp.zeros((1, PAIR), F32), value_bias[:, at]]
        cols = slice(group * 2 * cg, (group + 1) * 2 * cg)
        weight = jnp.concatenate(weights, axis=1)
        broad[:, cols] = (nn(normed[...], weight) + jnp.concatenate(biases, axis=1)).astype(BF16)

    project_group(0, [wq0[b].reshape(width, PAIR) for b in range(6)])
    gather_q1.arrive(1)

    def one_pair(pair, carry):
        @pl.when(pair == 1)
        def _():
            gather_q1.arrive(2)
            gather_u.arrive(0)
            gather_d.launch()

        @pl.when(pair == 2)
        def _():
            gather_q1.arrive(3)
            gather_q1.passed()
            for group in range(1, 3):
                at = slice((group - 1) * PAIR, group * PAIR)
                project_group(group, [wq1[(b, *box, slice(None), at)].reshape(width, PAIR) for b in range(6)])
            pltpu.make_async_copy(broad.at[:, : 3 * width], projected_out, load_sems.at[0]).start()

        @pl.when(pair == 3)
        def _():
            gather_u.arrive(1)
            gather_d.arrive(0)

        @pl.when(pair == 4)
        def _():
            gather_u.arrive(2)

        @pl.when(pair == 5)
        def _():
            gather_d.arrive(1)

        at_q = pl.ds(pl.multiple_of(pair * cg, PAIR), PAIR)
        at_k = pl.ds(pl.multiple_of(pair * cg + PAIR, PAIR), PAIR)
        at_v = pl.ds(pl.multiple_of(pair * cg + 2 * PAIR, PAIR), PAIR)
        at_out = pl.ds(pl.multiple_of(pair * PAIR, PAIR), PAIR)
        attend_pair(broad[:, at_q], broad[:, at_k], broad[:, at_v], start, context.at[:, at_out], lse.at[pair])
        return carry

    lax.fori_loop(0, pairs, one_pair, 0)
    save(context, context_out)
    save(lse, lse_out)
    save(wq0, wq0_out)
    save(wq1, wq1_out)
    gather_u.arrive(3)
    gather_u.passed()
    save(wuo, wuo_out)
    loads[1].wait()
    pltpu.make_async_copy(broad.at[:, : 3 * width], projected_out, load_sems.at[0]).wait()
    saves[0].wait()

    def row_saves(step):
        at = pl.ds(pl.multiple_of(step * BLOCK, BLOCK), BLOCK)
        pieces = [(mixed, mixed_out), (normed, nffn_out), (hidden, hidden_out), (mid, mid_out), (hat, hat_out),
                  (broad, slope_out)]
        return [
            pltpu.make_async_copy(source.at[at], target.at[at], row_sems.at[index, step])
            for index, (source, target) in enumerate(pieces)
        ]

    def one_block(step, carry):
        at = pl.ds(pl.multiple_of(step * BLOCK, BLOCK), BLOCK)
        alive = alive_rows(lengths_ref, core, step * BLOCK, BLOCK)
        ctx_hat, _ = normalized(context[at, :])
        mix = (ctx_hat * as_row(sg_ref) + as_row(ss_ref)).astype(BF16)
        mixed[at, :] = mix
        out_weight = jnp.concatenate([wuo[(b, *box, slice(None), slice(cu, cu + co))].reshape(width, co) for b in range(6)], axis=1)
        branch = nn(mix, out_weight) + as_row(ob_ref)
        hid = (hidden[at, :].astype(F32) + alive * branch).astype(BF16)
        hidden[at, :] = hid
        hid_hat, _ = normalized(hid.astype(F32))
        nffn = (hid_hat * as_row(fg_ref) + as_row(fs_ref)).astype(BF16)
        normed[at, :] = nffn
        up_weight = jnp.concatenate([wuo[(b, *box, slice(None), slice(0, cu))].reshape(width, cu) for b in range(6)], axis=1)
        units = 4 * width
        chunks = [slice(c, c + width) for c in range(0, units, width)]
        up_bias, mid_gain, mid_shift = as_row(ub_ref), as_row(mg_ref), as_row(ms_ref)
        lanes = jnp.zeros((BLOCK, 128), F32)
        for cols in chunks:
            value, slope = gelu_parts(nn(nffn, up_weight[:, cols]) + up_bias[:, cols])
            broad[at, cols] = slope.astype(BF16)
            active[:, cols] = value
            lanes = lanes + lane_groups(value)
        center = jnp.sum(lanes, axis=-1, keepdims=True) * (1.0 / units)
        lanes = jnp.zeros((BLOCK, 128), F32)
        for cols in chunks:
            centered = active[:, cols] - center
            lanes = lanes + lane_groups(centered * centered)
        act_scale = lax.rsqrt(jnp.sum(lanes, axis=-1, keepdims=True) * (1.0 / units) + EPS)
        for cols in chunks:
            act_hat = (active[:, cols] - center) * act_scale
            hat[at, cols] = act_hat.astype(BF16)
            mid[at, cols] = (act_hat * mid_gain[:, cols] + mid_shift[:, cols]).astype(BF16)
        scales[at, :] = act_scale
        gffn[at, :] = (alive * gffn[at, :].astype(F32)).astype(BF16)
        for copy in row_saves(step):
            copy.start()

        @pl.when(step == 1)
        def _():
            gather_d.arrive(2)

        return carry

    steps = rows // BLOCK
    lax.fori_loop(0, steps, one_block, 0)
    gather_d.arrive(3)
    save(scales, scale_out)

    def grad_save(h, k):
        return pltpu.make_async_copy(gdown.at[k], gdown_out.at[3 * h + k], grad_sems.at[h, k])

    for h in range(2):
        mid_t[...] = mid[:, 2 * h * width : 2 * (h + 1) * width].T
        for k in range(3):
            grad = nn(mid_t[...], gffn[:, k * cd : (k + 1) * cd]).astype(BF16)
            grad = grad.reshape(CHIPS, 2, mine, cd)
            if h:
                grad_save(0, k).wait()
            for n in range(2):
                gdown[k, :, :, n * cd : (n + 1) * cd] = grad[:, n]
            grad_save(h, k).start()
    for k in range(3):
        grad_save(1, k).wait()

    gather_d.passed()

    def finish(step, carry):
        for copy in row_saves(step):
            copy.wait()
        return carry

    lax.fori_loop(0, steps, finish, 0)
    for copy in saves[1:]:
        copy.wait()
    for gather in (gather_q0, gather_q1, gather_u, gather_d):
        gather.drain()


def front(tokens, upstream, lengths, half, down, vectors):
    width = tokens.shape[1]
    rows = tokens.shape[0] // 2
    mine = half.shape[0]
    box = BOX
    pairs = width // PAIR
    wide = 4 * width
    anywhere = pl.BlockSpec(memory_space=pl.ANY)
    vmem = pl.BlockSpec(memory_space=pltpu.VMEM)
    smem = pl.BlockSpec(memory_space=pltpu.SMEM)
    dma = pltpu.SemaphoreType.DMA
    sizes = dict(q0=PAIR, q1=2 * PAIR, u=5 * width // 6, d=2 * width // 3)
    shape = jax.ShapeDtypeStruct
    steps = rows // BLOCK
    return pl.pallas_call(
        front_kernel,
        in_specs=[anywhere, anywhere, smem, anywhere, anywhere] + [vmem] * len(vectors),
        out_specs=[anywhere] * 17,
        out_shape=[
            shape((rows, 3 * width), BF16), shape((rows, width), BF16), shape((rows, width), F32),
            shape((pairs, 2, rows), F32), shape((1, rows), jnp.int32),
            *[shape((6, *box, mine, columns), BF16) for columns in sizes.values()],
            shape((rows, width), BF16), shape((rows, width), BF16), shape((rows, width), BF16),
            shape((rows, wide), BF16), shape((rows, wide), BF16), shape((rows, wide), BF16), shape((rows, 1), F32),
            shape((6, CHIPS, mine, 2 * width // 3), BF16),
        ],
        scratch_shapes=[
            pltpu.VMEM((rows, width), BF16), pltpu.VMEM((rows, width), BF16), pltpu.VMEM((rows, wide), BF16),
            pltpu.VMEM((rows, wide), BF16), pltpu.VMEM((rows, wide), BF16), pltpu.VMEM((rows, width), BF16),
            pltpu.VMEM((rows, width), BF16), pltpu.VMEM((rows, width), F32), pltpu.VMEM((pairs, 2, rows), F32),
            pltpu.VMEM((1, rows), jnp.int32),
            *[pltpu.VMEM((6, *box, mine, sizes[name]), BF16) for name in ("q0", "q1", "u")],
            pltpu.VMEM((2 * width, rows), BF16), pltpu.VMEM((3, CHIPS, mine, 2 * width // 3), BF16),
            pltpu.VMEM((rows, 1), F32), pltpu.VMEM((BLOCK, wide), F32),
            dma((3, 6)), dma((3, 12)), dma((3, 6)), dma((3, 6)), dma((3, 6)),
            *[dma((2, MOVES))] * 4, *[dma((2, 6))] * 4,
            dma((2,)), dma((8,)), dma((6, steps)), dma((2, 3)),
        ],
        compiler_params=params(collective_id=1, has_side_effects=True),
        name="front",
    )(tokens, upstream, lengths, half, down, *vectors)


class Scatter:
    def __init__(self, total, landings, sems, final):
        self.me = Place()
        self.total, self.landings, self.sems, self.final = total, landings, sems, final

    def move(self, index, z, y, x, device):
        return remote(self.total.at[:, z, y, x], self.landings.at[index], (self.sems.at[0, index], self.sems.at[1, index]), device)

    def to_z(self, k):
        me = self.me
        return self.move(k - 1, me.zs[k], me.y, me.x, me.over_z(k))

    def to_x(self, k):
        me = self.me
        return self.move(X_AT + k, me.zs[k], me.y, 1 - me.x, me.over_x())

    def to_y(self, k):
        me = self.me
        return self.move(Y_AT + k, me.zs[k], 1 - me.y, me.x, me.over_y())

    def toward(self, k):
        me = self.me
        return self.move(D_AT + k, me.zs[k], 1 - me.y, 1 - me.x, me.over_y() if k < 2 else me.over_x())

    def add(self, z, y, x, landed):
        self.total[:, z, y, x] = functools.reduce(jnp.add, [part[...] for part in landed], self.total[:, z, y, x])

    def begin(self, other):
        me = self.me

        def both(z, y, x):
            self.add(z, y, x, [other.at[:, z, y, x]])

        for k in range(4):
            both(me.zs[k], 1 - me.y, 1 - me.x)
            self.toward(k).start()
        for k in range(4):
            both(me.zs[k], me.y, 1 - me.x)
            both(me.zs[k], 1 - me.y, me.x)
            both(me.zs[k], me.y, me.x)

    def arrive(self, stage):
        me = self.me
        if stage == 0:
            for k in range(4):
                self.toward(k).wait_recv()
                if k < 2:
                    self.add(me.zs[k], me.y, 1 - me.x, [self.landings.at[D_AT + k]])
                else:
                    self.add(me.zs[k], 1 - me.y, me.x, [self.landings.at[D_AT + k]])
            for k in (2, 3):
                self.to_x(k).start()
                self.to_y(k).start()
        elif stage < 3:
            if stage == 1:
                for k in (1, 0):
                    self.to_x(k).start()
                    self.to_y(k).start()
            for k in (2, 3) if stage == 1 else (1, 0):
                self.to_x(k).wait_recv()
                self.to_y(k).wait_recv()
                self.add(me.zs[k], me.y, me.x, [self.landings.at[X_AT + k], self.landings.at[Y_AT + k]])
                if k:
                    self.to_z(k).start()
        else:
            value = self.total[:, me.z, me.y, me.x].astype(F32)
            for k in (1, 2, 3):
                self.to_z(k).wait_recv()
                value = value + self.landings[k - 1].astype(F32)
            self.final[...] = value

    def drain(self):
        for k in (1, 2, 3):
            self.to_z(k).wait_send()
        for k in range(4):
            for move in (self.to_x(k), self.to_y(k), self.toward(k)):
                move.wait_send()


def feed_body(
    hidden_steps, upstream_ref, context_ref, hidden_ref, mid_ref, hat_ref, slope_ref, scale_ref, lengths_ref, wuo_ref, wd_ref,
    sg_ref, fg_ref, mg_ref, db_ref, gdown_ref,
    ghid_ref, gctx_ref, gbranch_ref, gup_ref, narrow_ref, wide_ref, layer_ref, down_ref,
    out_rows, scaled_grad, total, landed, landings, final, swap_sems, chain_sems, local_sems, out_sems,
):
    me = Place()
    core = me.core
    step = pl.program_id(0)
    steps = pl.num_programs(0)
    width = hidden_ref.shape[1]
    mine = width // CHIPS
    co, cu, cd = width // 6, 2 * width // 3, width // 3
    sibling = me.sibling()
    scatter = Scatter(total, landings, chain_sems, final)
    own = pltpu.make_async_copy(gdown_ref.at[pl.ds(3 * core, 3)], total, local_sems.at[0])
    far = remote(gdown_ref.at[pl.ds(3 * (1 - core), 3)], landed, (swap_sems.at[0], swap_sems.at[1]), sibling)

    def out_copies(at_step, which):
        at = pl.ds(pl.multiple_of(at_step * BLOCK, BLOCK), BLOCK)
        target = layer_ref.at[which, at]
        return (pltpu.make_async_copy(out_rows.at[at], target, out_sems.at[0, at_step]),
                remote(out_rows.at[at], target, (out_sems.at[1, at_step], out_sems.at[2, at_step]), sibling))

    @pl.when(step == 0)
    def _():
        greet(me)
        far.start()
        own.start()
        narrow_ref[...] = jnp.zeros_like(narrow_ref)
        wide_ref[...] = jnp.zeros_like(wide_ref)

    def hook(at_step, action):
        pl.when(step == at_step)(action)

    def begin():
        own.wait()
        far.wait_recv()
        scatter.begin(landed)

    up_weight = jnp.concatenate([wuo_ref[b, :, :cu] for b in range(6)], axis=1)
    out_weight = jnp.concatenate([wuo_ref[b, :, cu:] for b in range(6)], axis=1)
    halves = []
    for h in range(2):
        parts = []
        for n in range(2):
            part = jnp.concatenate([wd_ref[3 * h + k, :, n * cd : (n + 1) * cd] for k in range(3)], axis=1)
            parts.append(part.reshape(CHIPS, 1, mine, width))
        halves.append(jnp.concatenate(parts, axis=1).reshape(2 * width, width))
    down_weight = jnp.concatenate(halves, axis=0)

    hook(3, lambda: scatter.arrive(2))
    alive = alive_rows(lengths_ref, core, step * BLOCK, BLOCK)
    hidden = hidden_ref[...].astype(F32)
    upstream = upstream_ref[...].astype(F32)
    gffn = (alive * upstream).astype(BF16)
    mid_gain = as_row(mg_ref)
    units = 4 * width
    chunks = [slice(at, at + width) for at in range(0, units, width)]
    first_sum = jnp.zeros((BLOCK, 128), F32)
    second_sum = jnp.zeros((BLOCK, 128), F32)
    for cols in chunks:
        gmid = nt(gffn, down_weight[cols])
        weighted = gmid * hat_ref[:, cols].astype(F32)
        wide_ref[1:2, cols] += col_sum(weighted)
        wide_ref[2:3, cols] += col_sum(gmid)
        scaled = gmid * mid_gain[:, cols]
        scaled_grad[:, cols] = scaled
        first_sum = first_sum + lane_groups(scaled)
        second_sum = second_sum + lane_groups(weighted * mid_gain[:, cols])
    first_mean = jnp.sum(first_sum, axis=-1, keepdims=True) * (1.0 / units)
    second_mean = jnp.sum(second_sum, axis=-1, keepdims=True) * (1.0 / units)
    hook(0, begin)
    hook(1, lambda: scatter.arrive(0))
    hook(2, lambda: scatter.arrive(1))
    act_scale = scale_ref[...]
    gnffn = jnp.zeros((BLOCK, width), F32)
    result = jnp.zeros((BLOCK, width), F32)
    for cols in chunks:
        act_hat = hat_ref[:, cols].astype(F32)
        gact = (scaled_grad[:, cols] - first_mean - act_hat * second_mean) * act_scale
        gup = (gact * slope_ref[:, cols].astype(F32)).astype(BF16)
        gup_ref[:, cols] = gup
        wide_ref[0:1, cols] += col_sum(gup.astype(F32))
        gnffn = gnffn + nt(gup, up_weight[:, cols])
        result = result + nn(mid_ref[:, cols], down_weight[cols])
    result = (result + as_row(db_ref)).astype(BF16).astype(F32)
    out_rows[pl.ds(pl.multiple_of(step * BLOCK, BLOCK), BLOCK), :] = hidden + alive * result
    for copy in out_copies(step, core):
        copy.start()
    hid_hat, hid_scale = normalized(hidden)
    ghid = (upstream + norm_back(hid_hat, hid_scale, as_row(fg_ref), gnffn)).astype(BF16)
    ghid_ref[...] = ghid
    gbranch = (alive * ghid.astype(F32)).astype(BF16)
    gbranch_ref[...] = gbranch
    gmixed = nt(gbranch, out_weight)
    ctx_hat, ctx_scale = normalized(context_ref[...])
    gctx_ref[...] = norm_back(ctx_hat, ctx_scale, as_row(sg_ref), gmixed).astype(BF16)
    narrow_ref[0:1, :] += col_sum(gmixed * ctx_hat)
    narrow_ref[1:2, :] += col_sum(gmixed)
    narrow_ref[2:3, :] += col_sum(gbranch.astype(F32))
    narrow_ref[3:4, :] += col_sum(gnffn * hid_hat)
    narrow_ref[4:5, :] += col_sum(gnffn)
    narrow_ref[5:6, :] += col_sum(gffn.astype(F32))

    @pl.when(step == steps - 1)
    def _():
        scatter.arrive(3)
        for k in range(3):
            for n in range(2):
                down_ref[n * mine : (n + 1) * mine, k * cd : (k + 1) * cd] = final[k, :, n * cd : (n + 1) * cd]
        for index in range(hidden_steps):
            local, away = out_copies(index, core)
            local.wait()
            away.wait_send()
            out_copies(index, 1 - core)[1].wait_recv()
        far.wait_send()
        scatter.drain()


def feed(upstream, context, hidden, mid, hat, slope, scale, lengths, wuo, wd, vectors, gdown):
    rows, width = hidden.shape
    wide = 4 * width
    steps = rows // BLOCK
    box = BOX
    mine = width // CHIPS
    columns = 2 * width // 3
    row = pl.BlockSpec((BLOCK, width), lambda i: (i, 0))
    row_wide = pl.BlockSpec((BLOCK, wide), lambda i: (i, 0))
    once = dict(pipeline_mode=pl.Buffered(1))
    anywhere = pl.BlockSpec(memory_space=pl.ANY)
    vmem = pl.BlockSpec(memory_space=pltpu.VMEM)
    smem = pl.BlockSpec(memory_space=pltpu.SMEM)
    dma = pltpu.SemaphoreType.DMA
    shape = jax.ShapeDtypeStruct

    def held(*size, dtype=BF16):
        return pltpu.VMEM(size, dtype)

    return pl.pallas_call(
        functools.partial(feed_body, steps),
        grid=(steps,),
        in_specs=[
            pl.BlockSpec((BLOCK, width), lambda i: (lax.axis_index("section") * steps + i, 0)),
            row, row, row_wide, row_wide, row_wide, pl.BlockSpec((BLOCK, 1), lambda i: (i, 0)), smem,
            pl.BlockSpec(wuo.shape, lambda i: (0, 0, 0), **once),
            pl.BlockSpec(wd.shape, lambda i: (0, 0, 0), **once),
            *[vmem] * 4, anywhere,
        ],
        out_specs=[row, row, row, row_wide, whole((8, width)), whole((8, wide)), anywhere, vmem],
        out_shape=[
            shape((rows, width), BF16), shape((rows, width), BF16), shape((rows, width), BF16), shape((rows, wide), BF16),
            shape((8, width), F32), shape((8, wide), F32), shape((2, rows, width), F32), shape((2 * mine, width), F32),
        ],
        scratch_shapes=[
            held(rows, width, dtype=F32), held(BLOCK, wide, dtype=F32),
            held(3, *box, mine, columns), held(3, *box, mine, columns),
            held(MOVES, 3, mine, columns),
            held(3, mine, columns, dtype=F32),
            dma((2,)), dma((2, MOVES)), dma((1,)), dma((3, steps)),
        ],
        compiler_params=params(collective_id=3, has_side_effects=True),
        name="feed",
    )(upstream, context, hidden, mid, hat, slope, scale, lengths, wuo, wd, *vectors,
      gdown.reshape((6,) + box + (mine, columns)))


def outer_two_kernel(nffn_ref, gup_ref, mixed_ref, gbranch_ref, layer_ref, out_ref, copy_ref, nffn_t, mixed_t):
    block = pl.program_id(0)
    width = nffn_ref.shape[1]
    cu = 2 * width // 3
    copy_ref[...] = layer_ref[...]

    @pl.when(block == 0)
    def _():
        nffn_t[...] = nffn_ref[...].T
        mixed_t[...] = mixed_ref[...].T

    out_ref[0, :, :cu] = nn(nffn_t[...], gup_ref[...]).astype(BF16)
    out_ref[0, :, cu:] = nn(mixed_t[...], gbranch_ref[...]).astype(BF16)


def outer_two(nffn, gup, mixed, gbranch, layer):
    rows, width = nffn.shape
    cu, co = 2 * width // 3, width // 6
    columns = pl.BlockSpec((layer.shape[0], co), lambda b: (0, b))
    return pl.pallas_call(
        outer_two_kernel,
        grid=(6,),
        in_specs=[
            whole((rows, width)), pl.BlockSpec((rows, cu), lambda b: (0, b)),
            whole((rows, width)), pl.BlockSpec((rows, co), lambda b: (0, b)), columns,
        ],
        out_specs=[pl.BlockSpec((1, width, cu + co), lambda b: (b, 0, 0)), columns],
        out_shape=[jax.ShapeDtypeStruct((6, width, cu + co), BF16), jax.ShapeDtypeStruct(layer.shape, F32)],
        scratch_shapes=[pltpu.VMEM((width, rows), BF16), pltpu.VMEM((width, rows), BF16)],
        compiler_params=params(),
        name="outer_two",
    )(nffn, gup, mixed, gbranch, layer)


def back_kernel(
    projected_ref, gctx_ref, context_ref, lse_ref, start_ref, normed_ref, tokens_ref, ghid_ref, gain_ref, wq0_ref, wq1_ref,
    narrow_ref, wide_ref, rest_ref,
    grad_ref, half_ref, slim_ref, broad_ref,
    x_rows, dproj, dk_acc, dv_acc, normed_t, far_rows,
    total_r, first_r, landings_r, final_r, other_r,
    total_q, far_q, first_q, landings_q, final_q, other_q,
    small, small_in,
    local_sems, swap_sems, chain_r, chain_q, small_sems,
):
    me = Place()
    core = me.core
    rows, width = x_rows.shape
    mine = half_ref.shape[0]
    pairs = width // PAIR
    co, cu, cq = width // 6, 2 * width // 3, width // 2
    cg = 3 * PAIR
    sibling = me.sibling()
    first = core == 0
    second = core == 1

    def swap(index, source, target):
        return remote(source, target, (swap_sems.at[0, index], swap_sems.at[1, index]), sibling)

    sum_r = Scatter(total_r, landings_r, chain_r, final_r)
    sum_q = [Scatter(total_q.at[g], landings_q.at[g], chain_q.at[g], final_q.at[g]) for g in range(3)]

    own_x = pltpu.make_async_copy(
        tokens_ref.at[pl.ds(pl.multiple_of(core * rows, rows), rows)], x_rows, local_sems.at[1])
    own_x.start()
    greet(me)
    own_rest = pltpu.make_async_copy(rest_ref.at[pl.ds(3 * core, 3)], total_r, local_sems.at[0])
    far_rest = swap(0, rest_ref.at[pl.ds(3 * (1 - core), 3)], first_r)
    far_rest.start()
    own_rest.start()
    normed_t[...] = normed_ref[...].T

    def swap_q(group):
        return swap(3 + group, far_q.at[group], first_q.at[group])

    def make(group):
        for which, target in ((1 - core, far_q), (core, total_q)):
            at = pl.ds(pl.multiple_of(group * 2 * cg + which * cg, PAIR), cg)
            grad = nn(normed_t[...], dproj[:, at]).astype(BF16)
            for n in range(3):
                target[group, n] = grad[:, n * PAIR : (n + 1) * PAIR].reshape(BOX + (mine, PAIR))
            if target is far_q:
                swap_q(group).start()

    def begin(group):
        swap_q(group).wait_recv()
        sum_q[group].begin(first_q.at[group])

    def one_pair(pair, carry):
        @pl.when(pair == 1)
        def _():
            own_rest.wait()
            far_rest.wait_recv()
            sum_r.begin(first_r)

        @pl.when(pair == 2)
        def _():
            make(0)

        @pl.when(pair == 3)
        def _():
            begin(0)
            sum_r.arrive(0)

        @pl.when(pair == 4)
        def _():
            sum_q[0].arrive(0)
            make(1)

        @pl.when(pair == 5)
        def _():
            begin(1)
            sum_q[0].arrive(1)
            sum_r.arrive(1)

        at_q = pl.ds(pl.multiple_of(pair * cg, PAIR), PAIR)
        at_k = pl.ds(pl.multiple_of(pair * cg + PAIR, PAIR), PAIR)
        at_v = pl.ds(pl.multiple_of(pair * cg + 2 * PAIR, PAIR), PAIR)
        at_c = pl.ds(pl.multiple_of(pair * PAIR, PAIR), PAIR)
        attend_back_pair(
            projected_ref[:, at_q], projected_ref[:, at_k], projected_ref[:, at_v], gctx_ref[:, at_c],
            context_ref[:, at_c], lse_ref.at[pair], start_ref,
            dproj.at[:, at_q], dproj.at[:, at_k], dproj.at[:, at_v], dk_acc, dv_acc,
        )
        return carry

    lax.fori_loop(0, pairs, one_pair, 0)
    make(2)
    sum_q[1].arrive(0)
    sum_q[0].arrive(2)
    sum_r.arrive(2)
    begin(2)
    own_x.wait()
    small[0] = jnp.zeros_like(small[0])

    def one_block(step, carry):
        at = pl.ds(pl.multiple_of(step * BLOCK, BLOCK), BLOCK)
        gnormed = jnp.zeros((BLOCK, width), F32)
        for group in range(3):
            if group == 0:
                blocks = [wq0_ref[b].reshape(width, PAIR) for b in range(6)]
            else:
                cols = slice((group - 1) * PAIR, group * PAIR)
                blocks = [wq1_ref[(b,) + (slice(None),) * 4 + (cols,)].reshape(width, PAIR) for b in range(6)]
            weight = jnp.concatenate(blocks, axis=1)
            gnormed = gnormed + nt(dproj[at, group * 2 * cg : (group + 1) * 2 * cg], weight)
        hat, scale = normalized(x_rows[at, :].astype(F32))
        grad_x = ghid_ref[at, :].astype(F32) + norm_back(hat, scale, as_row(gain_ref), gnormed)

        @pl.when(first)
        def _():
            grad_ref[0, at, :] = grad_x[:, :cq]
            far_rows[at, :] = grad_x[:, cq:]

        @pl.when(second)
        def _():
            grad_ref[1, at, :] = grad_x[:, cq:]
            far_rows[at, :] = grad_x[:, :cq]

        small[0, 0:1, :] += col_sum(gnormed * hat)
        small[0, 1:2, :] += col_sum(gnormed)
        for row, part in ((2, 0), (3, 2)):
            grads = [dproj[at, p * cg + part * PAIR : p * cg + (part + 1) * PAIR].astype(F32) for p in range(pairs)]
            small[0, row : row + 1, :] += col_sum(jnp.concatenate(grads, axis=1))

        @pl.when(step == 0)
        def _():
            sum_q[1].arrive(1)

        @pl.when(step == 1)
        def _():
            sum_q[2].arrive(0)
            sum_q[1].arrive(2)

        @pl.when(step == 2)
        def _():
            sum_q[0].arrive(3)

        @pl.when(step == 3)
        def _():
            sum_q[2].arrive(1)

        return carry

    lax.fori_loop(0, rows // BLOCK, one_block, 0)
    swap_x = swap(1, far_rows, grad_ref.at[core])
    small[0, 4:10, :] = narrow_ref[0:6, :]
    for n in range(3):
        for part in range(4):
            row = 10 + 4 * n + part
            small[0, row : row + 1, :] = wide_ref[n : n + 1, part * width : (part + 1) * width]

    partners = [[sibling], [me.over_x(), me.over_y(), me.across()], [me.over_z(k) for k in (1, 2, 3)]]

    def small_moves(stage):
        at = (0, 1, 4)[stage]
        return [
            remote(small.at[stage], small_in.at[at + n], (small_sems.at[0, at + n], small_sems.at[1, at + n]), device)
            for n, device in enumerate(partners[stage])
        ]

    def small_start(stage):
        for move in small_moves(stage):
            move.start()

    def small_arrive(stage):
        at = (0, 1, 4)[stage]
        value = small[stage]
        for n, move in enumerate(small_moves(stage)):
            move.wait_recv()
            value = value + small_in[at + n]
        small[stage + 1] = value
        if stage < 2:
            small_start(stage + 1)

    small_start(0)
    swap_x.start()
    sum_q[2].arrive(2)
    sum_q[1].arrive(3)
    small_arrive(0)
    sum_r.arrive(3)
    swap_r = swap(2, final_r, other_r)
    swap_r.start()
    small_arrive(1)
    sum_q[2].arrive(3)
    swap_f = swap(6, final_q, other_q)
    swap_f.start()
    small_arrive(2)
    swap_r.wait_recv()

    sums = small[3]
    share = core * CHIPS + me.chip

    def pick(values, each):
        lane = lax.broadcasted_iota(jnp.int32, (values.shape[1], 128), 0)
        column = lax.broadcasted_iota(jnp.int32, (values.shape[1], 128), 1)
        wanted = ((lane == share * each + column) & (column < each)).astype(F32)
        return lax.dot_general(
            values, wanted, (((1,), (0,)), ((), ())), precision=lax.Precision.HIGHEST, preferred_element_type=F32
        )

    shares = 2 * CHIPS
    slim_ref[...] = pick(sums[0:16], width // shares)
    broad_ref[...] = jnp.zeros_like(broad_ref)
    for n in range(3):
        row = jnp.concatenate([sums[10 + 4 * n + part : 11 + 4 * n + part] for part in range(4)], axis=1)
        broad_ref[n : n + 1, :] = pick(jnp.broadcast_to(row, (8, 4 * width)), 4 * width // shares)[0:1]

    swap_f.wait_recv()

    @pl.when(first)
    def _():
        for k in range(3):
            for g in range(3):
                for c, source in ((0, final_q), (1, other_q)):
                    at = k * width + (2 * g + c) * PAIR
                    half_ref[:, at : at + PAIR] = source[g, k]
            half_ref[:, 3 * width + k * co : 3 * width + (k + 1) * co] = final_r[k, :, cu:]
            half_ref[:, 3 * width + (3 + k) * co : 3 * width + (4 + k) * co] = other_r[k, :, cu:]

    @pl.when(second)
    def _():
        for k in range(3):
            half_ref[:, k * cu : (k + 1) * cu] = other_r[k, :, :cu]
            half_ref[:, (3 + k) * cu : (4 + k) * cu] = final_r[k, :, :cu]

    swap(1, far_rows, grad_ref.at[1 - core]).wait_recv()
    for done in (far_rest, swap_x, swap_r, swap_f, swap_q(0), swap_q(1), swap_q(2)):
        done.wait_send()
    for stage in range(3):
        for move in small_moves(stage):
            move.wait_send()
    for each in [sum_r] + sum_q:
        each.drain()


def back(projected, gctx, context, lse, start, normed, tokens, ghid, gain, wq0, wq1, narrow, wide, rest):
    rows, width = normed.shape
    box = BOX
    mine = width // CHIPS
    cq, cr = width // 2, 5 * width // 6
    anywhere = pl.BlockSpec(memory_space=pl.ANY)
    vmem = pl.BlockSpec(memory_space=pltpu.VMEM)
    dma = pltpu.SemaphoreType.DMA

    def held(*shape, dtype=BF16):
        return pltpu.VMEM(shape, dtype)

    return pl.pallas_call(
        back_kernel,
        in_specs=[vmem] * 6 + [anywhere] + [vmem] * 6 + [anywhere],
        out_specs=[vmem] * 4,
        out_shape=[
            jax.ShapeDtypeStruct((2, rows, cq), F32),
            jax.ShapeDtypeStruct((mine, 4 * width), F32),
            jax.ShapeDtypeStruct((16, 128), F32),
            jax.ShapeDtypeStruct((8, 128), F32),
        ],
        scratch_shapes=[
            held(rows, width), held(rows, 3 * width), held(rows, PAIR, dtype=F32), held(rows, PAIR, dtype=F32),
            held(width, rows), held(rows, cq, dtype=F32),
            held(3, *box, mine, cr), held(3, *box, mine, cr), held(MOVES, 3, mine, cr),
            held(3, mine, cr, dtype=F32), held(3, mine, cr, dtype=F32),
            held(3, 3, *box, mine, PAIR), held(3, 3, *box, mine, PAIR), held(3, 3, *box, mine, PAIR),
            held(3, MOVES, 3, mine, PAIR),
            held(3, 3, mine, PAIR, dtype=F32), held(3, 3, mine, PAIR, dtype=F32),
            held(4, 24, width, dtype=F32), held(7, 24, width, dtype=F32),
            dma((2,)), dma((2, 7)), dma((2, MOVES)), dma((3, 2, MOVES)), dma((2, 7)),
        ],
        compiler_params=params(collective_id=2, has_side_effects=True),
        name="back",
    )(projected, gctx, context, lse, start, normed, tokens, ghid, gain, wq0, wq1, narrow, wide,
      rest.reshape((6,) + box + (mine, cr)))


def fused_batch(tokens, out_grad, lengths, half, down, vectors):
    (pre_gain, pre_shift, query_bias, value_bias, sub_gain, sub_shift, out_bias,
     ffn_gain, ffn_shift, up_bias, mid_gain, mid_shift, down_bias) = vectors
    width = tokens.shape[1]
    (projected, normed, context, lse, start, wq0, wq1, wuo, wd, mixed, nffn, hidden, mid, hat, slope, scale, gdown) = front(
        tokens, out_grad, lengths, half, down,
        (pre_gain, pre_shift, query_bias, value_bias, sub_gain, sub_shift, out_bias, ffn_gain, ffn_shift, up_bias,
         mid_gain, mid_shift),
    )
    ghid, gctx, gbranch, gup, narrow, wide, layer, down_grad = feed(
        out_grad, context, hidden, mid, hat, slope, scale, lengths, wuo.reshape(6, width, -1), wd.reshape(6, width, -1),
        (sub_gain, ffn_gain, mid_gain, down_bias), gdown,
    )
    grads, layer = outer_two(nffn, gup, mixed, gbranch, layer.reshape(-1, width))
    grad_x, half_grad, slim, broad = back(
        projected, gctx, context, lse, start, normed, tokens, ghid, pre_gain, wq0, wq1, narrow, wide, grads
    )
    shares = 2 * CHIPS
    slim = slim[:10, : width // shares]
    broad = broad[:3, : 4 * width // shares]
    small = (slim[0], slim[1], slim[2], slim[3], slim[4], slim[5], slim[6], slim[7], slim[8],
             broad[0], broad[1], broad[2], slim[9])
    return layer, grad_x.reshape(-1, width // 2), half_grad[None], down_grad, *small


def unpacked(vectors):
    return [vector[None, :] for vector in vectors]


def marks_and_bias(x, lengths_row, query_bias, value_bias):
    alive, start = row_marks(lengths_row, x.shape[0])
    bias = jnp.concatenate([query_bias, jnp.zeros_like(query_bias), value_bias], axis=1)
    return alive, start, bias


def one_batch(x, dy, lengths_row, qkv, rest, vectors):
    (pre_gain, pre_shift, query_bias, value_bias, sub_gain, sub_shift, out_bias,
     ffn_gain, ffn_shift, up_bias, mid_gain, mid_shift, down_bias) = unpacked(vectors)
    alive, start, bias = marks_and_bias(x, lengths_row, query_bias, value_bias)
    projected, normed = project(x, qkv, pre_gain, pre_shift, bias)
    context, lse = attend(projected, start)
    out, ghid, gctx, mixed, gbranch, nffn, gup, mid, gffn, narrow, wide = middle(
        x, dy, context, alive, rest,
        (sub_gain, sub_shift, out_bias, ffn_gain, ffn_shift, up_bias, mid_gain, mid_shift, down_bias),
    )
    grad_up = outer(nffn, gup, 256, F32, "outer_up")
    grad_down = outer(mid, gffn, 512, F32, "outer_down")
    dq, dk, dv = attend_back(projected, gctx, context, lse, start)
    grad_out = outer(mixed, gbranch, 256, F32, "outer_out")
    grad_x, pre = project_back(dq, dk, dv, qkv, x, ghid, pre_gain)
    grads = [outer(normed, d, 256, F32, "outer_qkv") for d in (dq, dk, dv)]
    grad_attention = jnp.concatenate(grads + [grad_out], axis=1)
    small = (pre[0], pre[1], pre[2], pre[3], narrow[0], narrow[1], narrow[2], narrow[3], narrow[4],
             wide[0], wide[1], wide[2], narrow[5])
    return (out, grad_x), (grad_attention, grad_up, grad_down, small)


def shards(tokens, out_grad, seq_lengths, half_weights, down_weight, *all_vectors):
    section = lax.axis_index("section")
    sections = lax.axis_size("section")
    both = ("section", "dp")
    width = tokens.shape[1]
    batches = seq_lengths.shape[0]
    count = tokens.shape[0] // batches
    own_batches = batches // sections
    own_rows = own_batches * count
    hidden_units = half_weights.shape[2]
    shares = sections * lax.axis_size("dp")

    if (
        sections == 2
        and shares == sections * CHIPS
        and own_batches == 1
        and half_weights.shape[1] % 16 == 0
        and down_weight.shape[0] == 2 * half_weights.shape[1]
        and hidden_units == 4 * width
    ):
        return fused_batch(tokens, out_grad, seq_lengths, half_weights[0], down_weight, all_vectors)

    def own(array, rows):
        return lax.dynamic_slice_in_dim(array, section * rows, rows, axis=0)

    x_rows = own(tokens, own_rows)
    dy_rows = own(out_grad, own_rows)
    lengths = own(seq_lengths, own_batches)
    blocks = lax.all_gather(half_weights[0], both, axis=0, tiled=True)
    blocks = blocks.reshape(sections, width, hidden_units)
    down_full = lax.all_gather(down_weight, both, axis=0, tiled=True)
    qkv = blocks[0][:, : 3 * width]

    def in_blocks(array):
        return array.reshape(array.shape[0], 6, -1).transpose(1, 0, 2)

    down_blocks = down_full.reshape(2, CHIPS, 2, width // CHIPS, 3, width // 3).transpose(0, 4, 1, 3, 2, 5)
    down_blocks = down_blocks.reshape(6, width, 2 * width // 3)
    rest = jnp.concatenate([in_blocks(blocks[1]), in_blocks(blocks[0][:, 3 * width :]), down_blocks], axis=2)
    rows, sums = [], None
    for index in range(own_batches):
        at = slice(index * count, (index + 1) * count)
        row, more = one_batch(x_rows[at], dy_rows[at], lengths[index], qkv, rest, all_vectors)
        rows.append(row)
        sums = more if sums is None else jax.tree.map(jnp.add, sums, more)
    out_block = jnp.concatenate([row[0] for row in rows], axis=0)
    grad_rows = jnp.concatenate([row[1] for row in rows], axis=0)
    grad_attention, grad_up, grad_down, vectors = sums

    block_part = lax.psum_scatter(
        jnp.concatenate([grad_attention, grad_up], axis=0), both, scatter_dimension=0, tiled=True
    )
    down_part = lax.psum_scatter(grad_down, both, scatter_dimension=0, tiled=True)
    packed = jnp.concatenate([vector.reshape(shares, -1) for vector in vectors], axis=1)
    packed = lax.psum_scatter(packed, both, scatter_dimension=0, tiled=True).reshape(-1)
    parts, start = [], 0
    for vector in vectors:
        size = vector.shape[0] // shares
        parts.append(packed[start : start + size])
        start += size

    layer_out = lax.all_gather(out_block, "section", axis=0, tiled=True)
    tokens_grad = lax.all_to_all(grad_rows, "section", split_axis=1, concat_axis=0, tiled=True)
    return (layer_out, tokens_grad, block_part[None], down_part, *parts)


def solution(mesh):
    replicated = P()
    return jax.shard_map(
        shards,
        mesh=mesh,
        in_specs=(P("dp", None), P("dp", None), P("dp", None), P("section", "dp", None), P(("section", "dp"), None))
        + (replicated,) * 13,
        out_specs=(P("dp", None), P("dp", "section"), P("section", "dp", None), P(("section", "dp"), None))
        + (P(("section", "dp")),) * 13,
        check_vma=False,
    )
```

```python
import functools
import math

import jax
import jax.numpy as jnp
from jax import lax
from jax.experimental import pallas as pl
from jax.experimental.pallas import tpu as pltpu
from jax.sharding import PartitionSpec as P

HEAD_DIM = 64
PAIR = 2 * HEAD_DIM
EPS = 1e-05
BLOCK = 256
F32 = jnp.float32
BF16 = jnp.bfloat16
VMEM_LIMIT = 60 * 1024 * 1024


def nn(left, right):
    return lax.dot_general(left, right, (((1,), (0,)), ((), ())), preferred_element_type=F32)


def nt(left, right):
    return lax.dot_general(left, right, (((1,), (1,)), ((), ())), preferred_element_type=F32)


def tn(left, right):
    return lax.dot_general(left, right, (((0,), (0,)), ((), ())), preferred_element_type=F32)


def col_sum(value):
    return jnp.sum(value, axis=0, keepdims=True)


def normalized(value):
    center = jnp.mean(value, axis=-1, keepdims=True)
    centered = value - center
    spread = jnp.mean(centered * centered, axis=-1, keepdims=True)
    scale = lax.rsqrt(spread + EPS)
    return centered * scale, scale


def norm_back(hat, scale, gain, upstream):
    scaled = upstream * gain
    first = jnp.mean(scaled, axis=-1, keepdims=True)
    second = jnp.mean(scaled * hat, axis=-1, keepdims=True)
    return (scaled - first - hat * second) * scale


def params(**more):
    return pltpu.CompilerParams(vmem_limit_bytes=VMEM_LIMIT, **more)


def split_rest(ref):
    _, width, columns = ref.shape
    cu, co, cd = 4 * columns // 9, columns // 9, 2 * columns // 9
    up = jnp.concatenate([ref[b, :, :cu] for b in range(6)], axis=1)
    out = jnp.concatenate([ref[b, :, cu : cu + co] for b in range(6)], axis=1)
    halves = []
    for h in range(2):
        parts = []
        for n in range(2):
            at = cu + co + n * cd
            part = jnp.concatenate([ref[3 * h + k, :, at : at + cd] for k in range(3)], axis=1)
            parts.append(part.reshape(CHIPS, 1, width // CHIPS, width))
        halves.append(jnp.concatenate(parts, axis=1).reshape(2 * width, width))
    return out, up, jnp.concatenate(halves, axis=0)


def whole(shape):
    return pl.BlockSpec(shape, lambda *_: (0,) * len(shape))


def project_kernel(x_ref, w_ref, gain_ref, shift_ref, bias_ref, out_ref, normed_ref):
    hat, _ = normalized(x_ref[...].astype(F32))
    normed = (hat * gain_ref[...] + shift_ref[...]).astype(BF16)
    normed_ref[...] = normed
    out_ref[...] = (nn(normed, w_ref[...]) + bias_ref[...]).astype(BF16)


def project(x, weight, gain, shift, bias):
    rows, width = x.shape
    return pl.pallas_call(
        project_kernel,
        grid=(rows // BLOCK,),
        in_specs=[
            pl.BlockSpec((BLOCK, width), lambda i: (i, 0)),
            whole((width, 3 * width)),
            whole((1, width)),
            whole((1, width)),
            whole((1, 3 * width)),
        ],
        out_specs=[
            pl.BlockSpec((BLOCK, 3 * width), lambda i: (i, 0)),
            pl.BlockSpec((BLOCK, width), lambda i: (i, 0)),
        ],
        out_shape=[
            jax.ShapeDtypeStruct((rows, 3 * width), BF16),
            jax.ShapeDtypeStruct((rows, width), BF16),
        ],
        compiler_params=params(),
        name="project",
    )(x, weight, gain, shift, bias)


def allowed_mask(start, key_at, keys, queries):
    key = key_at + lax.broadcasted_iota(jnp.int32, (keys, queries), 0)
    return key >= start


def head_rows(pair_t, head):
    row = lax.broadcasted_iota(jnp.int32, pair_t.shape, 0)
    mine = (row < HEAD_DIM) if head == 0 else (row >= HEAD_DIM)
    return jnp.where(mine, pair_t, jnp.zeros_like(pair_t))


def head_cols(pair, head):
    col = lax.broadcasted_iota(jnp.int32, pair.shape, 1)
    mine = (col < HEAD_DIM) if head == 0 else (col >= HEAD_DIM)
    return jnp.where(mine, pair, jnp.zeros_like(pair))


def score_parts(key, query_t, start, block):
    before = block * BLOCK
    parts = []
    if block:
        index = lax.broadcasted_iota(jnp.int32, (before, BLOCK), 0)
        parts.append((slice(0, before), jnp.where(index >= start, nn(key[:before], query_t), -1e30)))
    index = lax.broadcasted_iota(jnp.int32, (BLOCK, BLOCK), 0)
    last = lax.broadcasted_iota(jnp.int32, (BLOCK, BLOCK), 1)
    ok = (index >= start - before) & (index <= last)
    own = slice(before, before + BLOCK)
    parts.append((own, jnp.where(ok, nn(key[own], query_t), -1e30)))
    return parts


def attend_pair(query, key, value, start_ref, out_ref, lse_ref):
    query_t = (query.astype(F32) * HEAD_DIM**-0.5).T.astype(BF16)
    value_t = value.astype(F32).T.astype(BF16)
    for block in range(query.shape[0] // BLOCK):
        at = slice(block * BLOCK, (block + 1) * BLOCK)
        start = start_ref[:, at]
        outs = []
        for head in range(2):
            lanes = slice(head * HEAD_DIM, (head + 1) * HEAD_DIM)
            parts = score_parts(key, head_rows(query_t[:, at], head), start, block)
            peak = functools.reduce(jnp.maximum, [jnp.max(scores, axis=0, keepdims=True) for _, scores in parts])
            total = jnp.zeros((1, BLOCK), F32)
            out = jnp.zeros((HEAD_DIM, BLOCK), F32)
            for keys, scores in parts:
                raised = jnp.exp(scores - peak)
                total = total + col_sum(raised)
                out = out + nn(value_t[lanes, keys], raised.astype(BF16))
            outs.append(out * (1.0 / total))
            lse_ref[head : head + 1, at] = peak + jnp.log(total)
        out_ref[at, :] = jnp.concatenate(outs, axis=0).T


def attend_kernel(q_ref, k_ref, v_ref, start_ref, out_ref, lse_ref):
    attend_pair(q_ref[...], k_ref[...], v_ref[...], start_ref, out_ref, lse_ref.at[0])


def attend(projected, start):
    rows, columns = projected.shape
    width = columns // 3
    pairs = width // PAIR
    return pl.pallas_call(
        attend_kernel,
        grid=(pairs,),
        in_specs=[
            pl.BlockSpec((rows, PAIR), lambda p: (0, p)),
            pl.BlockSpec((rows, PAIR), lambda p: (0, pairs + p)),
            pl.BlockSpec((rows, PAIR), lambda p: (0, 2 * pairs + p)),
            whole((1, rows)),
        ],
        out_specs=[
            pl.BlockSpec((rows, PAIR), lambda p: (0, p)),
            pl.BlockSpec((1, 2, rows), lambda p: (p, 0, 0)),
        ],
        out_shape=[
            jax.ShapeDtypeStruct((rows, width), F32),
            jax.ShapeDtypeStruct((pairs, 2, rows), F32),
        ],
        compiler_params=params(),
        name="attend",
    )(projected, projected, projected, start)


def attend_back_pair(query, key, value, grad, context, lse_ref, start_ref, dq_ref, dk_ref, dv_ref, dk_acc, dv_acc):
    scale = HEAD_DIM**-0.5
    scaled = query.astype(F32) * scale
    query = scaled.astype(BF16)
    query_t = scaled.T.astype(BF16)
    key_t = key.astype(F32).T.astype(BF16)
    grad_f = grad.astype(F32)
    grad_t = grad_f.T.astype(BF16)
    weighted_t = (grad_f * context).T
    dk_acc[...] = jnp.zeros_like(dk_acc)
    dv_acc[...] = jnp.zeros_like(dv_acc)
    for block in range(query.shape[0] // BLOCK):
        at = slice(block * BLOCK, (block + 1) * BLOCK)
        start = start_ref[:, at]
        outs = []
        for head in range(2):
            lanes = slice(head * HEAD_DIM, (head + 1) * HEAD_DIM)
            inner = col_sum(weighted_t[lanes, at])
            log_total = lse_ref[head : head + 1, at]
            grad_head = head_rows(grad_t[:, at], head)
            out = jnp.zeros((HEAD_DIM, BLOCK), F32)
            for keys, scores in score_parts(key, head_rows(query_t[:, at], head), start, block):
                soft = jnp.exp(scores - log_total)
                grad_scores = (soft * (nn(value[keys], grad_head) - inner)).astype(BF16)
                dv_acc[keys, :] += nn(soft.astype(BF16), head_cols(grad[at], head))
                dk_acc[keys, :] += nn(grad_scores, head_cols(query[at], head))
                out = out + nn(key_t[lanes, keys], grad_scores)
            outs.append(out)
        dq_ref[at, :] = (jnp.concatenate(outs, axis=0) * scale).T.astype(BF16)
    dk_ref[...] = dk_acc[...].astype(BF16)
    dv_ref[...] = dv_acc[...].astype(BF16)


def attend_back_kernel(q_ref, k_ref, v_ref, g_ref, o_ref, lse_ref, start_ref, dq_ref, dk_ref, dv_ref, dk_acc, dv_acc):
    attend_back_pair(
        q_ref[...], k_ref[...], v_ref[...], g_ref[...], o_ref[...], lse_ref.at[0], start_ref,
        dq_ref, dk_ref, dv_ref, dk_acc, dv_acc,
    )


def attend_back(projected, grad_context, context, lse, start):
    rows, columns = projected.shape
    width = columns // 3
    pairs = width // PAIR
    pair = pl.BlockSpec((rows, PAIR), lambda p: (0, p))
    return pl.pallas_call(
        attend_back_kernel,
        grid=(pairs,),
        in_specs=[
            pair,
            pl.BlockSpec((rows, PAIR), lambda p: (0, pairs + p)),
            pl.BlockSpec((rows, PAIR), lambda p: (0, 2 * pairs + p)),
            pair,
            pair,
            pl.BlockSpec((1, 2, rows), lambda p: (p, 0, 0)),
            whole((1, rows)),
        ],
        out_specs=[pair] * 3,
        out_shape=[jax.ShapeDtypeStruct((rows, width), BF16)] * 3,
        scratch_shapes=[pltpu.VMEM((rows, PAIR), F32), pltpu.VMEM((rows, PAIR), F32)],
        compiler_params=params(),
        name="attend_back",
    )(projected, projected, projected, grad_context, context, lse, start)


def gelu_parts(value):
    phi = 0.5 * (1.0 + lax.erf(value * (1.0 / math.sqrt(2.0))))
    bell = jnp.exp(-0.5 * value * value) * (1.0 / math.sqrt(2.0 * math.pi))
    return value * phi, phi + value * bell


def middle_kernel(
    x_ref, dy_ref, ctx_ref, alive_ref, rest_ref,
    sg_ref, ss_ref, ob_ref, fg_ref, fs_ref, ub_ref, mg_ref, ms_ref, db_ref,
    out_ref, ghid_ref, gctx_ref, mixed_ref, gbranch_ref, nffn_ref, gup_ref, mid_ref, gffn_ref,
    narrow_ref, wide_ref,
):
    step = pl.program_id(0)

    @pl.when(step == 0)
    def _():
        narrow_ref[...] = jnp.zeros_like(narrow_ref)
        wide_ref[...] = jnp.zeros_like(wide_ref)

    out_weight, up_weight, down_weight = split_rest(rest_ref)
    alive = alive_ref[...]
    ctx_hat, ctx_scale = normalized(ctx_ref[...])
    mixed = (ctx_hat * sg_ref[...] + ss_ref[...]).astype(BF16)
    mixed_ref[...] = mixed
    branch = nn(mixed, out_weight) + ob_ref[...]
    hidden = (x_ref[...].astype(F32) + alive * branch).astype(BF16).astype(F32)
    hid_hat, hid_scale = normalized(hidden)
    nffn = (hid_hat * fg_ref[...] + fs_ref[...]).astype(BF16)
    nffn_ref[...] = nffn
    upper = nn(nffn, up_weight) + ub_ref[...]
    active, slope = gelu_parts(upper)
    act_hat, act_scale = normalized(active)
    mid = (act_hat * mg_ref[...] + ms_ref[...]).astype(BF16)
    mid_ref[...] = mid
    result = (nn(mid, down_weight) + db_ref[...]).astype(BF16).astype(F32)
    out_ref[...] = hidden + alive * result

    upstream = dy_ref[...].astype(F32)
    gffn = (alive * upstream).astype(BF16)
    gffn_ref[...] = gffn
    gmid = nt(gffn, down_weight)
    gact = norm_back(act_hat, act_scale, mg_ref[...], gmid)
    gup = (gact * slope).astype(BF16)
    gup_ref[...] = gup
    wide_ref[0:1, :] += col_sum(gup.astype(F32))
    wide_ref[1:2, :] += col_sum(gmid * act_hat)
    wide_ref[2:3, :] += col_sum(gmid)
    gnffn = nt(gup, up_weight)
    ghid = (upstream + norm_back(hid_hat, hid_scale, fg_ref[...], gnffn)).astype(BF16)
    ghid_ref[...] = ghid
    gbranch = (alive * ghid.astype(F32)).astype(BF16)
    gbranch_ref[...] = gbranch
    gmixed = nt(gbranch, out_weight)
    gctx_ref[...] = norm_back(ctx_hat, ctx_scale, sg_ref[...], gmixed).astype(BF16)
    narrow_ref[0:1, :] += col_sum(gmixed * ctx_hat)
    narrow_ref[1:2, :] += col_sum(gmixed)
    narrow_ref[2:3, :] += col_sum(gbranch.astype(F32))
    narrow_ref[3:4, :] += col_sum(gnffn * hid_hat)
    narrow_ref[4:5, :] += col_sum(gnffn)
    narrow_ref[5:6, :] += col_sum(gffn.astype(F32))


def middle(x, dy, context, alive, rest, vectors):
    rows, width = x.shape
    hidden = 4 * width
    row = pl.BlockSpec((BLOCK, width), lambda i: (i, 0))
    row_wide = pl.BlockSpec((BLOCK, hidden), lambda i: (i, 0))
    once = dict(pipeline_mode=pl.Buffered(1))
    narrow = whole((1, width))
    wide = whole((1, hidden))
    def shape(columns, dtype):
        return jax.ShapeDtypeStruct((rows, columns), dtype)
    return pl.pallas_call(
        middle_kernel,
        grid=(rows // BLOCK,),
        in_specs=[
            row, row, row,
            pl.BlockSpec((BLOCK, 1), lambda i: (i, 0)),
            pl.BlockSpec(rest.shape, lambda i: (0, 0, 0), **once),
            narrow, narrow, narrow, narrow, narrow, wide, wide, wide, narrow,
        ],
        out_specs=[row, row, row, row, row, row, row_wide, row_wide, row, whole((8, width)), whole((8, hidden))],
        out_shape=[
            shape(width, F32), shape(width, BF16), shape(width, BF16), shape(width, BF16), shape(width, BF16),
            shape(width, BF16), shape(hidden, BF16), shape(hidden, BF16), shape(width, BF16),
            jax.ShapeDtypeStruct((8, width), F32), jax.ShapeDtypeStruct((8, hidden), F32),
        ],
        compiler_params=params(),
        name="middle",
    )(x, dy, context, alive, rest, *vectors)


def outer_kernel(left_ref, right_ref, out_ref):
    out_ref[...] = tn(left_ref[...], right_ref[...]).astype(out_ref.dtype)


def outer(left, right, tile, dtype, name):
    rows, across = left.shape
    columns = right.shape[1]
    return pl.pallas_call(
        outer_kernel,
        grid=(across // tile,),
        in_specs=[pl.BlockSpec((rows, tile), lambda i: (0, i)), whole((rows, columns))],
        out_specs=pl.BlockSpec((tile, columns), lambda i: (i, 0)),
        out_shape=jax.ShapeDtypeStruct((across, columns), dtype),
        compiler_params=params(),
        name=name,
    )(left, right)


def project_back_kernel(dq_ref, dk_ref, dv_ref, w_ref, x_ref, ghid_ref, gain_ref, out_ref, narrow_ref):
    step = pl.program_id(0)
    width = x_ref.shape[1]

    @pl.when(step == 0)
    def _():
        narrow_ref[...] = jnp.zeros_like(narrow_ref)

    dq, dk, dv = dq_ref[...], dk_ref[...], dv_ref[...]
    gnormed = nt(dq, w_ref[:, :width]) + nt(dk, w_ref[:, width : 2 * width]) + nt(dv, w_ref[:, 2 * width :])
    hat, scale = normalized(x_ref[...].astype(F32))
    out_ref[...] = ghid_ref[...].astype(F32) + norm_back(hat, scale, gain_ref[...], gnormed)
    narrow_ref[0:1, :] += col_sum(gnormed * hat)
    narrow_ref[1:2, :] += col_sum(gnormed)
    narrow_ref[2:3, :] += col_sum(dq.astype(F32))
    narrow_ref[3:4, :] += col_sum(dv.astype(F32))


def project_back(dq, dk, dv, weight, x, ghid, gain):
    rows, width = x.shape
    row = pl.BlockSpec((BLOCK, width), lambda i: (i, 0))
    return pl.pallas_call(
        project_back_kernel,
        grid=(rows // BLOCK,),
        in_specs=[row, row, row, whole(weight.shape), row, row, whole((1, width))],
        out_specs=[row, whole((8, width))],
        out_shape=[jax.ShapeDtypeStruct((rows, width), F32), jax.ShapeDtypeStruct((8, width), F32)],
        compiler_params=params(),
        name="project_back",
    )(dq, dk, dv, weight, x, ghid, gain)


def row_marks(lengths_row, count):
    slots = jnp.arange(lengths_row.shape[0], dtype=jnp.int32)
    ends = jnp.sum(jnp.where(slots[:, None] <= slots[None, :], lengths_row[:, None], 0), axis=0)
    index = jnp.arange(count, dtype=jnp.int32)
    before = jnp.where(ends[None, :] <= index[:, None], ends[None, :], 0)
    alive = index < jnp.max(ends)
    start = jnp.where(alive, jnp.max(before, axis=1), index)
    return alive.astype(F32)[:, None], start[None, :]


MESH = pl.DeviceIdType.MESH
BOX = (4, 2, 2)
CHIPS = 16
X_AT, Y_AT, D_AT, MOVES = 3, 7, 11, 15


class Place:
    def __init__(self):
        self.core = lax.axis_index("section")
        self.chip = lax.axis_index("dp")
        self.z, self.y, self.x = self.chip // 4, (self.chip // 2) % 2, self.chip % 2
        high, low = self.z // 2, self.z % 2
        self.zs = [self.z, self.z + 1 - 2 * low, self.z + 2 - 4 * high, 3 - self.z]

    def at(self, z, y, x):
        return (self.core, z * 4 + y * 2 + x)

    def sibling(self):
        return (1 - self.core, self.chip)

    def over_z(self, k):
        return self.at(self.zs[k], self.y, self.x)

    def over_y(self):
        return self.at(self.z, 1 - self.y, self.x)

    def over_x(self):
        return self.at(self.z, self.y, 1 - self.x)

    def across(self):
        return self.at(self.z, 1 - self.y, 1 - self.x)


def remote(source, target, sems, device):
    return pltpu.make_async_remote_copy(
        src_ref=source, dst_ref=target, send_sem=sems[0], recv_sem=sems[1], device_id=device, device_id_type=MESH
    )


def greet(me):
    barrier = pltpu.get_barrier_semaphore()
    others = [me.sibling(), me.over_x(), me.over_y(), me.across()] + [me.over_z(k) for k in (1, 2, 3)]
    for other in others:
        pl.semaphore_signal(barrier, inc=1, device_id=other, device_id_type=MESH)
    pl.semaphore_wait(barrier, len(others))


class Gather:
    def __init__(self, full, sems, pass_sems, direct=False):
        self.me = Place()
        self.direct = direct
        self.own = full.at[pl.ds(3 * self.me.core, 3)]
        self.other = full.at[pl.ds(3 * (1 - self.me.core), 3)]
        self.sems, self.pass_sems = sems, pass_sems

    def move(self, index, z, y, x, device):
        part = self.own.at[:, z, y, x]
        return remote(part, part, (self.sems.at[0, index], self.sems.at[1, index]), device)

    def to_z(self, k):
        me = self.me
        return self.move(k - 1, me.z, me.y, me.x, me.over_z(k))

    def to_x(self, k):
        me = self.me
        return self.move(X_AT + k, me.zs[k], me.y, me.x, me.over_x())

    def to_y(self, k):
        me = self.me
        return self.move(Y_AT + k, me.zs[k], me.y, me.x, me.over_y())

    def onward(self, k):
        me = self.me
        if self.direct:
            return self.move(D_AT + k, me.zs[k], me.y, me.x, me.across())
        if k < 2:
            return self.move(D_AT + k, me.zs[k], me.y, 1 - me.x, me.over_y())
        return self.move(D_AT + k, me.zs[k], 1 - me.y, me.x, me.over_x())

    def across_core(self, index, ref):
        me = self.me
        every = slice(None)
        place = [(every, me.y, 1 - me.x), (every, 1 - me.y, me.x), (every, 1 - me.y, 1 - me.x)]
        z, y, x = (me.zs[index + 1], me.y, me.x) if index < 3 else place[index - 3]
        part = ref.at[:, z, y, x]
        return remote(part, part, (self.pass_sems.at[0, index], self.pass_sems.at[1, index]), me.sibling())

    def launch(self):
        for k in (1, 2, 3):
            self.to_z(k).start()
        self.spread(0)

    def spread(self, k):
        self.to_x(k).start()
        self.to_y(k).start()
        if self.direct:
            self.onward(k).start()

    def from_z(self, k):
        self.to_z(k).wait_recv()
        self.spread(k)
        self.across_core(k - 1, self.own).start()

    def arrive(self, stage):
        if stage == 0:
            self.from_z(1)
            self.to_x(0).wait_recv()
            if not self.direct:
                self.onward(0).start()
        elif stage == 1:
            self.from_z(2)
            self.from_z(3)
            self.to_x(1).wait_recv()
            if not self.direct:
                self.onward(1).start()
        elif stage == 2:
            for k in (2, 3):
                self.to_y(k).wait_recv()
                if not self.direct:
                    self.onward(k).start()
            for k in (2, 3):
                self.to_x(k).wait_recv()
            for k in (0, 1):
                self.to_y(k).wait_recv()
            self.across_core(3, self.own).start()
            self.across_core(4, self.own).start()
        else:
            for k in range(4):
                self.onward(k).wait_recv()
            self.across_core(5, self.own).start()

    def passed(self):
        for index in range(6):
            self.across_core(index, self.other).wait_recv()

    def drain(self):
        for k in (1, 2, 3):
            self.to_z(k).wait_send()
        for k in range(4):
            for move in (self.to_x(k), self.to_y(k), self.onward(k)):
                move.wait_send()
        for index in range(6):
            self.across_core(index, self.own).wait_send()


def seed(parts, sems):
    me = Place()
    moves = []
    for index, (source, full, block, cols) in enumerate(parts):
        here = full.at[block, me.z, me.y, me.x, :, cols]
        local = pltpu.make_async_copy(source, here, sems.at[0, index])
        far = remote(source, here, (sems.at[1, index], sems.at[2, index]), me.sibling())
        moves.append((local, far))

    def begin():
        for local, far in moves:
            local.start()
            far.start()

    def sent():
        for local, far in moves:
            local.wait()
            far.wait_send()

    def got():
        for _, far in moves:
            far.wait_recv()

    return begin, sent, got


def lane_groups(value):
    groups = [value[:, at : at + 128] for at in range(0, value.shape[1], 128)]
    return functools.reduce(jnp.add, groups)


def as_row(ref):
    return ref[...].reshape(1, -1)


def lengths_of(lengths_ref, core):
    return [lengths_ref[core, slot] for slot in range(lengths_ref.shape[1])]


def alive_rows(lengths_ref, core, at, rows):
    index = at + lax.broadcasted_iota(jnp.int32, (rows, 1), 0)
    return (index < sum(lengths_of(lengths_ref, core))).astype(F32)


def start_row(lengths_ref, core, count):
    index = lax.broadcasted_iota(jnp.int32, (1, count), 1)
    start = jnp.zeros((1, count), jnp.int32)
    end = jnp.int32(0)
    for length in lengths_of(lengths_ref, core):
        end = end + length
        start = jnp.where(index >= end, end, start)
    return jnp.where(index < end, start, index)


def front_kernel(
    tokens_ref, upstream_ref, lengths_ref, half_ref, down_ref,
    pg_ref, ps_ref, qb_ref, vb_ref, sg_ref, ss_ref, ob_ref, fg_ref, fs_ref, ub_ref, mg_ref, ms_ref,
    projected_out, normed_out, context_out, lse_out, start_out, wq0_out, wq1_out, wuo_out, wd_ref,
    mixed_out, nffn_out, hidden_out, mid_out, hat_out, slope_out, scale_out, gdown_out,
    hidden, gffn, broad, hat, mid, normed, mixed, context, lse, start, wq0, wq1, wuo, mid_t, gdown, scales, active,
    seed_q0, seed_q1, seed_o, seed_u, seed_d, chain_q0, chain_q1, chain_u, chain_d, pass_q0, pass_q1, pass_u, pass_d,
    load_sems, save_sems, row_sems, grad_sems,
):
    me = Place()
    core = me.core
    rows, width = hidden.shape
    mine = half_ref.shape[0]
    pairs = width // PAIR
    co, cu, cd = width // 6, 2 * width // 3, width // 3
    cg = 3 * PAIR
    first = core == 0
    second = core == 1
    box = (slice(None),) * 3

    def group_parts(full, groups):
        return [
            (half_ref.at[:, n * width + (2 * g + c) * PAIR : n * width + (2 * g + c + 1) * PAIR],
             full, 3 * c + n, slice(at * PAIR, (at + 1) * PAIR))
            for at, g in enumerate(groups) for c in range(2) for n in range(3)
        ]

    q0_begin, q0_sent, q0_got = seed(group_parts(wq0, [0]), seed_q0)
    q1_begin, q1_sent, q1_got = seed(group_parts(wq1, [1, 2]), seed_q1)
    o_begin, o_sent, o_got = seed(
        [(half_ref.at[:, 3 * width + b * co : 3 * width + (b + 1) * co],
          wuo, b, slice(cu, cu + co)) for b in range(6)], seed_o)
    u_begin, u_sent, u_got = seed(
        [(half_ref.at[:, b * cu : (b + 1) * cu],
          wuo, b, slice(0, cu)) for b in range(6)], seed_u)

    def down_parts(which):
        return [
            (down_ref.at[n * mine : (n + 1) * mine, k * cd : (k + 1) * cd],
             wd_ref, 3 * which + k, slice(n * cd, (n + 1) * cd))
            for k in range(3) for n in range(2)
        ]

    d_begin, d_sent, _ = seed(down_parts(core), seed_d)
    _, _, d_got = seed(down_parts(1 - core), seed_d)

    gather_q0 = Gather(wq0, chain_q0, pass_q0, direct=True)
    gather_q1 = Gather(wq1, chain_q1, pass_q1)
    gather_u = Gather(wuo, chain_u, pass_u)
    gather_d = Gather(wd_ref, chain_d, pass_d)

    own_rows = pl.ds(pl.multiple_of(core * rows, rows), rows)
    loads = [
        pltpu.make_async_copy(tokens_ref.at[own_rows], hidden, load_sems.at[0]),
        pltpu.make_async_copy(upstream_ref.at[own_rows], gffn, load_sems.at[1]),
    ]
    loads[0].start()
    greet(me)
    pl.when(first)(q0_begin)
    pl.when(first)(q1_begin)
    pl.when(first)(o_begin)
    pl.when(second)(u_begin)
    d_begin()
    loads[1].start()
    pl.when(first)(q0_sent)
    pl.when(second)(q0_got)
    gather_q0.launch()

    loads[0].wait()
    value, _ = normalized(hidden[...].astype(F32))
    normed[...] = (value * as_row(pg_ref) + as_row(ps_ref)).astype(BF16)
    start[...] = start_row(lengths_ref, core, rows)
    saves = []

    def save(source, target):
        saves.append(pltpu.make_async_copy(source, target, save_sems.at[len(saves)]))
        saves[-1].start()

    save(normed, normed_out)
    save(start, start_out)
    @pl.when(first)
    def _():
        q1_sent()
        o_sent()
        u_got()

    @pl.when(second)
    def _():
        u_sent()
        q1_got()
        o_got()

    gather_q0.arrive(0)
    gather_q1.launch()
    gather_q0.arrive(1)
    gather_u.launch()
    gather_q0.arrive(2)
    gather_q1.arrive(0)
    gather_q0.arrive(3)
    d_sent()
    d_got()
    gather_q0.passed()

    query_bias, value_bias = as_row(qb_ref), as_row(vb_ref)

    def project_group(group, weights):
        biases = []
        for c in range(2):
            at = slice((2 * group + c) * PAIR, (2 * group + c + 1) * PAIR)
            biases += [query_bias[:, at], jnp.zeros((1, PAIR), F32), value_bias[:, at]]
        cols = slice(group * 2 * cg, (group + 1) * 2 * cg)
        weight = jnp.concatenate(weights, axis=1)
        broad[:, cols] = (nn(normed[...], weight) + jnp.concatenate(biases, axis=1)).astype(BF16)

    project_group(0, [wq0[b].reshape(width, PAIR) for b in range(6)])
    gather_q1.arrive(1)

    def one_pair(pair, carry):
        @pl.when(pair == 0)
        def _():
            gather_u.arrive(0)

        @pl.when(pair == 1)
        def _():
            gather_q1.arrive(2)

        @pl.when(pair == 2)
        def _():
            gather_q1.arrive(3)
            gather_q1.passed()
            gather_u.arrive(1)
            for group in range(1, 3):
                at = slice((group - 1) * PAIR, group * PAIR)
                project_group(group, [wq1[(b, *box, slice(None), at)].reshape(width, PAIR) for b in range(6)])
            pltpu.make_async_copy(broad.at[:, : 3 * width], projected_out, load_sems.at[0]).start()

        @pl.when(pair == 3)
        def _():
            gather_d.launch()

        @pl.when(pair == 4)
        def _():
            gather_u.arrive(2)

        @pl.when(pair == 5)
        def _():
            gather_d.arrive(0)

        at_q = pl.ds(pl.multiple_of(pair * cg, PAIR), PAIR)
        at_k = pl.ds(pl.multiple_of(pair * cg + PAIR, PAIR), PAIR)
        at_v = pl.ds(pl.multiple_of(pair * cg + 2 * PAIR, PAIR), PAIR)
        at_out = pl.ds(pl.multiple_of(pair * PAIR, PAIR), PAIR)
        attend_pair(broad[:, at_q], broad[:, at_k], broad[:, at_v], start, context.at[:, at_out], lse.at[pair])
        return carry

    lax.fori_loop(0, pairs, one_pair, 0)
    save(context, context_out)
    save(lse, lse_out)
    save(wq0, wq0_out)
    save(wq1, wq1_out)
    gather_u.arrive(3)
    gather_u.passed()
    save(wuo, wuo_out)
    loads[1].wait()
    pltpu.make_async_copy(broad.at[:, : 3 * width], projected_out, load_sems.at[0]).wait()
    saves[0].wait()

    def row_saves(step):
        at = pl.ds(pl.multiple_of(step * BLOCK, BLOCK), BLOCK)
        pieces = [(mixed, mixed_out), (normed, nffn_out), (hidden, hidden_out), (mid, mid_out), (hat, hat_out),
                  (broad, slope_out)]
        return [
            pltpu.make_async_copy(source.at[at], target.at[at], row_sems.at[index, step])
            for index, (source, target) in enumerate(pieces)
        ]

    def one_block(step, carry):
        at = pl.ds(pl.multiple_of(step * BLOCK, BLOCK), BLOCK)
        alive = alive_rows(lengths_ref, core, step * BLOCK, BLOCK)
        ctx_hat, _ = normalized(context[at, :])
        mix = (ctx_hat * as_row(sg_ref) + as_row(ss_ref)).astype(BF16)
        mixed[at, :] = mix
        out_weight = jnp.concatenate([wuo[(b, *box, slice(None), slice(cu, cu + co))].reshape(width, co) for b in range(6)], axis=1)
        branch = nn(mix, out_weight) + as_row(ob_ref)
        hid = (hidden[at, :].astype(F32) + alive * branch).astype(BF16)
        hidden[at, :] = hid
        hid_hat, _ = normalized(hid.astype(F32))
        nffn = (hid_hat * as_row(fg_ref) + as_row(fs_ref)).astype(BF16)
        normed[at, :] = nffn
        up_weight = jnp.concatenate([wuo[(b, *box, slice(None), slice(0, cu))].reshape(width, cu) for b in range(6)], axis=1)
        units = 4 * width
        chunks = [slice(c, c + width) for c in range(0, units, width)]
        up_bias, mid_gain, mid_shift = as_row(ub_ref), as_row(mg_ref), as_row(ms_ref)
        lanes = jnp.zeros((BLOCK, 128), F32)
        for cols in chunks:
            value, slope = gelu_parts(nn(nffn, up_weight[:, cols]) + up_bias[:, cols])
            broad[at, cols] = slope.astype(BF16)
            active[:, cols] = value
            lanes = lanes + lane_groups(value)
        center = jnp.sum(lanes, axis=-1, keepdims=True) * (1.0 / units)
        lanes = jnp.zeros((BLOCK, 128), F32)
        for cols in chunks:
            centered = active[:, cols] - center
            lanes = lanes + lane_groups(centered * centered)
        act_scale = lax.rsqrt(jnp.sum(lanes, axis=-1, keepdims=True) * (1.0 / units) + EPS)
        for cols in chunks:
            act_hat = (active[:, cols] - center) * act_scale
            hat[at, cols] = act_hat.astype(BF16)
            mid[at, cols] = (act_hat * mid_gain[:, cols] + mid_shift[:, cols]).astype(BF16)
        scales[at, :] = act_scale
        gffn[at, :] = (alive * gffn[at, :].astype(F32)).astype(BF16)
        for copy in row_saves(step):
            copy.start()

        @pl.when(step == 0)
        def _():
            gather_d.arrive(1)

        @pl.when(step == 2)
        def _():
            gather_d.arrive(2)

        return carry

    steps = rows // BLOCK
    lax.fori_loop(0, steps, one_block, 0)
    save(scales, scale_out)

    def grad_save(h, k):
        return pltpu.make_async_copy(gdown.at[k], gdown_out.at[3 * h + k], grad_sems.at[h, k])

    for h in range(2):
        mid_t[...] = mid[:, 2 * h * width : 2 * (h + 1) * width].T
        for k in range(3):
            grad = nn(mid_t[...], gffn[:, k * cd : (k + 1) * cd]).astype(BF16)
            grad = grad.reshape(CHIPS, 2, mine, cd)
            if h:
                grad_save(0, k).wait()
            for n in range(2):
                gdown[k, :, :, n * cd : (n + 1) * cd] = grad[:, n]
            grad_save(h, k).start()
    gather_d.arrive(3)
    for k in range(3):
        grad_save(1, k).wait()
    gather_d.passed()

    def finish(step, carry):
        for copy in row_saves(step):
            copy.wait()
        return carry

    lax.fori_loop(0, steps, finish, 0)
    for copy in saves[1:]:
        copy.wait()
    for gather in (gather_q0, gather_q1, gather_u, gather_d):
        gather.drain()


def front(tokens, upstream, lengths, half, down, vectors):
    width = tokens.shape[1]
    rows = tokens.shape[0] // 2
    mine = half.shape[0]
    box = BOX
    pairs = width // PAIR
    wide = 4 * width
    anywhere = pl.BlockSpec(memory_space=pl.ANY)
    vmem = pl.BlockSpec(memory_space=pltpu.VMEM)
    smem = pl.BlockSpec(memory_space=pltpu.SMEM)
    dma = pltpu.SemaphoreType.DMA
    sizes = dict(q0=PAIR, q1=2 * PAIR, u=5 * width // 6, d=2 * width // 3)
    shape = jax.ShapeDtypeStruct
    steps = rows // BLOCK
    return pl.pallas_call(
        front_kernel,
        in_specs=[anywhere, anywhere, smem, anywhere, anywhere] + [vmem] * len(vectors),
        out_specs=[anywhere] * 17,
        out_shape=[
            shape((rows, 3 * width), BF16), shape((rows, width), BF16), shape((rows, width), F32),
            shape((pairs, 2, rows), F32), shape((1, rows), jnp.int32),
            *[shape((6, *box, mine, columns), BF16) for columns in sizes.values()],
            shape((rows, width), BF16), shape((rows, width), BF16), shape((rows, width), BF16),
            shape((rows, wide), BF16), shape((rows, wide), BF16), shape((rows, wide), BF16), shape((rows, 1), F32),
            shape((6, CHIPS, mine, 2 * width // 3), BF16),
        ],
        scratch_shapes=[
            pltpu.VMEM((rows, width), BF16), pltpu.VMEM((rows, width), BF16), pltpu.VMEM((rows, wide), BF16),
            pltpu.VMEM((rows, wide), BF16), pltpu.VMEM((rows, wide), BF16), pltpu.VMEM((rows, width), BF16),
            pltpu.VMEM((rows, width), BF16), pltpu.VMEM((rows, width), F32), pltpu.VMEM((pairs, 2, rows), F32),
            pltpu.VMEM((1, rows), jnp.int32),
            *[pltpu.VMEM((6, *box, mine, sizes[name]), BF16) for name in ("q0", "q1", "u")],
            pltpu.VMEM((2 * width, rows), BF16), pltpu.VMEM((3, CHIPS, mine, 2 * width // 3), BF16),
            pltpu.VMEM((rows, 1), F32), pltpu.VMEM((BLOCK, wide), F32),
            dma((3, 6)), dma((3, 12)), dma((3, 6)), dma((3, 6)), dma((3, 6)),
            *[dma((2, MOVES))] * 4, *[dma((2, 6))] * 4,
            dma((2,)), dma((8,)), dma((6, steps)), dma((2, 3)),
        ],
        compiler_params=params(collective_id=1, has_side_effects=True),
        name="front",
    )(tokens, upstream, lengths, half, down, *vectors)


class Scatter:
    def __init__(self, total, landings, sems, final, direct=False):
        self.me = Place()
        self.direct = direct
        self.total, self.landings, self.sems, self.final = total, landings, sems, final

    def move(self, index, z, y, x, device):
        return remote(self.total.at[:, z, y, x], self.landings.at[index], (self.sems.at[0, index], self.sems.at[1, index]), device)

    def to_z(self, k):
        me = self.me
        return self.move(k - 1, me.zs[k], me.y, me.x, me.over_z(k))

    def to_x(self, k):
        me = self.me
        return self.move(X_AT + k, me.zs[k], me.y, 1 - me.x, me.over_x())

    def to_y(self, k):
        me = self.me
        return self.move(Y_AT + k, me.zs[k], 1 - me.y, me.x, me.over_y())

    def toward(self, k):
        me = self.me
        return self.move(D_AT + k, me.zs[k], 1 - me.y, 1 - me.x, me.across() if self.direct else me.over_y() if k < 2 else me.over_x())

    def add(self, z, y, x, landed):
        self.total[:, z, y, x] = functools.reduce(jnp.add, [part[...] for part in landed], self.total[:, z, y, x])

    def begin(self, other):
        me = self.me

        def both(z, y, x):
            self.add(z, y, x, [other.at[:, z, y, x]])

        if self.direct:
            for k in (2, 3, 1, 0):
                both(me.zs[k], 1 - me.y, 1 - me.x)
                self.toward(k).start()
                both(me.zs[k], me.y, 1 - me.x)
                self.to_x(k).start()
                both(me.zs[k], 1 - me.y, me.x)
                self.to_y(k).start()
                both(me.zs[k], me.y, me.x)
            return
        for k in range(4):
            both(me.zs[k], 1 - me.y, 1 - me.x)
            self.toward(k).start()
        for k in range(4):
            both(me.zs[k], me.y, 1 - me.x)
            both(me.zs[k], 1 - me.y, me.x)
            both(me.zs[k], me.y, me.x)

    def arrive(self, stage):
        me = self.me
        if self.direct and stage < 3:
            for k in ((2, 3), (1, 0), ())[stage]:
                moves = (self.toward(k), self.to_x(k), self.to_y(k))
                for move in moves:
                    move.wait_recv()
                self.add(me.zs[k], me.y, me.x, [self.landings.at[at + k] for at in (D_AT, X_AT, Y_AT)])
                if k:
                    self.to_z(k).start()
        elif stage == 0:
            for k in range(4):
                self.toward(k).wait_recv()
                if k < 2:
                    self.add(me.zs[k], me.y, 1 - me.x, [self.landings.at[D_AT + k]])
                else:
                    self.add(me.zs[k], 1 - me.y, me.x, [self.landings.at[D_AT + k]])
            for k in (2, 3):
                self.to_x(k).start()
                self.to_y(k).start()
        elif stage < 3:
            if stage == 1:
                for k in (1, 0):
                    self.to_x(k).start()
                    self.to_y(k).start()
            for k in (2, 3) if stage == 1 else (1, 0):
                self.to_x(k).wait_recv()
                self.to_y(k).wait_recv()
                self.add(me.zs[k], me.y, me.x, [self.landings.at[X_AT + k], self.landings.at[Y_AT + k]])
                if k:
                    self.to_z(k).start()
        else:
            value = self.total[:, me.z, me.y, me.x].astype(F32)
            for k in (1, 2, 3):
                self.to_z(k).wait_recv()
                value = value + self.landings[k - 1].astype(F32)
            self.final[...] = value

    def drain(self):
        for k in (1, 2, 3):
            self.to_z(k).wait_send()
        for k in range(4):
            for move in (self.to_x(k), self.to_y(k), self.toward(k)):
                move.wait_send()


def feed_body(
    hidden_steps, upstream_ref, context_ref, hidden_ref, mid_ref, hat_ref, slope_ref, scale_ref, lengths_ref, wuo_any, wd_any,
    sg_ref, fg_ref, mg_ref, db_ref, gdown_ref,
    ghid_ref, gctx_ref, gbranch_ref, gup_ref, narrow_ref, wide_ref, layer_ref, down_ref,
    wuo_ref, wd_ref, out_rows, scaled_grad, total, landed, landings, final, swap_sems, chain_sems, local_sems, out_sems,
):
    me = Place()
    core = me.core
    step = pl.program_id(0)
    steps = pl.num_programs(0)
    width = hidden_ref.shape[1]
    mine = width // CHIPS
    co, cu, cd = width // 6, 2 * width // 3, width // 3
    sibling = me.sibling()
    scatter = Scatter(total, landings, chain_sems, final)
    own = pltpu.make_async_copy(gdown_ref.at[pl.ds(3 * core, 3)], total, local_sems.at[0])
    far = remote(gdown_ref.at[pl.ds(3 * (1 - core), 3)], landed, (swap_sems.at[0], swap_sems.at[1]), sibling)

    def out_copies(at_step, which):
        at = pl.ds(pl.multiple_of(at_step * BLOCK, BLOCK), BLOCK)
        target = layer_ref.at[which, at]
        return (pltpu.make_async_copy(out_rows.at[at], target, out_sems.at[0, at_step]),
                remote(out_rows.at[at], target, (out_sems.at[1, at_step], out_sems.at[2, at_step]), sibling))

    got_wd = pltpu.make_async_copy(wd_any, wd_ref, local_sems.at[1])
    got_wuo = pltpu.make_async_copy(wuo_any, wuo_ref, local_sems.at[2])

    @pl.when(step == 0)
    def _():
        got_wd.start()
        got_wuo.start()
        greet(me)
        far.start()
        own.start()
        got_wd.wait()
        narrow_ref[...] = jnp.zeros_like(narrow_ref)
        wide_ref[...] = jnp.zeros_like(wide_ref)

    def hook(at_step, action):
        pl.when(step == at_step)(action)

    def begin():
        own.wait()
        far.wait_recv()
        scatter.begin(landed)

    halves = []
    for h in range(2):
        parts = []
        for n in range(2):
            part = jnp.concatenate([wd_ref[3 * h + k, :, n * cd : (n + 1) * cd] for k in range(3)], axis=1)
            parts.append(part.reshape(CHIPS, 1, mine, width))
        halves.append(jnp.concatenate(parts, axis=1).reshape(2 * width, width))
    down_weight = jnp.concatenate(halves, axis=0)

    hook(3, lambda: scatter.arrive(2))
    alive = alive_rows(lengths_ref, core, step * BLOCK, BLOCK)
    hidden = hidden_ref[...].astype(F32)
    upstream = upstream_ref[...].astype(F32)
    gffn = (alive * upstream).astype(BF16)
    mid_gain = as_row(mg_ref)
    units = 4 * width
    chunks = [slice(at, at + width) for at in range(0, units, width)]
    first_sum = jnp.zeros((BLOCK, 128), F32)
    second_sum = jnp.zeros((BLOCK, 128), F32)
    for cols in chunks:
        gmid = nt(gffn, down_weight[cols])
        weighted = gmid * hat_ref[:, cols].astype(F32)
        wide_ref[1:2, cols] += col_sum(weighted)
        wide_ref[2:3, cols] += col_sum(gmid)
        scaled = gmid * mid_gain[:, cols]
        scaled_grad[:, cols] = scaled
        first_sum = first_sum + lane_groups(scaled)
        second_sum = second_sum + lane_groups(weighted * mid_gain[:, cols])
    first_mean = jnp.sum(first_sum, axis=-1, keepdims=True) * (1.0 / units)
    second_mean = jnp.sum(second_sum, axis=-1, keepdims=True) * (1.0 / units)
    hook(0, begin)
    hook(0, got_wuo.wait)
    up_weight = jnp.concatenate([wuo_ref[b, :, :cu] for b in range(6)], axis=1)
    out_weight = jnp.concatenate([wuo_ref[b, :, cu:] for b in range(6)], axis=1)
    hook(1, lambda: scatter.arrive(0))
    hook(2, lambda: scatter.arrive(1))
    act_scale = scale_ref[...]
    gnffn = jnp.zeros((BLOCK, width), F32)
    result = jnp.zeros((BLOCK, width), F32)
    for cols in chunks:
        act_hat = hat_ref[:, cols].astype(F32)
        gact = (scaled_grad[:, cols] - first_mean - act_hat * second_mean) * act_scale
        gup = (gact * slope_ref[:, cols].astype(F32)).astype(BF16)
        gup_ref[:, cols] = gup
        wide_ref[0:1, cols] += col_sum(gup.astype(F32))
        gnffn = gnffn + nt(gup, up_weight[:, cols])
        result = result + nn(mid_ref[:, cols], down_weight[cols])
    result = (result + as_row(db_ref)).astype(BF16).astype(F32)
    out_rows[pl.ds(pl.multiple_of(step * BLOCK, BLOCK), BLOCK), :] = hidden + alive * result
    for copy in out_copies(step, core):
        copy.start()
    hid_hat, hid_scale = normalized(hidden)
    ghid = (upstream + norm_back(hid_hat, hid_scale, as_row(fg_ref), gnffn)).astype(BF16)
    ghid_ref[...] = ghid
    gbranch = (alive * ghid.astype(F32)).astype(BF16)
    gbranch_ref[...] = gbranch
    gmixed = nt(gbranch, out_weight)
    ctx_hat, ctx_scale = normalized(context_ref[...])
    gctx_ref[...] = norm_back(ctx_hat, ctx_scale, as_row(sg_ref), gmixed).astype(BF16)
    narrow_ref[0:1, :] += col_sum(gmixed * ctx_hat)
    narrow_ref[1:2, :] += col_sum(gmixed)
    narrow_ref[2:3, :] += col_sum(gbranch.astype(F32))
    narrow_ref[3:4, :] += col_sum(gnffn * hid_hat)
    narrow_ref[4:5, :] += col_sum(gnffn)
    narrow_ref[5:6, :] += col_sum(gffn.astype(F32))

    @pl.when(step == steps - 1)
    def _():
        scatter.arrive(3)
        for k in range(3):
            for n in range(2):
                down_ref[n * mine : (n + 1) * mine, k * cd : (k + 1) * cd] = final[k, :, n * cd : (n + 1) * cd]
        for index in range(hidden_steps):
            local, away = out_copies(index, core)
            local.wait()
            away.wait_send()
            out_copies(index, 1 - core)[1].wait_recv()
        far.wait_send()
        scatter.drain()


def feed(upstream, context, hidden, mid, hat, slope, scale, lengths, wuo, wd, vectors, gdown):
    rows, width = hidden.shape
    wide = 4 * width
    steps = rows // BLOCK
    box = BOX
    mine = width // CHIPS
    columns = 2 * width // 3
    row = pl.BlockSpec((BLOCK, width), lambda i: (i, 0))
    row_wide = pl.BlockSpec((BLOCK, wide), lambda i: (i, 0))
    once = dict(pipeline_mode=pl.Buffered(1))
    anywhere = pl.BlockSpec(memory_space=pl.ANY)
    vmem = pl.BlockSpec(memory_space=pltpu.VMEM)
    smem = pl.BlockSpec(memory_space=pltpu.SMEM)
    dma = pltpu.SemaphoreType.DMA
    shape = jax.ShapeDtypeStruct

    def held(*size, dtype=BF16):
        return pltpu.VMEM(size, dtype)

    return pl.pallas_call(
        functools.partial(feed_body, steps),
        grid=(steps,),
        in_specs=[
            pl.BlockSpec((BLOCK, width), lambda i: (lax.axis_index("section") * steps + i, 0)),
            row, row, row_wide, row_wide, row_wide, pl.BlockSpec((BLOCK, 1), lambda i: (i, 0)), smem,
            anywhere, anywhere, *[vmem] * 4, anywhere,
        ],
        out_specs=[row, row, row, row_wide, whole((8, width)), whole((8, wide)), anywhere, vmem],
        out_shape=[
            shape((rows, width), BF16), shape((rows, width), BF16), shape((rows, width), BF16), shape((rows, wide), BF16),
            shape((8, width), F32), shape((8, wide), F32), shape((2, rows, width), F32), shape((2 * mine, width), F32),
        ],
        scratch_shapes=[
            held(*wuo.shape), held(*wd.shape), held(rows, width, dtype=F32), held(BLOCK, wide, dtype=F32),
            held(3, *box, mine, columns), held(3, *box, mine, columns),
            held(MOVES, 3, mine, columns),
            held(3, mine, columns, dtype=F32),
            dma((2,)), dma((2, MOVES)), dma((3,)), dma((3, steps)),
        ],
        compiler_params=params(collective_id=3, has_side_effects=True),
        name="feed",
    )(upstream, context, hidden, mid, hat, slope, scale, lengths, wuo, wd, *vectors,
      gdown.reshape((6,) + box + (mine, columns)))


def finish_kernel(*refs):
    layer_ref, grad_ref, half_ref, down_ref, slim_ref, broad_ref = refs[:6]
    layer_out, grad_out, half_out, down_out = refs[6:10]
    small, (layer, grad, half, down, sems) = refs[10:23], refs[23:]
    pieces = []
    for source, held, target, parts in (
        (layer_ref, layer, layer_out, 8), (grad_ref, grad, grad_out, 4), (half_ref, half, half_out, 1), (down_ref, down, down_out, 1)
    ):
        rows = source.shape[0] // parts
        for part in range(parts):
            at = pl.ds(part * rows, rows)
            n = len(pieces)
            pieces.append((pltpu.make_async_copy(source.at[at], held.at[at], sems.at[0, n]),
                           pltpu.make_async_copy(held.at[at], target.at[at], sems.at[1, n])))
    for get, _ in pieces:
        get.start()
    for row, out in enumerate(small[:10]):
        out[...] = slim_ref[row, : out.shape[0]]
    for row, out in enumerate(small[10:]):
        out[...] = broad_ref[row, : out.shape[0]]
    for get, put in pieces:
        get.wait()
        put.start()
    for _, put in pieces:
        put.wait()


def finish(layer, grad, half, down, slim, broad, narrow_share, wide_share):
    anywhere = pl.BlockSpec(memory_space=pl.ANY)
    vmem = pl.BlockSpec(memory_space=pltpu.VMEM)
    shape = jax.ShapeDtypeStruct
    big = [layer, grad, half, down]
    sizes = [narrow_share] * 10 + [wide_share] * 3
    return pl.pallas_call(
        finish_kernel,
        in_specs=[anywhere] * 4 + [vmem] * 2,
        out_specs=[anywhere] * 4 + [vmem] * len(sizes),
        out_shape=[shape(array.shape, F32) for array in big] + [shape((size,), F32) for size in sizes],
        scratch_shapes=[pltpu.VMEM(array.shape, F32) for array in big] + [pltpu.SemaphoreType.DMA((2, 14))],
        compiler_params=params(),
        name="finish",
    )(layer, grad, half, down, slim, broad)


def back_kernel(
    projected_any, gctx_any, context_any, lse_ref, start_ref, normed_any, tokens_any, ghid_any, gain_ref, wq0_any, wq1_any,
    narrow_ref, wide_ref, nffn_any, mixed_any, gup_any, gbranch_any,
    grad_ref, half_ref, slim_ref, broad_ref,
    projected_ref, gctx_ref, context_ref, ghid_ref, wq0_ref, wq1_ref, spare, gup_far, gbranch, mixed_t, far_r,
    x_rows, dproj, dk_acc, dv_acc, normed_t, far_rows,
    total_r, first_r, landings_r, final_r, other_r,
    total_q, far_q, first_q, landings_q, final_q, other_q,
    small, small_in,
    load_sems, swap_sems, far_sems, chain_r, chain_q, small_sems,
):
    me = Place()
    core = me.core
    rows, width = x_rows.shape
    mine = half_ref.shape[0]
    pairs = width // PAIR
    co, cu, cq = width // 6, 2 * width // 3, width // 2
    cg = 3 * PAIR
    sibling = me.sibling()
    first = core == 0
    second = core == 1

    def swap(index, source, target):
        return remote(source, target, (swap_sems.at[0, index], swap_sems.at[1, index]), sibling)

    sum_r = Scatter(total_r, landings_r, chain_r, final_r)
    sum_q = [Scatter(total_q.at[g], landings_q.at[g], chain_q.at[g], final_q.at[g], direct=True) for g in range(3)]

    loads = []

    def load(source, target):
        loads.append(pltpu.make_async_copy(source, target, load_sems.at[len(loads)]))
        loads[-1].start()
        return loads[-1]

    half = 2 * width
    far_cols = pl.ds(pl.multiple_of((1 - core) * half, PAIR), half)
    own_cols = pl.ds(pl.multiple_of(core * half, PAIR), half)
    got_nffn = load(nffn_any, x_rows)
    got_mixed = load(mixed_any, spare)
    got_far = load(gup_any.at[:, far_cols], gup_far)
    got_branch = load(gbranch_any, gbranch)
    got_own = load(gup_any.at[:, own_cols], dproj.at[:, :half])
    later = [
        load(source, target)
        for source, target in ((projected_any, projected_ref), (gctx_any, gctx_ref), (context_any, context_ref))
    ]
    greet(me)
    got_nffn.wait()
    normed_t[...] = x_rows[...].T
    got_x = load(tokens_any.at[pl.ds(pl.multiple_of(core * rows, rows), rows)], x_rows)
    got_mixed.wait()
    mixed_t[...] = spare[...].T
    got_normed = load(normed_any, spare)
    last = [
        load(source, target)
        for source, target in ((ghid_any, ghid_ref), (wq0_any, wq0_ref), (wq1_any, wq1_ref))
    ]

    def up_out(source, k, block, target):
        up = nn(normed_t[...], source[:, k * cu : (k + 1) * cu]).astype(BF16)
        at = pl.ds(pl.multiple_of(block * co, PAIR), co)
        out = nn(mixed_t[...], gbranch[:, at]).astype(BF16)
        target[k, :, :, :, :, :cu] = up.reshape(BOX + (mine, cu))
        target[k, :, :, :, :, cu:] = out.reshape(BOX + (mine, co))

    def swap_far(k):
        return remote(far_r.at[k], first_r.at[k], (far_sems.at[0, k], far_sems.at[1, k]), sibling)

    got_far.wait()
    got_branch.wait()
    for k in range(3):
        up_out(gup_far, k, 3 * (1 - core) + k, far_r)
        swap_far(k).start()
    got_own.wait()
    for k in range(3):
        up_out(dproj, k, 3 * core + k, total_r)
    for k in range(3):
        swap_far(k).wait_recv()
    sum_r.begin(first_r)
    got_normed.wait()
    normed_t[...] = spare[...].T
    for copy in later:
        copy.wait()

    def swap_q(group):
        return swap(3 + group, far_q.at[group], first_q.at[group])

    def make(group):
        for which, target in ((1 - core, far_q), (core, total_q)):
            at = pl.ds(pl.multiple_of(group * 2 * cg + which * cg, PAIR), cg)
            grad = nn(normed_t[...], dproj[:, at]).astype(BF16)
            for n in range(3):
                target[group, n] = grad[:, n * PAIR : (n + 1) * PAIR].reshape(BOX + (mine, PAIR))
            if target is far_q:
                swap_q(group).start()

    def begin(group):
        swap_q(group).wait_recv()
        sum_q[group].begin(first_q.at[group])

    def one_pair(pair, carry):
        @pl.when(pair == 2)
        def _():
            make(0)
            sum_r.arrive(0)

        @pl.when(pair == 3)
        def _():
            begin(0)

        @pl.when(pair == 4)
        def _():
            sum_r.arrive(1)
            make(1)
            sum_q[0].arrive(0)

        @pl.when(pair == 5)
        def _():
            begin(1)
            sum_q[0].arrive(1)

        at_q = pl.ds(pl.multiple_of(pair * cg, PAIR), PAIR)
        at_k = pl.ds(pl.multiple_of(pair * cg + PAIR, PAIR), PAIR)
        at_v = pl.ds(pl.multiple_of(pair * cg + 2 * PAIR, PAIR), PAIR)
        at_c = pl.ds(pl.multiple_of(pair * PAIR, PAIR), PAIR)
        attend_back_pair(
            projected_ref[:, at_q], projected_ref[:, at_k], projected_ref[:, at_v], gctx_ref[:, at_c],
            context_ref[:, at_c], lse_ref.at[pair], start_ref,
            dproj.at[:, at_q], dproj.at[:, at_k], dproj.at[:, at_v], dk_acc, dv_acc,
        )
        return carry

    lax.fori_loop(0, pairs, one_pair, 0)
    make(2)
    sum_q[1].arrive(0)
    sum_r.arrive(2)
    begin(2)
    got_x.wait()
    for copy in last:
        copy.wait()
    small[0] = jnp.zeros_like(small[0])

    def one_block(step, carry):
        at = pl.ds(pl.multiple_of(step * BLOCK, BLOCK), BLOCK)
        gnormed = jnp.zeros((BLOCK, width), F32)
        for group in range(3):
            if group == 0:
                blocks = [wq0_ref[b].reshape(width, PAIR) for b in range(6)]
            else:
                cols = slice((group - 1) * PAIR, group * PAIR)
                blocks = [wq1_ref[(b,) + (slice(None),) * 4 + (cols,)].reshape(width, PAIR) for b in range(6)]
            weight = jnp.concatenate(blocks, axis=1)
            gnormed = gnormed + nt(dproj[at, group * 2 * cg : (group + 1) * 2 * cg], weight)
        hat, scale = normalized(x_rows[at, :].astype(F32))
        grad_x = ghid_ref[at, :].astype(F32) + norm_back(hat, scale, as_row(gain_ref), gnormed)

        @pl.when(first)
        def _():
            grad_ref[0, at, :] = grad_x[:, :cq]
            far_rows[at, :] = grad_x[:, cq:]

        @pl.when(second)
        def _():
            grad_ref[1, at, :] = grad_x[:, cq:]
            far_rows[at, :] = grad_x[:, :cq]

        small[0, 0:1, :] += col_sum(gnormed * hat)
        small[0, 1:2, :] += col_sum(gnormed)
        for row, part in ((2, 0), (3, 2)):
            grads = [dproj[at, p * cg + part * PAIR : p * cg + (part + 1) * PAIR].astype(F32) for p in range(pairs)]
            small[0, row : row + 1, :] += col_sum(jnp.concatenate(grads, axis=1))

        @pl.when(step == 1)
        def _():
            sum_q[1].arrive(1)
            sum_q[0].arrive(3)

        @pl.when(step == 3)
        def _():
            sum_q[2].arrive(0)

        return carry

    lax.fori_loop(0, rows // BLOCK, one_block, 0)
    swap_x = swap(1, far_rows, grad_ref.at[core])
    small[0, 4:10, :] = narrow_ref[0:6, :]
    for n in range(3):
        for part in range(4):
            row = 10 + 4 * n + part
            small[0, row : row + 1, :] = wide_ref[n : n + 1, part * width : (part + 1) * width]

    partners = [[sibling], [me.over_x(), me.over_y(), me.across()], [me.over_z(k) for k in (1, 2, 3)]]

    def small_moves(stage):
        at = (0, 1, 4)[stage]
        return [
            remote(small.at[stage], small_in.at[at + n], (small_sems.at[0, at + n], small_sems.at[1, at + n]), device)
            for n, device in enumerate(partners[stage])
        ]

    def small_start(stage):
        for move in small_moves(stage):
            move.start()

    def small_arrive(stage):
        at = (0, 1, 4)[stage]
        value = small[stage]
        for n, move in enumerate(small_moves(stage)):
            move.wait_recv()
            value = value + small_in[at + n]
        small[stage + 1] = value
        if stage < 2:
            small_start(stage + 1)

    small_start(0)
    swap_x.start()
    sum_q[2].arrive(1)
    small_arrive(0)
    sum_r.arrive(3)
    swap_r = swap(2, final_r, other_r)
    swap_r.start()
    sum_q[1].arrive(3)
    small_arrive(1)
    sum_q[2].arrive(3)
    swap_f = swap(6, final_q, other_q)
    swap_f.start()
    small_arrive(2)
    swap_r.wait_recv()

    sums = small[3]
    share = core * CHIPS + me.chip

    def pick(values, each):
        size = values.shape[1]
        return pltpu.roll(values, (size - share * each) % size, 1)[:, :128]

    shares = 2 * CHIPS
    slim_ref[...] = pick(sums[0:16], width // shares)
    rows_of = [jnp.concatenate([sums[10 + 4 * n + part : 11 + 4 * n + part] for part in range(4)], axis=1) for n in range(3)]
    broad_ref[...] = pick(jnp.concatenate(rows_of + [jnp.zeros((5, 4 * width), F32)], axis=0), 4 * width // shares)

    swap_f.wait_recv()

    @pl.when(first)
    def _():
        for k in range(3):
            for g in range(3):
                for c, source in ((0, final_q), (1, other_q)):
                    at = k * width + (2 * g + c) * PAIR
                    half_ref[:, at : at + PAIR] = source[g, k]
            half_ref[:, 3 * width + k * co : 3 * width + (k + 1) * co] = final_r[k, :, cu:]
            half_ref[:, 3 * width + (3 + k) * co : 3 * width + (4 + k) * co] = other_r[k, :, cu:]

    @pl.when(second)
    def _():
        for k in range(3):
            half_ref[:, k * cu : (k + 1) * cu] = other_r[k, :, :cu]
            half_ref[:, (3 + k) * cu : (4 + k) * cu] = final_r[k, :, :cu]

    swap(1, far_rows, grad_ref.at[1 - core]).wait_recv()
    for done in (swap_far(0), swap_far(1), swap_far(2), swap_x, swap_r, swap_f, swap_q(0), swap_q(1), swap_q(2)):
        done.wait_send()
    for stage in range(3):
        for move in small_moves(stage):
            move.wait_send()
    for each in [sum_r] + sum_q:
        each.drain()


def back(projected, gctx, context, lse, start, normed, tokens, ghid, gain, wq0, wq1, narrow, wide, nffn, mixed, gup, gbranch):
    rows, width = normed.shape
    box = BOX
    mine = width // CHIPS
    cq, cr = width // 2, 5 * width // 6
    anywhere = pl.BlockSpec(memory_space=pl.ANY)
    vmem = pl.BlockSpec(memory_space=pltpu.VMEM)
    dma = pltpu.SemaphoreType.DMA

    def held(*shape, dtype=BF16):
        return pltpu.VMEM(shape, dtype)

    return pl.pallas_call(
        back_kernel,
        in_specs=[anywhere] * 3 + [vmem] * 2 + [anywhere] * 3 + [vmem] + [anywhere] * 2 + [vmem] * 2 + [anywhere] * 4,
        out_specs=[vmem] * 4,
        out_shape=[
            jax.ShapeDtypeStruct((2, rows, cq), F32),
            jax.ShapeDtypeStruct((mine, 4 * width), F32),
            jax.ShapeDtypeStruct((16, 128), F32),
            jax.ShapeDtypeStruct((8, 128), F32),
        ],
        scratch_shapes=[
            held(rows, 3 * width), held(rows, width), held(rows, width, dtype=F32), held(rows, width),
            held(*wq0.shape), held(*wq1.shape), held(rows, width), held(rows, 2 * width), held(rows, width),
            held(width, rows), held(3, *box, mine, cr),
            held(rows, width), held(rows, 3 * width), held(rows, PAIR, dtype=F32), held(rows, PAIR, dtype=F32),
            held(width, rows), held(rows, cq, dtype=F32),
            held(3, *box, mine, cr), held(3, *box, mine, cr), held(MOVES, 3, mine, cr),
            held(3, mine, cr, dtype=F32), held(3, mine, cr, dtype=F32),
            held(3, 3, *box, mine, PAIR), held(3, 3, *box, mine, PAIR), held(3, 3, *box, mine, PAIR),
            held(3, MOVES, 3, mine, PAIR),
            held(3, 3, mine, PAIR, dtype=F32), held(3, 3, mine, PAIR, dtype=F32),
            held(4, 24, width, dtype=F32), held(7, 24, width, dtype=F32),
            dma((13,)), dma((2, 7)), dma((2, 3)), dma((2, MOVES)), dma((3, 2, MOVES)), dma((2, 7)),
        ],
        compiler_params=params(collective_id=2, has_side_effects=True),
        name="back",
    )(projected, gctx, context, lse, start, normed, tokens, ghid, gain, wq0, wq1, narrow, wide, nffn, mixed, gup, gbranch)


def fused_batch(tokens, out_grad, lengths, half, down, vectors):
    (pre_gain, pre_shift, query_bias, value_bias, sub_gain, sub_shift, out_bias,
     ffn_gain, ffn_shift, up_bias, mid_gain, mid_shift, down_bias) = vectors
    width = tokens.shape[1]
    (projected, normed, context, lse, start, wq0, wq1, wuo, wd, mixed, nffn, hidden, mid, hat, slope, scale, gdown) = front(
        tokens, out_grad, lengths, half, down,
        (pre_gain, pre_shift, query_bias, value_bias, sub_gain, sub_shift, out_bias, ffn_gain, ffn_shift, up_bias,
         mid_gain, mid_shift),
    )
    ghid, gctx, gbranch, gup, narrow, wide, layer, down_grad = feed(
        out_grad, context, hidden, mid, hat, slope, scale, lengths, wuo.reshape(6, width, -1), wd.reshape(6, width, -1),
        (sub_gain, ffn_gain, mid_gain, down_bias), gdown,
    )
    grad_x, half_grad, slim, broad = back(
        projected, gctx, context, lse, start, normed, tokens, ghid, pre_gain, wq0, wq1, narrow, wide,
        nffn, mixed, gup, gbranch,
    )
    shares = 2 * CHIPS
    layer, grad_x, half_grad, down_grad, *small = finish(
        layer.reshape(-1, width), grad_x.reshape(-1, width // 2), half_grad, down_grad, slim, broad,
        width // shares, 4 * width // shares,
    )
    return layer, grad_x, half_grad[None], down_grad, *small[:9], *small[10:], small[9]


def unpacked(vectors):
    return [vector[None, :] for vector in vectors]


def marks_and_bias(x, lengths_row, query_bias, value_bias):
    alive, start = row_marks(lengths_row, x.shape[0])
    bias = jnp.concatenate([query_bias, jnp.zeros_like(query_bias), value_bias], axis=1)
    return alive, start, bias


def one_batch(x, dy, lengths_row, qkv, rest, vectors):
    (pre_gain, pre_shift, query_bias, value_bias, sub_gain, sub_shift, out_bias,
     ffn_gain, ffn_shift, up_bias, mid_gain, mid_shift, down_bias) = unpacked(vectors)
    alive, start, bias = marks_and_bias(x, lengths_row, query_bias, value_bias)
    projected, normed = project(x, qkv, pre_gain, pre_shift, bias)
    context, lse = attend(projected, start)
    out, ghid, gctx, mixed, gbranch, nffn, gup, mid, gffn, narrow, wide = middle(
        x, dy, context, alive, rest,
        (sub_gain, sub_shift, out_bias, ffn_gain, ffn_shift, up_bias, mid_gain, mid_shift, down_bias),
    )
    grad_up = outer(nffn, gup, 256, F32, "outer_up")
    grad_down = outer(mid, gffn, 512, F32, "outer_down")
    dq, dk, dv = attend_back(projected, gctx, context, lse, start)
    grad_out = outer(mixed, gbranch, 256, F32, "outer_out")
    grad_x, pre = project_back(dq, dk, dv, qkv, x, ghid, pre_gain)
    grads = [outer(normed, d, 256, F32, "outer_qkv") for d in (dq, dk, dv)]
    grad_attention = jnp.concatenate(grads + [grad_out], axis=1)
    small = (pre[0], pre[1], pre[2], pre[3], narrow[0], narrow[1], narrow[2], narrow[3], narrow[4],
             wide[0], wide[1], wide[2], narrow[5])
    return (out, grad_x), (grad_attention, grad_up, grad_down, small)


def shards(tokens, out_grad, seq_lengths, half_weights, down_weight, *all_vectors):
    section = lax.axis_index("section")
    sections = lax.axis_size("section")
    both = ("section", "dp")
    width = tokens.shape[1]
    batches = seq_lengths.shape[0]
    count = tokens.shape[0] // batches
    own_batches = batches // sections
    own_rows = own_batches * count
    hidden_units = half_weights.shape[2]
    shares = sections * lax.axis_size("dp")

    if (
        sections == 2
        and shares == sections * CHIPS
        and own_batches == 1
        and half_weights.shape[1] % 16 == 0
        and down_weight.shape[0] == 2 * half_weights.shape[1]
        and hidden_units == 4 * width
    ):
        return fused_batch(tokens, out_grad, seq_lengths, half_weights[0], down_weight, all_vectors)

    def own(array, rows):
        return lax.dynamic_slice_in_dim(array, section * rows, rows, axis=0)

    x_rows = own(tokens, own_rows)
    dy_rows = own(out_grad, own_rows)
    lengths = own(seq_lengths, own_batches)
    blocks = lax.all_gather(half_weights[0], both, axis=0, tiled=True)
    blocks = blocks.reshape(sections, width, hidden_units)
    down_full = lax.all_gather(down_weight, both, axis=0, tiled=True)
    qkv = blocks[0][:, : 3 * width]

    def in_blocks(array):
        return array.reshape(array.shape[0], 6, -1).transpose(1, 0, 2)

    down_blocks = down_full.reshape(2, CHIPS, 2, width // CHIPS, 3, width // 3).transpose(0, 4, 1, 3, 2, 5)
    down_blocks = down_blocks.reshape(6, width, 2 * width // 3)
    rest = jnp.concatenate([in_blocks(blocks[1]), in_blocks(blocks[0][:, 3 * width :]), down_blocks], axis=2)
    rows, sums = [], None
    for index in range(own_batches):
        at = slice(index * count, (index + 1) * count)
        row, more = one_batch(x_rows[at], dy_rows[at], lengths[index], qkv, rest, all_vectors)
        rows.append(row)
        sums = more if sums is None else jax.tree.map(jnp.add, sums, more)
    out_block = jnp.concatenate([row[0] for row in rows], axis=0)
    grad_rows = jnp.concatenate([row[1] for row in rows], axis=0)
    grad_attention, grad_up, grad_down, vectors = sums

    block_part = lax.psum_scatter(
        jnp.concatenate([grad_attention, grad_up], axis=0), both, scatter_dimension=0, tiled=True
    )
    down_part = lax.psum_scatter(grad_down, both, scatter_dimension=0, tiled=True)
    packed = jnp.concatenate([vector.reshape(shares, -1) for vector in vectors], axis=1)
    packed = lax.psum_scatter(packed, both, scatter_dimension=0, tiled=True).reshape(-1)
    parts, start = [], 0
    for vector in vectors:
        size = vector.shape[0] // shares
        parts.append(packed[start : start + size])
        start += size

    layer_out = lax.all_gather(out_block, "section", axis=0, tiled=True)
    tokens_grad = lax.all_to_all(grad_rows, "section", split_axis=1, concat_axis=0, tiled=True)
    return (layer_out, tokens_grad, block_part[None], down_part, *parts)


def solution(mesh):
    replicated = P()
    return jax.shard_map(
        shards,
        mesh=mesh,
        in_specs=(P("dp", None), P("dp", None), P("dp", None), P("section", "dp", None), P(("section", "dp"), None))
        + (replicated,) * 13,
        out_specs=(P("dp", None), P("dp", "section"), P("section", "dp", None), P(("section", "dp"), None))
        + (P(("section", "dp")),) * 13,
        check_vma=False,
    )
```

```python
import functools
import math

import jax
import jax.numpy as jnp
from jax import lax
from jax.experimental import pallas as pl
from jax.experimental.pallas import tpu as pltpu
from jax.sharding import PartitionSpec as P

HEAD_DIM = 64
PAIR = 2 * HEAD_DIM
EPS = 1e-05
BLOCK = 256
F32 = jnp.float32
BF16 = jnp.bfloat16
VMEM_LIMIT = 60 * 1024 * 1024


def nn(left, right):
    return lax.dot_general(left, right, (((1,), (0,)), ((), ())), preferred_element_type=F32)


def nt(left, right):
    return lax.dot_general(left, right, (((1,), (1,)), ((), ())), preferred_element_type=F32)


def tn(left, right):
    return lax.dot_general(left, right, (((0,), (0,)), ((), ())), preferred_element_type=F32)


def col_sum(value):
    return jnp.sum(value, axis=0, keepdims=True)


def normalized(value):
    center = jnp.mean(value, axis=-1, keepdims=True)
    centered = value - center
    spread = jnp.mean(centered * centered, axis=-1, keepdims=True)
    scale = lax.rsqrt(spread + EPS)
    return centered * scale, scale


def norm_back(hat, scale, gain, upstream):
    scaled = upstream * gain
    first = jnp.mean(scaled, axis=-1, keepdims=True)
    second = jnp.mean(scaled * hat, axis=-1, keepdims=True)
    return (scaled - first - hat * second) * scale


def params(**more):
    return pltpu.CompilerParams(vmem_limit_bytes=VMEM_LIMIT, **more)


def split_rest(ref):
    _, width, columns = ref.shape
    cu, co, cd = 4 * columns // 9, columns // 9, 2 * columns // 9
    up = jnp.concatenate([ref[b, :, :cu] for b in range(6)], axis=1)
    out = jnp.concatenate([ref[b, :, cu : cu + co] for b in range(6)], axis=1)
    halves = []
    for h in range(2):
        parts = []
        for n in range(2):
            at = cu + co + n * cd
            part = jnp.concatenate([ref[3 * h + k, :, at : at + cd] for k in range(3)], axis=1)
            parts.append(part.reshape(CHIPS, 1, width // CHIPS, width))
        halves.append(jnp.concatenate(parts, axis=1).reshape(2 * width, width))
    return out, up, jnp.concatenate(halves, axis=0)


def whole(shape):
    return pl.BlockSpec(shape, lambda *_: (0,) * len(shape))


def project_kernel(x_ref, w_ref, gain_ref, shift_ref, bias_ref, out_ref, normed_ref):
    hat, _ = normalized(x_ref[...].astype(F32))
    normed = (hat * gain_ref[...] + shift_ref[...]).astype(BF16)
    normed_ref[...] = normed
    out_ref[...] = (nn(normed, w_ref[...]) + bias_ref[...]).astype(BF16)


def project(x, weight, gain, shift, bias):
    rows, width = x.shape
    return pl.pallas_call(
        project_kernel,
        grid=(rows // BLOCK,),
        in_specs=[
            pl.BlockSpec((BLOCK, width), lambda i: (i, 0)),
            whole((width, 3 * width)),
            whole((1, width)),
            whole((1, width)),
            whole((1, 3 * width)),
        ],
        out_specs=[
            pl.BlockSpec((BLOCK, 3 * width), lambda i: (i, 0)),
            pl.BlockSpec((BLOCK, width), lambda i: (i, 0)),
        ],
        out_shape=[
            jax.ShapeDtypeStruct((rows, 3 * width), BF16),
            jax.ShapeDtypeStruct((rows, width), BF16),
        ],
        compiler_params=params(),
        name="project",
    )(x, weight, gain, shift, bias)


def allowed_mask(start, key_at, keys, queries):
    key = key_at + lax.broadcasted_iota(jnp.int32, (keys, queries), 0)
    return key >= start


def head_rows(pair_t, head):
    row = lax.broadcasted_iota(jnp.int32, pair_t.shape, 0)
    mine = (row < HEAD_DIM) if head == 0 else (row >= HEAD_DIM)
    return jnp.where(mine, pair_t, jnp.zeros_like(pair_t))


def head_cols(pair, head):
    col = lax.broadcasted_iota(jnp.int32, pair.shape, 1)
    mine = (col < HEAD_DIM) if head == 0 else (col >= HEAD_DIM)
    return jnp.where(mine, pair, jnp.zeros_like(pair))


def score_parts(key, query_t, start, block):
    before = block * BLOCK
    parts = []
    if block:
        index = lax.broadcasted_iota(jnp.int32, (before, BLOCK), 0)
        parts.append((slice(0, before), jnp.where(index >= start, nn(key[:before], query_t), -1e30)))
    index = lax.broadcasted_iota(jnp.int32, (BLOCK, BLOCK), 0)
    last = lax.broadcasted_iota(jnp.int32, (BLOCK, BLOCK), 1)
    ok = (index >= start - before) & (index <= last)
    own = slice(before, before + BLOCK)
    parts.append((own, jnp.where(ok, nn(key[own], query_t), -1e30)))
    return parts


def attend_pair(query, key, value, start_ref, out_ref, lse_ref):
    query_t = (query.astype(F32) * HEAD_DIM**-0.5).T.astype(BF16)
    value_t = value.astype(F32).T.astype(BF16)
    for block in range(query.shape[0] // BLOCK):
        at = slice(block * BLOCK, (block + 1) * BLOCK)
        start = start_ref[:, at]
        outs = []
        for head in range(2):
            lanes = slice(head * HEAD_DIM, (head + 1) * HEAD_DIM)
            parts = score_parts(key, head_rows(query_t[:, at], head), start, block)
            peak = functools.reduce(jnp.maximum, [jnp.max(scores, axis=0, keepdims=True) for _, scores in parts])
            total = jnp.zeros((1, BLOCK), F32)
            out = jnp.zeros((HEAD_DIM, BLOCK), F32)
            for keys, scores in parts:
                raised = jnp.exp(scores - peak)
                total = total + col_sum(raised)
                out = out + nn(value_t[lanes, keys], raised.astype(BF16))
            outs.append(out * (1.0 / total))
            lse_ref[head : head + 1, at] = peak + jnp.log(total)
        out_ref[at, :] = jnp.concatenate(outs, axis=0).T


def attend_kernel(q_ref, k_ref, v_ref, start_ref, out_ref, lse_ref):
    attend_pair(q_ref[...], k_ref[...], v_ref[...], start_ref, out_ref, lse_ref.at[0])


def attend(projected, start):
    rows, columns = projected.shape
    width = columns // 3
    pairs = width // PAIR
    return pl.pallas_call(
        attend_kernel,
        grid=(pairs,),
        in_specs=[
            pl.BlockSpec((rows, PAIR), lambda p: (0, p)),
            pl.BlockSpec((rows, PAIR), lambda p: (0, pairs + p)),
            pl.BlockSpec((rows, PAIR), lambda p: (0, 2 * pairs + p)),
            whole((1, rows)),
        ],
        out_specs=[
            pl.BlockSpec((rows, PAIR), lambda p: (0, p)),
            pl.BlockSpec((1, 2, rows), lambda p: (p, 0, 0)),
        ],
        out_shape=[
            jax.ShapeDtypeStruct((rows, width), F32),
            jax.ShapeDtypeStruct((pairs, 2, rows), F32),
        ],
        compiler_params=params(),
        name="attend",
    )(projected, projected, projected, start)


def attend_back_pair(query, key, value, grad, context, lse_ref, start_ref, dq_ref, dk_ref, dv_ref, dk_acc, dv_acc):
    scale = HEAD_DIM**-0.5
    scaled = query.astype(F32) * scale
    query = scaled.astype(BF16)
    query_t = scaled.T.astype(BF16)
    key_t = key.astype(F32).T.astype(BF16)
    grad_f = grad.astype(F32)
    grad_t = grad_f.T.astype(BF16)
    weighted_t = (grad_f * context).T
    dk_acc[...] = jnp.zeros_like(dk_acc)
    dv_acc[...] = jnp.zeros_like(dv_acc)
    for block in range(query.shape[0] // BLOCK):
        at = slice(block * BLOCK, (block + 1) * BLOCK)
        start = start_ref[:, at]
        outs = []
        for head in range(2):
            lanes = slice(head * HEAD_DIM, (head + 1) * HEAD_DIM)
            inner = col_sum(weighted_t[lanes, at])
            log_total = lse_ref[head : head + 1, at]
            grad_head = head_rows(grad_t[:, at], head)
            out = jnp.zeros((HEAD_DIM, BLOCK), F32)
            for keys, scores in score_parts(key, head_rows(query_t[:, at], head), start, block):
                soft = jnp.exp(scores - log_total)
                grad_scores = (soft * (nn(value[keys], grad_head) - inner)).astype(BF16)
                dv_acc[keys, :] += nn(soft.astype(BF16), head_cols(grad[at], head))
                dk_acc[keys, :] += nn(grad_scores, head_cols(query[at], head))
                out = out + nn(key_t[lanes, keys], grad_scores)
            outs.append(out)
        dq_ref[at, :] = (jnp.concatenate(outs, axis=0) * scale).T.astype(BF16)
    dk_ref[...] = dk_acc[...].astype(BF16)
    dv_ref[...] = dv_acc[...].astype(BF16)


def attend_back_kernel(q_ref, k_ref, v_ref, g_ref, o_ref, lse_ref, start_ref, dq_ref, dk_ref, dv_ref, dk_acc, dv_acc):
    attend_back_pair(
        q_ref[...], k_ref[...], v_ref[...], g_ref[...], o_ref[...], lse_ref.at[0], start_ref,
        dq_ref, dk_ref, dv_ref, dk_acc, dv_acc,
    )


def attend_back(projected, grad_context, context, lse, start):
    rows, columns = projected.shape
    width = columns // 3
    pairs = width // PAIR
    pair = pl.BlockSpec((rows, PAIR), lambda p: (0, p))
    return pl.pallas_call(
        attend_back_kernel,
        grid=(pairs,),
        in_specs=[
            pair,
            pl.BlockSpec((rows, PAIR), lambda p: (0, pairs + p)),
            pl.BlockSpec((rows, PAIR), lambda p: (0, 2 * pairs + p)),
            pair,
            pair,
            pl.BlockSpec((1, 2, rows), lambda p: (p, 0, 0)),
            whole((1, rows)),
        ],
        out_specs=[pair] * 3,
        out_shape=[jax.ShapeDtypeStruct((rows, width), BF16)] * 3,
        scratch_shapes=[pltpu.VMEM((rows, PAIR), F32), pltpu.VMEM((rows, PAIR), F32)],
        compiler_params=params(),
        name="attend_back",
    )(projected, projected, projected, grad_context, context, lse, start)


def gelu_parts(value):
    phi = 0.5 * (1.0 + lax.erf(value * (1.0 / math.sqrt(2.0))))
    bell = jnp.exp(-0.5 * value * value) * (1.0 / math.sqrt(2.0 * math.pi))
    return value * phi, phi + value * bell


def middle_kernel(
    x_ref, dy_ref, ctx_ref, alive_ref, rest_ref,
    sg_ref, ss_ref, ob_ref, fg_ref, fs_ref, ub_ref, mg_ref, ms_ref, db_ref,
    out_ref, ghid_ref, gctx_ref, mixed_ref, gbranch_ref, nffn_ref, gup_ref, mid_ref, gffn_ref,
    narrow_ref, wide_ref,
):
    step = pl.program_id(0)

    @pl.when(step == 0)
    def _():
        narrow_ref[...] = jnp.zeros_like(narrow_ref)
        wide_ref[...] = jnp.zeros_like(wide_ref)

    out_weight, up_weight, down_weight = split_rest(rest_ref)
    alive = alive_ref[...]
    ctx_hat, ctx_scale = normalized(ctx_ref[...])
    mixed = (ctx_hat * sg_ref[...] + ss_ref[...]).astype(BF16)
    mixed_ref[...] = mixed
    branch = nn(mixed, out_weight) + ob_ref[...]
    hidden = (x_ref[...].astype(F32) + alive * branch).astype(BF16).astype(F32)
    hid_hat, hid_scale = normalized(hidden)
    nffn = (hid_hat * fg_ref[...] + fs_ref[...]).astype(BF16)
    nffn_ref[...] = nffn
    upper = nn(nffn, up_weight) + ub_ref[...]
    active, slope = gelu_parts(upper)
    act_hat, act_scale = normalized(active)
    mid = (act_hat * mg_ref[...] + ms_ref[...]).astype(BF16)
    mid_ref[...] = mid
    result = (nn(mid, down_weight) + db_ref[...]).astype(BF16).astype(F32)
    out_ref[...] = hidden + alive * result

    upstream = dy_ref[...].astype(F32)
    gffn = (alive * upstream).astype(BF16)
    gffn_ref[...] = gffn
    gmid = nt(gffn, down_weight)
    gact = norm_back(act_hat, act_scale, mg_ref[...], gmid)
    gup = (gact * slope).astype(BF16)
    gup_ref[...] = gup
    wide_ref[0:1, :] += col_sum(gup.astype(F32))
    wide_ref[1:2, :] += col_sum(gmid * act_hat)
    wide_ref[2:3, :] += col_sum(gmid)
    gnffn = nt(gup, up_weight)
    ghid = (upstream + norm_back(hid_hat, hid_scale, fg_ref[...], gnffn)).astype(BF16)
    ghid_ref[...] = ghid
    gbranch = (alive * ghid.astype(F32)).astype(BF16)
    gbranch_ref[...] = gbranch
    gmixed = nt(gbranch, out_weight)
    gctx_ref[...] = norm_back(ctx_hat, ctx_scale, sg_ref[...], gmixed).astype(BF16)
    narrow_ref[0:1, :] += col_sum(gmixed * ctx_hat)
    narrow_ref[1:2, :] += col_sum(gmixed)
    narrow_ref[2:3, :] += col_sum(gbranch.astype(F32))
    narrow_ref[3:4, :] += col_sum(gnffn * hid_hat)
    narrow_ref[4:5, :] += col_sum(gnffn)
    narrow_ref[5:6, :] += col_sum(gffn.astype(F32))


def middle(x, dy, context, alive, rest, vectors):
    rows, width = x.shape
    hidden = 4 * width
    row = pl.BlockSpec((BLOCK, width), lambda i: (i, 0))
    row_wide = pl.BlockSpec((BLOCK, hidden), lambda i: (i, 0))
    once = dict(pipeline_mode=pl.Buffered(1))
    narrow = whole((1, width))
    wide = whole((1, hidden))
    def shape(columns, dtype):
        return jax.ShapeDtypeStruct((rows, columns), dtype)
    return pl.pallas_call(
        middle_kernel,
        grid=(rows // BLOCK,),
        in_specs=[
            row, row, row,
            pl.BlockSpec((BLOCK, 1), lambda i: (i, 0)),
            pl.BlockSpec(rest.shape, lambda i: (0, 0, 0), **once),
            narrow, narrow, narrow, narrow, narrow, wide, wide, wide, narrow,
        ],
        out_specs=[row, row, row, row, row, row, row_wide, row_wide, row, whole((8, width)), whole((8, hidden))],
        out_shape=[
            shape(width, F32), shape(width, BF16), shape(width, BF16), shape(width, BF16), shape(width, BF16),
            shape(width, BF16), shape(hidden, BF16), shape(hidden, BF16), shape(width, BF16),
            jax.ShapeDtypeStruct((8, width), F32), jax.ShapeDtypeStruct((8, hidden), F32),
        ],
        compiler_params=params(),
        name="middle",
    )(x, dy, context, alive, rest, *vectors)


def outer_kernel(left_ref, right_ref, out_ref):
    out_ref[...] = tn(left_ref[...], right_ref[...]).astype(out_ref.dtype)


def outer(left, right, tile, dtype, name):
    rows, across = left.shape
    columns = right.shape[1]
    return pl.pallas_call(
        outer_kernel,
        grid=(across // tile,),
        in_specs=[pl.BlockSpec((rows, tile), lambda i: (0, i)), whole((rows, columns))],
        out_specs=pl.BlockSpec((tile, columns), lambda i: (i, 0)),
        out_shape=jax.ShapeDtypeStruct((across, columns), dtype),
        compiler_params=params(),
        name=name,
    )(left, right)


def project_back_kernel(dq_ref, dk_ref, dv_ref, w_ref, x_ref, ghid_ref, gain_ref, out_ref, narrow_ref):
    step = pl.program_id(0)
    width = x_ref.shape[1]

    @pl.when(step == 0)
    def _():
        narrow_ref[...] = jnp.zeros_like(narrow_ref)

    dq, dk, dv = dq_ref[...], dk_ref[...], dv_ref[...]
    gnormed = nt(dq, w_ref[:, :width]) + nt(dk, w_ref[:, width : 2 * width]) + nt(dv, w_ref[:, 2 * width :])
    hat, scale = normalized(x_ref[...].astype(F32))
    out_ref[...] = ghid_ref[...].astype(F32) + norm_back(hat, scale, gain_ref[...], gnormed)
    narrow_ref[0:1, :] += col_sum(gnormed * hat)
    narrow_ref[1:2, :] += col_sum(gnormed)
    narrow_ref[2:3, :] += col_sum(dq.astype(F32))
    narrow_ref[3:4, :] += col_sum(dv.astype(F32))


def project_back(dq, dk, dv, weight, x, ghid, gain):
    rows, width = x.shape
    row = pl.BlockSpec((BLOCK, width), lambda i: (i, 0))
    return pl.pallas_call(
        project_back_kernel,
        grid=(rows // BLOCK,),
        in_specs=[row, row, row, whole(weight.shape), row, row, whole((1, width))],
        out_specs=[row, whole((8, width))],
        out_shape=[jax.ShapeDtypeStruct((rows, width), F32), jax.ShapeDtypeStruct((8, width), F32)],
        compiler_params=params(),
        name="project_back",
    )(dq, dk, dv, weight, x, ghid, gain)


def row_marks(lengths_row, count):
    slots = jnp.arange(lengths_row.shape[0], dtype=jnp.int32)
    ends = jnp.sum(jnp.where(slots[:, None] <= slots[None, :], lengths_row[:, None], 0), axis=0)
    index = jnp.arange(count, dtype=jnp.int32)
    before = jnp.where(ends[None, :] <= index[:, None], ends[None, :], 0)
    alive = index < jnp.max(ends)
    start = jnp.where(alive, jnp.max(before, axis=1), index)
    return alive.astype(F32)[:, None], start[None, :]


MESH = pl.DeviceIdType.MESH
BOX = (4, 2, 2)
CHIPS = 16
X_AT, Y_AT, D_AT, MOVES = 3, 7, 11, 15


class Place:
    def __init__(self):
        self.core = lax.axis_index("section")
        self.chip = lax.axis_index("dp")
        self.z, self.y, self.x = self.chip // 4, (self.chip // 2) % 2, self.chip % 2
        high, low = self.z // 2, self.z % 2
        self.zs = [self.z, self.z + 1 - 2 * low, self.z + 2 - 4 * high, 3 - self.z]

    def at(self, z, y, x):
        return (self.core, z * 4 + y * 2 + x)

    def sibling(self):
        return (1 - self.core, self.chip)

    def over_z(self, k):
        return self.at(self.zs[k], self.y, self.x)

    def over_y(self):
        return self.at(self.z, 1 - self.y, self.x)

    def over_x(self):
        return self.at(self.z, self.y, 1 - self.x)

    def across(self):
        return self.at(self.z, 1 - self.y, 1 - self.x)


def remote(source, target, sems, device):
    return pltpu.make_async_remote_copy(
        src_ref=source, dst_ref=target, send_sem=sems[0], recv_sem=sems[1], device_id=device, device_id_type=MESH
    )


def greet(me):
    barrier = pltpu.get_barrier_semaphore()
    others = [me.sibling(), me.over_x(), me.over_y(), me.across()] + [me.over_z(k) for k in (1, 2, 3)]
    for other in others:
        pl.semaphore_signal(barrier, inc=1, device_id=other, device_id_type=MESH)
    pl.semaphore_wait(barrier, len(others))


class Gather:
    def __init__(self, full, sems, pass_sems, direct=False):
        self.me = Place()
        self.direct = direct
        self.own = full.at[pl.ds(3 * self.me.core, 3)]
        self.other = full.at[pl.ds(3 * (1 - self.me.core), 3)]
        self.sems, self.pass_sems = sems, pass_sems

    def move(self, index, z, y, x, device):
        part = self.own.at[:, z, y, x]
        return remote(part, part, (self.sems.at[0, index], self.sems.at[1, index]), device)

    def to_z(self, k):
        me = self.me
        return self.move(k - 1, me.z, me.y, me.x, me.over_z(k))

    def to_x(self, k):
        me = self.me
        return self.move(X_AT + k, me.zs[k], me.y, me.x, me.over_x())

    def to_y(self, k):
        me = self.me
        return self.move(Y_AT + k, me.zs[k], me.y, me.x, me.over_y())

    def onward(self, k):
        me = self.me
        if self.direct:
            return self.move(D_AT + k, me.zs[k], me.y, me.x, me.across())
        if k < 2:
            return self.move(D_AT + k, me.zs[k], me.y, 1 - me.x, me.over_y())
        return self.move(D_AT + k, me.zs[k], 1 - me.y, me.x, me.over_x())

    def across_core(self, index, ref):
        me = self.me
        every = slice(None)
        place = [(every, me.y, 1 - me.x), (every, 1 - me.y, me.x), (every, 1 - me.y, 1 - me.x)]
        z, y, x = (me.zs[index + 1], me.y, me.x) if index < 3 else place[index - 3]
        part = ref.at[:, z, y, x]
        return remote(part, part, (self.pass_sems.at[0, index], self.pass_sems.at[1, index]), me.sibling())

    def launch(self):
        for k in (1, 2, 3):
            self.to_z(k).start()
        self.spread(0)

    def spread(self, k):
        self.to_x(k).start()
        self.to_y(k).start()
        if self.direct:
            self.onward(k).start()

    def from_z(self, k):
        self.to_z(k).wait_recv()
        self.spread(k)
        self.across_core(k - 1, self.own).start()

    def arrive(self, stage):
        if stage == 0:
            self.from_z(1)
            self.to_x(0).wait_recv()
            if not self.direct:
                self.onward(0).start()
        elif stage == 1:
            self.from_z(2)
            self.from_z(3)
            self.to_x(1).wait_recv()
            if not self.direct:
                self.onward(1).start()
        elif stage == 2:
            for k in (2, 3):
                self.to_y(k).wait_recv()
                if not self.direct:
                    self.onward(k).start()
            for k in (2, 3):
                self.to_x(k).wait_recv()
            for k in (0, 1):
                self.to_y(k).wait_recv()
            self.across_core(3, self.own).start()
            self.across_core(4, self.own).start()
        else:
            for k in range(4):
                self.onward(k).wait_recv()
            self.across_core(5, self.own).start()

    def passed(self):
        for index in range(6):
            self.across_core(index, self.other).wait_recv()

    def drain(self):
        for k in (1, 2, 3):
            self.to_z(k).wait_send()
        for k in range(4):
            for move in (self.to_x(k), self.to_y(k), self.onward(k)):
                move.wait_send()
        for index in range(6):
            self.across_core(index, self.own).wait_send()


def seed(parts, sems):
    me = Place()
    moves = []
    for index, (source, full, block, cols) in enumerate(parts):
        here = full.at[block, me.z, me.y, me.x, :, cols]
        local = pltpu.make_async_copy(source, here, sems.at[0, index])
        far = remote(source, here, (sems.at[1, index], sems.at[2, index]), me.sibling())
        moves.append((local, far))

    def begin():
        for local, far in moves:
            local.start()
            far.start()

    def sent():
        for local, far in moves:
            local.wait()
            far.wait_send()

    def got():
        for _, far in moves:
            far.wait_recv()

    return begin, sent, got


def lane_groups(value):
    groups = [value[:, at : at + 128] for at in range(0, value.shape[1], 128)]
    return functools.reduce(jnp.add, groups)


def as_row(ref):
    return ref[...].reshape(1, -1)


def lengths_of(lengths_ref, core):
    return [lengths_ref[core, slot] for slot in range(lengths_ref.shape[1])]


def alive_rows(lengths_ref, core, at, rows):
    index = at + lax.broadcasted_iota(jnp.int32, (rows, 1), 0)
    return (index < sum(lengths_of(lengths_ref, core))).astype(F32)


def start_row(lengths_ref, core, count):
    index = lax.broadcasted_iota(jnp.int32, (1, count), 1)
    start = jnp.zeros((1, count), jnp.int32)
    end = jnp.int32(0)
    for length in lengths_of(lengths_ref, core):
        end = end + length
        start = jnp.where(index >= end, end, start)
    return jnp.where(index < end, start, index)


def front_kernel(
    tokens_ref, upstream_ref, lengths_ref, half_ref, down_ref,
    pg_ref, ps_ref, qb_ref, vb_ref, sg_ref, ss_ref, ob_ref, fg_ref, fs_ref, ub_ref, mg_ref, ms_ref,
    projected_out, normed_out, context_out, lse_out, start_out, wq0_out, wq1_out, wuo_out, wd_ref,
    mixed_out, nffn_out, hidden_out, mid_out, hat_out, slope_out, scale_out, gdown_out,
    hidden, gffn, broad, hat, mid, normed, mixed, context, lse, start, wq0, wq1, wuo, mid_t, gdown, scales, active,
    seed_q0, seed_q1, seed_o, seed_u, seed_d, chain_q0, chain_q1, chain_u, chain_d, pass_q0, pass_q1, pass_u, pass_d,
    load_sems, save_sems, row_sems, grad_sems,
):
    me = Place()
    core = me.core
    rows, width = hidden.shape
    mine = half_ref.shape[0]
    pairs = width // PAIR
    co, cu, cd = width // 6, 2 * width // 3, width // 3
    cg = 3 * PAIR
    first = core == 0
    second = core == 1
    box = (slice(None),) * 3

    def group_parts(full, groups):
        return [
            (half_ref.at[:, n * width + (2 * g + c) * PAIR : n * width + (2 * g + c + 1) * PAIR],
             full, 3 * c + n, slice(at * PAIR, (at + 1) * PAIR))
            for at, g in enumerate(groups) for c in range(2) for n in range(3)
        ]

    q0_begin, q0_sent, q0_got = seed(group_parts(wq0, [0]), seed_q0)
    q1_begin, q1_sent, q1_got = seed(group_parts(wq1, [1, 2]), seed_q1)
    o_begin, o_sent, o_got = seed(
        [(half_ref.at[:, 3 * width + b * co : 3 * width + (b + 1) * co],
          wuo, b, slice(cu, cu + co)) for b in range(6)], seed_o)
    u_begin, u_sent, u_got = seed(
        [(half_ref.at[:, b * cu : (b + 1) * cu],
          wuo, b, slice(0, cu)) for b in range(6)], seed_u)

    def down_parts(which):
        return [
            (down_ref.at[n * mine : (n + 1) * mine, k * cd : (k + 1) * cd],
             wd_ref, 3 * which + k, slice(n * cd, (n + 1) * cd))
            for k in range(3) for n in range(2)
        ]

    d_begin, d_sent, _ = seed(down_parts(core), seed_d)
    _, _, d_got = seed(down_parts(1 - core), seed_d)

    gather_q0 = Gather(wq0, chain_q0, pass_q0, direct=True)
    gather_q1 = Gather(wq1, chain_q1, pass_q1)
    gather_u = Gather(wuo, chain_u, pass_u)
    gather_d = Gather(wd_ref, chain_d, pass_d)

    own_rows = pl.ds(pl.multiple_of(core * rows, rows), rows)
    loads = [
        pltpu.make_async_copy(tokens_ref.at[own_rows], hidden, load_sems.at[0]),
        pltpu.make_async_copy(upstream_ref.at[own_rows], gffn, load_sems.at[1]),
    ]
    loads[0].start()
    greet(me)
    pl.when(first)(q0_begin)
    pl.when(first)(q1_begin)
    pl.when(first)(o_begin)
    pl.when(second)(u_begin)
    d_begin()
    loads[1].start()
    pl.when(first)(q0_sent)
    pl.when(second)(q0_got)
    gather_q0.launch()

    loads[0].wait()
    value, _ = normalized(hidden[...].astype(F32))
    normed[...] = (value * as_row(pg_ref) + as_row(ps_ref)).astype(BF16)
    start[...] = start_row(lengths_ref, core, rows)
    saves = []

    def save(source, target):
        saves.append(pltpu.make_async_copy(source, target, save_sems.at[len(saves)]))
        saves[-1].start()

    save(normed, normed_out)
    save(start, start_out)
    @pl.when(first)
    def _():
        q1_sent()
        o_sent()
        u_got()

    @pl.when(second)
    def _():
        u_sent()
        q1_got()
        o_got()

    gather_q0.arrive(0)
    gather_q1.launch()
    gather_q0.arrive(1)
    gather_u.launch()
    gather_q0.arrive(2)
    gather_q1.arrive(0)
    gather_q0.arrive(3)
    d_sent()
    d_got()
    gather_q0.passed()

    query_bias, value_bias = as_row(qb_ref), as_row(vb_ref)

    def project_group(group, weights):
        biases = []
        for c in range(2):
            at = slice((2 * group + c) * PAIR, (2 * group + c + 1) * PAIR)
            biases += [query_bias[:, at], jnp.zeros((1, PAIR), F32), value_bias[:, at]]
        cols = slice(group * 2 * cg, (group + 1) * 2 * cg)
        weight = jnp.concatenate(weights, axis=1)
        broad[:, cols] = (nn(normed[...], weight) + jnp.concatenate(biases, axis=1)).astype(BF16)

    project_group(0, [wq0[b].reshape(width, PAIR) for b in range(6)])
    gather_q1.arrive(1)

    def one_pair(pair, carry):
        @pl.when(pair == 0)
        def _():
            gather_u.arrive(0)

        @pl.when(pair == 1)
        def _():
            gather_q1.arrive(2)

        @pl.when(pair == 2)
        def _():
            gather_q1.arrive(3)
            gather_q1.passed()
            gather_u.arrive(1)
            for group in range(1, 3):
                at = slice((group - 1) * PAIR, group * PAIR)
                project_group(group, [wq1[(b, *box, slice(None), at)].reshape(width, PAIR) for b in range(6)])
            pltpu.make_async_copy(broad.at[:, : 3 * width], projected_out, load_sems.at[0]).start()

        @pl.when(pair == 3)
        def _():
            gather_d.launch()

        @pl.when(pair == 4)
        def _():
            gather_u.arrive(2)

        @pl.when(pair == 5)
        def _():
            gather_d.arrive(0)

        at_q = pl.ds(pl.multiple_of(pair * cg, PAIR), PAIR)
        at_k = pl.ds(pl.multiple_of(pair * cg + PAIR, PAIR), PAIR)
        at_v = pl.ds(pl.multiple_of(pair * cg + 2 * PAIR, PAIR), PAIR)
        at_out = pl.ds(pl.multiple_of(pair * PAIR, PAIR), PAIR)
        attend_pair(broad[:, at_q], broad[:, at_k], broad[:, at_v], start, context.at[:, at_out], lse.at[pair])
        return carry

    lax.fori_loop(0, pairs, one_pair, 0)
    save(context, context_out)
    save(lse, lse_out)
    save(wq0, wq0_out)
    save(wq1, wq1_out)
    gather_u.arrive(3)
    gather_u.passed()
    save(wuo, wuo_out)
    loads[1].wait()
    pltpu.make_async_copy(broad.at[:, : 3 * width], projected_out, load_sems.at[0]).wait()
    saves[0].wait()

    def row_saves(step):
        at = pl.ds(pl.multiple_of(step * BLOCK, BLOCK), BLOCK)
        pieces = [(mixed, mixed_out), (normed, nffn_out), (hidden, hidden_out), (mid, mid_out), (hat, hat_out),
                  (broad, slope_out)]
        return [
            pltpu.make_async_copy(source.at[at], target.at[at], row_sems.at[index, step])
            for index, (source, target) in enumerate(pieces)
        ]

    def one_block(step, carry):
        at = pl.ds(pl.multiple_of(step * BLOCK, BLOCK), BLOCK)
        alive = alive_rows(lengths_ref, core, step * BLOCK, BLOCK)
        ctx_hat, _ = normalized(context[at, :])
        mix = (ctx_hat * as_row(sg_ref) + as_row(ss_ref)).astype(BF16)
        mixed[at, :] = mix
        out_weight = jnp.concatenate([wuo[(b, *box, slice(None), slice(cu, cu + co))].reshape(width, co) for b in range(6)], axis=1)
        branch = nn(mix, out_weight) + as_row(ob_ref)
        hid = (hidden[at, :].astype(F32) + alive * branch).astype(BF16)
        hidden[at, :] = hid
        hid_hat, _ = normalized(hid.astype(F32))
        nffn = (hid_hat * as_row(fg_ref) + as_row(fs_ref)).astype(BF16)
        normed[at, :] = nffn
        up_weight = jnp.concatenate([wuo[(b, *box, slice(None), slice(0, cu))].reshape(width, cu) for b in range(6)], axis=1)
        units = 4 * width
        chunks = [slice(c, c + width) for c in range(0, units, width)]
        up_bias, mid_gain, mid_shift = as_row(ub_ref), as_row(mg_ref), as_row(ms_ref)
        lanes = jnp.zeros((BLOCK, 128), F32)
        for cols in chunks:
            value, slope = gelu_parts(nn(nffn, up_weight[:, cols]) + up_bias[:, cols])
            broad[at, cols] = slope.astype(BF16)
            active[:, cols] = value
            lanes = lanes + lane_groups(value)
        center = jnp.sum(lanes, axis=-1, keepdims=True) * (1.0 / units)
        lanes = jnp.zeros((BLOCK, 128), F32)
        for cols in chunks:
            centered = active[:, cols] - center
            lanes = lanes + lane_groups(centered * centered)
        act_scale = lax.rsqrt(jnp.sum(lanes, axis=-1, keepdims=True) * (1.0 / units) + EPS)
        for cols in chunks:
            act_hat = (active[:, cols] - center) * act_scale
            hat[at, cols] = act_hat.astype(BF16)
            mid[at, cols] = (act_hat * mid_gain[:, cols] + mid_shift[:, cols]).astype(BF16)
        scales[at, :] = act_scale
        gffn[at, :] = (alive * gffn[at, :].astype(F32)).astype(BF16)
        for copy in row_saves(step):
            copy.start()

        @pl.when(step == 0)
        def _():
            gather_d.arrive(1)

        @pl.when(step == 2)
        def _():
            gather_d.arrive(2)

        return carry

    steps = rows // BLOCK
    lax.fori_loop(0, steps, one_block, 0)
    save(scales, scale_out)

    def grad_save(h, k):
        return pltpu.make_async_copy(gdown.at[k], gdown_out.at[3 * h + k], grad_sems.at[h, k])

    for h in range(2):
        mid_t[...] = mid[:, 2 * h * width : 2 * (h + 1) * width].T
        for k in range(3):
            grad = nn(mid_t[...], gffn[:, k * cd : (k + 1) * cd]).astype(BF16)
            grad = grad.reshape(CHIPS, 2, mine, cd)
            if h:
                grad_save(0, k).wait()
            for n in range(2):
                gdown[k, :, :, n * cd : (n + 1) * cd] = grad[:, n]
            grad_save(h, k).start()
    gather_d.arrive(3)
    for k in range(3):
        grad_save(1, k).wait()
    gather_d.passed()

    def finish(step, carry):
        for copy in row_saves(step):
            copy.wait()
        return carry

    lax.fori_loop(0, steps, finish, 0)
    for copy in saves[1:]:
        copy.wait()
    for gather in (gather_q0, gather_q1, gather_u, gather_d):
        gather.drain()


def front(tokens, upstream, lengths, half, down, vectors):
    width = tokens.shape[1]
    rows = tokens.shape[0] // 2
    mine = half.shape[0]
    box = BOX
    pairs = width // PAIR
    wide = 4 * width
    anywhere = pl.BlockSpec(memory_space=pl.ANY)
    vmem = pl.BlockSpec(memory_space=pltpu.VMEM)
    smem = pl.BlockSpec(memory_space=pltpu.SMEM)
    dma = pltpu.SemaphoreType.DMA
    sizes = dict(q0=PAIR, q1=2 * PAIR, u=5 * width // 6, d=2 * width // 3)
    shape = jax.ShapeDtypeStruct
    steps = rows // BLOCK
    return pl.pallas_call(
        front_kernel,
        in_specs=[anywhere, anywhere, smem, anywhere, anywhere] + [vmem] * len(vectors),
        out_specs=[anywhere] * 17,
        out_shape=[
            shape((rows, 3 * width), BF16), shape((rows, width), BF16), shape((rows, width), F32),
            shape((pairs, 2, rows), F32), shape((1, rows), jnp.int32),
            *[shape((6, *box, mine, columns), BF16) for columns in sizes.values()],
            shape((rows, width), BF16), shape((rows, width), BF16), shape((rows, width), BF16),
            shape((rows, wide), BF16), shape((rows, wide), BF16), shape((rows, wide), BF16), shape((rows, 1), F32),
            shape((6, CHIPS, mine, 2 * width // 3), BF16),
        ],
        scratch_shapes=[
            pltpu.VMEM((rows, width), BF16), pltpu.VMEM((rows, width), BF16), pltpu.VMEM((rows, wide), BF16),
            pltpu.VMEM((rows, wide), BF16), pltpu.VMEM((rows, wide), BF16), pltpu.VMEM((rows, width), BF16),
            pltpu.VMEM((rows, width), BF16), pltpu.VMEM((rows, width), F32), pltpu.VMEM((pairs, 2, rows), F32),
            pltpu.VMEM((1, rows), jnp.int32),
            *[pltpu.VMEM((6, *box, mine, sizes[name]), BF16) for name in ("q0", "q1", "u")],
            pltpu.VMEM((2 * width, rows), BF16), pltpu.VMEM((3, CHIPS, mine, 2 * width // 3), BF16),
            pltpu.VMEM((rows, 1), F32), pltpu.VMEM((BLOCK, wide), F32),
            dma((3, 6)), dma((3, 12)), dma((3, 6)), dma((3, 6)), dma((3, 6)),
            *[dma((2, MOVES))] * 4, *[dma((2, 6))] * 4,
            dma((2,)), dma((8,)), dma((6, steps)), dma((2, 3)),
        ],
        compiler_params=params(collective_id=1, has_side_effects=True),
        name="front",
    )(tokens, upstream, lengths, half, down, *vectors)


class Scatter:
    def __init__(self, total, landings, sems, final, direct=False):
        self.me = Place()
        self.direct = direct
        self.total, self.landings, self.sems, self.final = total, landings, sems, final

    def move(self, index, z, y, x, device):
        return remote(self.total.at[:, z, y, x], self.landings.at[index], (self.sems.at[0, index], self.sems.at[1, index]), device)

    def to_z(self, k):
        me = self.me
        return self.move(k - 1, me.zs[k], me.y, me.x, me.over_z(k))

    def to_x(self, k):
        me = self.me
        return self.move(X_AT + k, me.zs[k], me.y, 1 - me.x, me.over_x())

    def to_y(self, k):
        me = self.me
        return self.move(Y_AT + k, me.zs[k], 1 - me.y, me.x, me.over_y())

    def toward(self, k):
        me = self.me
        return self.move(D_AT + k, me.zs[k], 1 - me.y, 1 - me.x, me.across() if self.direct else me.over_y() if k < 2 else me.over_x())

    def add(self, z, y, x, landed):
        self.total[:, z, y, x] = functools.reduce(jnp.add, [part[...] for part in landed], self.total[:, z, y, x])

    def begin(self, other):
        me = self.me

        def both(z, y, x):
            self.add(z, y, x, [other.at[:, z, y, x]])

        if self.direct:
            for k in (2, 3, 1, 0):
                both(me.zs[k], 1 - me.y, 1 - me.x)
                self.toward(k).start()
                both(me.zs[k], me.y, 1 - me.x)
                self.to_x(k).start()
                both(me.zs[k], 1 - me.y, me.x)
                self.to_y(k).start()
                both(me.zs[k], me.y, me.x)
            return
        for k in range(4):
            both(me.zs[k], 1 - me.y, 1 - me.x)
            self.toward(k).start()
        for k in range(4):
            both(me.zs[k], me.y, 1 - me.x)
            both(me.zs[k], 1 - me.y, me.x)
            both(me.zs[k], me.y, me.x)

    def arrive(self, stage):
        me = self.me
        if self.direct and stage < 3:
            for k in ((2, 3), (1, 0), ())[stage]:
                moves = (self.toward(k), self.to_x(k), self.to_y(k))
                for move in moves:
                    move.wait_recv()
                self.add(me.zs[k], me.y, me.x, [self.landings.at[at + k] for at in (D_AT, X_AT, Y_AT)])
                if k:
                    self.to_z(k).start()
        elif stage == 0:
            for k in range(4):
                self.toward(k).wait_recv()
                if k < 2:
                    self.add(me.zs[k], me.y, 1 - me.x, [self.landings.at[D_AT + k]])
                else:
                    self.add(me.zs[k], 1 - me.y, me.x, [self.landings.at[D_AT + k]])
            for k in (2, 3):
                self.to_x(k).start()
                self.to_y(k).start()
        elif stage < 3:
            if stage == 1:
                for k in (1, 0):
                    self.to_x(k).start()
                    self.to_y(k).start()
            for k in (2, 3) if stage == 1 else (1, 0):
                self.to_x(k).wait_recv()
                self.to_y(k).wait_recv()
                self.add(me.zs[k], me.y, me.x, [self.landings.at[X_AT + k], self.landings.at[Y_AT + k]])
                if k:
                    self.to_z(k).start()
        else:
            value = self.total[:, me.z, me.y, me.x].astype(F32)
            for k in (1, 2, 3):
                self.to_z(k).wait_recv()
                value = value + self.landings[k - 1].astype(F32)
            self.final[...] = value

    def drain(self):
        for k in (1, 2, 3):
            self.to_z(k).wait_send()
        for k in range(4):
            for move in (self.to_x(k), self.to_y(k), self.toward(k)):
                move.wait_send()


class Total:
    def __init__(self, rows, landed, sems):
        me = Place()
        self.rows, self.landed, self.sems = rows, landed, sems
        self.partners = [
            [me.sibling()], [me.over_x(), me.over_y(), me.across()], [me.over_z(k) for k in (1, 2, 3)]
        ]

    def moves(self, stage):
        at = (0, 1, 4)[stage]
        return [
            remote(self.rows.at[stage], self.landed.at[at + n], (self.sems.at[0, at + n], self.sems.at[1, at + n]), device)
            for n, device in enumerate(self.partners[stage])
        ]

    def start(self, stage):
        for move in self.moves(stage):
            move.start()

    def arrive(self, stage):
        at = (0, 1, 4)[stage]
        value = self.rows[stage]
        for n, move in enumerate(self.moves(stage)):
            move.wait_recv()
            value = value + self.landed[at + n]
        self.rows[stage + 1] = value
        if stage < 2:
            self.start(stage + 1)

    def drain(self):
        for stage in range(3):
            for move in self.moves(stage):
                move.wait_send()


def feed_body(
    hidden_steps, upstream_ref, context_ref, hidden_ref, mid_ref, hat_ref, slope_ref, scale_ref, lengths_ref, wuo_any, wd_any,
    sg_ref, fg_ref, mg_ref, db_ref, gdown_ref,
    ghid_ref, gctx_ref, gbranch_ref, gup_ref, narrow_ref, wide_ref, layer_ref, down_ref,
    wuo_ref, wd_ref, out_rows, scaled_grad, total, landed, landings, final, swap_sems, chain_sems, local_sems, out_sems,
):
    me = Place()
    core = me.core
    step = pl.program_id(0)
    steps = pl.num_programs(0)
    width = hidden_ref.shape[1]
    mine = width // CHIPS
    co, cu, cd = width // 6, 2 * width // 3, width // 3
    sibling = me.sibling()
    scatter = Scatter(total, landings, chain_sems, final)
    own = pltpu.make_async_copy(gdown_ref.at[pl.ds(3 * core, 3)], total, local_sems.at[0])
    far = remote(gdown_ref.at[pl.ds(3 * (1 - core), 3)], landed, (swap_sems.at[0], swap_sems.at[1]), sibling)

    def out_copies(at_step, which):
        at = pl.ds(pl.multiple_of(at_step * BLOCK, BLOCK), BLOCK)
        target = layer_ref.at[which, at]
        return (pltpu.make_async_copy(out_rows.at[at], target, out_sems.at[0, at_step]),
                remote(out_rows.at[at], target, (out_sems.at[1, at_step], out_sems.at[2, at_step]), sibling))

    got_wd = pltpu.make_async_copy(wd_any, wd_ref, local_sems.at[1])
    got_wuo = pltpu.make_async_copy(wuo_any, wuo_ref, local_sems.at[2])

    @pl.when(step == 0)
    def _():
        got_wd.start()
        got_wuo.start()
        greet(me)
        far.start()
        own.start()
        got_wd.wait()
        narrow_ref[...] = jnp.zeros_like(narrow_ref)
        wide_ref[...] = jnp.zeros_like(wide_ref)

    def hook(at_step, action):
        pl.when(step == at_step)(action)

    def begin():
        own.wait()
        far.wait_recv()
        scatter.begin(landed)

    halves = []
    for h in range(2):
        parts = []
        for n in range(2):
            part = jnp.concatenate([wd_ref[3 * h + k, :, n * cd : (n + 1) * cd] for k in range(3)], axis=1)
            parts.append(part.reshape(CHIPS, 1, mine, width))
        halves.append(jnp.concatenate(parts, axis=1).reshape(2 * width, width))
    down_weight = jnp.concatenate(halves, axis=0)

    hook(3, lambda: scatter.arrive(2))
    alive = alive_rows(lengths_ref, core, step * BLOCK, BLOCK)
    hidden = hidden_ref[...].astype(F32)
    upstream = upstream_ref[...].astype(F32)
    gffn = (alive * upstream).astype(BF16)
    mid_gain = as_row(mg_ref)
    units = 4 * width
    chunks = [slice(at, at + width) for at in range(0, units, width)]
    first_sum = jnp.zeros((BLOCK, 128), F32)
    second_sum = jnp.zeros((BLOCK, 128), F32)
    for cols in chunks:
        gmid = nt(gffn, down_weight[cols])
        weighted = gmid * hat_ref[:, cols].astype(F32)
        wide_ref[1:2, cols] += col_sum(weighted)
        wide_ref[2:3, cols] += col_sum(gmid)
        scaled = gmid * mid_gain[:, cols]
        scaled_grad[:, cols] = scaled
        first_sum = first_sum + lane_groups(scaled)
        second_sum = second_sum + lane_groups(weighted * mid_gain[:, cols])
    first_mean = jnp.sum(first_sum, axis=-1, keepdims=True) * (1.0 / units)
    second_mean = jnp.sum(second_sum, axis=-1, keepdims=True) * (1.0 / units)
    hook(0, begin)
    hook(0, got_wuo.wait)
    up_weight = jnp.concatenate([wuo_ref[b, :, :cu] for b in range(6)], axis=1)
    out_weight = jnp.concatenate([wuo_ref[b, :, cu:] for b in range(6)], axis=1)
    hook(1, lambda: scatter.arrive(0))
    hook(2, lambda: scatter.arrive(1))
    act_scale = scale_ref[...]
    gnffn = jnp.zeros((BLOCK, width), F32)
    result = jnp.zeros((BLOCK, width), F32)
    for cols in chunks:
        act_hat = hat_ref[:, cols].astype(F32)
        gact = (scaled_grad[:, cols] - first_mean - act_hat * second_mean) * act_scale
        gup = (gact * slope_ref[:, cols].astype(F32)).astype(BF16)
        gup_ref[:, cols] = gup
        wide_ref[0:1, cols] += col_sum(gup.astype(F32))
        gnffn = gnffn + nt(gup, up_weight[:, cols])
        result = result + nn(mid_ref[:, cols], down_weight[cols])
    result = (result + as_row(db_ref)).astype(BF16).astype(F32)
    out_rows[pl.ds(pl.multiple_of(step * BLOCK, BLOCK), BLOCK), :] = hidden + alive * result
    for copy in out_copies(step, core):
        copy.start()
    hid_hat, hid_scale = normalized(hidden)
    ghid = (upstream + norm_back(hid_hat, hid_scale, as_row(fg_ref), gnffn)).astype(BF16)
    ghid_ref[...] = ghid
    gbranch = (alive * ghid.astype(F32)).astype(BF16)
    gbranch_ref[...] = gbranch
    gmixed = nt(gbranch, out_weight)
    ctx_hat, ctx_scale = normalized(context_ref[...])
    gctx_ref[...] = norm_back(ctx_hat, ctx_scale, as_row(sg_ref), gmixed).astype(BF16)
    narrow_ref[0:1, :] += col_sum(gmixed * ctx_hat)
    narrow_ref[1:2, :] += col_sum(gmixed)
    narrow_ref[2:3, :] += col_sum(gbranch.astype(F32))
    narrow_ref[3:4, :] += col_sum(gnffn * hid_hat)
    narrow_ref[4:5, :] += col_sum(gnffn)
    narrow_ref[5:6, :] += col_sum(gffn.astype(F32))

    @pl.when(step == steps - 1)
    def _():
        scatter.arrive(3)
        for k in range(3):
            for n in range(2):
                down_ref[n * mine : (n + 1) * mine, k * cd : (k + 1) * cd] = final[k, :, n * cd : (n + 1) * cd]
        for index in range(hidden_steps):
            local, away = out_copies(index, core)
            local.wait()
            away.wait_send()
            out_copies(index, 1 - core)[1].wait_recv()
        far.wait_send()
        scatter.drain()


def feed(upstream, context, hidden, mid, hat, slope, scale, lengths, wuo, wd, vectors, gdown):
    rows, width = hidden.shape
    wide = 4 * width
    steps = rows // BLOCK
    box = BOX
    mine = width // CHIPS
    columns = 2 * width // 3
    row = pl.BlockSpec((BLOCK, width), lambda i: (i, 0))
    row_wide = pl.BlockSpec((BLOCK, wide), lambda i: (i, 0))
    once = dict(pipeline_mode=pl.Buffered(1))
    anywhere = pl.BlockSpec(memory_space=pl.ANY)
    vmem = pl.BlockSpec(memory_space=pltpu.VMEM)
    smem = pl.BlockSpec(memory_space=pltpu.SMEM)
    dma = pltpu.SemaphoreType.DMA
    shape = jax.ShapeDtypeStruct

    def held(*size, dtype=BF16):
        return pltpu.VMEM(size, dtype)

    return pl.pallas_call(
        functools.partial(feed_body, steps),
        grid=(steps,),
        in_specs=[
            pl.BlockSpec((BLOCK, width), lambda i: (lax.axis_index("section") * steps + i, 0)),
            row, row, row_wide, row_wide, row_wide, pl.BlockSpec((BLOCK, 1), lambda i: (i, 0)), smem,
            anywhere, anywhere, *[vmem] * 4, anywhere,
        ],
        out_specs=[row, row, row, row_wide, whole((8, width)), whole((8, wide)), anywhere, vmem],
        out_shape=[
            shape((rows, width), BF16), shape((rows, width), BF16), shape((rows, width), BF16), shape((rows, wide), BF16),
            shape((8, width), F32), shape((8, wide), F32), shape((2, rows, width), F32), shape((2 * mine, width), F32),
        ],
        scratch_shapes=[
            held(*wuo.shape), held(*wd.shape), held(rows, width, dtype=F32), held(BLOCK, wide, dtype=F32),
            held(3, *box, mine, columns), held(3, *box, mine, columns),
            held(MOVES, 3, mine, columns),
            held(3, mine, columns, dtype=F32),
            dma((2,)), dma((2, MOVES)), dma((3,)), dma((3, steps)),
        ],
        compiler_params=params(collective_id=3, has_side_effects=True),
        name="feed",
    )(upstream, context, hidden, mid, hat, slope, scale, lengths, wuo, wd, *vectors,
      gdown.reshape((6,) + box + (mine, columns)))


def finish_kernel(*refs):
    layer_ref, grad_ref, half_ref, down_ref, slim_ref, broad_ref = refs[:6]
    layer_out, grad_out, half_out, down_out = refs[6:10]
    small, (layer, grad, half, down, sems) = refs[10:23], refs[23:]
    pieces = []
    for source, held, target, parts in (
        (layer_ref, layer, layer_out, 8), (grad_ref, grad, grad_out, 4), (half_ref, half, half_out, 1), (down_ref, down, down_out, 1)
    ):
        rows = source.shape[0] // parts
        for part in range(parts):
            at = pl.ds(part * rows, rows)
            n = len(pieces)
            pieces.append((pltpu.make_async_copy(source.at[at], held.at[at], sems.at[0, n]),
                           pltpu.make_async_copy(held.at[at], target.at[at], sems.at[1, n])))
    for get, _ in pieces:
        get.start()
    for row, out in zip((0, 1, 2, 3, 8, 9, 10, 11, 12, 13), small[:10]):
        out[...] = slim_ref[row, : out.shape[0]]
    for row, out in enumerate(small[10:]):
        out[...] = broad_ref[row, : out.shape[0]]
    for get, put in pieces:
        get.wait()
        put.start()
    for _, put in pieces:
        put.wait()


def finish(layer, grad, half, down, slim, broad, narrow_share, wide_share):
    anywhere = pl.BlockSpec(memory_space=pl.ANY)
    vmem = pl.BlockSpec(memory_space=pltpu.VMEM)
    shape = jax.ShapeDtypeStruct
    big = [layer, grad, half, down]
    sizes = [narrow_share] * 10 + [wide_share] * 3
    return pl.pallas_call(
        finish_kernel,
        in_specs=[anywhere] * 4 + [vmem] * 2,
        out_specs=[anywhere] * 4 + [vmem] * len(sizes),
        out_shape=[shape(array.shape, F32) for array in big] + [shape((size,), F32) for size in sizes],
        scratch_shapes=[pltpu.VMEM(array.shape, F32) for array in big] + [pltpu.SemaphoreType.DMA((2, 14))],
        compiler_params=params(),
        name="finish",
    )(layer, grad, half, down, slim, broad)


def back_kernel(
    projected_any, gctx_any, context_any, lse_ref, start_ref, normed_any, tokens_any, ghid_any, gain_ref, wq0_any, wq1_any,
    narrow_ref, wide_ref, nffn_any, mixed_any, gup_any, gbranch_any,
    grad_ref, half_ref, slim_ref, broad_ref,
    projected_ref, gctx_ref, context_ref, ghid_ref, wq0_ref, wq1_ref, spare, gup_far, gbranch, mixed_t, far_r,
    x_rows, dproj, dk_acc, dv_acc, normed_t, near_rows, far_rows,
    total_r, first_r, landings_r, final_r, other_r,
    total_q, far_q, first_q, landings_q, final_q, other_q,
    early, early_in, late, late_in,
    load_sems, swap_sems, far_sems, chain_r, chain_q, early_sems, late_sems, row_sems,
):
    me = Place()
    core = me.core
    rows, width = x_rows.shape
    mine = half_ref.shape[0]
    pairs = width // PAIR
    co, cu, cq = width // 6, 2 * width // 3, width // 2
    cg = 3 * PAIR
    sibling = me.sibling()
    first = core == 0
    second = core == 1

    def swap(index, source, target):
        return remote(source, target, (swap_sems.at[0, index], swap_sems.at[1, index]), sibling)

    sum_r = Scatter(total_r, landings_r, chain_r, final_r)
    sum_q = [Scatter(total_q.at[g], landings_q.at[g], chain_q.at[g], final_q.at[g], direct=True) for g in range(3)]

    loads = []

    def load(source, target):
        loads.append(pltpu.make_async_copy(source, target, load_sems.at[len(loads)]))
        loads[-1].start()
        return loads[-1]

    half = 2 * width
    far_cols = pl.ds(pl.multiple_of((1 - core) * half, PAIR), half)
    own_cols = pl.ds(pl.multiple_of(core * half, PAIR), half)
    got_nffn = load(nffn_any, x_rows)
    got_mixed = load(mixed_any, spare)
    got_far = load(gup_any.at[:, far_cols], gup_far)
    got_branch = load(gbranch_any, gbranch)
    got_own = load(gup_any.at[:, own_cols], dproj.at[:, :half])
    later = [
        load(source, target)
        for source, target in ((projected_any, projected_ref), (gctx_any, gctx_ref), (context_any, context_ref))
    ]
    greet(me)
    early_sum = Total(early, early_in, early_sems)
    late_sum = Total(late, late_in, late_sems)
    early[0] = jnp.zeros_like(early[0])
    early[0, 0:6, :] = narrow_ref[0:6, :]
    for n in range(3):
        for part in range(4):
            row = 8 + 4 * n + part
            early[0, row : row + 1, :] = wide_ref[n : n + 1, part * width : (part + 1) * width]
    early_sum.start(0)
    got_nffn.wait()
    normed_t[...] = x_rows[...].T
    got_x = load(tokens_any.at[pl.ds(pl.multiple_of(core * rows, rows), rows)], x_rows)
    got_mixed.wait()
    mixed_t[...] = spare[...].T
    got_normed = load(normed_any, spare)
    last = [
        load(source, target)
        for source, target in ((ghid_any, ghid_ref), (wq0_any, wq0_ref), (wq1_any, wq1_ref))
    ]

    def up_out(source, k, block, target):
        up = nn(normed_t[...], source[:, k * cu : (k + 1) * cu]).astype(BF16)
        at = pl.ds(pl.multiple_of(block * co, PAIR), co)
        out = nn(mixed_t[...], gbranch[:, at]).astype(BF16)
        target[k, :, :, :, :, :cu] = up.reshape(BOX + (mine, cu))
        target[k, :, :, :, :, cu:] = out.reshape(BOX + (mine, co))

    def swap_far(k):
        return remote(far_r.at[k], first_r.at[k], (far_sems.at[0, k], far_sems.at[1, k]), sibling)

    got_far.wait()
    got_branch.wait()
    for k in range(3):
        up_out(gup_far, k, 3 * (1 - core) + k, far_r)
        swap_far(k).start()
    got_own.wait()
    for k in range(3):
        up_out(dproj, k, 3 * core + k, total_r)
    for k in range(3):
        swap_far(k).wait_recv()
    sum_r.begin(first_r)
    got_normed.wait()
    normed_t[...] = spare[...].T
    for copy in later:
        copy.wait()

    def swap_q(group):
        return swap(3 + group, far_q.at[group], first_q.at[group])

    def make(group):
        for which, target in ((1 - core, far_q), (core, total_q)):
            at = pl.ds(pl.multiple_of(group * 2 * cg + which * cg, PAIR), cg)
            grad = nn(normed_t[...], dproj[:, at]).astype(BF16)
            for n in range(3):
                target[group, n] = grad[:, n * PAIR : (n + 1) * PAIR].reshape(BOX + (mine, PAIR))
            if target is far_q:
                swap_q(group).start()

    def begin(group):
        swap_q(group).wait_recv()
        sum_q[group].begin(first_q.at[group])

    def one_pair(pair, carry):
        @pl.when(pair == 1)
        def _():
            early_sum.arrive(0)

        @pl.when(pair == 2)
        def _():
            make(0)
            sum_r.arrive(0)

        @pl.when(pair == 3)
        def _():
            begin(0)
            early_sum.arrive(1)

        @pl.when(pair == 4)
        def _():
            sum_r.arrive(1)
            make(1)

        @pl.when(pair == 5)
        def _():
            begin(1)
            sum_q[0].arrive(0)

        at_q = pl.ds(pl.multiple_of(pair * cg, PAIR), PAIR)
        at_k = pl.ds(pl.multiple_of(pair * cg + PAIR, PAIR), PAIR)
        at_v = pl.ds(pl.multiple_of(pair * cg + 2 * PAIR, PAIR), PAIR)
        at_c = pl.ds(pl.multiple_of(pair * PAIR, PAIR), PAIR)
        attend_back_pair(
            projected_ref[:, at_q], projected_ref[:, at_k], projected_ref[:, at_v], gctx_ref[:, at_c],
            context_ref[:, at_c], lse_ref.at[pair], start_ref,
            dproj.at[:, at_q], dproj.at[:, at_k], dproj.at[:, at_v], dk_acc, dv_acc,
        )
        return carry

    lax.fori_loop(0, pairs, one_pair, 0)
    make(2)
    early_sum.arrive(2)
    sum_q[0].arrive(1)
    sum_q[1].arrive(0)
    sum_r.arrive(2)
    begin(2)
    got_x.wait()
    for copy in last:
        copy.wait()
    late[0] = jnp.zeros_like(late[0])

    def row_copies(step, which):
        at = pl.ds(pl.multiple_of(step * BLOCK, BLOCK), BLOCK)
        target = grad_ref.at[which, at]
        return (pltpu.make_async_copy(near_rows.at[at], target, row_sems.at[0, step]),
                remote(far_rows.at[at], target, (row_sems.at[1, step], row_sems.at[2, step]), sibling))

    def one_block(step, carry):
        at = pl.ds(pl.multiple_of(step * BLOCK, BLOCK), BLOCK)
        gnormed = jnp.zeros((BLOCK, width), F32)
        for group in range(3):
            if group == 0:
                blocks = [wq0_ref[b].reshape(width, PAIR) for b in range(6)]
            else:
                cols = slice((group - 1) * PAIR, group * PAIR)
                blocks = [wq1_ref[(b,) + (slice(None),) * 4 + (cols,)].reshape(width, PAIR) for b in range(6)]
            weight = jnp.concatenate(blocks, axis=1)
            gnormed = gnormed + nt(dproj[at, group * 2 * cg : (group + 1) * 2 * cg], weight)
        hat, scale = normalized(x_rows[at, :].astype(F32))
        grad_x = ghid_ref[at, :].astype(F32) + norm_back(hat, scale, as_row(gain_ref), gnormed)

        @pl.when(first)
        def _():
            near_rows[at, :] = grad_x[:, :cq]
            far_rows[at, :] = grad_x[:, cq:]

        @pl.when(second)
        def _():
            near_rows[at, :] = grad_x[:, cq:]
            far_rows[at, :] = grad_x[:, :cq]

        for copy in row_copies(step, core):
            copy.start()

        late[0, 0:1, :] += col_sum(gnormed * hat)
        late[0, 1:2, :] += col_sum(gnormed)
        for row, part in ((2, 0), (3, 2)):
            grads = [dproj[at, p * cg + part * PAIR : p * cg + (part + 1) * PAIR].astype(F32) for p in range(pairs)]
            late[0, row : row + 1, :] += col_sum(jnp.concatenate(grads, axis=1))

        @pl.when(step == 1)
        def _():
            sum_q[1].arrive(1)
            sum_q[0].arrive(3)

        @pl.when(step == 3)
        def _():
            sum_q[2].arrive(0)

        return carry

    lax.fori_loop(0, rows // BLOCK, one_block, 0)
    late_sum.start(0)
    sum_q[2].arrive(1)
    late_sum.arrive(0)
    sum_r.arrive(3)
    swap_r = swap(2, final_r, other_r)
    swap_r.start()
    sum_q[1].arrive(3)
    late_sum.arrive(1)
    sum_q[2].arrive(3)
    swap_f = swap(6, final_q, other_q)
    swap_f.start()
    late_sum.arrive(2)
    swap_r.wait_recv()

    share = core * CHIPS + me.chip

    def pick(values, each):
        size = values.shape[1]
        return pltpu.roll(values, (size - share * each) % size, 1)[:, :128]

    shares = 2 * CHIPS
    sums = early[3]
    rows_of = [jnp.concatenate([sums[8 + 4 * n + part : 9 + 4 * n + part] for part in range(4)], axis=1) for n in range(3)]
    broad_ref[...] = pick(jnp.concatenate(rows_of + [jnp.zeros((5, 4 * width), F32)], axis=0), 4 * width // shares)
    slim_ref[8:16, :] = pick(sums[0:8], width // shares)
    slim_ref[0:8, :] = pick(late[3], width // shares)

    swap_f.wait_recv()

    @pl.when(first)
    def _():
        for k in range(3):
            for g in range(3):
                for c, source in ((0, final_q), (1, other_q)):
                    at = k * width + (2 * g + c) * PAIR
                    half_ref[:, at : at + PAIR] = source[g, k]
            half_ref[:, 3 * width + k * co : 3 * width + (k + 1) * co] = final_r[k, :, cu:]
            half_ref[:, 3 * width + (3 + k) * co : 3 * width + (4 + k) * co] = other_r[k, :, cu:]

    @pl.when(second)
    def _():
        for k in range(3):
            half_ref[:, k * cu : (k + 1) * cu] = other_r[k, :, :cu]
            half_ref[:, (3 + k) * cu : (4 + k) * cu] = final_r[k, :, :cu]

    for step in range(rows // BLOCK):
        near, far = row_copies(step, core)
        near.wait()
        far.wait_send()
        row_copies(step, 1 - core)[1].wait_recv()
    for done in (swap_far(0), swap_far(1), swap_far(2), swap_r, swap_f, swap_q(0), swap_q(1), swap_q(2)):
        done.wait_send()
    early_sum.drain()
    late_sum.drain()
    for each in [sum_r] + sum_q:
        each.drain()


def back(projected, gctx, context, lse, start, normed, tokens, ghid, gain, wq0, wq1, narrow, wide, nffn, mixed, gup, gbranch):
    rows, width = normed.shape
    box = BOX
    mine = width // CHIPS
    cq, cr = width // 2, 5 * width // 6
    anywhere = pl.BlockSpec(memory_space=pl.ANY)
    vmem = pl.BlockSpec(memory_space=pltpu.VMEM)
    dma = pltpu.SemaphoreType.DMA

    def held(*shape, dtype=BF16):
        return pltpu.VMEM(shape, dtype)

    return pl.pallas_call(
        back_kernel,
        in_specs=[anywhere] * 3 + [vmem] * 2 + [anywhere] * 3 + [vmem] + [anywhere] * 2 + [vmem] * 2 + [anywhere] * 4,
        out_specs=[anywhere] + [vmem] * 3,
        out_shape=[
            jax.ShapeDtypeStruct((2, rows, cq), F32),
            jax.ShapeDtypeStruct((mine, 4 * width), F32),
            jax.ShapeDtypeStruct((16, 128), F32),
            jax.ShapeDtypeStruct((8, 128), F32),
        ],
        scratch_shapes=[
            held(rows, 3 * width), held(rows, width), held(rows, width, dtype=F32), held(rows, width),
            held(*wq0.shape), held(*wq1.shape), held(rows, width), held(rows, 2 * width), held(rows, width),
            held(width, rows), held(3, *box, mine, cr),
            held(rows, width), held(rows, 3 * width), held(rows, PAIR, dtype=F32), held(rows, PAIR, dtype=F32),
            held(width, rows), held(rows, cq, dtype=F32), held(rows, cq, dtype=F32),
            held(3, *box, mine, cr), held(3, *box, mine, cr), held(MOVES, 3, mine, cr),
            held(3, mine, cr, dtype=F32), held(3, mine, cr, dtype=F32),
            held(3, 3, *box, mine, PAIR), held(3, 3, *box, mine, PAIR), held(3, 3, *box, mine, PAIR),
            held(3, MOVES, 3, mine, PAIR),
            held(3, 3, mine, PAIR, dtype=F32), held(3, 3, mine, PAIR, dtype=F32),
            held(4, 24, width, dtype=F32), held(7, 24, width, dtype=F32),
            held(4, 8, width, dtype=F32), held(7, 8, width, dtype=F32),
            dma((13,)), dma((2, 7)), dma((2, 3)), dma((2, MOVES)), dma((3, 2, MOVES)), dma((2, 7)), dma((2, 7)), dma((3, 4)),
        ],
        compiler_params=params(collective_id=2, has_side_effects=True),
        name="back",
    )(projected, gctx, context, lse, start, normed, tokens, ghid, gain, wq0, wq1, narrow, wide, nffn, mixed, gup, gbranch)


def fused_batch(tokens, out_grad, lengths, half, down, vectors):
    (pre_gain, pre_shift, query_bias, value_bias, sub_gain, sub_shift, out_bias,
     ffn_gain, ffn_shift, up_bias, mid_gain, mid_shift, down_bias) = vectors
    width = tokens.shape[1]
    (projected, normed, context, lse, start, wq0, wq1, wuo, wd, mixed, nffn, hidden, mid, hat, slope, scale, gdown) = front(
        tokens, out_grad, lengths, half, down,
        (pre_gain, pre_shift, query_bias, value_bias, sub_gain, sub_shift, out_bias, ffn_gain, ffn_shift, up_bias,
         mid_gain, mid_shift),
    )
    ghid, gctx, gbranch, gup, narrow, wide, layer, down_grad = feed(
        out_grad, context, hidden, mid, hat, slope, scale, lengths, wuo.reshape(6, width, -1), wd.reshape(6, width, -1),
        (sub_gain, ffn_gain, mid_gain, down_bias), gdown,
    )
    grad_x, half_grad, slim, broad = back(
        projected, gctx, context, lse, start, normed, tokens, ghid, pre_gain, wq0, wq1, narrow, wide,
        nffn, mixed, gup, gbranch,
    )
    shares = 2 * CHIPS
    layer, grad_x, half_grad, down_grad, *small = finish(
        layer.reshape(-1, width), grad_x.reshape(-1, width // 2), half_grad, down_grad, slim, broad,
        width // shares, 4 * width // shares,
    )
    return layer, grad_x, half_grad[None], down_grad, *small[:9], *small[10:], small[9]


def unpacked(vectors):
    return [vector[None, :] for vector in vectors]


def marks_and_bias(x, lengths_row, query_bias, value_bias):
    alive, start = row_marks(lengths_row, x.shape[0])
    bias = jnp.concatenate([query_bias, jnp.zeros_like(query_bias), value_bias], axis=1)
    return alive, start, bias


def one_batch(x, dy, lengths_row, qkv, rest, vectors):
    (pre_gain, pre_shift, query_bias, value_bias, sub_gain, sub_shift, out_bias,
     ffn_gain, ffn_shift, up_bias, mid_gain, mid_shift, down_bias) = unpacked(vectors)
    alive, start, bias = marks_and_bias(x, lengths_row, query_bias, value_bias)
    projected, normed = project(x, qkv, pre_gain, pre_shift, bias)
    context, lse = attend(projected, start)
    out, ghid, gctx, mixed, gbranch, nffn, gup, mid, gffn, narrow, wide = middle(
        x, dy, context, alive, rest,
        (sub_gain, sub_shift, out_bias, ffn_gain, ffn_shift, up_bias, mid_gain, mid_shift, down_bias),
    )
    grad_up = outer(nffn, gup, 256, F32, "outer_up")
    grad_down = outer(mid, gffn, 512, F32, "outer_down")
    dq, dk, dv = attend_back(projected, gctx, context, lse, start)
    grad_out = outer(mixed, gbranch, 256, F32, "outer_out")
    grad_x, pre = project_back(dq, dk, dv, qkv, x, ghid, pre_gain)
    grads = [outer(normed, d, 256, F32, "outer_qkv") for d in (dq, dk, dv)]
    grad_attention = jnp.concatenate(grads + [grad_out], axis=1)
    small = (pre[0], pre[1], pre[2], pre[3], narrow[0], narrow[1], narrow[2], narrow[3], narrow[4],
             wide[0], wide[1], wide[2], narrow[5])
    return (out, grad_x), (grad_attention, grad_up, grad_down, small)


def shards(tokens, out_grad, seq_lengths, half_weights, down_weight, *all_vectors):
    section = lax.axis_index("section")
    sections = lax.axis_size("section")
    both = ("section", "dp")
    width = tokens.shape[1]
    batches = seq_lengths.shape[0]
    count = tokens.shape[0] // batches
    own_batches = batches // sections
    own_rows = own_batches * count
    hidden_units = half_weights.shape[2]
    shares = sections * lax.axis_size("dp")

    if (
        sections == 2
        and shares == sections * CHIPS
        and own_batches == 1
        and half_weights.shape[1] % 16 == 0
        and down_weight.shape[0] == 2 * half_weights.shape[1]
        and hidden_units == 4 * width
    ):
        return fused_batch(tokens, out_grad, seq_lengths, half_weights[0], down_weight, all_vectors)

    def own(array, rows):
        return lax.dynamic_slice_in_dim(array, section * rows, rows, axis=0)

    x_rows = own(tokens, own_rows)
    dy_rows = own(out_grad, own_rows)
    lengths = own(seq_lengths, own_batches)
    blocks = lax.all_gather(half_weights[0], both, axis=0, tiled=True)
    blocks = blocks.reshape(sections, width, hidden_units)
    down_full = lax.all_gather(down_weight, both, axis=0, tiled=True)
    qkv = blocks[0][:, : 3 * width]

    def in_blocks(array):
        return array.reshape(array.shape[0], 6, -1).transpose(1, 0, 2)

    down_blocks = down_full.reshape(2, CHIPS, 2, width // CHIPS, 3, width // 3).transpose(0, 4, 1, 3, 2, 5)
    down_blocks = down_blocks.reshape(6, width, 2 * width // 3)
    rest = jnp.concatenate([in_blocks(blocks[1]), in_blocks(blocks[0][:, 3 * width :]), down_blocks], axis=2)
    rows, sums = [], None
    for index in range(own_batches):
        at = slice(index * count, (index + 1) * count)
        row, more = one_batch(x_rows[at], dy_rows[at], lengths[index], qkv, rest, all_vectors)
        rows.append(row)
        sums = more if sums is None else jax.tree.map(jnp.add, sums, more)
    out_block = jnp.concatenate([row[0] for row in rows], axis=0)
    grad_rows = jnp.concatenate([row[1] for row in rows], axis=0)
    grad_attention, grad_up, grad_down, vectors = sums

    block_part = lax.psum_scatter(
        jnp.concatenate([grad_attention, grad_up], axis=0), both, scatter_dimension=0, tiled=True
    )
    down_part = lax.psum_scatter(grad_down, both, scatter_dimension=0, tiled=True)
    packed = jnp.concatenate([vector.reshape(shares, -1) for vector in vectors], axis=1)
    packed = lax.psum_scatter(packed, both, scatter_dimension=0, tiled=True).reshape(-1)
    parts, start = [], 0
    for vector in vectors:
        size = vector.shape[0] // shares
        parts.append(packed[start : start + size])
        start += size

    layer_out = lax.all_gather(out_block, "section", axis=0, tiled=True)
    tokens_grad = lax.all_to_all(grad_rows, "section", split_axis=1, concat_axis=0, tiled=True)
    return (layer_out, tokens_grad, block_part[None], down_part, *parts)


def solution(mesh):
    replicated = P()
    return jax.shard_map(
        shards,
        mesh=mesh,
        in_specs=(P("dp", None), P("dp", None), P("dp", None), P("section", "dp", None), P(("section", "dp"), None))
        + (replicated,) * 13,
        out_specs=(P("dp", None), P("dp", "section"), P("section", "dp", None), P(("section", "dp"), None))
        + (P(("section", "dp")),) * 13,
        check_vma=False,
    )
```

```python
import functools
import math

import jax
import jax.numpy as jnp
from jax import lax
from jax.experimental import pallas as pl
from jax.experimental.pallas import tpu as pltpu
from jax.sharding import PartitionSpec as P

HEAD_DIM = 64
PAIR = 2 * HEAD_DIM
EPS = 1e-05
BLOCK = 256
F32 = jnp.float32
BF16 = jnp.bfloat16
VMEM_LIMIT = 60 * 1024 * 1024


def nn(left, right):
    return lax.dot_general(left, right, (((1,), (0,)), ((), ())), preferred_element_type=F32)


def nt(left, right):
    return lax.dot_general(left, right, (((1,), (1,)), ((), ())), preferred_element_type=F32)


def tn(left, right):
    return lax.dot_general(left, right, (((0,), (0,)), ((), ())), preferred_element_type=F32)


def col_sum(value):
    return jnp.sum(value, axis=0, keepdims=True)


def normalized(value):
    center = jnp.mean(value, axis=-1, keepdims=True)
    centered = value - center
    spread = jnp.mean(centered * centered, axis=-1, keepdims=True)
    scale = lax.rsqrt(spread + EPS)
    return centered * scale, scale


def norm_back(hat, scale, gain, upstream):
    scaled = upstream * gain
    first = jnp.mean(scaled, axis=-1, keepdims=True)
    second = jnp.mean(scaled * hat, axis=-1, keepdims=True)
    return (scaled - first - hat * second) * scale


def params(**more):
    return pltpu.CompilerParams(vmem_limit_bytes=VMEM_LIMIT, **more)


def split_rest(ref):
    _, width, columns = ref.shape
    cu, co, cd = 4 * columns // 9, columns // 9, 2 * columns // 9
    up = jnp.concatenate([ref[b, :, :cu] for b in range(6)], axis=1)
    out = jnp.concatenate([ref[b, :, cu : cu + co] for b in range(6)], axis=1)
    halves = []
    for h in range(2):
        parts = []
        for n in range(2):
            at = cu + co + n * cd
            part = jnp.concatenate([ref[3 * h + k, :, at : at + cd] for k in range(3)], axis=1)
            parts.append(part.reshape(CHIPS, 1, width // CHIPS, width))
        halves.append(jnp.concatenate(parts, axis=1).reshape(2 * width, width))
    return out, up, jnp.concatenate(halves, axis=0)


def whole(shape):
    return pl.BlockSpec(shape, lambda *_: (0,) * len(shape))


def project_kernel(x_ref, w_ref, gain_ref, shift_ref, bias_ref, out_ref, normed_ref):
    hat, _ = normalized(x_ref[...].astype(F32))
    normed = (hat * gain_ref[...] + shift_ref[...]).astype(BF16)
    normed_ref[...] = normed
    out_ref[...] = (nn(normed, w_ref[...]) + bias_ref[...]).astype(BF16)


def project(x, weight, gain, shift, bias):
    rows, width = x.shape
    return pl.pallas_call(
        project_kernel,
        grid=(rows // BLOCK,),
        in_specs=[
            pl.BlockSpec((BLOCK, width), lambda i: (i, 0)),
            whole((width, 3 * width)),
            whole((1, width)),
            whole((1, width)),
            whole((1, 3 * width)),
        ],
        out_specs=[
            pl.BlockSpec((BLOCK, 3 * width), lambda i: (i, 0)),
            pl.BlockSpec((BLOCK, width), lambda i: (i, 0)),
        ],
        out_shape=[
            jax.ShapeDtypeStruct((rows, 3 * width), BF16),
            jax.ShapeDtypeStruct((rows, width), BF16),
        ],
        compiler_params=params(),
        name="project",
    )(x, weight, gain, shift, bias)


def allowed_mask(start, key_at, keys, queries):
    key = key_at + lax.broadcasted_iota(jnp.int32, (keys, queries), 0)
    return key >= start


def head_rows(pair_t, head):
    row = lax.broadcasted_iota(jnp.int32, pair_t.shape, 0)
    mine = (row < HEAD_DIM) if head == 0 else (row >= HEAD_DIM)
    return jnp.where(mine, pair_t, jnp.zeros_like(pair_t))


def head_cols(pair, head):
    col = lax.broadcasted_iota(jnp.int32, pair.shape, 1)
    mine = (col < HEAD_DIM) if head == 0 else (col >= HEAD_DIM)
    return jnp.where(mine, pair, jnp.zeros_like(pair))


def score_parts(key, query_t, start, block):
    before = block * BLOCK
    parts = []
    if block:
        index = lax.broadcasted_iota(jnp.int32, (before, BLOCK), 0)
        parts.append((slice(0, before), jnp.where(index >= start, nn(key[:before], query_t), -1e30)))
    index = lax.broadcasted_iota(jnp.int32, (BLOCK, BLOCK), 0)
    last = lax.broadcasted_iota(jnp.int32, (BLOCK, BLOCK), 1)
    ok = (index >= start - before) & (index <= last)
    own = slice(before, before + BLOCK)
    parts.append((own, jnp.where(ok, nn(key[own], query_t), -1e30)))
    return parts


def attend_pair(query, key, value, start_ref, out_ref, lse_ref):
    query_t = (query.astype(F32) * HEAD_DIM**-0.5).T.astype(BF16)
    value_t = value.astype(F32).T.astype(BF16)
    for block in range(query.shape[0] // BLOCK):
        at = slice(block * BLOCK, (block + 1) * BLOCK)
        start = start_ref[:, at]
        outs = []
        for head in range(2):
            lanes = slice(head * HEAD_DIM, (head + 1) * HEAD_DIM)
            parts = score_parts(key, head_rows(query_t[:, at], head), start, block)
            peak = functools.reduce(jnp.maximum, [jnp.max(scores, axis=0, keepdims=True) for _, scores in parts])
            total = jnp.zeros((1, BLOCK), F32)
            out = jnp.zeros((HEAD_DIM, BLOCK), F32)
            for keys, scores in parts:
                raised = jnp.exp(scores - peak)
                total = total + col_sum(raised)
                out = out + nn(value_t[lanes, keys], raised.astype(BF16))
            outs.append(out * (1.0 / total))
            lse_ref[head : head + 1, at] = peak + jnp.log(total)
        out_ref[at, :] = jnp.concatenate(outs, axis=0).T


def attend_kernel(q_ref, k_ref, v_ref, start_ref, out_ref, lse_ref):
    attend_pair(q_ref[...], k_ref[...], v_ref[...], start_ref, out_ref, lse_ref.at[0])


def attend(projected, start):
    rows, columns = projected.shape
    width = columns // 3
    pairs = width // PAIR
    return pl.pallas_call(
        attend_kernel,
        grid=(pairs,),
        in_specs=[
            pl.BlockSpec((rows, PAIR), lambda p: (0, p)),
            pl.BlockSpec((rows, PAIR), lambda p: (0, pairs + p)),
            pl.BlockSpec((rows, PAIR), lambda p: (0, 2 * pairs + p)),
            whole((1, rows)),
        ],
        out_specs=[
            pl.BlockSpec((rows, PAIR), lambda p: (0, p)),
            pl.BlockSpec((1, 2, rows), lambda p: (p, 0, 0)),
        ],
        out_shape=[
            jax.ShapeDtypeStruct((rows, width), F32),
            jax.ShapeDtypeStruct((pairs, 2, rows), F32),
        ],
        compiler_params=params(),
        name="attend",
    )(projected, projected, projected, start)


def attend_back_pair(query, key, value, grad, context, lse_ref, start_ref, dq_ref, dk_ref, dv_ref, dk_acc, dv_acc):
    scale = HEAD_DIM**-0.5
    scaled = query.astype(F32) * scale
    query = scaled.astype(BF16)
    query_t = scaled.T.astype(BF16)
    key_t = key.astype(F32).T.astype(BF16)
    grad_f = grad.astype(F32)
    grad_t = grad_f.T.astype(BF16)
    weighted_t = (grad_f * context).T
    dk_acc[...] = jnp.zeros_like(dk_acc)
    dv_acc[...] = jnp.zeros_like(dv_acc)
    for block in range(query.shape[0] // BLOCK):
        at = slice(block * BLOCK, (block + 1) * BLOCK)
        start = start_ref[:, at]
        outs = []
        for head in range(2):
            lanes = slice(head * HEAD_DIM, (head + 1) * HEAD_DIM)
            inner = col_sum(weighted_t[lanes, at])
            log_total = lse_ref[head : head + 1, at]
            grad_head = head_rows(grad_t[:, at], head)
            out = jnp.zeros((HEAD_DIM, BLOCK), F32)
            for keys, scores in score_parts(key, head_rows(query_t[:, at], head), start, block):
                soft = jnp.exp(scores - log_total)
                grad_scores = (soft * (nn(value[keys], grad_head) - inner)).astype(BF16)
                dv_acc[keys, :] += nn(soft.astype(BF16), head_cols(grad[at], head))
                dk_acc[keys, :] += nn(grad_scores, head_cols(query[at], head))
                out = out + nn(key_t[lanes, keys], grad_scores)
            outs.append(out)
        dq_ref[at, :] = (jnp.concatenate(outs, axis=0) * scale).T.astype(BF16)
    dk_ref[...] = dk_acc[...].astype(BF16)
    dv_ref[...] = dv_acc[...].astype(BF16)


def attend_back_kernel(q_ref, k_ref, v_ref, g_ref, o_ref, lse_ref, start_ref, dq_ref, dk_ref, dv_ref, dk_acc, dv_acc):
    attend_back_pair(
        q_ref[...], k_ref[...], v_ref[...], g_ref[...], o_ref[...], lse_ref.at[0], start_ref,
        dq_ref, dk_ref, dv_ref, dk_acc, dv_acc,
    )


def attend_back(projected, grad_context, context, lse, start):
    rows, columns = projected.shape
    width = columns // 3
    pairs = width // PAIR
    pair = pl.BlockSpec((rows, PAIR), lambda p: (0, p))
    return pl.pallas_call(
        attend_back_kernel,
        grid=(pairs,),
        in_specs=[
            pair,
            pl.BlockSpec((rows, PAIR), lambda p: (0, pairs + p)),
            pl.BlockSpec((rows, PAIR), lambda p: (0, 2 * pairs + p)),
            pair,
            pair,
            pl.BlockSpec((1, 2, rows), lambda p: (p, 0, 0)),
            whole((1, rows)),
        ],
        out_specs=[pair] * 3,
        out_shape=[jax.ShapeDtypeStruct((rows, width), BF16)] * 3,
        scratch_shapes=[pltpu.VMEM((rows, PAIR), F32), pltpu.VMEM((rows, PAIR), F32)],
        compiler_params=params(),
        name="attend_back",
    )(projected, projected, projected, grad_context, context, lse, start)


def gelu_parts(value):
    phi = 0.5 * (1.0 + lax.erf(value * (1.0 / math.sqrt(2.0))))
    bell = jnp.exp(-0.5 * value * value) * (1.0 / math.sqrt(2.0 * math.pi))
    return value * phi, phi + value * bell


def middle_kernel(
    x_ref, dy_ref, ctx_ref, alive_ref, rest_ref,
    sg_ref, ss_ref, ob_ref, fg_ref, fs_ref, ub_ref, mg_ref, ms_ref, db_ref,
    out_ref, ghid_ref, gctx_ref, mixed_ref, gbranch_ref, nffn_ref, gup_ref, mid_ref, gffn_ref,
    narrow_ref, wide_ref,
):
    step = pl.program_id(0)

    @pl.when(step == 0)
    def _():
        narrow_ref[...] = jnp.zeros_like(narrow_ref)
        wide_ref[...] = jnp.zeros_like(wide_ref)

    out_weight, up_weight, down_weight = split_rest(rest_ref)
    alive = alive_ref[...]
    ctx_hat, ctx_scale = normalized(ctx_ref[...])
    mixed = (ctx_hat * sg_ref[...] + ss_ref[...]).astype(BF16)
    mixed_ref[...] = mixed
    branch = nn(mixed, out_weight) + ob_ref[...]
    hidden = (x_ref[...].astype(F32) + alive * branch).astype(BF16).astype(F32)
    hid_hat, hid_scale = normalized(hidden)
    nffn = (hid_hat * fg_ref[...] + fs_ref[...]).astype(BF16)
    nffn_ref[...] = nffn
    upper = nn(nffn, up_weight) + ub_ref[...]
    active, slope = gelu_parts(upper)
    act_hat, act_scale = normalized(active)
    mid = (act_hat * mg_ref[...] + ms_ref[...]).astype(BF16)
    mid_ref[...] = mid
    result = (nn(mid, down_weight) + db_ref[...]).astype(BF16).astype(F32)
    out_ref[...] = hidden + alive * result

    upstream = dy_ref[...].astype(F32)
    gffn = (alive * upstream).astype(BF16)
    gffn_ref[...] = gffn
    gmid = nt(gffn, down_weight)
    gact = norm_back(act_hat, act_scale, mg_ref[...], gmid)
    gup = (gact * slope).astype(BF16)
    gup_ref[...] = gup
    wide_ref[0:1, :] += col_sum(gup.astype(F32))
    wide_ref[1:2, :] += col_sum(gmid * act_hat)
    wide_ref[2:3, :] += col_sum(gmid)
    gnffn = nt(gup, up_weight)
    ghid = (upstream + norm_back(hid_hat, hid_scale, fg_ref[...], gnffn)).astype(BF16)
    ghid_ref[...] = ghid
    gbranch = (alive * ghid.astype(F32)).astype(BF16)
    gbranch_ref[...] = gbranch
    gmixed = nt(gbranch, out_weight)
    gctx_ref[...] = norm_back(ctx_hat, ctx_scale, sg_ref[...], gmixed).astype(BF16)
    narrow_ref[0:1, :] += col_sum(gmixed * ctx_hat)
    narrow_ref[1:2, :] += col_sum(gmixed)
    narrow_ref[2:3, :] += col_sum(gbranch.astype(F32))
    narrow_ref[3:4, :] += col_sum(gnffn * hid_hat)
    narrow_ref[4:5, :] += col_sum(gnffn)
    narrow_ref[5:6, :] += col_sum(gffn.astype(F32))


def middle(x, dy, context, alive, rest, vectors):
    rows, width = x.shape
    hidden = 4 * width
    row = pl.BlockSpec((BLOCK, width), lambda i: (i, 0))
    row_wide = pl.BlockSpec((BLOCK, hidden), lambda i: (i, 0))
    once = dict(pipeline_mode=pl.Buffered(1))
    narrow = whole((1, width))
    wide = whole((1, hidden))
    def shape(columns, dtype):
        return jax.ShapeDtypeStruct((rows, columns), dtype)
    return pl.pallas_call(
        middle_kernel,
        grid=(rows // BLOCK,),
        in_specs=[
            row, row, row,
            pl.BlockSpec((BLOCK, 1), lambda i: (i, 0)),
            pl.BlockSpec(rest.shape, lambda i: (0, 0, 0), **once),
            narrow, narrow, narrow, narrow, narrow, wide, wide, wide, narrow,
        ],
        out_specs=[row, row, row, row, row, row, row_wide, row_wide, row, whole((8, width)), whole((8, hidden))],
        out_shape=[
            shape(width, F32), shape(width, BF16), shape(width, BF16), shape(width, BF16), shape(width, BF16),
            shape(width, BF16), shape(hidden, BF16), shape(hidden, BF16), shape(width, BF16),
            jax.ShapeDtypeStruct((8, width), F32), jax.ShapeDtypeStruct((8, hidden), F32),
        ],
        compiler_params=params(),
        name="middle",
    )(x, dy, context, alive, rest, *vectors)


def outer_kernel(left_ref, right_ref, out_ref):
    out_ref[...] = tn(left_ref[...], right_ref[...]).astype(out_ref.dtype)


def outer(left, right, tile, dtype, name):
    rows, across = left.shape
    columns = right.shape[1]
    return pl.pallas_call(
        outer_kernel,
        grid=(across // tile,),
        in_specs=[pl.BlockSpec((rows, tile), lambda i: (0, i)), whole((rows, columns))],
        out_specs=pl.BlockSpec((tile, columns), lambda i: (i, 0)),
        out_shape=jax.ShapeDtypeStruct((across, columns), dtype),
        compiler_params=params(),
        name=name,
    )(left, right)


def project_back_kernel(dq_ref, dk_ref, dv_ref, w_ref, x_ref, ghid_ref, gain_ref, out_ref, narrow_ref):
    step = pl.program_id(0)
    width = x_ref.shape[1]

    @pl.when(step == 0)
    def _():
        narrow_ref[...] = jnp.zeros_like(narrow_ref)

    dq, dk, dv = dq_ref[...], dk_ref[...], dv_ref[...]
    gnormed = nt(dq, w_ref[:, :width]) + nt(dk, w_ref[:, width : 2 * width]) + nt(dv, w_ref[:, 2 * width :])
    hat, scale = normalized(x_ref[...].astype(F32))
    out_ref[...] = ghid_ref[...].astype(F32) + norm_back(hat, scale, gain_ref[...], gnormed)
    narrow_ref[0:1, :] += col_sum(gnormed * hat)
    narrow_ref[1:2, :] += col_sum(gnormed)
    narrow_ref[2:3, :] += col_sum(dq.astype(F32))
    narrow_ref[3:4, :] += col_sum(dv.astype(F32))


def project_back(dq, dk, dv, weight, x, ghid, gain):
    rows, width = x.shape
    row = pl.BlockSpec((BLOCK, width), lambda i: (i, 0))
    return pl.pallas_call(
        project_back_kernel,
        grid=(rows // BLOCK,),
        in_specs=[row, row, row, whole(weight.shape), row, row, whole((1, width))],
        out_specs=[row, whole((8, width))],
        out_shape=[jax.ShapeDtypeStruct((rows, width), F32), jax.ShapeDtypeStruct((8, width), F32)],
        compiler_params=params(),
        name="project_back",
    )(dq, dk, dv, weight, x, ghid, gain)


def row_marks(lengths_row, count):
    slots = jnp.arange(lengths_row.shape[0], dtype=jnp.int32)
    ends = jnp.sum(jnp.where(slots[:, None] <= slots[None, :], lengths_row[:, None], 0), axis=0)
    index = jnp.arange(count, dtype=jnp.int32)
    before = jnp.where(ends[None, :] <= index[:, None], ends[None, :], 0)
    alive = index < jnp.max(ends)
    start = jnp.where(alive, jnp.max(before, axis=1), index)
    return alive.astype(F32)[:, None], start[None, :]


MESH = pl.DeviceIdType.MESH
BOX = (4, 2, 2)
CHIPS = 16
X_AT, Y_AT, D_AT, MOVES = 3, 7, 11, 15


class Place:
    def __init__(self):
        self.core = lax.axis_index("section")
        self.chip = lax.axis_index("dp")
        self.z, self.y, self.x = self.chip // 4, (self.chip // 2) % 2, self.chip % 2
        high, low = self.z // 2, self.z % 2
        self.zs = [self.z, self.z + 1 - 2 * low, self.z + 2 - 4 * high, 3 - self.z]

    def at(self, z, y, x):
        return (self.core, z * 4 + y * 2 + x)

    def sibling(self):
        return (1 - self.core, self.chip)

    def over_z(self, k):
        return self.at(self.zs[k], self.y, self.x)

    def over_y(self):
        return self.at(self.z, 1 - self.y, self.x)

    def over_x(self):
        return self.at(self.z, self.y, 1 - self.x)

    def across(self):
        return self.at(self.z, 1 - self.y, 1 - self.x)


def remote(source, target, sems, device):
    return pltpu.make_async_remote_copy(
        src_ref=source, dst_ref=target, send_sem=sems[0], recv_sem=sems[1], device_id=device, device_id_type=MESH
    )


def greet(me):
    barrier = pltpu.get_barrier_semaphore()
    others = [me.sibling(), me.over_x(), me.over_y(), me.across()] + [me.over_z(k) for k in (1, 2, 3)]
    for other in others:
        pl.semaphore_signal(barrier, inc=1, device_id=other, device_id_type=MESH)
    pl.semaphore_wait(barrier, len(others))


class Gather:
    def __init__(self, full, sems, pass_sems, direct=False):
        self.me = Place()
        self.direct = direct
        self.own = full.at[pl.ds(3 * self.me.core, 3)]
        self.other = full.at[pl.ds(3 * (1 - self.me.core), 3)]
        self.sems, self.pass_sems = sems, pass_sems

    def move(self, index, z, y, x, device):
        part = self.own.at[:, z, y, x]
        return remote(part, part, (self.sems.at[0, index], self.sems.at[1, index]), device)

    def to_z(self, k):
        me = self.me
        return self.move(k - 1, me.z, me.y, me.x, me.over_z(k))

    def to_x(self, k):
        me = self.me
        return self.move(X_AT + k, me.zs[k], me.y, me.x, me.over_x())

    def to_y(self, k):
        me = self.me
        return self.move(Y_AT + k, me.zs[k], me.y, me.x, me.over_y())

    def onward(self, k):
        me = self.me
        if self.direct:
            return self.move(D_AT + k, me.zs[k], me.y, me.x, me.across())
        if k < 2:
            return self.move(D_AT + k, me.zs[k], me.y, 1 - me.x, me.over_y())
        return self.move(D_AT + k, me.zs[k], 1 - me.y, me.x, me.over_x())

    def across_core(self, index, ref):
        me = self.me
        every = slice(None)
        place = [(every, me.y, 1 - me.x), (every, 1 - me.y, me.x), (every, 1 - me.y, 1 - me.x)]
        z, y, x = (me.zs[index + 1], me.y, me.x) if index < 3 else place[index - 3]
        part = ref.at[:, z, y, x]
        return remote(part, part, (self.pass_sems.at[0, index], self.pass_sems.at[1, index]), me.sibling())

    def launch(self):
        for k in (1, 2, 3):
            self.to_z(k).start()
        self.spread(0)

    def spread(self, k):
        self.to_x(k).start()
        self.to_y(k).start()
        if self.direct:
            self.onward(k).start()

    def from_z(self, k):
        self.to_z(k).wait_recv()
        self.spread(k)
        self.across_core(k - 1, self.own).start()

    def arrive(self, stage):
        if stage == 0:
            self.from_z(1)
            self.to_x(0).wait_recv()
            if not self.direct:
                self.onward(0).start()
        elif stage == 1:
            self.from_z(2)
            self.from_z(3)
            self.to_x(1).wait_recv()
            if not self.direct:
                self.onward(1).start()
        elif stage == 2:
            for k in (2, 3):
                self.to_y(k).wait_recv()
                if not self.direct:
                    self.onward(k).start()
            for k in (2, 3):
                self.to_x(k).wait_recv()
            for k in (0, 1):
                self.to_y(k).wait_recv()
            self.across_core(3, self.own).start()
            self.across_core(4, self.own).start()
        else:
            for k in range(4):
                self.onward(k).wait_recv()
            self.across_core(5, self.own).start()

    def passed(self):
        for index in range(6):
            self.across_core(index, self.other).wait_recv()

    def drain(self):
        for k in (1, 2, 3):
            self.to_z(k).wait_send()
        for k in range(4):
            for move in (self.to_x(k), self.to_y(k), self.onward(k)):
                move.wait_send()
        for index in range(6):
            self.across_core(index, self.own).wait_send()


def seed(parts, sems):
    me = Place()
    moves = []
    for index, (source, full, block, cols) in enumerate(parts):
        here = full.at[block, me.z, me.y, me.x, :, cols]
        local = pltpu.make_async_copy(source, here, sems.at[0, index])
        far = remote(source, here, (sems.at[1, index], sems.at[2, index]), me.sibling())
        moves.append((local, far))

    def begin():
        for local, far in moves:
            local.start()
            far.start()

    def sent():
        for local, far in moves:
            local.wait()
            far.wait_send()

    def got():
        for _, far in moves:
            far.wait_recv()

    return begin, sent, got


def lane_groups(value):
    groups = [value[:, at : at + 128] for at in range(0, value.shape[1], 128)]
    return functools.reduce(jnp.add, groups)


def as_row(ref):
    return ref[...].reshape(1, -1)


def lengths_of(lengths_ref, core):
    return [lengths_ref[core, slot] for slot in range(lengths_ref.shape[1])]


def alive_rows(lengths_ref, core, at, rows):
    index = at + lax.broadcasted_iota(jnp.int32, (rows, 1), 0)
    return (index < sum(lengths_of(lengths_ref, core))).astype(F32)


def start_row(lengths_ref, core, count):
    index = lax.broadcasted_iota(jnp.int32, (1, count), 1)
    start = jnp.zeros((1, count), jnp.int32)
    end = jnp.int32(0)
    for length in lengths_of(lengths_ref, core):
        end = end + length
        start = jnp.where(index >= end, end, start)
    return jnp.where(index < end, start, index)


def front_kernel(
    tokens_ref, upstream_ref, lengths_ref, half_ref, down_ref,
    pg_ref, ps_ref, qb_ref, vb_ref, sg_ref, ss_ref, ob_ref, fg_ref, fs_ref, ub_ref, mg_ref, ms_ref,
    projected_out, normed_out, context_out, lse_out, start_out, wq0_out, wq1_out, wuo_out, wd_ref,
    mixed_out, nffn_out, hidden_out, mid_out, hat_out, slope_out, scale_out, gdown_out,
    hidden, gffn, broad, hat, mid, normed, mixed, context, lse, start, wq0, wq1, wuo, mid_t, gdown, scales, active,
    seed_q0, seed_q1, seed_o, seed_u, seed_d, chain_q0, chain_q1, chain_u, chain_d, pass_q0, pass_q1, pass_u, pass_d,
    load_sems, save_sems, row_sems, grad_sems,
):
    me = Place()
    core = me.core
    rows, width = hidden.shape
    mine = half_ref.shape[0]
    pairs = width // PAIR
    co, cu, cd = width // 6, 2 * width // 3, width // 3
    cg = 3 * PAIR
    first = core == 0
    second = core == 1
    box = (slice(None),) * 3

    def group_parts(full, groups):
        return [
            (half_ref.at[:, n * width + (2 * g + c) * PAIR : n * width + (2 * g + c + 1) * PAIR],
             full, 3 * c + n, slice(at * PAIR, (at + 1) * PAIR))
            for at, g in enumerate(groups) for c in range(2) for n in range(3)
        ]

    q0_begin, q0_sent, q0_got = seed(group_parts(wq0, [0]), seed_q0)
    q1_begin, q1_sent, q1_got = seed(group_parts(wq1, [1, 2]), seed_q1)
    o_begin, o_sent, o_got = seed(
        [(half_ref.at[:, 3 * width + b * co : 3 * width + (b + 1) * co],
          wuo, b, slice(cu, cu + co)) for b in range(6)], seed_o)
    u_begin, u_sent, u_got = seed(
        [(half_ref.at[:, b * cu : (b + 1) * cu],
          wuo, b, slice(0, cu)) for b in range(6)], seed_u)

    def down_parts(which):
        return [
            (down_ref.at[n * mine : (n + 1) * mine, k * cd : (k + 1) * cd],
             wd_ref, 3 * which + k, slice(n * cd, (n + 1) * cd))
            for k in range(3) for n in range(2)
        ]

    d_begin, d_sent, _ = seed(down_parts(core), seed_d)
    _, _, d_got = seed(down_parts(1 - core), seed_d)

    gather_q0 = Gather(wq0, chain_q0, pass_q0, direct=True)
    gather_q1 = Gather(wq1, chain_q1, pass_q1)
    gather_u = Gather(wuo, chain_u, pass_u)
    gather_d = Gather(wd_ref, chain_d, pass_d)

    own_rows = pl.ds(pl.multiple_of(core * rows, rows), rows)
    loads = [
        pltpu.make_async_copy(tokens_ref.at[own_rows], hidden, load_sems.at[0]),
        pltpu.make_async_copy(upstream_ref.at[own_rows], gffn, load_sems.at[1]),
    ]
    loads[0].start()
    greet(me)
    pl.when(first)(q0_begin)
    pl.when(first)(q1_begin)
    pl.when(first)(o_begin)
    pl.when(second)(u_begin)
    d_begin()
    loads[1].start()
    pl.when(first)(q0_sent)
    pl.when(second)(q0_got)
    gather_q0.launch()

    loads[0].wait()
    value, _ = normalized(hidden[...].astype(F32))
    normed[...] = (value * as_row(pg_ref) + as_row(ps_ref)).astype(BF16)
    start[...] = start_row(lengths_ref, core, rows)
    saves = []

    def save(source, target):
        saves.append(pltpu.make_async_copy(source, target, save_sems.at[len(saves)]))
        saves[-1].start()

    save(normed, normed_out)
    save(start, start_out)
    @pl.when(first)
    def _():
        q1_sent()
        o_sent()
        u_got()

    @pl.when(second)
    def _():
        u_sent()
        q1_got()
        o_got()

    gather_q0.arrive(0)
    gather_q1.launch()
    gather_q0.arrive(1)
    gather_u.launch()
    gather_q0.arrive(2)
    gather_q1.arrive(0)
    gather_q0.arrive(3)
    d_sent()
    d_got()
    gather_q0.passed()

    query_bias, value_bias = as_row(qb_ref), as_row(vb_ref)

    def project_group(group, weights):
        biases = []
        for c in range(2):
            at = slice((2 * group + c) * PAIR, (2 * group + c + 1) * PAIR)
            biases += [query_bias[:, at], jnp.zeros((1, PAIR), F32), value_bias[:, at]]
        cols = slice(group * 2 * cg, (group + 1) * 2 * cg)
        weight = jnp.concatenate(weights, axis=1)
        broad[:, cols] = (nn(normed[...], weight) + jnp.concatenate(biases, axis=1)).astype(BF16)

    project_group(0, [wq0[b].reshape(width, PAIR) for b in range(6)])
    gather_q1.arrive(1)

    def one_pair(pair, carry):
        @pl.when(pair == 0)
        def _():
            gather_u.arrive(0)

        @pl.when(pair == 1)
        def _():
            gather_q1.arrive(2)

        @pl.when(pair == 2)
        def _():
            gather_q1.arrive(3)
            gather_q1.passed()
            gather_u.arrive(1)
            for group in range(1, 3):
                at = slice((group - 1) * PAIR, group * PAIR)
                project_group(group, [wq1[(b, *box, slice(None), at)].reshape(width, PAIR) for b in range(6)])
            pltpu.make_async_copy(broad.at[:, : 3 * width], projected_out, load_sems.at[0]).start()

        @pl.when(pair == 3)
        def _():
            gather_d.launch()

        @pl.when(pair == 4)
        def _():
            gather_u.arrive(2)

        @pl.when(pair == 5)
        def _():
            gather_d.arrive(0)

        at_q = pl.ds(pl.multiple_of(pair * cg, PAIR), PAIR)
        at_k = pl.ds(pl.multiple_of(pair * cg + PAIR, PAIR), PAIR)
        at_v = pl.ds(pl.multiple_of(pair * cg + 2 * PAIR, PAIR), PAIR)
        at_out = pl.ds(pl.multiple_of(pair * PAIR, PAIR), PAIR)
        attend_pair(broad[:, at_q], broad[:, at_k], broad[:, at_v], start, context.at[:, at_out], lse.at[pair])
        return carry

    lax.fori_loop(0, pairs, one_pair, 0)
    save(context, context_out)
    save(lse, lse_out)
    save(wq0, wq0_out)
    save(wq1, wq1_out)
    gather_u.arrive(3)
    gather_u.passed()
    save(wuo, wuo_out)
    loads[1].wait()
    pltpu.make_async_copy(broad.at[:, : 3 * width], projected_out, load_sems.at[0]).wait()
    saves[0].wait()

    def row_saves(step):
        at = pl.ds(pl.multiple_of(step * BLOCK, BLOCK), BLOCK)
        pieces = [(mixed, mixed_out), (normed, nffn_out), (hidden, hidden_out), (mid, mid_out), (hat, hat_out),
                  (broad, slope_out)]
        return [
            pltpu.make_async_copy(source.at[at], target.at[at], row_sems.at[index, step])
            for index, (source, target) in enumerate(pieces)
        ]

    def one_block(step, carry):
        at = pl.ds(pl.multiple_of(step * BLOCK, BLOCK), BLOCK)
        alive = alive_rows(lengths_ref, core, step * BLOCK, BLOCK)
        ctx_hat, _ = normalized(context[at, :])
        mix = (ctx_hat * as_row(sg_ref) + as_row(ss_ref)).astype(BF16)
        mixed[at, :] = mix
        out_weight = jnp.concatenate([wuo[(b, *box, slice(None), slice(cu, cu + co))].reshape(width, co) for b in range(6)], axis=1)
        branch = nn(mix, out_weight) + as_row(ob_ref)
        hid = (hidden[at, :].astype(F32) + alive * branch).astype(BF16)
        hidden[at, :] = hid
        hid_hat, _ = normalized(hid.astype(F32))
        nffn = (hid_hat * as_row(fg_ref) + as_row(fs_ref)).astype(BF16)
        normed[at, :] = nffn
        up_weight = jnp.concatenate([wuo[(b, *box, slice(None), slice(0, cu))].reshape(width, cu) for b in range(6)], axis=1)
        units = 4 * width
        chunks = [slice(c, c + width) for c in range(0, units, width)]
        up_bias, mid_gain, mid_shift = as_row(ub_ref), as_row(mg_ref), as_row(ms_ref)
        lanes = jnp.zeros((BLOCK, 128), F32)
        for cols in chunks:
            value, slope = gelu_parts(nn(nffn, up_weight[:, cols]) + up_bias[:, cols])
            broad[at, cols] = slope.astype(BF16)
            active[:, cols] = value
            lanes = lanes + lane_groups(value)
        center = jnp.sum(lanes, axis=-1, keepdims=True) * (1.0 / units)
        lanes = jnp.zeros((BLOCK, 128), F32)
        for cols in chunks:
            centered = active[:, cols] - center
            lanes = lanes + lane_groups(centered * centered)
        act_scale = lax.rsqrt(jnp.sum(lanes, axis=-1, keepdims=True) * (1.0 / units) + EPS)
        for cols in chunks:
            act_hat = (active[:, cols] - center) * act_scale
            hat[at, cols] = act_hat.astype(BF16)
            mid[at, cols] = (act_hat * mid_gain[:, cols] + mid_shift[:, cols]).astype(BF16)
        scales[at, :] = act_scale
        gffn[at, :] = (alive * gffn[at, :].astype(F32)).astype(BF16)
        for copy in row_saves(step):
            copy.start()

        @pl.when(step == 0)
        def _():
            gather_d.arrive(1)

        @pl.when(step == 2)
        def _():
            gather_d.arrive(2)

        return carry

    steps = rows // BLOCK
    lax.fori_loop(0, steps, one_block, 0)
    save(scales, scale_out)

    def grad_save(h, k):
        return pltpu.make_async_copy(gdown.at[k], gdown_out.at[3 * h + k], grad_sems.at[h, k])

    for h in range(2):
        mid_t[...] = mid[:, 2 * h * width : 2 * (h + 1) * width].T
        for k in range(3):
            grad = nn(mid_t[...], gffn[:, k * cd : (k + 1) * cd]).astype(BF16)
            grad = grad.reshape(CHIPS, 2, mine, cd)
            if h:
                grad_save(0, k).wait()
            for n in range(2):
                gdown[k, :, :, n * cd : (n + 1) * cd] = grad[:, n]
            grad_save(h, k).start()
    gather_d.arrive(3)
    for k in range(3):
        grad_save(1, k).wait()
    gather_d.passed()

    def finish(step, carry):
        for copy in row_saves(step):
            copy.wait()
        return carry

    lax.fori_loop(0, steps, finish, 0)
    for copy in saves[1:]:
        copy.wait()
    for gather in (gather_q0, gather_q1, gather_u, gather_d):
        gather.drain()


def front(tokens, upstream, lengths, half, down, vectors):
    width = tokens.shape[1]
    rows = tokens.shape[0] // 2
    mine = half.shape[0]
    box = BOX
    pairs = width // PAIR
    wide = 4 * width
    anywhere = pl.BlockSpec(memory_space=pl.ANY)
    vmem = pl.BlockSpec(memory_space=pltpu.VMEM)
    smem = pl.BlockSpec(memory_space=pltpu.SMEM)
    dma = pltpu.SemaphoreType.DMA
    sizes = dict(q0=PAIR, q1=2 * PAIR, u=5 * width // 6, d=2 * width // 3)
    shape = jax.ShapeDtypeStruct
    steps = rows // BLOCK
    return pl.pallas_call(
        front_kernel,
        in_specs=[anywhere, anywhere, smem, anywhere, anywhere] + [vmem] * len(vectors),
        out_specs=[anywhere] * 17,
        out_shape=[
            shape((rows, 3 * width), BF16), shape((rows, width), BF16), shape((rows, width), F32),
            shape((pairs, 2, rows), F32), shape((1, rows), jnp.int32),
            *[shape((6, *box, mine, columns), BF16) for columns in sizes.values()],
            shape((rows, width), BF16), shape((rows, width), BF16), shape((rows, width), BF16),
            shape((rows, wide), BF16), shape((rows, wide), BF16), shape((rows, wide), BF16), shape((rows, 1), F32),
            shape((6, CHIPS, mine, 2 * width // 3), BF16),
        ],
        scratch_shapes=[
            pltpu.VMEM((rows, width), BF16), pltpu.VMEM((rows, width), BF16), pltpu.VMEM((rows, wide), BF16),
            pltpu.VMEM((rows, wide), BF16), pltpu.VMEM((rows, wide), BF16), pltpu.VMEM((rows, width), BF16),
            pltpu.VMEM((rows, width), BF16), pltpu.VMEM((rows, width), F32), pltpu.VMEM((pairs, 2, rows), F32),
            pltpu.VMEM((1, rows), jnp.int32),
            *[pltpu.VMEM((6, *box, mine, sizes[name]), BF16) for name in ("q0", "q1", "u")],
            pltpu.VMEM((2 * width, rows), BF16), pltpu.VMEM((3, CHIPS, mine, 2 * width // 3), BF16),
            pltpu.VMEM((rows, 1), F32), pltpu.VMEM((BLOCK, wide), F32),
            dma((3, 6)), dma((3, 12)), dma((3, 6)), dma((3, 6)), dma((3, 6)),
            *[dma((2, MOVES))] * 4, *[dma((2, 6))] * 4,
            dma((2,)), dma((8,)), dma((6, steps)), dma((2, 3)),
        ],
        compiler_params=params(collective_id=1, has_side_effects=True),
        name="front",
    )(tokens, upstream, lengths, half, down, *vectors)


class Scatter:
    def __init__(self, total, landings, sems, final, direct=False):
        self.me = Place()
        self.direct = direct
        self.total, self.landings, self.sems, self.final = total, landings, sems, final

    def move(self, index, z, y, x, device):
        return remote(self.total.at[:, z, y, x], self.landings.at[index], (self.sems.at[0, index], self.sems.at[1, index]), device)

    def to_z(self, k):
        me = self.me
        return self.move(k - 1, me.zs[k], me.y, me.x, me.over_z(k))

    def to_x(self, k):
        me = self.me
        return self.move(X_AT + k, me.zs[k], me.y, 1 - me.x, me.over_x())

    def to_y(self, k):
        me = self.me
        return self.move(Y_AT + k, me.zs[k], 1 - me.y, me.x, me.over_y())

    def toward(self, k):
        me = self.me
        return self.move(D_AT + k, me.zs[k], 1 - me.y, 1 - me.x, me.across() if self.direct else me.over_y() if k < 2 else me.over_x())

    def add(self, z, y, x, landed):
        self.total[:, z, y, x] = functools.reduce(jnp.add, [part[...] for part in landed], self.total[:, z, y, x])

    def begin(self, other):
        me = self.me

        def both(z, y, x):
            self.add(z, y, x, [other.at[:, z, y, x]])

        if self.direct:
            for k in (2, 3, 1, 0):
                both(me.zs[k], 1 - me.y, 1 - me.x)
                self.toward(k).start()
                both(me.zs[k], me.y, 1 - me.x)
                self.to_x(k).start()
                both(me.zs[k], 1 - me.y, me.x)
                self.to_y(k).start()
                both(me.zs[k], me.y, me.x)
            return
        for k in range(4):
            both(me.zs[k], 1 - me.y, 1 - me.x)
            self.toward(k).start()
        for k in range(4):
            both(me.zs[k], me.y, 1 - me.x)
            both(me.zs[k], 1 - me.y, me.x)
            both(me.zs[k], me.y, me.x)

    def arrive(self, stage):
        me = self.me
        if self.direct and stage < 3:
            for k in ((2, 3), (1, 0), ())[stage]:
                moves = (self.toward(k), self.to_x(k), self.to_y(k))
                for move in moves:
                    move.wait_recv()
                self.add(me.zs[k], me.y, me.x, [self.landings.at[at + k] for at in (D_AT, X_AT, Y_AT)])
                if k:
                    self.to_z(k).start()
        elif stage == 0:
            for k in range(4):
                self.toward(k).wait_recv()
                if k < 2:
                    self.add(me.zs[k], me.y, 1 - me.x, [self.landings.at[D_AT + k]])
                else:
                    self.add(me.zs[k], 1 - me.y, me.x, [self.landings.at[D_AT + k]])
            for k in (2, 3):
                self.to_x(k).start()
                self.to_y(k).start()
        elif stage < 3:
            if stage == 1:
                for k in (1, 0):
                    self.to_x(k).start()
                    self.to_y(k).start()
            for k in (2, 3) if stage == 1 else (1, 0):
                self.to_x(k).wait_recv()
                self.to_y(k).wait_recv()
                self.add(me.zs[k], me.y, me.x, [self.landings.at[X_AT + k], self.landings.at[Y_AT + k]])
                if k:
                    self.to_z(k).start()
        else:
            value = self.total[:, me.z, me.y, me.x].astype(F32)
            for k in (1, 2, 3):
                self.to_z(k).wait_recv()
                value = value + self.landings[k - 1].astype(F32)
            self.final[...] = value

    def drain(self):
        for k in (1, 2, 3):
            self.to_z(k).wait_send()
        for k in range(4):
            for move in (self.to_x(k), self.to_y(k), self.toward(k)):
                move.wait_send()


class Total:
    def __init__(self, rows, landed, sems):
        me = Place()
        self.rows, self.landed, self.sems = rows, landed, sems
        self.partners = [
            [me.sibling()], [me.over_x(), me.over_y(), me.across()], [me.over_z(k) for k in (1, 2, 3)]
        ]

    def moves(self, stage):
        at = (0, 1, 4)[stage]
        return [
            remote(self.rows.at[stage], self.landed.at[at + n], (self.sems.at[0, at + n], self.sems.at[1, at + n]), device)
            for n, device in enumerate(self.partners[stage])
        ]

    def start(self, stage):
        for move in self.moves(stage):
            move.start()

    def arrive(self, stage):
        at = (0, 1, 4)[stage]
        value = self.rows[stage]
        for n, move in enumerate(self.moves(stage)):
            move.wait_recv()
            value = value + self.landed[at + n]
        self.rows[stage + 1] = value
        if stage < 2:
            self.start(stage + 1)

    def drain(self):
        for stage in range(3):
            for move in self.moves(stage):
                move.wait_send()


def feed_body(
    hidden_steps, upstream_ref, context_ref, hidden_ref, mid_ref, hat_ref, slope_ref, scale_ref, lengths_ref, wuo_any, wd_any,
    sg_ref, fg_ref, mg_ref, db_ref, gdown_ref,
    ghid_ref, gctx_ref, gbranch_ref, gup_ref, narrow_ref, wide_ref, layer_ref, down_ref,
    wuo_ref, wd_ref, out_rows, scaled_grad, total, landed, landings, final, swap_sems, chain_sems, local_sems, out_sems,
):
    me = Place()
    core = me.core
    step = pl.program_id(0)
    steps = pl.num_programs(0)
    width = hidden_ref.shape[1]
    mine = width // CHIPS
    co, cu, cd = width // 6, 2 * width // 3, width // 3
    sibling = me.sibling()
    scatter = Scatter(total, landings, chain_sems, final)
    own = pltpu.make_async_copy(gdown_ref.at[pl.ds(3 * core, 3)], total, local_sems.at[0])
    far = remote(gdown_ref.at[pl.ds(3 * (1 - core), 3)], landed, (swap_sems.at[0], swap_sems.at[1]), sibling)

    def out_copies(at_step, which):
        at = pl.ds(pl.multiple_of(at_step * BLOCK, BLOCK), BLOCK)
        target = layer_ref.at[which, at]
        return (pltpu.make_async_copy(out_rows.at[at], target, out_sems.at[0, at_step]),
                remote(out_rows.at[at], target, (out_sems.at[1, at_step], out_sems.at[2, at_step]), sibling))

    got_wd = pltpu.make_async_copy(wd_any, wd_ref, local_sems.at[1])
    got_wuo = pltpu.make_async_copy(wuo_any, wuo_ref, local_sems.at[2])

    @pl.when(step == 0)
    def _():
        got_wd.start()
        got_wuo.start()
        greet(me)
        far.start()
        own.start()
        got_wd.wait()
        narrow_ref[...] = jnp.zeros_like(narrow_ref)
        wide_ref[...] = jnp.zeros_like(wide_ref)

    def hook(at_step, action):
        pl.when(step == at_step)(action)

    def begin():
        own.wait()
        far.wait_recv()
        scatter.begin(landed)

    halves = []
    for h in range(2):
        parts = []
        for n in range(2):
            part = jnp.concatenate([wd_ref[3 * h + k, :, n * cd : (n + 1) * cd] for k in range(3)], axis=1)
            parts.append(part.reshape(CHIPS, 1, mine, width))
        halves.append(jnp.concatenate(parts, axis=1).reshape(2 * width, width))
    down_weight = jnp.concatenate(halves, axis=0)

    alive = alive_rows(lengths_ref, core, step * BLOCK, BLOCK)
    hidden = hidden_ref[...].astype(F32)
    upstream = upstream_ref[...].astype(F32)
    gffn = (alive * upstream).astype(BF16)
    mid_gain = as_row(mg_ref)
    units = 4 * width
    chunks = [slice(at, at + width) for at in range(0, units, width)]
    first_sum = jnp.zeros((BLOCK, 128), F32)
    second_sum = jnp.zeros((BLOCK, 128), F32)
    for cols in chunks:
        gmid = nt(gffn, down_weight[cols])
        weighted = gmid * hat_ref[:, cols].astype(F32)
        wide_ref[1:2, cols] += col_sum(weighted)
        wide_ref[2:3, cols] += col_sum(gmid)
        scaled = gmid * mid_gain[:, cols]
        scaled_grad[:, cols] = scaled
        first_sum = first_sum + lane_groups(scaled)
        second_sum = second_sum + lane_groups(weighted * mid_gain[:, cols])
    first_mean = jnp.sum(first_sum, axis=-1, keepdims=True) * (1.0 / units)
    second_mean = jnp.sum(second_sum, axis=-1, keepdims=True) * (1.0 / units)
    hook(0, begin)
    hook(0, got_wuo.wait)
    up_weight = jnp.concatenate([wuo_ref[b, :, :cu] for b in range(6)], axis=1)
    out_weight = jnp.concatenate([wuo_ref[b, :, cu:] for b in range(6)], axis=1)
    hook(1, lambda: scatter.arrive(0))
    hook(2, lambda: scatter.arrive(1))
    hook(3, lambda: scatter.arrive(2))
    act_scale = scale_ref[...]
    gnffn = jnp.zeros((BLOCK, width), F32)
    result = jnp.zeros((BLOCK, width), F32)
    for cols in chunks:
        act_hat = hat_ref[:, cols].astype(F32)
        gact = (scaled_grad[:, cols] - first_mean - act_hat * second_mean) * act_scale
        gup = (gact * slope_ref[:, cols].astype(F32)).astype(BF16)
        gup_ref[:, cols] = gup
        wide_ref[0:1, cols] += col_sum(gup.astype(F32))
        gnffn = gnffn + nt(gup, up_weight[:, cols])
        result = result + nn(mid_ref[:, cols], down_weight[cols])
    result = (result + as_row(db_ref)).astype(BF16).astype(F32)
    out_rows[pl.ds(pl.multiple_of(step * BLOCK, BLOCK), BLOCK), :] = hidden + alive * result
    for copy in out_copies(step, core):
        copy.start()
    hid_hat, hid_scale = normalized(hidden)
    ghid = (upstream + norm_back(hid_hat, hid_scale, as_row(fg_ref), gnffn)).astype(BF16)
    ghid_ref[...] = ghid
    gbranch = (alive * ghid.astype(F32)).astype(BF16)
    gbranch_ref[...] = gbranch
    gmixed = nt(gbranch, out_weight)
    ctx_hat, ctx_scale = normalized(context_ref[...])
    gctx_ref[...] = norm_back(ctx_hat, ctx_scale, as_row(sg_ref), gmixed).astype(BF16)
    narrow_ref[0:1, :] += col_sum(gmixed * ctx_hat)
    narrow_ref[1:2, :] += col_sum(gmixed)
    narrow_ref[2:3, :] += col_sum(gbranch.astype(F32))
    narrow_ref[3:4, :] += col_sum(gnffn * hid_hat)
    narrow_ref[4:5, :] += col_sum(gnffn)
    narrow_ref[5:6, :] += col_sum(gffn.astype(F32))

    @pl.when(step == steps - 1)
    def _():
        scatter.arrive(3)
        for k in range(3):
            for n in range(2):
                down_ref[n * mine : (n + 1) * mine, k * cd : (k + 1) * cd] = final[k, :, n * cd : (n + 1) * cd]
        for index in range(hidden_steps):
            local, away = out_copies(index, core)
            local.wait()
            away.wait_send()
            out_copies(index, 1 - core)[1].wait_recv()
        far.wait_send()
        scatter.drain()


def feed(upstream, context, hidden, mid, hat, slope, scale, lengths, wuo, wd, vectors, gdown):
    rows, width = hidden.shape
    wide = 4 * width
    steps = rows // BLOCK
    box = BOX
    mine = width // CHIPS
    columns = 2 * width // 3
    row = pl.BlockSpec((BLOCK, width), lambda i: (i, 0))
    row_wide = pl.BlockSpec((BLOCK, wide), lambda i: (i, 0))
    once = dict(pipeline_mode=pl.Buffered(1))
    anywhere = pl.BlockSpec(memory_space=pl.ANY)
    vmem = pl.BlockSpec(memory_space=pltpu.VMEM)
    smem = pl.BlockSpec(memory_space=pltpu.SMEM)
    dma = pltpu.SemaphoreType.DMA
    shape = jax.ShapeDtypeStruct

    def held(*size, dtype=BF16):
        return pltpu.VMEM(size, dtype)

    return pl.pallas_call(
        functools.partial(feed_body, steps),
        grid=(steps,),
        in_specs=[
            pl.BlockSpec((BLOCK, width), lambda i: (lax.axis_index("section") * steps + i, 0)),
            row, row, row_wide, row_wide, row_wide, pl.BlockSpec((BLOCK, 1), lambda i: (i, 0)), smem,
            anywhere, anywhere, *[vmem] * 4, anywhere,
        ],
        out_specs=[row, row, row, row_wide, whole((8, width)), whole((8, wide)), anywhere, vmem],
        out_shape=[
            shape((rows, width), BF16), shape((rows, width), BF16), shape((rows, width), BF16), shape((rows, wide), BF16),
            shape((8, width), F32), shape((8, wide), F32), shape((2, rows, width), F32), shape((2 * mine, width), F32),
        ],
        scratch_shapes=[
            held(*wuo.shape), held(*wd.shape), held(rows, width, dtype=F32), held(BLOCK, wide, dtype=F32),
            held(3, *box, mine, columns), held(3, *box, mine, columns),
            held(MOVES, 3, mine, columns),
            held(3, mine, columns, dtype=F32),
            dma((2,)), dma((2, MOVES)), dma((3,)), dma((3, steps)),
        ],
        compiler_params=params(collective_id=3, has_side_effects=True),
        name="feed",
    )(upstream, context, hidden, mid, hat, slope, scale, lengths, wuo, wd, *vectors,
      gdown.reshape((6,) + box + (mine, columns)))


def finish_kernel(*refs):
    layer_ref, grad_ref, half_ref, down_ref, slim_ref, broad_ref = refs[:6]
    layer_out, grad_out, half_out, down_out = refs[6:10]
    small, (layer, grad, half, down, sems) = refs[10:23], refs[23:]
    pieces = []
    for source, held, target, parts in (
        (layer_ref, layer, layer_out, 4), (grad_ref, grad, grad_out, 2), (half_ref, half, half_out, 1), (down_ref, down, down_out, 1)
    ):
        rows = source.shape[0] // parts
        for part in range(parts):
            at = pl.ds(part * rows, rows)
            n = len(pieces)
            pieces.append((pltpu.make_async_copy(source.at[at], held.at[at], sems.at[0, n]),
                           pltpu.make_async_copy(held.at[at], target.at[at], sems.at[1, n])))
    for get, _ in pieces:
        get.start()
    for row, out in zip((0, 1, 2, 3, 8, 9, 10, 11, 12, 13), small[:10]):
        out[...] = slim_ref[row, : out.shape[0]]
    for row, out in enumerate(small[10:]):
        out[...] = broad_ref[row, : out.shape[0]]
    for get, put in pieces:
        get.wait()
        put.start()
    for _, put in pieces:
        put.wait()


def finish(layer, grad, half, down, slim, broad, narrow_share, wide_share):
    anywhere = pl.BlockSpec(memory_space=pl.ANY)
    vmem = pl.BlockSpec(memory_space=pltpu.VMEM)
    shape = jax.ShapeDtypeStruct
    big = [layer, grad, half, down]
    sizes = [narrow_share] * 10 + [wide_share] * 3
    return pl.pallas_call(
        finish_kernel,
        in_specs=[anywhere] * 4 + [vmem] * 2,
        out_specs=[anywhere] * 4 + [vmem] * len(sizes),
        out_shape=[shape(array.shape, F32) for array in big] + [shape((size,), F32) for size in sizes],
        scratch_shapes=[pltpu.VMEM(array.shape, F32) for array in big] + [pltpu.SemaphoreType.DMA((2, 14))],
        compiler_params=params(),
        name="finish",
    )(layer, grad, half, down, slim, broad)


def back_kernel(
    projected_any, gctx_any, context_any, lse_ref, start_ref, normed_any, tokens_any, ghid_any, gain_ref, wq0_any, wq1_any,
    narrow_ref, wide_ref, nffn_any, mixed_any, gup_any, gbranch_any,
    grad_ref, half_ref, slim_ref, broad_ref,
    projected_ref, gctx_ref, context_ref, ghid_ref, wq0_ref, wq1_ref, spare, gup_far, gbranch, mixed_t, far_r,
    x_rows, dproj, dk_acc, dv_acc, normed_t, near_rows, far_rows,
    total_r, first_r, landings_r, final_r, other_r,
    total_q, far_q, first_q, landings_q, final_q, other_q,
    early, early_in, late, late_in,
    load_sems, swap_sems, far_sems, chain_r, chain_q, early_sems, late_sems, row_sems,
):
    me = Place()
    core = me.core
    rows, width = x_rows.shape
    mine = half_ref.shape[0]
    pairs = width // PAIR
    co, cu, cq = width // 6, 2 * width // 3, width // 2
    cg = 3 * PAIR
    sibling = me.sibling()
    first = core == 0
    second = core == 1

    def swap(index, source, target):
        return remote(source, target, (swap_sems.at[0, index], swap_sems.at[1, index]), sibling)

    sum_r = Scatter(total_r, landings_r, chain_r, final_r)
    sum_q = [Scatter(total_q.at[g], landings_q.at[g], chain_q.at[g], final_q.at[g], direct=True) for g in range(3)]

    loads = []

    def load(source, target):
        loads.append(pltpu.make_async_copy(source, target, load_sems.at[len(loads)]))
        loads[-1].start()
        return loads[-1]

    half = 2 * width
    far_cols = pl.ds(pl.multiple_of((1 - core) * half, PAIR), half)
    own_cols = pl.ds(pl.multiple_of(core * half, PAIR), half)
    got_nffn = load(nffn_any, x_rows)
    got_mixed = load(mixed_any, spare)
    got_far = load(gup_any.at[:, far_cols], gup_far)
    got_branch = load(gbranch_any, gbranch)
    got_own = load(gup_any.at[:, own_cols], dproj.at[:, :half])
    later = [
        load(source, target)
        for source, target in ((projected_any, projected_ref), (gctx_any, gctx_ref), (context_any, context_ref))
    ]
    greet(me)
    early_sum = Total(early, early_in, early_sems)
    late_sum = Total(late, late_in, late_sems)
    early[0] = jnp.zeros_like(early[0])
    early[0, 0:6, :] = narrow_ref[0:6, :]
    for n in range(3):
        for part in range(4):
            row = 8 + 4 * n + part
            early[0, row : row + 1, :] = wide_ref[n : n + 1, part * width : (part + 1) * width]
    early_sum.start(0)
    got_nffn.wait()
    normed_t[...] = x_rows[...].T
    got_x = load(tokens_any.at[pl.ds(pl.multiple_of(core * rows, rows), rows)], x_rows)
    got_mixed.wait()
    mixed_t[...] = spare[...].T
    got_normed = load(normed_any, spare)
    last = [
        load(source, target)
        for source, target in ((ghid_any, ghid_ref), (wq0_any, wq0_ref), (wq1_any, wq1_ref))
    ]

    def up_out(source, k, block, target):
        up = nn(normed_t[...], source[:, k * cu : (k + 1) * cu]).astype(BF16)
        at = pl.ds(pl.multiple_of(block * co, PAIR), co)
        out = nn(mixed_t[...], gbranch[:, at]).astype(BF16)
        target[k, :, :, :, :, :cu] = up.reshape(BOX + (mine, cu))
        target[k, :, :, :, :, cu:] = out.reshape(BOX + (mine, co))

    def swap_far(k):
        return remote(far_r.at[k], first_r.at[k], (far_sems.at[0, k], far_sems.at[1, k]), sibling)

    got_far.wait()
    got_branch.wait()
    for k in range(3):
        up_out(gup_far, k, 3 * (1 - core) + k, far_r)
        swap_far(k).start()
    got_own.wait()
    for k in range(3):
        up_out(dproj, k, 3 * core + k, total_r)
    for k in range(3):
        swap_far(k).wait_recv()
    sum_r.begin(first_r)
    got_normed.wait()
    normed_t[...] = spare[...].T
    for copy in later:
        copy.wait()

    def swap_q(group):
        return swap(3 + group, far_q.at[group], first_q.at[group])

    def make(group):
        for which, target in ((1 - core, far_q), (core, total_q)):
            at = pl.ds(pl.multiple_of(group * 2 * cg + which * cg, PAIR), cg)
            grad = nn(normed_t[...], dproj[:, at]).astype(BF16)
            for n in range(3):
                target[group, n] = grad[:, n * PAIR : (n + 1) * PAIR].reshape(BOX + (mine, PAIR))
            if target is far_q:
                swap_q(group).start()

    def begin(group):
        swap_q(group).wait_recv()
        sum_q[group].begin(first_q.at[group])

    def one_pair(pair, carry):
        @pl.when(pair == 1)
        def _():
            early_sum.arrive(0)

        @pl.when(pair == 2)
        def _():
            make(0)
            sum_r.arrive(0)

        @pl.when(pair == 3)
        def _():
            begin(0)
            early_sum.arrive(1)

        @pl.when(pair == 4)
        def _():
            sum_r.arrive(1)
            make(1)

        @pl.when(pair == 5)
        def _():
            begin(1)

        at_q = pl.ds(pl.multiple_of(pair * cg, PAIR), PAIR)
        at_k = pl.ds(pl.multiple_of(pair * cg + PAIR, PAIR), PAIR)
        at_v = pl.ds(pl.multiple_of(pair * cg + 2 * PAIR, PAIR), PAIR)
        at_c = pl.ds(pl.multiple_of(pair * PAIR, PAIR), PAIR)
        attend_back_pair(
            projected_ref[:, at_q], projected_ref[:, at_k], projected_ref[:, at_v], gctx_ref[:, at_c],
            context_ref[:, at_c], lse_ref.at[pair], start_ref,
            dproj.at[:, at_q], dproj.at[:, at_k], dproj.at[:, at_v], dk_acc, dv_acc,
        )
        return carry

    lax.fori_loop(0, pairs, one_pair, 0)
    make(2)
    early_sum.arrive(2)
    sum_q[0].arrive(0)
    sum_q[1].arrive(0)
    sum_r.arrive(2)
    begin(2)
    got_x.wait()
    for copy in last:
        copy.wait()
    late[0] = jnp.zeros_like(late[0])

    def row_copies(step, which):
        at = pl.ds(pl.multiple_of(step * BLOCK, BLOCK), BLOCK)
        target = grad_ref.at[which, at]
        return (pltpu.make_async_copy(near_rows.at[at], target, row_sems.at[0, step]),
                remote(far_rows.at[at], target, (row_sems.at[1, step], row_sems.at[2, step]), sibling))

    def one_block(step, carry):
        at = pl.ds(pl.multiple_of(step * BLOCK, BLOCK), BLOCK)
        gnormed = jnp.zeros((BLOCK, width), F32)
        for group in range(3):
            if group == 0:
                blocks = [wq0_ref[b].reshape(width, PAIR) for b in range(6)]
            else:
                cols = slice((group - 1) * PAIR, group * PAIR)
                blocks = [wq1_ref[(b,) + (slice(None),) * 4 + (cols,)].reshape(width, PAIR) for b in range(6)]
            weight = jnp.concatenate(blocks, axis=1)
            gnormed = gnormed + nt(dproj[at, group * 2 * cg : (group + 1) * 2 * cg], weight)
        hat, scale = normalized(x_rows[at, :].astype(F32))
        grad_x = ghid_ref[at, :].astype(F32) + norm_back(hat, scale, as_row(gain_ref), gnormed)

        @pl.when(first)
        def _():
            near_rows[at, :] = grad_x[:, :cq]
            far_rows[at, :] = grad_x[:, cq:]

        @pl.when(second)
        def _():
            near_rows[at, :] = grad_x[:, cq:]
            far_rows[at, :] = grad_x[:, :cq]

        for copy in row_copies(step, core):
            copy.start()

        late[0, 0:1, :] += col_sum(gnormed * hat)
        late[0, 1:2, :] += col_sum(gnormed)
        for row, part in ((2, 0), (3, 2)):
            grads = [dproj[at, p * cg + part * PAIR : p * cg + (part + 1) * PAIR].astype(F32) for p in range(pairs)]
            late[0, row : row + 1, :] += col_sum(jnp.concatenate(grads, axis=1))

        @pl.when(step == 1)
        def _():
            sum_q[0].arrive(1)
            sum_q[1].arrive(1)

        @pl.when(step == 3)
        def _():
            sum_q[2].arrive(0)

        return carry

    lax.fori_loop(0, rows // BLOCK, one_block, 0)
    late_sum.start(0)
    sum_q[2].arrive(1)
    late_sum.arrive(0)
    sum_r.arrive(3)
    swap_r = swap(2, final_r, other_r)
    swap_r.start()
    sum_q[0].arrive(3)
    sum_q[1].arrive(3)
    late_sum.arrive(1)
    sum_q[2].arrive(3)
    swap_f = swap(6, final_q, other_q)
    swap_f.start()
    late_sum.arrive(2)
    swap_r.wait_recv()

    share = core * CHIPS + me.chip

    def pick(values, each):
        size = values.shape[1]
        return pltpu.roll(values, (size - share * each) % size, 1)[:, :128]

    shares = 2 * CHIPS
    sums = early[3]
    rows_of = [jnp.concatenate([sums[8 + 4 * n + part : 9 + 4 * n + part] for part in range(4)], axis=1) for n in range(3)]
    broad_ref[...] = pick(jnp.concatenate(rows_of + [jnp.zeros((5, 4 * width), F32)], axis=0), 4 * width // shares)
    slim_ref[8:16, :] = pick(sums[0:8], width // shares)
    slim_ref[0:8, :] = pick(late[3], width // shares)

    swap_f.wait_recv()

    @pl.when(first)
    def _():
        for k in range(3):
            for g in range(3):
                for c, source in ((0, final_q), (1, other_q)):
                    at = k * width + (2 * g + c) * PAIR
                    half_ref[:, at : at + PAIR] = source[g, k]
            half_ref[:, 3 * width + k * co : 3 * width + (k + 1) * co] = final_r[k, :, cu:]
            half_ref[:, 3 * width + (3 + k) * co : 3 * width + (4 + k) * co] = other_r[k, :, cu:]

    @pl.when(second)
    def _():
        for k in range(3):
            half_ref[:, k * cu : (k + 1) * cu] = other_r[k, :, :cu]
            half_ref[:, (3 + k) * cu : (4 + k) * cu] = final_r[k, :, :cu]

    for step in range(rows // BLOCK):
        near, far = row_copies(step, core)
        near.wait()
        far.wait_send()
        row_copies(step, 1 - core)[1].wait_recv()
    for done in (swap_far(0), swap_far(1), swap_far(2), swap_r, swap_f, swap_q(0), swap_q(1), swap_q(2)):
        done.wait_send()
    early_sum.drain()
    late_sum.drain()
    for each in [sum_r] + sum_q:
        each.drain()


def back(projected, gctx, context, lse, start, normed, tokens, ghid, gain, wq0, wq1, narrow, wide, nffn, mixed, gup, gbranch):
    rows, width = normed.shape
    box = BOX
    mine = width // CHIPS
    cq, cr = width // 2, 5 * width // 6
    anywhere = pl.BlockSpec(memory_space=pl.ANY)
    vmem = pl.BlockSpec(memory_space=pltpu.VMEM)
    dma = pltpu.SemaphoreType.DMA

    def held(*shape, dtype=BF16):
        return pltpu.VMEM(shape, dtype)

    return pl.pallas_call(
        back_kernel,
        in_specs=[anywhere] * 3 + [vmem] * 2 + [anywhere] * 3 + [vmem] + [anywhere] * 2 + [vmem] * 2 + [anywhere] * 4,
        out_specs=[anywhere] + [vmem] * 3,
        out_shape=[
            jax.ShapeDtypeStruct((2, rows, cq), F32),
            jax.ShapeDtypeStruct((mine, 4 * width), F32),
            jax.ShapeDtypeStruct((16, 128), F32),
            jax.ShapeDtypeStruct((8, 128), F32),
        ],
        scratch_shapes=[
            held(rows, 3 * width), held(rows, width), held(rows, width, dtype=F32), held(rows, width),
            held(*wq0.shape), held(*wq1.shape), held(rows, width), held(rows, 2 * width), held(rows, width),
            held(width, rows), held(3, *box, mine, cr),
            held(rows, width), held(rows, 3 * width), held(rows, PAIR, dtype=F32), held(rows, PAIR, dtype=F32),
            held(width, rows), held(rows, cq, dtype=F32), held(rows, cq, dtype=F32),
            held(3, *box, mine, cr), held(3, *box, mine, cr), held(MOVES, 3, mine, cr),
            held(3, mine, cr, dtype=F32), held(3, mine, cr, dtype=F32),
            held(3, 3, *box, mine, PAIR), held(3, 3, *box, mine, PAIR), held(3, 3, *box, mine, PAIR),
            held(3, MOVES, 3, mine, PAIR),
            held(3, 3, mine, PAIR, dtype=F32), held(3, 3, mine, PAIR, dtype=F32),
            held(4, 24, width, dtype=F32), held(7, 24, width, dtype=F32),
            held(4, 8, width, dtype=F32), held(7, 8, width, dtype=F32),
            dma((13,)), dma((2, 7)), dma((2, 3)), dma((2, MOVES)), dma((3, 2, MOVES)), dma((2, 7)), dma((2, 7)), dma((3, 4)),
        ],
        compiler_params=params(collective_id=2, has_side_effects=True),
        name="back",
    )(projected, gctx, context, lse, start, normed, tokens, ghid, gain, wq0, wq1, narrow, wide, nffn, mixed, gup, gbranch)


def fused_batch(tokens, out_grad, lengths, half, down, vectors):
    (pre_gain, pre_shift, query_bias, value_bias, sub_gain, sub_shift, out_bias,
     ffn_gain, ffn_shift, up_bias, mid_gain, mid_shift, down_bias) = vectors
    width = tokens.shape[1]
    (projected, normed, context, lse, start, wq0, wq1, wuo, wd, mixed, nffn, hidden, mid, hat, slope, scale, gdown) = front(
        tokens, out_grad, lengths, half, down,
        (pre_gain, pre_shift, query_bias, value_bias, sub_gain, sub_shift, out_bias, ffn_gain, ffn_shift, up_bias,
         mid_gain, mid_shift),
    )
    ghid, gctx, gbranch, gup, narrow, wide, layer, down_grad = feed(
        out_grad, context, hidden, mid, hat, slope, scale, lengths, wuo.reshape(6, width, -1), wd.reshape(6, width, -1),
        (sub_gain, ffn_gain, mid_gain, down_bias), gdown,
    )
    grad_x, half_grad, slim, broad = back(
        projected, gctx, context, lse, start, normed, tokens, ghid, pre_gain, wq0, wq1, narrow, wide,
        nffn, mixed, gup, gbranch,
    )
    shares = 2 * CHIPS
    layer, grad_x, half_grad, down_grad, *small = finish(
        layer.reshape(-1, width), grad_x.reshape(-1, width // 2), half_grad, down_grad, slim, broad,
        width // shares, 4 * width // shares,
    )
    return layer, grad_x, half_grad[None], down_grad, *small[:9], *small[10:], small[9]


def unpacked(vectors):
    return [vector[None, :] for vector in vectors]


def marks_and_bias(x, lengths_row, query_bias, value_bias):
    alive, start = row_marks(lengths_row, x.shape[0])
    bias = jnp.concatenate([query_bias, jnp.zeros_like(query_bias), value_bias], axis=1)
    return alive, start, bias


def one_batch(x, dy, lengths_row, qkv, rest, vectors):
    (pre_gain, pre_shift, query_bias, value_bias, sub_gain, sub_shift, out_bias,
     ffn_gain, ffn_shift, up_bias, mid_gain, mid_shift, down_bias) = unpacked(vectors)
    alive, start, bias = marks_and_bias(x, lengths_row, query_bias, value_bias)
    projected, normed = project(x, qkv, pre_gain, pre_shift, bias)
    context, lse = attend(projected, start)
    out, ghid, gctx, mixed, gbranch, nffn, gup, mid, gffn, narrow, wide = middle(
        x, dy, context, alive, rest,
        (sub_gain, sub_shift, out_bias, ffn_gain, ffn_shift, up_bias, mid_gain, mid_shift, down_bias),
    )
    grad_up = outer(nffn, gup, 256, F32, "outer_up")
    grad_down = outer(mid, gffn, 512, F32, "outer_down")
    dq, dk, dv = attend_back(projected, gctx, context, lse, start)
    grad_out = outer(mixed, gbranch, 256, F32, "outer_out")
    grad_x, pre = project_back(dq, dk, dv, qkv, x, ghid, pre_gain)
    grads = [outer(normed, d, 256, F32, "outer_qkv") for d in (dq, dk, dv)]
    grad_attention = jnp.concatenate(grads + [grad_out], axis=1)
    small = (pre[0], pre[1], pre[2], pre[3], narrow[0], narrow[1], narrow[2], narrow[3], narrow[4],
             wide[0], wide[1], wide[2], narrow[5])
    return (out, grad_x), (grad_attention, grad_up, grad_down, small)


def shards(tokens, out_grad, seq_lengths, half_weights, down_weight, *all_vectors):
    section = lax.axis_index("section")
    sections = lax.axis_size("section")
    both = ("section", "dp")
    width = tokens.shape[1]
    batches = seq_lengths.shape[0]
    count = tokens.shape[0] // batches
    own_batches = batches // sections
    own_rows = own_batches * count
    hidden_units = half_weights.shape[2]
    shares = sections * lax.axis_size("dp")

    if (
        sections == 2
        and shares == sections * CHIPS
        and own_batches == 1
        and half_weights.shape[1] % 16 == 0
        and down_weight.shape[0] == 2 * half_weights.shape[1]
        and hidden_units == 4 * width
    ):
        return fused_batch(tokens, out_grad, seq_lengths, half_weights[0], down_weight, all_vectors)

    def own(array, rows):
        return lax.dynamic_slice_in_dim(array, section * rows, rows, axis=0)

    x_rows = own(tokens, own_rows)
    dy_rows = own(out_grad, own_rows)
    lengths = own(seq_lengths, own_batches)
    blocks = lax.all_gather(half_weights[0], both, axis=0, tiled=True)
    blocks = blocks.reshape(sections, width, hidden_units)
    down_full = lax.all_gather(down_weight, both, axis=0, tiled=True)
    qkv = blocks[0][:, : 3 * width]

    def in_blocks(array):
        return array.reshape(array.shape[0], 6, -1).transpose(1, 0, 2)

    down_blocks = down_full.reshape(2, CHIPS, 2, width // CHIPS, 3, width // 3).transpose(0, 4, 1, 3, 2, 5)
    down_blocks = down_blocks.reshape(6, width, 2 * width // 3)
    rest = jnp.concatenate([in_blocks(blocks[1]), in_blocks(blocks[0][:, 3 * width :]), down_blocks], axis=2)
    rows, sums = [], None
    for index in range(own_batches):
        at = slice(index * count, (index + 1) * count)
        row, more = one_batch(x_rows[at], dy_rows[at], lengths[index], qkv, rest, all_vectors)
        rows.append(row)
        sums = more if sums is None else jax.tree.map(jnp.add, sums, more)
    out_block = jnp.concatenate([row[0] for row in rows], axis=0)
    grad_rows = jnp.concatenate([row[1] for row in rows], axis=0)
    grad_attention, grad_up, grad_down, vectors = sums

    block_part = lax.psum_scatter(
        jnp.concatenate([grad_attention, grad_up], axis=0), both, scatter_dimension=0, tiled=True
    )
    down_part = lax.psum_scatter(grad_down, both, scatter_dimension=0, tiled=True)
    packed = jnp.concatenate([vector.reshape(shares, -1) for vector in vectors], axis=1)
    packed = lax.psum_scatter(packed, both, scatter_dimension=0, tiled=True).reshape(-1)
    parts, start = [], 0
    for vector in vectors:
        size = vector.shape[0] // shares
        parts.append(packed[start : start + size])
        start += size

    layer_out = lax.all_gather(out_block, "section", axis=0, tiled=True)
    tokens_grad = lax.all_to_all(grad_rows, "section", split_axis=1, concat_axis=0, tiled=True)
    return (layer_out, tokens_grad, block_part[None], down_part, *parts)


def solution(mesh):
    replicated = P()
    return jax.shard_map(
        shards,
        mesh=mesh,
        in_specs=(P("dp", None), P("dp", None), P("dp", None), P("section", "dp", None), P(("section", "dp"), None))
        + (replicated,) * 13,
        out_specs=(P("dp", None), P("dp", "section"), P("section", "dp", None), P(("section", "dp"), None))
        + (P(("section", "dp")),) * 13,
        check_vma=False,
    )
```

```python
import functools
import math

import jax
import jax.numpy as jnp
from jax import lax
from jax.experimental import pallas as pl
from jax.experimental.pallas import tpu as pltpu
from jax.sharding import PartitionSpec as P

HEAD_DIM = 64
PAIR = 2 * HEAD_DIM
EPS = 1e-05
BLOCK = 256
F32 = jnp.float32
BF16 = jnp.bfloat16
VMEM_LIMIT = 60 * 1024 * 1024


def nn(left, right):
    return lax.dot_general(left, right, (((1,), (0,)), ((), ())), preferred_element_type=F32)


def nt(left, right):
    return lax.dot_general(left, right, (((1,), (1,)), ((), ())), preferred_element_type=F32)


def tn(left, right):
    return lax.dot_general(left, right, (((0,), (0,)), ((), ())), preferred_element_type=F32)


def col_sum(value):
    return jnp.sum(value, axis=0, keepdims=True)


def normalized(value):
    center = jnp.mean(value, axis=-1, keepdims=True)
    centered = value - center
    spread = jnp.mean(centered * centered, axis=-1, keepdims=True)
    scale = lax.rsqrt(spread + EPS)
    return centered * scale, scale


def norm_back(hat, scale, gain, upstream):
    scaled = upstream * gain
    first = jnp.mean(scaled, axis=-1, keepdims=True)
    second = jnp.mean(scaled * hat, axis=-1, keepdims=True)
    return (scaled - first - hat * second) * scale


def params(**more):
    return pltpu.CompilerParams(vmem_limit_bytes=VMEM_LIMIT, **more)


def split_rest(ref):
    _, width, columns = ref.shape
    cu, co, cd = 4 * columns // 9, columns // 9, 2 * columns // 9
    up = jnp.concatenate([ref[b, :, :cu] for b in range(6)], axis=1)
    out = jnp.concatenate([ref[b, :, cu : cu + co] for b in range(6)], axis=1)
    halves = []
    for h in range(2):
        parts = []
        for n in range(2):
            at = cu + co + n * cd
            part = jnp.concatenate([ref[3 * h + k, :, at : at + cd] for k in range(3)], axis=1)
            parts.append(part.reshape(CHIPS, 1, width // CHIPS, width))
        halves.append(jnp.concatenate(parts, axis=1).reshape(2 * width, width))
    return out, up, jnp.concatenate(halves, axis=0)


def whole(shape):
    return pl.BlockSpec(shape, lambda *_: (0,) * len(shape))


def project_kernel(x_ref, w_ref, gain_ref, shift_ref, bias_ref, out_ref, normed_ref):
    hat, _ = normalized(x_ref[...].astype(F32))
    normed = (hat * gain_ref[...] + shift_ref[...]).astype(BF16)
    normed_ref[...] = normed
    out_ref[...] = (nn(normed, w_ref[...]) + bias_ref[...]).astype(BF16)


def project(x, weight, gain, shift, bias):
    rows, width = x.shape
    return pl.pallas_call(
        project_kernel,
        grid=(rows // BLOCK,),
        in_specs=[
            pl.BlockSpec((BLOCK, width), lambda i: (i, 0)),
            whole((width, 3 * width)),
            whole((1, width)),
            whole((1, width)),
            whole((1, 3 * width)),
        ],
        out_specs=[
            pl.BlockSpec((BLOCK, 3 * width), lambda i: (i, 0)),
            pl.BlockSpec((BLOCK, width), lambda i: (i, 0)),
        ],
        out_shape=[
            jax.ShapeDtypeStruct((rows, 3 * width), BF16),
            jax.ShapeDtypeStruct((rows, width), BF16),
        ],
        compiler_params=params(),
        name="project",
    )(x, weight, gain, shift, bias)


def allowed_mask(start, key_at, keys, queries):
    key = key_at + lax.broadcasted_iota(jnp.int32, (keys, queries), 0)
    return key >= start


def head_rows(pair_t, head):
    row = lax.broadcasted_iota(jnp.int32, pair_t.shape, 0)
    mine = (row < HEAD_DIM) if head == 0 else (row >= HEAD_DIM)
    return jnp.where(mine, pair_t, jnp.zeros_like(pair_t))


def head_cols(pair, head):
    col = lax.broadcasted_iota(jnp.int32, pair.shape, 1)
    mine = (col < HEAD_DIM) if head == 0 else (col >= HEAD_DIM)
    return jnp.where(mine, pair, jnp.zeros_like(pair))


def score_parts(key, query_t, start, block):
    before = block * BLOCK
    parts = []
    if block:
        index = lax.broadcasted_iota(jnp.int32, (before, BLOCK), 0)
        parts.append((slice(0, before), jnp.where(index >= start, nn(key[:before], query_t), -1e30)))
    index = lax.broadcasted_iota(jnp.int32, (BLOCK, BLOCK), 0)
    last = lax.broadcasted_iota(jnp.int32, (BLOCK, BLOCK), 1)
    ok = (index >= start - before) & (index <= last)
    own = slice(before, before + BLOCK)
    parts.append((own, jnp.where(ok, nn(key[own], query_t), -1e30)))
    return parts


def attend_pair(query, key, value, start_ref, out_ref, lse_ref):
    query_t = (query.astype(F32) * HEAD_DIM**-0.5).T.astype(BF16)
    value_t = value.astype(F32).T.astype(BF16)
    for block in range(query.shape[0] // BLOCK):
        at = slice(block * BLOCK, (block + 1) * BLOCK)
        start = start_ref[:, at]
        outs = []
        for head in range(2):
            lanes = slice(head * HEAD_DIM, (head + 1) * HEAD_DIM)
            parts = score_parts(key, head_rows(query_t[:, at], head), start, block)
            peak = functools.reduce(jnp.maximum, [jnp.max(scores, axis=0, keepdims=True) for _, scores in parts])
            total = jnp.zeros((1, BLOCK), F32)
            out = jnp.zeros((HEAD_DIM, BLOCK), F32)
            for keys, scores in parts:
                raised = jnp.exp(scores - peak)
                total = total + col_sum(raised)
                out = out + nn(value_t[lanes, keys], raised.astype(BF16))
            outs.append(out * (1.0 / total))
            lse_ref[head : head + 1, at] = peak + jnp.log(total)
        out_ref[at, :] = jnp.concatenate(outs, axis=0).T


def attend_kernel(q_ref, k_ref, v_ref, start_ref, out_ref, lse_ref):
    attend_pair(q_ref[...], k_ref[...], v_ref[...], start_ref, out_ref, lse_ref.at[0])


def attend(projected, start):
    rows, columns = projected.shape
    width = columns // 3
    pairs = width // PAIR
    return pl.pallas_call(
        attend_kernel,
        grid=(pairs,),
        in_specs=[
            pl.BlockSpec((rows, PAIR), lambda p: (0, p)),
            pl.BlockSpec((rows, PAIR), lambda p: (0, pairs + p)),
            pl.BlockSpec((rows, PAIR), lambda p: (0, 2 * pairs + p)),
            whole((1, rows)),
        ],
        out_specs=[
            pl.BlockSpec((rows, PAIR), lambda p: (0, p)),
            pl.BlockSpec((1, 2, rows), lambda p: (p, 0, 0)),
        ],
        out_shape=[
            jax.ShapeDtypeStruct((rows, width), F32),
            jax.ShapeDtypeStruct((pairs, 2, rows), F32),
        ],
        compiler_params=params(),
        name="attend",
    )(projected, projected, projected, start)


def attend_back_pair(query, key, value, grad, context, lse_ref, start_ref, dq_ref, dk_ref, dv_ref, dk_acc, dv_acc):
    scale = HEAD_DIM**-0.5
    scaled = query.astype(F32) * scale
    query = scaled.astype(BF16)
    query_t = scaled.T.astype(BF16)
    key_t = key.astype(F32).T.astype(BF16)
    grad_f = grad.astype(F32)
    grad_t = grad_f.T.astype(BF16)
    weighted_t = (grad_f * context).T
    dk_acc[...] = jnp.zeros_like(dk_acc)
    dv_acc[...] = jnp.zeros_like(dv_acc)
    for block in range(query.shape[0] // BLOCK):
        at = slice(block * BLOCK, (block + 1) * BLOCK)
        start = start_ref[:, at]
        outs = []
        for head in range(2):
            lanes = slice(head * HEAD_DIM, (head + 1) * HEAD_DIM)
            inner = col_sum(weighted_t[lanes, at])
            log_total = lse_ref[head : head + 1, at]
            grad_head = head_rows(grad_t[:, at], head)
            out = jnp.zeros((HEAD_DIM, BLOCK), F32)
            for keys, scores in score_parts(key, head_rows(query_t[:, at], head), start, block):
                soft = jnp.exp(scores - log_total)
                grad_scores = (soft * (nn(value[keys], grad_head) - inner)).astype(BF16)
                dv_acc[keys, :] += nn(soft.astype(BF16), head_cols(grad[at], head))
                dk_acc[keys, :] += nn(grad_scores, head_cols(query[at], head))
                out = out + nn(key_t[lanes, keys], grad_scores)
            outs.append(out)
        dq_ref[at, :] = (jnp.concatenate(outs, axis=0) * scale).T.astype(BF16)
    dk_ref[...] = dk_acc[...].astype(BF16)
    dv_ref[...] = dv_acc[...].astype(BF16)


def attend_back_kernel(q_ref, k_ref, v_ref, g_ref, o_ref, lse_ref, start_ref, dq_ref, dk_ref, dv_ref, dk_acc, dv_acc):
    attend_back_pair(
        q_ref[...], k_ref[...], v_ref[...], g_ref[...], o_ref[...], lse_ref.at[0], start_ref,
        dq_ref, dk_ref, dv_ref, dk_acc, dv_acc,
    )


def attend_back(projected, grad_context, context, lse, start):
    rows, columns = projected.shape
    width = columns // 3
    pairs = width // PAIR
    pair = pl.BlockSpec((rows, PAIR), lambda p: (0, p))
    return pl.pallas_call(
        attend_back_kernel,
        grid=(pairs,),
        in_specs=[
            pair,
            pl.BlockSpec((rows, PAIR), lambda p: (0, pairs + p)),
            pl.BlockSpec((rows, PAIR), lambda p: (0, 2 * pairs + p)),
            pair,
            pair,
            pl.BlockSpec((1, 2, rows), lambda p: (p, 0, 0)),
            whole((1, rows)),
        ],
        out_specs=[pair] * 3,
        out_shape=[jax.ShapeDtypeStruct((rows, width), BF16)] * 3,
        scratch_shapes=[pltpu.VMEM((rows, PAIR), F32), pltpu.VMEM((rows, PAIR), F32)],
        compiler_params=params(),
        name="attend_back",
    )(projected, projected, projected, grad_context, context, lse, start)


def gelu_parts(value):
    phi = 0.5 * (1.0 + lax.erf(value * (1.0 / math.sqrt(2.0))))
    bell = jnp.exp(-0.5 * value * value) * (1.0 / math.sqrt(2.0 * math.pi))
    return value * phi, phi + value * bell


def middle_kernel(
    x_ref, dy_ref, ctx_ref, alive_ref, rest_ref,
    sg_ref, ss_ref, ob_ref, fg_ref, fs_ref, ub_ref, mg_ref, ms_ref, db_ref,
    out_ref, ghid_ref, gctx_ref, mixed_ref, gbranch_ref, nffn_ref, gup_ref, mid_ref, gffn_ref,
    narrow_ref, wide_ref,
):
    step = pl.program_id(0)

    @pl.when(step == 0)
    def _():
        narrow_ref[...] = jnp.zeros_like(narrow_ref)
        wide_ref[...] = jnp.zeros_like(wide_ref)

    out_weight, up_weight, down_weight = split_rest(rest_ref)
    alive = alive_ref[...]
    ctx_hat, ctx_scale = normalized(ctx_ref[...])
    mixed = (ctx_hat * sg_ref[...] + ss_ref[...]).astype(BF16)
    mixed_ref[...] = mixed
    branch = nn(mixed, out_weight) + ob_ref[...]
    hidden = (x_ref[...].astype(F32) + alive * branch).astype(BF16).astype(F32)
    hid_hat, hid_scale = normalized(hidden)
    nffn = (hid_hat * fg_ref[...] + fs_ref[...]).astype(BF16)
    nffn_ref[...] = nffn
    upper = nn(nffn, up_weight) + ub_ref[...]
    active, slope = gelu_parts(upper)
    act_hat, act_scale = normalized(active)
    mid = (act_hat * mg_ref[...] + ms_ref[...]).astype(BF16)
    mid_ref[...] = mid
    result = (nn(mid, down_weight) + db_ref[...]).astype(BF16).astype(F32)
    out_ref[...] = hidden + alive * result

    upstream = dy_ref[...].astype(F32)
    gffn = (alive * upstream).astype(BF16)
    gffn_ref[...] = gffn
    gmid = nt(gffn, down_weight)
    gact = norm_back(act_hat, act_scale, mg_ref[...], gmid)
    gup = (gact * slope).astype(BF16)
    gup_ref[...] = gup
    wide_ref[0:1, :] += col_sum(gup.astype(F32))
    wide_ref[1:2, :] += col_sum(gmid * act_hat)
    wide_ref[2:3, :] += col_sum(gmid)
    gnffn = nt(gup, up_weight)
    ghid = (upstream + norm_back(hid_hat, hid_scale, fg_ref[...], gnffn)).astype(BF16)
    ghid_ref[...] = ghid
    gbranch = (alive * ghid.astype(F32)).astype(BF16)
    gbranch_ref[...] = gbranch
    gmixed = nt(gbranch, out_weight)
    gctx_ref[...] = norm_back(ctx_hat, ctx_scale, sg_ref[...], gmixed).astype(BF16)
    narrow_ref[0:1, :] += col_sum(gmixed * ctx_hat)
    narrow_ref[1:2, :] += col_sum(gmixed)
    narrow_ref[2:3, :] += col_sum(gbranch.astype(F32))
    narrow_ref[3:4, :] += col_sum(gnffn * hid_hat)
    narrow_ref[4:5, :] += col_sum(gnffn)
    narrow_ref[5:6, :] += col_sum(gffn.astype(F32))


def middle(x, dy, context, alive, rest, vectors):
    rows, width = x.shape
    hidden = 4 * width
    row = pl.BlockSpec((BLOCK, width), lambda i: (i, 0))
    row_wide = pl.BlockSpec((BLOCK, hidden), lambda i: (i, 0))
    once = dict(pipeline_mode=pl.Buffered(1))
    narrow = whole((1, width))
    wide = whole((1, hidden))
    def shape(columns, dtype):
        return jax.ShapeDtypeStruct((rows, columns), dtype)
    return pl.pallas_call(
        middle_kernel,
        grid=(rows // BLOCK,),
        in_specs=[
            row, row, row,
            pl.BlockSpec((BLOCK, 1), lambda i: (i, 0)),
            pl.BlockSpec(rest.shape, lambda i: (0, 0, 0), **once),
            narrow, narrow, narrow, narrow, narrow, wide, wide, wide, narrow,
        ],
        out_specs=[row, row, row, row, row, row, row_wide, row_wide, row, whole((8, width)), whole((8, hidden))],
        out_shape=[
            shape(width, F32), shape(width, BF16), shape(width, BF16), shape(width, BF16), shape(width, BF16),
            shape(width, BF16), shape(hidden, BF16), shape(hidden, BF16), shape(width, BF16),
            jax.ShapeDtypeStruct((8, width), F32), jax.ShapeDtypeStruct((8, hidden), F32),
        ],
        compiler_params=params(),
        name="middle",
    )(x, dy, context, alive, rest, *vectors)


def outer_kernel(left_ref, right_ref, out_ref):
    out_ref[...] = tn(left_ref[...], right_ref[...]).astype(out_ref.dtype)


def outer(left, right, tile, dtype, name):
    rows, across = left.shape
    columns = right.shape[1]
    return pl.pallas_call(
        outer_kernel,
        grid=(across // tile,),
        in_specs=[pl.BlockSpec((rows, tile), lambda i: (0, i)), whole((rows, columns))],
        out_specs=pl.BlockSpec((tile, columns), lambda i: (i, 0)),
        out_shape=jax.ShapeDtypeStruct((across, columns), dtype),
        compiler_params=params(),
        name=name,
    )(left, right)


def project_back_kernel(dq_ref, dk_ref, dv_ref, w_ref, x_ref, ghid_ref, gain_ref, out_ref, narrow_ref):
    step = pl.program_id(0)
    width = x_ref.shape[1]

    @pl.when(step == 0)
    def _():
        narrow_ref[...] = jnp.zeros_like(narrow_ref)

    dq, dk, dv = dq_ref[...], dk_ref[...], dv_ref[...]
    gnormed = nt(dq, w_ref[:, :width]) + nt(dk, w_ref[:, width : 2 * width]) + nt(dv, w_ref[:, 2 * width :])
    hat, scale = normalized(x_ref[...].astype(F32))
    out_ref[...] = ghid_ref[...].astype(F32) + norm_back(hat, scale, gain_ref[...], gnormed)
    narrow_ref[0:1, :] += col_sum(gnormed * hat)
    narrow_ref[1:2, :] += col_sum(gnormed)
    narrow_ref[2:3, :] += col_sum(dq.astype(F32))
    narrow_ref[3:4, :] += col_sum(dv.astype(F32))


def project_back(dq, dk, dv, weight, x, ghid, gain):
    rows, width = x.shape
    row = pl.BlockSpec((BLOCK, width), lambda i: (i, 0))
    return pl.pallas_call(
        project_back_kernel,
        grid=(rows // BLOCK,),
        in_specs=[row, row, row, whole(weight.shape), row, row, whole((1, width))],
        out_specs=[row, whole((8, width))],
        out_shape=[jax.ShapeDtypeStruct((rows, width), F32), jax.ShapeDtypeStruct((8, width), F32)],
        compiler_params=params(),
        name="project_back",
    )(dq, dk, dv, weight, x, ghid, gain)


def row_marks(lengths_row, count):
    slots = jnp.arange(lengths_row.shape[0], dtype=jnp.int32)
    ends = jnp.sum(jnp.where(slots[:, None] <= slots[None, :], lengths_row[:, None], 0), axis=0)
    index = jnp.arange(count, dtype=jnp.int32)
    before = jnp.where(ends[None, :] <= index[:, None], ends[None, :], 0)
    alive = index < jnp.max(ends)
    start = jnp.where(alive, jnp.max(before, axis=1), index)
    return alive.astype(F32)[:, None], start[None, :]


MESH = pl.DeviceIdType.MESH
BOX = (4, 2, 2)
CHIPS = 16
X_AT, Y_AT, D_AT, MOVES = 3, 7, 11, 15


class Place:
    def __init__(self):
        self.core = lax.axis_index("section")
        self.chip = lax.axis_index("dp")
        self.z, self.y, self.x = self.chip // 4, (self.chip // 2) % 2, self.chip % 2
        high, low = self.z // 2, self.z % 2
        self.zs = [self.z, self.z + 1 - 2 * low, self.z + 2 - 4 * high, 3 - self.z]

    def at(self, z, y, x):
        return (self.core, z * 4 + y * 2 + x)

    def sibling(self):
        return (1 - self.core, self.chip)

    def over_z(self, k):
        return self.at(self.zs[k], self.y, self.x)

    def over_y(self):
        return self.at(self.z, 1 - self.y, self.x)

    def over_x(self):
        return self.at(self.z, self.y, 1 - self.x)

    def across(self):
        return self.at(self.z, 1 - self.y, 1 - self.x)


def remote(source, target, sems, device):
    return pltpu.make_async_remote_copy(
        src_ref=source, dst_ref=target, send_sem=sems[0], recv_sem=sems[1], device_id=device, device_id_type=MESH
    )


def greet(me):
    barrier = pltpu.get_barrier_semaphore()
    others = [me.sibling(), me.over_x(), me.over_y(), me.across()] + [me.over_z(k) for k in (1, 2, 3)]
    for other in others:
        pl.semaphore_signal(barrier, inc=1, device_id=other, device_id_type=MESH)
    pl.semaphore_wait(barrier, len(others))


class Gather:
    def __init__(self, full, sems, pass_sems, direct=False):
        self.me = Place()
        self.direct = direct
        self.own = full.at[pl.ds(3 * self.me.core, 3)]
        self.other = full.at[pl.ds(3 * (1 - self.me.core), 3)]
        self.sems, self.pass_sems = sems, pass_sems

    def move(self, index, z, y, x, device):
        part = self.own.at[:, z, y, x]
        return remote(part, part, (self.sems.at[0, index], self.sems.at[1, index]), device)

    def to_z(self, k):
        me = self.me
        return self.move(k - 1, me.z, me.y, me.x, me.over_z(k))

    def to_x(self, k):
        me = self.me
        return self.move(X_AT + k, me.zs[k], me.y, me.x, me.over_x())

    def to_y(self, k):
        me = self.me
        return self.move(Y_AT + k, me.zs[k], me.y, me.x, me.over_y())

    def onward(self, k):
        me = self.me
        if self.direct:
            return self.move(D_AT + k, me.zs[k], me.y, me.x, me.across())
        if k < 2:
            return self.move(D_AT + k, me.zs[k], me.y, 1 - me.x, me.over_y())
        return self.move(D_AT + k, me.zs[k], 1 - me.y, me.x, me.over_x())

    def across_core(self, index, ref):
        me = self.me
        every = slice(None)
        place = [(every, me.y, 1 - me.x), (every, 1 - me.y, me.x), (every, 1 - me.y, 1 - me.x)]
        z, y, x = (me.zs[index + 1], me.y, me.x) if index < 3 else place[index - 3]
        part = ref.at[:, z, y, x]
        return remote(part, part, (self.pass_sems.at[0, index], self.pass_sems.at[1, index]), me.sibling())

    def launch(self):
        for k in (1, 2, 3):
            self.to_z(k).start()
        self.spread(0)

    def spread(self, k):
        self.to_x(k).start()
        self.to_y(k).start()
        if self.direct:
            self.onward(k).start()

    def from_z(self, k):
        self.to_z(k).wait_recv()
        self.spread(k)
        self.across_core(k - 1, self.own).start()

    def arrive(self, stage):
        if stage == 0:
            self.from_z(1)
            self.to_x(0).wait_recv()
            if not self.direct:
                self.onward(0).start()
        elif stage == 1:
            self.from_z(2)
            self.from_z(3)
            self.to_x(1).wait_recv()
            if not self.direct:
                self.onward(1).start()
        elif stage == 2:
            for k in (2, 3):
                self.to_y(k).wait_recv()
                if not self.direct:
                    self.onward(k).start()
            for k in (2, 3):
                self.to_x(k).wait_recv()
            for k in (0, 1):
                self.to_y(k).wait_recv()
            self.across_core(3, self.own).start()
            self.across_core(4, self.own).start()
        else:
            for k in range(4):
                self.onward(k).wait_recv()
            self.across_core(5, self.own).start()

    def passed(self):
        for index in range(6):
            self.across_core(index, self.other).wait_recv()

    def drain(self):
        for k in (1, 2, 3):
            self.to_z(k).wait_send()
        for k in range(4):
            for move in (self.to_x(k), self.to_y(k), self.onward(k)):
                move.wait_send()
        for index in range(6):
            self.across_core(index, self.own).wait_send()


def seed(parts, sems):
    me = Place()
    moves = []
    for index, (source, full, block, cols) in enumerate(parts):
        here = full.at[block, me.z, me.y, me.x, :, cols]
        local = pltpu.make_async_copy(source, here, sems.at[0, index])
        far = remote(source, here, (sems.at[1, index], sems.at[2, index]), me.sibling())
        moves.append((local, far))

    def begin():
        for local, far in moves:
            local.start()
            far.start()

    def sent():
        for local, far in moves:
            local.wait()
            far.wait_send()

    def got():
        for _, far in moves:
            far.wait_recv()

    return begin, sent, got


def lane_groups(value):
    groups = [value[:, at : at + 128] for at in range(0, value.shape[1], 128)]
    return functools.reduce(jnp.add, groups)


def as_row(ref):
    return ref[...].reshape(1, -1)


def lengths_of(lengths_ref, core):
    return [lengths_ref[core, slot] for slot in range(lengths_ref.shape[1])]


def alive_rows(lengths_ref, core, at, rows):
    index = at + lax.broadcasted_iota(jnp.int32, (rows, 1), 0)
    return (index < sum(lengths_of(lengths_ref, core))).astype(F32)


def start_row(lengths_ref, core, count):
    index = lax.broadcasted_iota(jnp.int32, (1, count), 1)
    start = jnp.zeros((1, count), jnp.int32)
    end = jnp.int32(0)
    for length in lengths_of(lengths_ref, core):
        end = end + length
        start = jnp.where(index >= end, end, start)
    return jnp.where(index < end, start, index)


def front_kernel(
    tokens_ref, upstream_ref, lengths_ref, half_ref, down_ref,
    pg_ref, ps_ref, qb_ref, vb_ref, sg_ref, ss_ref, ob_ref, fg_ref, fs_ref, ub_ref, mg_ref, ms_ref,
    projected_out, normed_out, context_out, lse_out, start_out, wq0_out, wq1_out, wuo_out, wd_ref,
    mixed_out, nffn_out, hidden_out, mid_out, hat_out, slope_out, scale_out, gdown_out,
    hidden, gffn, broad, hat, mid, normed, mixed, context, lse, start, wq0, wq1, wuo, mid_t, gdown, scales, active,
    seed_q0, seed_q1, seed_o, seed_u, seed_d, chain_q0, chain_q1, chain_u, chain_d, pass_q0, pass_q1, pass_u, pass_d,
    load_sems, save_sems, row_sems, grad_sems,
):
    me = Place()
    core = me.core
    rows, width = hidden.shape
    mine = half_ref.shape[0]
    pairs = width // PAIR
    co, cu, cd = width // 6, 2 * width // 3, width // 3
    cg = 3 * PAIR
    first = core == 0
    second = core == 1
    box = (slice(None),) * 3

    def group_parts(full, groups):
        return [
            (half_ref.at[:, n * width + (2 * g + c) * PAIR : n * width + (2 * g + c + 1) * PAIR],
             full, 3 * c + n, slice(at * PAIR, (at + 1) * PAIR))
            for at, g in enumerate(groups) for c in range(2) for n in range(3)
        ]

    q0_begin, q0_sent, q0_got = seed(group_parts(wq0, [0]), seed_q0)
    q1_begin, q1_sent, q1_got = seed(group_parts(wq1, [1, 2]), seed_q1)
    o_begin, o_sent, o_got = seed(
        [(half_ref.at[:, 3 * width + b * co : 3 * width + (b + 1) * co],
          wuo, b, slice(cu, cu + co)) for b in range(6)], seed_o)
    u_begin, u_sent, u_got = seed(
        [(half_ref.at[:, b * cu : (b + 1) * cu],
          wuo, b, slice(0, cu)) for b in range(6)], seed_u)

    def down_parts(which):
        return [
            (down_ref.at[n * mine : (n + 1) * mine, k * cd : (k + 1) * cd],
             wd_ref, 3 * which + k, slice(n * cd, (n + 1) * cd))
            for k in range(3) for n in range(2)
        ]

    d_begin, d_sent, _ = seed(down_parts(core), seed_d)
    _, _, d_got = seed(down_parts(1 - core), seed_d)

    gather_q0 = Gather(wq0, chain_q0, pass_q0, direct=True)
    gather_q1 = Gather(wq1, chain_q1, pass_q1)
    gather_u = Gather(wuo, chain_u, pass_u)
    gather_d = Gather(wd_ref, chain_d, pass_d)

    own_rows = pl.ds(pl.multiple_of(core * rows, rows), rows)
    loads = [
        pltpu.make_async_copy(tokens_ref.at[own_rows], hidden, load_sems.at[0]),
        pltpu.make_async_copy(upstream_ref.at[own_rows], gffn, load_sems.at[1]),
    ]
    loads[0].start()
    greet(me)
    pl.when(first)(q0_begin)
    pl.when(first)(q1_begin)
    pl.when(first)(o_begin)
    pl.when(second)(u_begin)
    d_begin()
    loads[1].start()
    pl.when(first)(q0_sent)
    pl.when(second)(q0_got)
    gather_q0.launch()

    loads[0].wait()
    value, _ = normalized(hidden[...].astype(F32))
    normed[...] = (value * as_row(pg_ref) + as_row(ps_ref)).astype(BF16)
    start[...] = start_row(lengths_ref, core, rows)
    saves = []

    def save(source, target):
        saves.append(pltpu.make_async_copy(source, target, save_sems.at[len(saves)]))
        saves[-1].start()

    save(normed, normed_out)
    save(start, start_out)
    @pl.when(first)
    def _():
        q1_sent()
        o_sent()
        u_got()

    @pl.when(second)
    def _():
        u_sent()
        q1_got()
        o_got()

    gather_q0.arrive(0)
    gather_q1.launch()
    gather_q0.arrive(1)
    gather_u.launch()
    gather_q0.arrive(2)
    gather_q1.arrive(0)
    gather_q0.arrive(3)
    d_sent()
    d_got()
    gather_q0.passed()

    query_bias, value_bias = as_row(qb_ref), as_row(vb_ref)

    def project_group(group, weights):
        biases = []
        for c in range(2):
            at = slice((2 * group + c) * PAIR, (2 * group + c + 1) * PAIR)
            biases += [query_bias[:, at], jnp.zeros((1, PAIR), F32), value_bias[:, at]]
        cols = slice(group * 2 * cg, (group + 1) * 2 * cg)
        weight = jnp.concatenate(weights, axis=1)
        broad[:, cols] = (nn(normed[...], weight) + jnp.concatenate(biases, axis=1)).astype(BF16)

    project_group(0, [wq0[b].reshape(width, PAIR) for b in range(6)])
    gather_q1.arrive(1)

    def one_pair(pair, carry):
        @pl.when(pair == 0)
        def _():
            gather_u.arrive(0)

        @pl.when(pair == 1)
        def _():
            gather_q1.arrive(2)

        @pl.when(pair == 2)
        def _():
            gather_q1.arrive(3)
            gather_q1.passed()
            gather_u.arrive(1)
            for group in range(1, 3):
                at = slice((group - 1) * PAIR, group * PAIR)
                project_group(group, [wq1[(b, *box, slice(None), at)].reshape(width, PAIR) for b in range(6)])
            pltpu.make_async_copy(broad.at[:, : 3 * width], projected_out, load_sems.at[0]).start()

        @pl.when(pair == 3)
        def _():
            gather_d.launch()

        @pl.when(pair == 4)
        def _():
            gather_u.arrive(2)

        @pl.when(pair == 5)
        def _():
            gather_d.arrive(0)

        at_q = pl.ds(pl.multiple_of(pair * cg, PAIR), PAIR)
        at_k = pl.ds(pl.multiple_of(pair * cg + PAIR, PAIR), PAIR)
        at_v = pl.ds(pl.multiple_of(pair * cg + 2 * PAIR, PAIR), PAIR)
        at_out = pl.ds(pl.multiple_of(pair * PAIR, PAIR), PAIR)
        attend_pair(broad[:, at_q], broad[:, at_k], broad[:, at_v], start, context.at[:, at_out], lse.at[pair])
        return carry

    lax.fori_loop(0, pairs, one_pair, 0)
    save(context, context_out)
    save(lse, lse_out)
    save(wq0, wq0_out)
    save(wq1, wq1_out)
    gather_u.arrive(3)
    gather_u.passed()
    save(wuo, wuo_out)
    loads[1].wait()
    pltpu.make_async_copy(broad.at[:, : 3 * width], projected_out, load_sems.at[0]).wait()
    saves[0].wait()

    def row_saves(step):
        at = pl.ds(pl.multiple_of(step * BLOCK, BLOCK), BLOCK)
        pieces = [(mixed, mixed_out), (normed, nffn_out), (hidden, hidden_out), (mid, mid_out), (hat, hat_out),
                  (broad, slope_out)]
        return [
            pltpu.make_async_copy(source.at[at], target.at[at], row_sems.at[index, step])
            for index, (source, target) in enumerate(pieces)
        ]

    def one_block(step, carry):
        at = pl.ds(pl.multiple_of(step * BLOCK, BLOCK), BLOCK)
        alive = alive_rows(lengths_ref, core, step * BLOCK, BLOCK)
        ctx_hat, _ = normalized(context[at, :])
        mix = (ctx_hat * as_row(sg_ref) + as_row(ss_ref)).astype(BF16)
        mixed[at, :] = mix
        out_weight = jnp.concatenate([wuo[(b, *box, slice(None), slice(cu, cu + co))].reshape(width, co) for b in range(6)], axis=1)
        branch = nn(mix, out_weight) + as_row(ob_ref)
        hid = (hidden[at, :].astype(F32) + alive * branch).astype(BF16)
        hidden[at, :] = hid
        hid_hat, _ = normalized(hid.astype(F32))
        nffn = (hid_hat * as_row(fg_ref) + as_row(fs_ref)).astype(BF16)
        normed[at, :] = nffn
        up_weight = jnp.concatenate([wuo[(b, *box, slice(None), slice(0, cu))].reshape(width, cu) for b in range(6)], axis=1)
        units = 4 * width
        chunks = [slice(c, c + width) for c in range(0, units, width)]
        up_bias, mid_gain, mid_shift = as_row(ub_ref), as_row(mg_ref), as_row(ms_ref)
        lanes = jnp.zeros((BLOCK, 128), F32)
        for cols in chunks:
            value, slope = gelu_parts(nn(nffn, up_weight[:, cols]) + up_bias[:, cols])
            broad[at, cols] = slope.astype(BF16)
            active[:, cols] = value
            lanes = lanes + lane_groups(value)
        center = jnp.sum(lanes, axis=-1, keepdims=True) * (1.0 / units)
        lanes = jnp.zeros((BLOCK, 128), F32)
        for cols in chunks:
            centered = active[:, cols] - center
            lanes = lanes + lane_groups(centered * centered)
        act_scale = lax.rsqrt(jnp.sum(lanes, axis=-1, keepdims=True) * (1.0 / units) + EPS)
        for cols in chunks:
            act_hat = (active[:, cols] - center) * act_scale
            hat[at, cols] = act_hat.astype(BF16)
            mid[at, cols] = (act_hat * mid_gain[:, cols] + mid_shift[:, cols]).astype(BF16)
        scales[at, :] = act_scale
        gffn[at, :] = (alive * gffn[at, :].astype(F32)).astype(BF16)
        for copy in row_saves(step):
            copy.start()

        @pl.when(step == 0)
        def _():
            gather_d.arrive(1)

        @pl.when(step == 3)
        def _():
            gather_d.arrive(2)

        return carry

    steps = rows // BLOCK
    lax.fori_loop(0, steps, one_block, 0)
    save(scales, scale_out)

    def grad_save(h, k):
        return pltpu.make_async_copy(gdown.at[k], gdown_out.at[3 * h + k], grad_sems.at[h, k])

    for h in range(2):
        mid_t[...] = mid[:, 2 * h * width : 2 * (h + 1) * width].T
        for k in range(3):
            grad = nn(mid_t[...], gffn[:, k * cd : (k + 1) * cd]).astype(BF16)
            grad = grad.reshape(CHIPS, 2, mine, cd)
            if h:
                grad_save(0, k).wait()
            for n in range(2):
                gdown[k, :, :, n * cd : (n + 1) * cd] = grad[:, n]
            grad_save(h, k).start()
    gather_d.arrive(3)
    for k in range(3):
        grad_save(1, k).wait()
    gather_d.passed()

    def finish(step, carry):
        for copy in row_saves(step):
            copy.wait()
        return carry

    lax.fori_loop(0, steps, finish, 0)
    for copy in saves[1:]:
        copy.wait()
    for gather in (gather_q0, gather_q1, gather_u, gather_d):
        gather.drain()


def front(tokens, upstream, lengths, half, down, vectors):
    width = tokens.shape[1]
    rows = tokens.shape[0] // 2
    mine = half.shape[0]
    box = BOX
    pairs = width // PAIR
    wide = 4 * width
    anywhere = pl.BlockSpec(memory_space=pl.ANY)
    vmem = pl.BlockSpec(memory_space=pltpu.VMEM)
    smem = pl.BlockSpec(memory_space=pltpu.SMEM)
    dma = pltpu.SemaphoreType.DMA
    sizes = dict(q0=PAIR, q1=2 * PAIR, u=5 * width // 6, d=2 * width // 3)
    shape = jax.ShapeDtypeStruct
    steps = rows // BLOCK
    return pl.pallas_call(
        front_kernel,
        in_specs=[anywhere, anywhere, smem, anywhere, anywhere] + [vmem] * len(vectors),
        out_specs=[anywhere] * 17,
        out_shape=[
            shape((rows, 3 * width), BF16), shape((rows, width), BF16), shape((rows, width), F32),
            shape((pairs, 2, rows), F32), shape((1, rows), jnp.int32),
            *[shape((6, *box, mine, columns), BF16) for columns in sizes.values()],
            shape((rows, width), BF16), shape((rows, width), BF16), shape((rows, width), BF16),
            shape((rows, wide), BF16), shape((rows, wide), BF16), shape((rows, wide), BF16), shape((rows, 1), F32),
            shape((6, CHIPS, mine, 2 * width // 3), BF16),
        ],
        scratch_shapes=[
            pltpu.VMEM((rows, width), BF16), pltpu.VMEM((rows, width), BF16), pltpu.VMEM((rows, wide), BF16),
            pltpu.VMEM((rows, wide), BF16), pltpu.VMEM((rows, wide), BF16), pltpu.VMEM((rows, width), BF16),
            pltpu.VMEM((rows, width), BF16), pltpu.VMEM((rows, width), F32), pltpu.VMEM((pairs, 2, rows), F32),
            pltpu.VMEM((1, rows), jnp.int32),
            *[pltpu.VMEM((6, *box, mine, sizes[name]), BF16) for name in ("q0", "q1", "u")],
            pltpu.VMEM((2 * width, rows), BF16), pltpu.VMEM((3, CHIPS, mine, 2 * width // 3), BF16),
            pltpu.VMEM((rows, 1), F32), pltpu.VMEM((BLOCK, wide), F32),
            dma((3, 6)), dma((3, 12)), dma((3, 6)), dma((3, 6)), dma((3, 6)),
            *[dma((2, MOVES))] * 4, *[dma((2, 6))] * 4,
            dma((2,)), dma((8,)), dma((6, steps)), dma((2, 3)),
        ],
        compiler_params=params(collective_id=1, has_side_effects=True),
        name="front",
    )(tokens, upstream, lengths, half, down, *vectors)


class Scatter:
    def __init__(self, total, landings, sems, final, direct=False):
        self.me = Place()
        self.direct = direct
        self.total, self.landings, self.sems, self.final = total, landings, sems, final

    def move(self, index, z, y, x, device):
        return remote(self.total.at[:, z, y, x], self.landings.at[index], (self.sems.at[0, index], self.sems.at[1, index]), device)

    def to_z(self, k):
        me = self.me
        return self.move(k - 1, me.zs[k], me.y, me.x, me.over_z(k))

    def to_x(self, k):
        me = self.me
        return self.move(X_AT + k, me.zs[k], me.y, 1 - me.x, me.over_x())

    def to_y(self, k):
        me = self.me
        return self.move(Y_AT + k, me.zs[k], 1 - me.y, me.x, me.over_y())

    def toward(self, k):
        me = self.me
        return self.move(D_AT + k, me.zs[k], 1 - me.y, 1 - me.x, me.across() if self.direct else me.over_y() if k < 2 else me.over_x())

    def add(self, z, y, x, landed):
        self.total[:, z, y, x] = functools.reduce(jnp.add, [part[...] for part in landed], self.total[:, z, y, x])

    def begin(self, other):
        me = self.me

        def both(z, y, x):
            self.add(z, y, x, [other.at[:, z, y, x]])

        if self.direct:
            for k in (2, 3, 1, 0):
                both(me.zs[k], 1 - me.y, 1 - me.x)
                self.toward(k).start()
                both(me.zs[k], me.y, 1 - me.x)
                self.to_x(k).start()
                both(me.zs[k], 1 - me.y, me.x)
                self.to_y(k).start()
                both(me.zs[k], me.y, me.x)
            return
        for k in range(4):
            both(me.zs[k], 1 - me.y, 1 - me.x)
            self.toward(k).start()
        for k in range(4):
            both(me.zs[k], me.y, 1 - me.x)
            both(me.zs[k], 1 - me.y, me.x)
            both(me.zs[k], me.y, me.x)

    def arrive(self, stage):
        me = self.me
        if self.direct and stage < 3:
            for k in ((2, 3), (1, 0), ())[stage]:
                moves = (self.toward(k), self.to_x(k), self.to_y(k))
                for move in moves:
                    move.wait_recv()
                self.add(me.zs[k], me.y, me.x, [self.landings.at[at + k] for at in (D_AT, X_AT, Y_AT)])
                if k:
                    self.to_z(k).start()
        elif stage == 0:
            for k in range(4):
                self.toward(k).wait_recv()
                if k < 2:
                    self.add(me.zs[k], me.y, 1 - me.x, [self.landings.at[D_AT + k]])
                else:
                    self.add(me.zs[k], 1 - me.y, me.x, [self.landings.at[D_AT + k]])
            for k in (2, 3):
                self.to_x(k).start()
                self.to_y(k).start()
        elif stage < 3:
            if stage == 1:
                for k in (1, 0):
                    self.to_x(k).start()
                    self.to_y(k).start()
            for k in (2, 3) if stage == 1 else (1, 0):
                self.to_x(k).wait_recv()
                self.to_y(k).wait_recv()
                self.add(me.zs[k], me.y, me.x, [self.landings.at[X_AT + k], self.landings.at[Y_AT + k]])
                if k:
                    self.to_z(k).start()
        else:
            value = self.total[:, me.z, me.y, me.x].astype(F32)
            for k in (1, 2, 3):
                self.to_z(k).wait_recv()
                value = value + self.landings[k - 1].astype(F32)
            self.final[...] = value

    def drain(self):
        for k in (1, 2, 3):
            self.to_z(k).wait_send()
        for k in range(4):
            for move in (self.to_x(k), self.to_y(k), self.toward(k)):
                move.wait_send()


class Total:
    def __init__(self, rows, landed, sems):
        me = Place()
        self.rows, self.landed, self.sems = rows, landed, sems
        self.partners = [
            [me.sibling()], [me.over_x(), me.over_y(), me.across()], [me.over_z(k) for k in (1, 2, 3)]
        ]

    def moves(self, stage):
        at = (0, 1, 4)[stage]
        return [
            remote(self.rows.at[stage], self.landed.at[at + n], (self.sems.at[0, at + n], self.sems.at[1, at + n]), device)
            for n, device in enumerate(self.partners[stage])
        ]

    def start(self, stage):
        for move in self.moves(stage):
            move.start()

    def arrive(self, stage):
        at = (0, 1, 4)[stage]
        value = self.rows[stage]
        for n, move in enumerate(self.moves(stage)):
            move.wait_recv()
            value = value + self.landed[at + n]
        self.rows[stage + 1] = value
        if stage < 2:
            self.start(stage + 1)

    def drain(self):
        for stage in range(3):
            for move in self.moves(stage):
                move.wait_send()


def feed_body(
    hidden_steps, upstream_ref, context_ref, hidden_ref, mid_ref, hat_ref, slope_ref, scale_ref, lengths_ref, wuo_any, wd_any,
    sg_ref, fg_ref, mg_ref, db_ref, gdown_ref,
    ghid_ref, gctx_ref, gbranch_ref, gup_ref, narrow_ref, wide_ref, layer_ref, down_ref,
    wuo_ref, wd_ref, out_rows, scaled_grad, total, landed, landings, final, swap_sems, chain_sems, local_sems, out_sems,
):
    me = Place()
    core = me.core
    step = pl.program_id(0)
    steps = pl.num_programs(0)
    width = hidden_ref.shape[1]
    mine = width // CHIPS
    co, cu, cd = width // 6, 2 * width // 3, width // 3
    sibling = me.sibling()
    scatter = Scatter(total, landings, chain_sems, final)
    own = pltpu.make_async_copy(gdown_ref.at[pl.ds(3 * core, 3)], total, local_sems.at[0])
    far = remote(gdown_ref.at[pl.ds(3 * (1 - core), 3)], landed, (swap_sems.at[0], swap_sems.at[1]), sibling)

    def out_copies(at_step, which):
        at = pl.ds(pl.multiple_of(at_step * BLOCK, BLOCK), BLOCK)
        target = layer_ref.at[which, at]
        return (pltpu.make_async_copy(out_rows.at[at], target, out_sems.at[0, at_step]),
                remote(out_rows.at[at], target, (out_sems.at[1, at_step], out_sems.at[2, at_step]), sibling))

    got_wd = pltpu.make_async_copy(wd_any, wd_ref, local_sems.at[1])
    got_wuo = pltpu.make_async_copy(wuo_any, wuo_ref, local_sems.at[2])

    @pl.when(step == 0)
    def _():
        got_wd.start()
        got_wuo.start()
        greet(me)
        far.start()
        own.start()
        got_wd.wait()
        narrow_ref[...] = jnp.zeros_like(narrow_ref)
        wide_ref[...] = jnp.zeros_like(wide_ref)

    def hook(at_step, action):
        pl.when(step == at_step)(action)

    def begin():
        own.wait()
        far.wait_recv()
        scatter.begin(landed)

    halves = []
    for h in range(2):
        parts = []
        for n in range(2):
            part = jnp.concatenate([wd_ref[3 * h + k, :, n * cd : (n + 1) * cd] for k in range(3)], axis=1)
            parts.append(part.reshape(CHIPS, 1, mine, width))
        halves.append(jnp.concatenate(parts, axis=1).reshape(2 * width, width))
    down_weight = jnp.concatenate(halves, axis=0)

    alive = alive_rows(lengths_ref, core, step * BLOCK, BLOCK)
    hidden = hidden_ref[...].astype(F32)
    upstream = upstream_ref[...].astype(F32)
    gffn = (alive * upstream).astype(BF16)
    mid_gain = as_row(mg_ref)
    units = 4 * width
    chunks = [slice(at, at + width) for at in range(0, units, width)]
    first_sum = jnp.zeros((BLOCK, 128), F32)
    second_sum = jnp.zeros((BLOCK, 128), F32)
    for cols in chunks:
        gmid = nt(gffn, down_weight[cols])
        weighted = gmid * hat_ref[:, cols].astype(F32)
        wide_ref[1:2, cols] += col_sum(weighted)
        wide_ref[2:3, cols] += col_sum(gmid)
        scaled = gmid * mid_gain[:, cols]
        scaled_grad[:, cols] = scaled
        first_sum = first_sum + lane_groups(scaled)
        second_sum = second_sum + lane_groups(weighted * mid_gain[:, cols])
    first_mean = jnp.sum(first_sum, axis=-1, keepdims=True) * (1.0 / units)
    second_mean = jnp.sum(second_sum, axis=-1, keepdims=True) * (1.0 / units)
    hook(0, begin)
    hook(0, got_wuo.wait)
    up_weight = jnp.concatenate([wuo_ref[b, :, :cu] for b in range(6)], axis=1)
    out_weight = jnp.concatenate([wuo_ref[b, :, cu:] for b in range(6)], axis=1)
    hook(1, lambda: scatter.arrive(0))
    hook(2, lambda: scatter.arrive(1))
    hook(3, lambda: scatter.arrive(2))
    act_scale = scale_ref[...]
    gnffn = jnp.zeros((BLOCK, width), F32)
    result = jnp.zeros((BLOCK, width), F32)
    for cols in chunks:
        act_hat = hat_ref[:, cols].astype(F32)
        gact = (scaled_grad[:, cols] - first_mean - act_hat * second_mean) * act_scale
        gup = (gact * slope_ref[:, cols].astype(F32)).astype(BF16)
        gup_ref[:, cols] = gup
        wide_ref[0:1, cols] += col_sum(gup.astype(F32))
        gnffn = gnffn + nt(gup, up_weight[:, cols])
        result = result + nn(mid_ref[:, cols], down_weight[cols])
    result = (result + as_row(db_ref)).astype(BF16).astype(F32)
    out_rows[pl.ds(pl.multiple_of(step * BLOCK, BLOCK), BLOCK), :] = hidden + alive * result
    for copy in out_copies(step, core):
        copy.start()
    hid_hat, hid_scale = normalized(hidden)
    ghid = (upstream + norm_back(hid_hat, hid_scale, as_row(fg_ref), gnffn)).astype(BF16)
    ghid_ref[...] = ghid
    gbranch = (alive * ghid.astype(F32)).astype(BF16)
    gbranch_ref[...] = gbranch
    gmixed = nt(gbranch, out_weight)
    ctx_hat, ctx_scale = normalized(context_ref[...])
    gctx_ref[...] = norm_back(ctx_hat, ctx_scale, as_row(sg_ref), gmixed).astype(BF16)
    narrow_ref[0:1, :] += col_sum(gmixed * ctx_hat)
    narrow_ref[1:2, :] += col_sum(gmixed)
    narrow_ref[2:3, :] += col_sum(gbranch.astype(F32))
    narrow_ref[3:4, :] += col_sum(gnffn * hid_hat)
    narrow_ref[4:5, :] += col_sum(gnffn)
    narrow_ref[5:6, :] += col_sum(gffn.astype(F32))

    @pl.when(step == steps - 1)
    def _():
        scatter.arrive(3)
        for k in range(3):
            for n in range(2):
                down_ref[n * mine : (n + 1) * mine, k * cd : (k + 1) * cd] = final[k, :, n * cd : (n + 1) * cd]
        for index in range(hidden_steps):
            local, away = out_copies(index, core)
            local.wait()
            away.wait_send()
            out_copies(index, 1 - core)[1].wait_recv()
        far.wait_send()
        scatter.drain()


def feed(upstream, context, hidden, mid, hat, slope, scale, lengths, wuo, wd, vectors, gdown):
    rows, width = hidden.shape
    wide = 4 * width
    steps = rows // BLOCK
    box = BOX
    mine = width // CHIPS
    columns = 2 * width // 3
    row = pl.BlockSpec((BLOCK, width), lambda i: (i, 0))
    row_wide = pl.BlockSpec((BLOCK, wide), lambda i: (i, 0))
    once = dict(pipeline_mode=pl.Buffered(1))
    anywhere = pl.BlockSpec(memory_space=pl.ANY)
    vmem = pl.BlockSpec(memory_space=pltpu.VMEM)
    smem = pl.BlockSpec(memory_space=pltpu.SMEM)
    dma = pltpu.SemaphoreType.DMA
    shape = jax.ShapeDtypeStruct

    def held(*size, dtype=BF16):
        return pltpu.VMEM(size, dtype)

    return pl.pallas_call(
        functools.partial(feed_body, steps),
        grid=(steps,),
        in_specs=[
            pl.BlockSpec((BLOCK, width), lambda i: (lax.axis_index("section") * steps + i, 0)),
            row, row, row_wide, row_wide, row_wide, pl.BlockSpec((BLOCK, 1), lambda i: (i, 0)), smem,
            anywhere, anywhere, *[vmem] * 4, anywhere,
        ],
        out_specs=[row, row, row, row_wide, whole((8, width)), whole((8, wide)), anywhere, vmem],
        out_shape=[
            shape((rows, width), BF16), shape((rows, width), BF16), shape((rows, width), BF16), shape((rows, wide), BF16),
            shape((8, width), F32), shape((8, wide), F32), shape((2, rows, width), F32), shape((2 * mine, width), F32),
        ],
        scratch_shapes=[
            held(*wuo.shape), held(*wd.shape), held(rows, width, dtype=F32), held(BLOCK, wide, dtype=F32),
            held(3, *box, mine, columns), held(3, *box, mine, columns),
            held(MOVES, 3, mine, columns),
            held(3, mine, columns, dtype=F32),
            dma((2,)), dma((2, MOVES)), dma((3,)), dma((3, steps)),
        ],
        compiler_params=params(collective_id=3, has_side_effects=True),
        name="feed",
    )(upstream, context, hidden, mid, hat, slope, scale, lengths, wuo, wd, *vectors,
      gdown.reshape((6,) + box + (mine, columns)))


def finish_kernel(*refs):
    layer_ref, grad_ref, half_ref, down_ref, slim_ref, broad_ref = refs[:6]
    layer_out, grad_out, half_out, down_out = refs[6:10]
    small, (layer, grad, half, down, sems) = refs[10:23], refs[23:]
    pieces = []
    for source, held, target, parts in (
        (layer_ref, layer, layer_out, 4), (grad_ref, grad, grad_out, 2), (half_ref, half, half_out, 1), (down_ref, down, down_out, 1)
    ):
        rows = source.shape[0] // parts
        for part in range(parts):
            at = pl.ds(part * rows, rows)
            n = len(pieces)
            pieces.append((pltpu.make_async_copy(source.at[at], held.at[at], sems.at[0, n]),
                           pltpu.make_async_copy(held.at[at], target.at[at], sems.at[1, n])))
    for get, _ in pieces:
        get.start()
    for row, out in zip((0, 1, 2, 3, 8, 9, 10, 11, 12, 13), small[:10]):
        out[...] = slim_ref[row, : out.shape[0]]
    for row, out in enumerate(small[10:]):
        out[...] = broad_ref[row, : out.shape[0]]
    for get, put in pieces:
        get.wait()
        put.start()
    for _, put in pieces:
        put.wait()


def finish(layer, grad, half, down, slim, broad, narrow_share, wide_share):
    anywhere = pl.BlockSpec(memory_space=pl.ANY)
    vmem = pl.BlockSpec(memory_space=pltpu.VMEM)
    shape = jax.ShapeDtypeStruct
    big = [layer, grad, half, down]
    sizes = [narrow_share] * 10 + [wide_share] * 3
    return pl.pallas_call(
        finish_kernel,
        in_specs=[anywhere] * 4 + [vmem] * 2,
        out_specs=[anywhere] * 4 + [vmem] * len(sizes),
        out_shape=[shape(array.shape, F32) for array in big] + [shape((size,), F32) for size in sizes],
        scratch_shapes=[pltpu.VMEM(array.shape, F32) for array in big] + [pltpu.SemaphoreType.DMA((2, 14))],
        compiler_params=params(),
        name="finish",
    )(layer, grad, half, down, slim, broad)


def back_kernel(
    projected_any, gctx_any, context_any, lse_ref, start_ref, normed_any, tokens_any, ghid_any, gain_ref, wq0_any, wq1_any,
    narrow_ref, wide_ref, nffn_any, mixed_any, gup_any, gbranch_any,
    grad_ref, half_ref, slim_ref, broad_ref,
    projected_ref, gctx_ref, context_ref, ghid_ref, wq0_ref, wq1_ref, spare, gup_far, gbranch, mixed_t, far_r,
    x_rows, dproj, dk_acc, dv_acc, normed_t, near_rows, far_rows,
    total_r, first_r, landings_r, final_r, other_r,
    total_q, far_q, first_q, landings_q, final_q, other_q,
    early, early_in, late, late_in,
    load_sems, swap_sems, far_sems, chain_r, chain_q, early_sems, late_sems, row_sems,
):
    me = Place()
    core = me.core
    rows, width = x_rows.shape
    mine = half_ref.shape[0]
    pairs = width // PAIR
    co, cu, cq = width // 6, 2 * width // 3, width // 2
    cg = 3 * PAIR
    sibling = me.sibling()
    first = core == 0
    second = core == 1

    def swap(index, source, target):
        return remote(source, target, (swap_sems.at[0, index], swap_sems.at[1, index]), sibling)

    sum_r = Scatter(total_r, landings_r, chain_r, final_r)
    sum_q = [Scatter(total_q.at[g], landings_q.at[g], chain_q.at[g], final_q.at[g], direct=True) for g in range(3)]

    loads = []

    def load(source, target):
        loads.append(pltpu.make_async_copy(source, target, load_sems.at[len(loads)]))
        loads[-1].start()
        return loads[-1]

    half = 2 * width
    far_cols = pl.ds(pl.multiple_of((1 - core) * half, PAIR), half)
    own_cols = pl.ds(pl.multiple_of(core * half, PAIR), half)
    got_nffn = load(nffn_any, x_rows)
    got_mixed = load(mixed_any, spare)
    got_far = load(gup_any.at[:, far_cols], gup_far)
    got_branch = load(gbranch_any, gbranch)
    got_own = load(gup_any.at[:, own_cols], dproj.at[:, :half])
    later = [
        load(source, target)
        for source, target in ((projected_any, projected_ref), (gctx_any, gctx_ref), (context_any, context_ref))
    ]
    greet(me)
    early_sum = Total(early, early_in, early_sems)
    late_sum = Total(late, late_in, late_sems)
    early[0] = jnp.zeros_like(early[0])
    early[0, 0:6, :] = narrow_ref[0:6, :]
    for n in range(3):
        for part in range(4):
            row = 8 + 4 * n + part
            early[0, row : row + 1, :] = wide_ref[n : n + 1, part * width : (part + 1) * width]
    early_sum.start(0)
    got_nffn.wait()
    normed_t[...] = x_rows[...].T
    got_x = load(tokens_any.at[pl.ds(pl.multiple_of(core * rows, rows), rows)], x_rows)
    got_mixed.wait()
    mixed_t[...] = spare[...].T
    got_normed = load(normed_any, spare)
    last = [
        load(source, target)
        for source, target in ((ghid_any, ghid_ref), (wq0_any, wq0_ref), (wq1_any, wq1_ref))
    ]

    def up_out(source, k, block, target):
        up = nn(normed_t[...], source[:, k * cu : (k + 1) * cu]).astype(BF16)
        at = pl.ds(pl.multiple_of(block * co, PAIR), co)
        out = nn(mixed_t[...], gbranch[:, at]).astype(BF16)
        target[k, :, :, :, :, :cu] = up.reshape(BOX + (mine, cu))
        target[k, :, :, :, :, cu:] = out.reshape(BOX + (mine, co))

    def swap_far(k):
        return remote(far_r.at[k], first_r.at[k], (far_sems.at[0, k], far_sems.at[1, k]), sibling)

    got_far.wait()
    got_branch.wait()
    for k in range(3):
        up_out(gup_far, k, 3 * (1 - core) + k, far_r)
        swap_far(k).start()
    got_own.wait()
    for k in range(3):
        up_out(dproj, k, 3 * core + k, total_r)
    for k in range(3):
        swap_far(k).wait_recv()
    sum_r.begin(first_r)
    got_normed.wait()
    normed_t[...] = spare[...].T
    for copy in later:
        copy.wait()

    def swap_q(group):
        return swap(3 + group, far_q.at[group], first_q.at[group])

    def make(group):
        for which, target in ((1 - core, far_q), (core, total_q)):
            at = pl.ds(pl.multiple_of(group * 2 * cg + which * cg, PAIR), cg)
            grad = nn(normed_t[...], dproj[:, at]).astype(BF16)
            for n in range(3):
                target[group, n] = grad[:, n * PAIR : (n + 1) * PAIR].reshape(BOX + (mine, PAIR))
            if target is far_q:
                swap_q(group).start()

    def begin(group):
        swap_q(group).wait_recv()
        sum_q[group].begin(first_q.at[group])

    def one_pair(pair, carry):
        @pl.when(pair == 1)
        def _():
            early_sum.arrive(0)

        @pl.when(pair == 2)
        def _():
            make(0)
            sum_r.arrive(0)

        @pl.when(pair == 3)
        def _():
            begin(0)
            early_sum.arrive(1)

        @pl.when(pair == 4)
        def _():
            sum_r.arrive(1)
            make(1)

        @pl.when(pair == 5)
        def _():
            begin(1)

        at_q = pl.ds(pl.multiple_of(pair * cg, PAIR), PAIR)
        at_k = pl.ds(pl.multiple_of(pair * cg + PAIR, PAIR), PAIR)
        at_v = pl.ds(pl.multiple_of(pair * cg + 2 * PAIR, PAIR), PAIR)
        at_c = pl.ds(pl.multiple_of(pair * PAIR, PAIR), PAIR)
        attend_back_pair(
            projected_ref[:, at_q], projected_ref[:, at_k], projected_ref[:, at_v], gctx_ref[:, at_c],
            context_ref[:, at_c], lse_ref.at[pair], start_ref,
            dproj.at[:, at_q], dproj.at[:, at_k], dproj.at[:, at_v], dk_acc, dv_acc,
        )
        return carry

    lax.fori_loop(0, pairs, one_pair, 0)
    make(2)
    early_sum.arrive(2)
    sum_q[0].arrive(0)
    sum_q[1].arrive(0)
    sum_r.arrive(2)
    begin(2)
    got_x.wait()
    for copy in last:
        copy.wait()
    late[0] = jnp.zeros_like(late[0])

    def row_copies(step, which):
        at = pl.ds(pl.multiple_of(step * BLOCK, BLOCK), BLOCK)
        target = grad_ref.at[which, at]
        return (pltpu.make_async_copy(near_rows.at[at], target, row_sems.at[0, step]),
                remote(far_rows.at[at], target, (row_sems.at[1, step], row_sems.at[2, step]), sibling))

    def one_block(step, carry):
        at = pl.ds(pl.multiple_of(step * BLOCK, BLOCK), BLOCK)
        gnormed = jnp.zeros((BLOCK, width), F32)
        for group in range(3):
            if group == 0:
                blocks = [wq0_ref[b].reshape(width, PAIR) for b in range(6)]
            else:
                cols = slice((group - 1) * PAIR, group * PAIR)
                blocks = [wq1_ref[(b,) + (slice(None),) * 4 + (cols,)].reshape(width, PAIR) for b in range(6)]
            weight = jnp.concatenate(blocks, axis=1)
            gnormed = gnormed + nt(dproj[at, group * 2 * cg : (group + 1) * 2 * cg], weight)
        hat, scale = normalized(x_rows[at, :].astype(F32))
        grad_x = ghid_ref[at, :].astype(F32) + norm_back(hat, scale, as_row(gain_ref), gnormed)

        @pl.when(first)
        def _():
            near_rows[at, :] = grad_x[:, :cq]
            far_rows[at, :] = grad_x[:, cq:]

        @pl.when(second)
        def _():
            near_rows[at, :] = grad_x[:, cq:]
            far_rows[at, :] = grad_x[:, :cq]

        for copy in row_copies(step, core):
            copy.start()

        late[0, 0:1, :] += col_sum(gnormed * hat)
        late[0, 1:2, :] += col_sum(gnormed)
        for row, part in ((2, 0), (3, 2)):
            grads = [dproj[at, p * cg + part * PAIR : p * cg + (part + 1) * PAIR].astype(F32) for p in range(pairs)]
            late[0, row : row + 1, :] += col_sum(jnp.concatenate(grads, axis=1))

        @pl.when(step == 1)
        def _():
            sum_q[0].arrive(1)
            sum_q[1].arrive(1)

        @pl.when(step == 3)
        def _():
            sum_q[2].arrive(0)

        return carry

    lax.fori_loop(0, rows // BLOCK, one_block, 0)
    late_sum.start(0)
    sum_q[2].arrive(1)
    late_sum.arrive(0)
    sum_r.arrive(3)
    swap_r = swap(2, final_r, other_r)
    swap_r.start()
    sum_q[0].arrive(3)
    sum_q[1].arrive(3)
    late_sum.arrive(1)
    sum_q[2].arrive(3)
    swap_f = swap(6, final_q, other_q)
    swap_f.start()
    late_sum.arrive(2)
    swap_r.wait_recv()

    share = core * CHIPS + me.chip

    def pick(values, each):
        size = values.shape[1]
        return pltpu.roll(values, (size - share * each) % size, 1)[:, :128]

    shares = 2 * CHIPS
    sums = early[3]
    rows_of = [jnp.concatenate([sums[8 + 4 * n + part : 9 + 4 * n + part] for part in range(4)], axis=1) for n in range(3)]
    broad_ref[...] = pick(jnp.concatenate(rows_of + [jnp.zeros((5, 4 * width), F32)], axis=0), 4 * width // shares)
    slim_ref[8:16, :] = pick(sums[0:8], width // shares)
    slim_ref[0:8, :] = pick(late[3], width // shares)

    swap_f.wait_recv()

    @pl.when(first)
    def _():
        for k in range(3):
            for g in range(3):
                for c, source in ((0, final_q), (1, other_q)):
                    at = k * width + (2 * g + c) * PAIR
                    half_ref[:, at : at + PAIR] = source[g, k]
            half_ref[:, 3 * width + k * co : 3 * width + (k + 1) * co] = final_r[k, :, cu:]
            half_ref[:, 3 * width + (3 + k) * co : 3 * width + (4 + k) * co] = other_r[k, :, cu:]

    @pl.when(second)
    def _():
        for k in range(3):
            half_ref[:, k * cu : (k + 1) * cu] = other_r[k, :, :cu]
            half_ref[:, (3 + k) * cu : (4 + k) * cu] = final_r[k, :, :cu]

    for step in range(rows // BLOCK):
        near, far = row_copies(step, core)
        near.wait()
        far.wait_send()
        row_copies(step, 1 - core)[1].wait_recv()
    for done in (swap_far(0), swap_far(1), swap_far(2), swap_r, swap_f, swap_q(0), swap_q(1), swap_q(2)):
        done.wait_send()
    early_sum.drain()
    late_sum.drain()
    for each in [sum_r] + sum_q:
        each.drain()


def back(projected, gctx, context, lse, start, normed, tokens, ghid, gain, wq0, wq1, narrow, wide, nffn, mixed, gup, gbranch):
    rows, width = normed.shape
    box = BOX
    mine = width // CHIPS
    cq, cr = width // 2, 5 * width // 6
    anywhere = pl.BlockSpec(memory_space=pl.ANY)
    vmem = pl.BlockSpec(memory_space=pltpu.VMEM)
    dma = pltpu.SemaphoreType.DMA

    def held(*shape, dtype=BF16):
        return pltpu.VMEM(shape, dtype)

    return pl.pallas_call(
        back_kernel,
        in_specs=[anywhere] * 3 + [vmem] * 2 + [anywhere] * 3 + [vmem] + [anywhere] * 2 + [vmem] * 2 + [anywhere] * 4,
        out_specs=[anywhere] + [vmem] * 3,
        out_shape=[
            jax.ShapeDtypeStruct((2, rows, cq), F32),
            jax.ShapeDtypeStruct((mine, 4 * width), F32),
            jax.ShapeDtypeStruct((16, 128), F32),
            jax.ShapeDtypeStruct((8, 128), F32),
        ],
        scratch_shapes=[
            held(rows, 3 * width), held(rows, width), held(rows, width, dtype=F32), held(rows, width),
            held(*wq0.shape), held(*wq1.shape), held(rows, width), held(rows, 2 * width), held(rows, width),
            held(width, rows), held(3, *box, mine, cr),
            held(rows, width), held(rows, 3 * width), held(rows, PAIR, dtype=F32), held(rows, PAIR, dtype=F32),
            held(width, rows), held(rows, cq, dtype=F32), held(rows, cq, dtype=F32),
            held(3, *box, mine, cr), held(3, *box, mine, cr), held(MOVES, 3, mine, cr),
            held(3, mine, cr, dtype=F32), held(3, mine, cr, dtype=F32),
            held(3, 3, *box, mine, PAIR), held(3, 3, *box, mine, PAIR), held(3, 3, *box, mine, PAIR),
            held(3, MOVES, 3, mine, PAIR),
            held(3, 3, mine, PAIR, dtype=F32), held(3, 3, mine, PAIR, dtype=F32),
            held(4, 24, width, dtype=F32), held(7, 24, width, dtype=F32),
            held(4, 8, width, dtype=F32), held(7, 8, width, dtype=F32),
            dma((13,)), dma((2, 7)), dma((2, 3)), dma((2, MOVES)), dma((3, 2, MOVES)), dma((2, 7)), dma((2, 7)), dma((3, 4)),
        ],
        compiler_params=params(collective_id=2, has_side_effects=True),
        name="back",
    )(projected, gctx, context, lse, start, normed, tokens, ghid, gain, wq0, wq1, narrow, wide, nffn, mixed, gup, gbranch)


def fused_batch(tokens, out_grad, lengths, half, down, vectors):
    (pre_gain, pre_shift, query_bias, value_bias, sub_gain, sub_shift, out_bias,
     ffn_gain, ffn_shift, up_bias, mid_gain, mid_shift, down_bias) = vectors
    width = tokens.shape[1]
    (projected, normed, context, lse, start, wq0, wq1, wuo, wd, mixed, nffn, hidden, mid, hat, slope, scale, gdown) = front(
        tokens, out_grad, lengths, half, down,
        (pre_gain, pre_shift, query_bias, value_bias, sub_gain, sub_shift, out_bias, ffn_gain, ffn_shift, up_bias,
         mid_gain, mid_shift),
    )
    ghid, gctx, gbranch, gup, narrow, wide, layer, down_grad = feed(
        out_grad, context, hidden, mid, hat, slope, scale, lengths, wuo.reshape(6, width, -1), wd.reshape(6, width, -1),
        (sub_gain, ffn_gain, mid_gain, down_bias), gdown,
    )
    grad_x, half_grad, slim, broad = back(
        projected, gctx, context, lse, start, normed, tokens, ghid, pre_gain, wq0, wq1, narrow, wide,
        nffn, mixed, gup, gbranch,
    )
    shares = 2 * CHIPS
    layer, grad_x, half_grad, down_grad, *small = finish(
        layer.reshape(-1, width), grad_x.reshape(-1, width // 2), half_grad, down_grad, slim, broad,
        width // shares, 4 * width // shares,
    )
    return layer, grad_x, half_grad[None], down_grad, *small[:9], *small[10:], small[9]


def unpacked(vectors):
    return [vector[None, :] for vector in vectors]


def marks_and_bias(x, lengths_row, query_bias, value_bias):
    alive, start = row_marks(lengths_row, x.shape[0])
    bias = jnp.concatenate([query_bias, jnp.zeros_like(query_bias), value_bias], axis=1)
    return alive, start, bias


def one_batch(x, dy, lengths_row, qkv, rest, vectors):
    (pre_gain, pre_shift, query_bias, value_bias, sub_gain, sub_shift, out_bias,
     ffn_gain, ffn_shift, up_bias, mid_gain, mid_shift, down_bias) = unpacked(vectors)
    alive, start, bias = marks_and_bias(x, lengths_row, query_bias, value_bias)
    projected, normed = project(x, qkv, pre_gain, pre_shift, bias)
    context, lse = attend(projected, start)
    out, ghid, gctx, mixed, gbranch, nffn, gup, mid, gffn, narrow, wide = middle(
        x, dy, context, alive, rest,
        (sub_gain, sub_shift, out_bias, ffn_gain, ffn_shift, up_bias, mid_gain, mid_shift, down_bias),
    )
    grad_up = outer(nffn, gup, 256, F32, "outer_up")
    grad_down = outer(mid, gffn, 512, F32, "outer_down")
    dq, dk, dv = attend_back(projected, gctx, context, lse, start)
    grad_out = outer(mixed, gbranch, 256, F32, "outer_out")
    grad_x, pre = project_back(dq, dk, dv, qkv, x, ghid, pre_gain)
    grads = [outer(normed, d, 256, F32, "outer_qkv") for d in (dq, dk, dv)]
    grad_attention = jnp.concatenate(grads + [grad_out], axis=1)
    small = (pre[0], pre[1], pre[2], pre[3], narrow[0], narrow[1], narrow[2], narrow[3], narrow[4],
             wide[0], wide[1], wide[2], narrow[5])
    return (out, grad_x), (grad_attention, grad_up, grad_down, small)


def shards(tokens, out_grad, seq_lengths, half_weights, down_weight, *all_vectors):
    section = lax.axis_index("section")
    sections = lax.axis_size("section")
    both = ("section", "dp")
    width = tokens.shape[1]
    batches = seq_lengths.shape[0]
    count = tokens.shape[0] // batches
    own_batches = batches // sections
    own_rows = own_batches * count
    hidden_units = half_weights.shape[2]
    shares = sections * lax.axis_size("dp")

    if (
        sections == 2
        and shares == sections * CHIPS
        and own_batches == 1
        and half_weights.shape[1] % 16 == 0
        and down_weight.shape[0] == 2 * half_weights.shape[1]
        and hidden_units == 4 * width
    ):
        return fused_batch(tokens, out_grad, seq_lengths, half_weights[0], down_weight, all_vectors)

    def own(array, rows):
        return lax.dynamic_slice_in_dim(array, section * rows, rows, axis=0)

    x_rows = own(tokens, own_rows)
    dy_rows = own(out_grad, own_rows)
    lengths = own(seq_lengths, own_batches)
    blocks = lax.all_gather(half_weights[0], both, axis=0, tiled=True)
    blocks = blocks.reshape(sections, width, hidden_units)
    down_full = lax.all_gather(down_weight, both, axis=0, tiled=True)
    qkv = blocks[0][:, : 3 * width]

    def in_blocks(array):
        return array.reshape(array.shape[0], 6, -1).transpose(1, 0, 2)

    down_blocks = down_full.reshape(2, CHIPS, 2, width // CHIPS, 3, width // 3).transpose(0, 4, 1, 3, 2, 5)
    down_blocks = down_blocks.reshape(6, width, 2 * width // 3)
    rest = jnp.concatenate([in_blocks(blocks[1]), in_blocks(blocks[0][:, 3 * width :]), down_blocks], axis=2)
    rows, sums = [], None
    for index in range(own_batches):
        at = slice(index * count, (index + 1) * count)
        row, more = one_batch(x_rows[at], dy_rows[at], lengths[index], qkv, rest, all_vectors)
        rows.append(row)
        sums = more if sums is None else jax.tree.map(jnp.add, sums, more)
    out_block = jnp.concatenate([row[0] for row in rows], axis=0)
    grad_rows = jnp.concatenate([row[1] for row in rows], axis=0)
    grad_attention, grad_up, grad_down, vectors = sums

    block_part = lax.psum_scatter(
        jnp.concatenate([grad_attention, grad_up], axis=0), both, scatter_dimension=0, tiled=True
    )
    down_part = lax.psum_scatter(grad_down, both, scatter_dimension=0, tiled=True)
    packed = jnp.concatenate([vector.reshape(shares, -1) for vector in vectors], axis=1)
    packed = lax.psum_scatter(packed, both, scatter_dimension=0, tiled=True).reshape(-1)
    parts, start = [], 0
    for vector in vectors:
        size = vector.shape[0] // shares
        parts.append(packed[start : start + size])
        start += size

    layer_out = lax.all_gather(out_block, "section", axis=0, tiled=True)
    tokens_grad = lax.all_to_all(grad_rows, "section", split_axis=1, concat_axis=0, tiled=True)
    return (layer_out, tokens_grad, block_part[None], down_part, *parts)


def solution(mesh):
    replicated = P()
    return jax.shard_map(
        shards,
        mesh=mesh,
        in_specs=(P("dp", None), P("dp", None), P("dp", None), P("section", "dp", None), P(("section", "dp"), None))
        + (replicated,) * 13,
        out_specs=(P("dp", None), P("dp", "section"), P("section", "dp", None), P(("section", "dp"), None))
        + (P(("section", "dp")),) * 13,
        check_vma=False,
    )
```
